32 devices in a mesh: dp: 4 (over y, x), ctx: 2 (over core), tensor: 4 (over z).
Axes of the slice: x: 2, y: 2, z: 4, core: 2. Of those that a mesh axis runs over, the one named last changes fastest.
Arguments:
- hidden_in: bfloat16 [4, 1024, 1024], P('dp', 'ctx'), may hold values from -6 to 6
- teacher: bfloat16 [4, 1024, 1024], P('dp', 'ctx'), may hold values from -6 to 6
- seg_ids: int32 [4, 1024], P('dp'), may hold values from 0 to 15, never falling along the last dimension, each value on 1 to 512 neighbouring positions
- valid: int32 [4, 1024], P('dp', 'ctx'), may hold values from 0 to 1, as said below
- routed_idx: int32 [4, 128], P('dp'), may hold values from 0 to 1023, as said below
- attn_gain: float32 [2, 1024], replicated, may hold values from 0.1 to 1.9
- w_qkv: bfloat16 [2, 3, 1024, 1024], P(None, None, None, 'tensor'), may hold values from -0.1875 to 0.1875
- w_out: bfloat16 [2, 1024, 1024], P(None, 'tensor'), may hold values from -1.5 to 1.5
- mlp_gain: float32 [2, 1024], replicated, may hold values from 0.1 to 1.9
- w_up: bfloat16 [2, 1024, 4096], P(None, None, 'tensor'), may hold values from -0.1875 to 0.1875
- w_down: bfloat16 [2, 4096, 1024], P(None, 'tensor'), may hold values from -0.09375 to 0.09375
- w_router: float32 [1024], replicated, may hold values from -0.09375 to 0.09375
Outputs:
- hidden_out: bfloat16 [4, 1024, 1024], P('dp', 'ctx')
- loss: float32 [], replicated
- grad_in: float32 [4, 1024, 1024], P('dp', 'ctx')
- grad_attn_gain: float32 [2, 1024], P(None, ('dp', 'ctx'))
- query_key_value_gradient: float32 [2, 3, 1024, 1024], P(None, None, ('dp', 'ctx'), 'tensor')
- grad_out: float32 [2, 1024, 1024], P(None, 'tensor', ('dp', 'ctx'))
- grad_mlp_gain: float32 [2, 1024], P(None, ('dp', 'ctx'))
- up_weight_gradient: float32 [2, 1024, 4096], P(None, ('dp', 'ctx'), 'tensor')
- down_weight_gradient: float32 [2, 4096, 1024], P(None, 'tensor', ('dp', 'ctx'))
- grad_router: float32 [1024], P(('dp', 'ctx'))
The draws below stay inside these ranges and needn't reach their ends.
Inputs may be any that keep to these rules, and one draw needn't show every extreme that they name: `seg_ids`: each sequence holds 16 documents whose ids never fall along it. `valid`: the first position of every sequence is 0 and the last is 1. `routed_idx`: in each sequence the 128 positions are distinct and ascending; its first and last positions are always among them.
All inputs are finite; a program needn't handle non-finite values.
Results may differ from the reference program's by a relative error of at most 0.01.
The reference program's roundings to bfloat16 on the way count: a program that leaves them out, or rounds other values in their place, can miss the bound.
Values may be sent and summed in bfloat16 or wider, within the bound.
A program may use at most 192 MiB of HBM per device.

```python
import math
import jax
import jax.numpy as jnp
import numpy as np
from jax import lax

D = 1024
HEADS = 16
HEAD = 64
FF = 4096
DOCS = 16
SEQ_LEN = 1024
SEQS = 4
ROUTED = 128


def draw_valid(key, part):
    places = jnp.arange(SEQ_LEN, dtype=jnp.int32)
    threshold = 250 + 700 * places // SEQ_LEN
    rolled = jax.random.randint(key, (SEQS, SEQ_LEN), 0, 1000)
    valid_rows = (rolled < threshold[None, :]).astype(jnp.int32)
    valid_rows = valid_rows.at[:, 0].set(0)
    return valid_rows.at[:, SEQ_LEN - 1].set(1)


def draw_routed_idx(key, part):
    lift_key, noise_key = jax.random.split(key)
    places = jnp.arange(SEQ_LEN, dtype=jnp.int32)
    region = places * 8 // SEQ_LEN
    region_lift = jax.random.randint(lift_key, (SEQS, 8), 0, 4)
    noise_rank = jax.random.randint(noise_key, (SEQS, SEQ_LEN), 0, 1024)
    ranked = region_lift[:, region] * 384 + noise_rank
    ranked = ranked * SEQ_LEN + places[None, :]
    edge_rows = (places == 0) | (places == SEQ_LEN - 1)
    ranked = jnp.where(edge_rows[None, :], 1073741824 + places[None, :], ranked)
    picked = lax.top_k(ranked, ROUTED)[1]
    return jnp.sort(picked, axis=-1).astype(jnp.int32)


def block_levels(stream_key, extent, cuts, smallest, high):
    def one(dim, shards_of):
        draws = jax.random.uniform(jax.random.fold_in(jax.random.fold_in(stream_key, 6), dim), (shards_of,), jnp.float32, smallest / len(cuts), high / len(cuts))
        return jnp.repeat(jnp.exp(draws), extent[dim] // shards_of).reshape((-1,) + (1,) * (len(extent) - dim - 1))

    level = one(*cuts[0])
    for cut in cuts[1:]:
        level = level * one(*cut)
    return level


def length_profile(number_of, total, most, slope):
    portions = [(1 << 20) // math.isqrt(rank ** slope) + 1 for rank in range(2, number_of + 1)]
    rest, given = total - most - (number_of - 1), [1] * (number_of - 1)
    while rest > 0:
        movable = [i for i in range(number_of - 1) if given[i] < most]
        mass, remaining = sum([portions[i] for i in movable]), rest
        for i in movable:
            extra = min(most - given[i], max(1, remaining * portions[i] // mass), rest)
            given[i] = given[i] + extra
            rest = rest - extra
    return np.array([most] + given)


def uneven(rng, count, total, bound, slope):
    if count == 2:
        one = jax.random.randint(rng, (), max(1, total - bound), min(bound, total - 1) + 1)
        return jnp.stack([one, total - one])
    lengths = jnp.asarray(length_profile(count, total, bound, slope), jnp.int32)
    pairs = (count - 1) // 2
    donor, sink = lengths[1:1 + 2 * pairs:2], lengths[2:2 + 2 * pairs:2]
    room = jnp.minimum(donor - 1, bound - sink)
    passed = jax.random.randint(jax.random.fold_in(rng, 1), (pairs,), 0, 1 << 20) % (room + 1)
    lengths = lengths.at[1:1 + 2 * pairs:2].set(donor - passed).at[2:2 + 2 * pairs:2].set(sink + passed)
    return lengths[jax.random.permutation(jax.random.fold_in(rng, 2), count)]


def scatter_about(own_key, shape, spread, bound, cuts=(), held_as=jnp.bfloat16):
    drawn = spread * jax.random.normal(own_key, shape, jnp.float32)
    if cuts:
        drawn = drawn * block_levels(own_key, shape, cuts, -0.22, 0.18)
    return jnp.clip(drawn, -bound, bound).astype(held_as)


def setup_inputs(seed: int = 0) -> dict:
    key_of = jax.random.split(jax.random.key(seed), 13)
    return {
        "hidden_in": scatter_about(key_of[0], (SEQS, SEQ_LEN, D), 1.0, 6.0, ((0, 4), (1, 2))),
        "teacher": scatter_about(key_of[1], (SEQS, SEQ_LEN, D), 1.0, 6.0, ((0, 4), (1, 2))),
        "seg_ids": jax.vmap(lambda own: jnp.searchsorted(jnp.cumsum(uneven(own, DOCS, SEQ_LEN, SEQ_LEN // 2, 2)), jnp.arange(SEQ_LEN), side="right"))(jax.random.split(key_of[2], SEQS)).reshape((SEQS, SEQ_LEN)).astype(jnp.int32),
        "valid": draw_valid(jax.random.fold_in(key_of[12], 71), 0),
        "routed_idx": draw_routed_idx(jax.random.fold_in(key_of[12], 71), 0),
        "attn_gain": jnp.clip(1.0 + 0.18 * jax.random.normal(key_of[5], (2, D), jnp.float32), 0.1, 1.9),
        "w_qkv": scatter_about(key_of[6], (2, 3, D, D), D ** -0.5, 0.1875, ((3, 4),)),
        "w_out": scatter_about(key_of[7], (2, D, D), (D // 64) ** -0.5, 1.5, ((1, 4),)),
        "mlp_gain": jnp.clip(1.0 + 0.18 * jax.random.normal(key_of[8], (2, D), jnp.float32), 0.1, 1.9),
        "w_up": scatter_about(key_of[9], (2, D, FF), D ** -0.5, 0.1875, ((2, 4),)),
        "w_down": scatter_about(key_of[10], (2, FF, D), FF ** -0.5, 0.09375, ((1, 4),)),
        "w_router": scatter_about(key_of[11], (D,), (4 * D) ** -0.5, 0.09375, (), jnp.float32),
    }


@jax.custom_vjp
def low(v):
    return lax.optimization_barrier(v.astype(jnp.bfloat16)).astype(jnp.float32)

@jax.custom_vjp
def low_back(v):
    return v

def low_keep(v):
    return (low(v), None)

def low_pass(kept, grad):
    return (grad,)

def back_keep(v):
    return (v, None)

def back_low(kept, grad):
    return (low(grad),)
low.defvjp(low_keep, low_pass)
low_back.defvjp(back_keep, back_low)
epsilon = 1e-06
masked_value = -1e+30
highest = lax.Precision.HIGHEST

def rms_scale(values, gain):
    return values * lax.rsqrt(lax.optimization_barrier(jnp.mean(values * values, axis=-1, keepdims=True)) + epsilon) * gain

def gelu_tanh(values):
    return jax.nn.gelu(values, approximate=True)

def attention(queries, key_rows, value_rows, positions, segments):
    length = queries.shape[0]
    block_rows = min(512, length)
    blocks = length // block_rows
    score_scale = 1.0 / HEAD ** 0.5
    key_heads = key_rows.reshape(length, HEADS, HEAD)
    value_heads = value_rows.reshape(length, HEADS, HEAD)

    def per_block(block_args):
        q_block, q_pos, q_seg = block_args
        scores = low_back(jnp.einsum('qhe,khe->hqk', q_block, key_heads, precision=highest) * score_scale)
        visible = (positions[None, :] <= q_pos[:, None]) & (segments[None, :] == q_seg[:, None])
        scores = jnp.where(visible[None], scores, masked_value)
        weights = low(jax.nn.softmax(scores, axis=-1))
        mixed_state = jnp.einsum('hqk,khe->qhe', weights, value_heads, precision=highest)
        return mixed_state.reshape(block_rows, D)
    mixed_state = lax.map(jax.checkpoint(per_block), (queries.reshape(blocks, block_rows, HEADS, HEAD), positions.reshape(blocks, block_rows), segments.reshape(blocks, block_rows)))
    return mixed_state.reshape(length, D)

def mixed_layer(values, gain_a, query_key_value_weight, output_weight_matrix, gain_m, up_weight_matrix, down_weight_matrix, positions, segments):
    attention_norm = low(rms_scale(values, gain_a))
    projected = jnp.einsum('ld,cde->cle', attention_norm, query_key_value_weight, precision=highest)
    queries = low_back(low(projected[0]))
    key_rows = low_back(low(projected[1]))
    value_rows = low_back(low(projected[2]))
    mixed_state = low_back(low(attention(queries, key_rows, value_rows, positions, segments)))
    attn_out = low_back(jnp.dot(mixed_state, output_weight_matrix, precision=highest))
    middle = values + attn_out
    feedforward_norm = low(rms_scale(middle, gain_m))
    hidden_preactivation = low_back(jnp.dot(feedforward_norm, up_weight_matrix, precision=highest))
    hidden_activation = low(gelu_tanh(hidden_preactivation))
    mlp_out = low_back(jnp.dot(hidden_activation, down_weight_matrix, precision=highest))
    return (attn_out, middle, mlp_out)

def sequence_forward(params, values, target, segments, valid_row, routes, valid_count, token_total):
    attn_gain, w_qkv, w_out, mlp_gain, w_up, w_down, w_router = params
    positions = jnp.arange(values.shape[0], dtype=jnp.int32)
    attn_d, middle_d, mlp_d = mixed_layer(values, attn_gain[0], w_qkv[0], w_out[0], mlp_gain[0], w_up[0], w_down[0], positions, segments)
    layer_mid = middle_d + mlp_d
    chosen = low_back(low(layer_mid[routes]))
    attn_r, middle_r, mlp_r = mixed_layer(chosen, attn_gain[1], w_qkv[1], w_out[1], mlp_gain[1], w_up[1], w_down[1], routes, segments[routes])
    branch_sum = attn_r + mlp_r
    gating = jax.nn.sigmoid(lax.optimization_barrier(jnp.sum(chosen * w_router, axis=-1)))
    returned = low_back(low(gating[:, None] * branch_sum))
    layer_out = layer_mid.at[routes].add(returned)
    error_rows = layer_out - target
    scaled = jnp.sum(valid_row[:, None] * error_rows * error_rows) * (token_total / (2.0 * valid_count))
    return (layer_out, scaled)

def reference(hidden_in, teacher, seg_ids, valid, routed_idx, attn_gain, w_qkv, w_out, mlp_gain, w_up, w_down, w_router):
    params = tuple((item.astype(jnp.float32) for item in (attn_gain, w_qkv, w_out, mlp_gain, w_up, w_down, w_router)))
    valid_count = jnp.sum(valid.astype(jnp.float32))
    token_total = float(SEQS * SEQ_LEN)

    def per_sequence(carry, seq_args):
        values, target, segments, valid_int, routes = seq_args
        valid_row = valid_int.astype(jnp.float32)
        target_f = target.astype(jnp.float32)

        def forward(prm, inputs):
            return sequence_forward(prm, inputs, target_f, segments, valid_row, routes, valid_count, token_total)
        (layer_out, scaled), pullback = jax.vjp(forward, params, values.astype(jnp.float32))
        grad_params, grad_values = pullback((jnp.zeros_like(layer_out), jnp.ones((), jnp.float32)))
        error_rows = layer_out - target_f
        error_sum = jnp.sum(valid_row[:, None] * error_rows * error_rows)
        carry = tuple((c + g for c, g in zip(carry, grad_params)))
        return (carry, (layer_out.astype(jnp.bfloat16), grad_values, error_sum))
    initial = tuple((jnp.zeros_like(item) for item in params))
    summed_grads, (outputs, grad_inputs, errors) = lax.scan(per_sequence, initial, (hidden_in, teacher, seg_ids, valid, routed_idx))
    loss_value = jnp.sum(errors) / (valid_count * D)
    return (outputs, loss_value, grad_inputs, summed_grads[0], summed_grads[1], summed_grads[2], summed_grads[3], summed_grads[4], summed_grads[5], summed_grads[6])
```

```python
import functools

import jax
import jax.numpy as jnp
from jax import lax
from jax.experimental import pallas as pl
from jax.experimental.pallas import tpu as pltpu
from jax.sharding import PartitionSpec as P

HEAD = 64
epsilon = 1e-06
masked_value = -1e30
MESH = pl.DeviceIdType.MESH
BF = jnp.bfloat16
F32 = jnp.float32
VM = pltpu.VMEM
ANY = pl.ANY


def rcopy(src, dst, send, recv, where):
    return pltpu.make_async_remote_copy(
        src_ref=src, dst_ref=dst, send_sem=send, recv_sem=recv, device_id=where, device_id_type=MESH
    )


def dot_nn(a, b):
    return lax.dot_general(a, b, (((1,), (0,)), ((), ())), preferred_element_type=F32)


def dot_nt(a, b):
    return lax.dot_general(a, b, (((1,), (1,)), ((), ())), preferred_element_type=F32)


def dot_tn(a, b):
    return lax.dot_general(a, b, (((0,), (0,)), ((), ())), preferred_element_type=F32)


def rms_parts(values):
    r = lax.rsqrt(jnp.mean(values * values, axis=-1, keepdims=True) + epsilon)
    return r, values * r


def rms_back(values, gain, grad):
    r, unit = rms_parts(values)
    scaled = grad * gain
    return r * (scaled - unit * jnp.mean(scaled * unit, axis=-1, keepdims=True)), grad * unit


def gelu_pair(u):
    c = 0.7978845608028654
    t = jnp.tanh(c * (u + 0.044715 * (u * u * u)))
    return t


def fold8(rows):
    return jnp.sum(rows.reshape(rows.shape[0] // 8, 8, rows.shape[1]), axis=0)


class Line:
    def __init__(self):
        t = lax.axis_index("tensor")
        self.t = t
        self.side = t // 2
        self.is_end = (t == 0) | (t == 3)
        self.is_mid = (t == 1) | (t == 2)
        self.end = {"tensor": self.side * 3}
        self.mid = {"tensor": 1 + self.side}
        self.other = {"tensor": 2 - self.side}


def greet(peers):
    bar = pltpu.get_barrier_semaphore()
    for p in peers:
        pl.semaphore_signal(bar, inc=1, device_id=p, device_id_type=MESH)
    pl.semaphore_wait(bar, len(peers))


def tensor_peers(n):
    t = lax.axis_index("tensor")
    return [{"tensor": lax.rem(t + j, n)} for j in range(1, n)]


def row_peers(n_dp, n_ctx):
    d, c = lax.axis_index("dp"), lax.axis_index("ctx")
    out = []
    for j in range(n_dp):
        for k in range(n_ctx):
            if j or k:
                out.append({"dp": lax.rem(d + j, n_dp), "ctx": lax.rem(c + k, n_ctx)})
    return out


def rms_scale(values, gain):
    return values * lax.rsqrt(jnp.mean(values * values, axis=-1, keepdims=True) + epsilon) * gain


def gelu_tanh(values):
    return jax.nn.gelu(values, approximate=True)


def gating_fn(chosen, router):
    return jax.nn.sigmoid(jnp.sum(chosen * router, axis=-1))


def tensor_sum(partial_sum):
    return lax.psum(partial_sum, "tensor")


def gather_keys(projected):
    return (
        lax.all_gather(projected[1], "ctx", axis=1, tiled=True),
        lax.all_gather(projected[2], "ctx", axis=1, tiled=True),
    )


def scatter_key_grads(grad_k, grad_v):
    stacked = jnp.stack([grad_k, grad_v])
    summed = lax.psum_scatter(stacked, "ctx", scatter_dimension=2, tiled=True)
    return (summed[0], summed[1])


def to_workers(picked):
    return lax.psum_scatter(
        picked.astype(jnp.bfloat16), "ctx", scatter_dimension=1, tiled=True
    ).astype(jnp.float32)


def to_owners(rows_low):
    return lax.all_gather(rows_low, "ctx", axis=1, tiled=True)


def take_rows(table, places):
    return jax.vmap(lambda t, i: t[i])(table, places)


def add_rows(table, places, addend):
    return jax.vmap(lambda t, i, a: t.at[i].add(a))(table, places, addend)


def tile_scores(q_tile, k_tile, qpos_tile, kpos_tile, qseg_tile, kseg_tile, score_scale):
    scores = (
        jnp.einsum("qhe,khe->hqk", q_tile, k_tile, preferred_element_type=jnp.float32) * score_scale
    )
    visible = (kpos_tile[None, :] <= qpos_tile[:, None]) & (
        kseg_tile[None, :] == qseg_tile[:, None]
    )
    return (scores, visible[None])


def tile_layout(queries, key_rows, value_rows, k_pos, k_seg):
    q_len, row_width = queries.shape
    k_len = key_rows.shape[0]
    head_count = row_width // HEAD
    q_step = min(512, q_len)
    k_step = min(2048, k_len)
    k_count = k_len // k_step
    key_tiles = key_rows.reshape(k_count, k_step, head_count, HEAD)
    value_tiles = value_rows.reshape(k_count, k_step, head_count, HEAD)
    kpos_tiles = k_pos.reshape(k_count, k_step)
    kseg_tiles = k_seg.reshape(k_count, k_step)
    return (
        q_len,
        row_width,
        k_len,
        head_count,
        q_step,
        (key_tiles, value_tiles, kpos_tiles, kseg_tiles),
    )


def attend_one(queries, key_rows, value_rows, q_pos, k_pos, q_seg, k_seg):
    q_len, row_width, k_len, head_count, q_step, tiles = tile_layout(
        queries, key_rows, value_rows, k_pos, k_seg
    )
    score_scale = 1.0 / HEAD**0.5

    def per_query(q_args):
        q_tile, qpos_tile, qseg_tile = q_args

        def total_step(carry, k_args):
            running, summed = carry
            k_tile, v_tile, kpos_tile, kseg_tile = k_args
            scores, visible = tile_scores(
                q_tile, k_tile, qpos_tile, kpos_tile, qseg_tile, kseg_tile, score_scale
            )
            raised = jnp.maximum(
                running, jnp.max(jnp.where(visible, scores, masked_value), axis=-1)
            )
            weights = jnp.where(visible, jnp.exp(scores - raised[..., None]), 0.0)
            return ((raised, summed * jnp.exp(running - raised) + jnp.sum(weights, axis=-1)), None)

        initial = (
            jnp.full((head_count, q_step), masked_value, jnp.float32),
            jnp.zeros((head_count, q_step), jnp.float32),
        )
        (running, summed), _ = lax.scan(total_step, initial, tiles)
        log_total = running + jnp.log(summed)

        def value_step(output, k_args):
            k_tile, v_tile, kpos_tile, kseg_tile = k_args
            scores, visible = tile_scores(
                q_tile, k_tile, qpos_tile, kpos_tile, qseg_tile, kseg_tile, score_scale
            )
            weights_low = jnp.where(visible, jnp.exp(scores - log_total[..., None]), 0.0).astype(
                jnp.bfloat16
            )
            return (
                output
                + jnp.einsum(
                    "hqk,khe->qhe", weights_low, v_tile, preferred_element_type=jnp.float32
                ),
                None,
            )

        output, _ = lax.scan(value_step, jnp.zeros((q_step, head_count, HEAD), jnp.float32), tiles)
        return (output, log_total)

    q_count = q_len // q_step
    output, log_total = lax.map(
        per_query,
        (
            queries.reshape(q_count, q_step, head_count, HEAD),
            q_pos.reshape(q_count, q_step),
            q_seg.reshape(q_count, q_step),
        ),
    )
    return (output.reshape(q_len, row_width), log_total)


def attend_back(queries, key_rows, value_rows, grad_mixed, log_total, q_pos, k_pos, q_seg, k_seg):
    q_len, row_width, k_len, head_count, q_step, tiles = tile_layout(
        queries, key_rows, value_rows, k_pos, k_seg
    )
    score_scale = 1.0 / HEAD**0.5

    def per_query(q_args):
        q_tile, g_tile, total_tile, qpos_tile, qseg_tile = q_args

        def tile_probs(k_tile, kpos_tile, kseg_tile):
            scores, visible = tile_scores(
                q_tile, k_tile, qpos_tile, kpos_tile, qseg_tile, kseg_tile, score_scale
            )
            return jnp.where(visible, jnp.exp(scores - total_tile[..., None]), 0.0)

        def inner_step(carry, k_args):
            k_tile, v_tile, kpos_tile, kseg_tile = k_args
            weights = tile_probs(k_tile, kpos_tile, kseg_tile)
            grad_weights = jnp.einsum(
                "qhe,khe->hqk", g_tile, v_tile, preferred_element_type=jnp.float32
            )
            return (carry + jnp.sum(weights * grad_weights, axis=-1), None)

        inner, _ = lax.scan(inner_step, jnp.zeros((head_count, q_step), jnp.float32), tiles)

        def grad_step(carry, k_args):
            k_tile, v_tile, kpos_tile, kseg_tile = k_args
            weights = tile_probs(k_tile, kpos_tile, kseg_tile)
            grad_weights = jnp.einsum(
                "qhe,khe->hqk", g_tile, v_tile, preferred_element_type=jnp.float32
            )
            grad_scores = (weights * (grad_weights - inner[..., None])).astype(jnp.bfloat16)
            carry = carry + jnp.einsum(
                "hqk,khe->qhe", grad_scores, k_tile, preferred_element_type=jnp.float32
            )
            grad_keys = jnp.einsum(
                "hqk,qhe->khe", grad_scores, q_tile, preferred_element_type=jnp.float32
            )
            grad_values = jnp.einsum(
                "hqk,qhe->khe",
                weights.astype(jnp.bfloat16),
                g_tile,
                preferred_element_type=jnp.float32,
            )
            return (carry, (grad_keys, grad_values))

        grad_q, (grad_keys, grad_values) = lax.scan(
            grad_step, jnp.zeros((q_step, head_count, HEAD), jnp.float32), tiles
        )
        return (
            grad_q * score_scale,
            grad_keys.reshape(k_len, row_width) * score_scale,
            grad_values.reshape(k_len, row_width),
        )

    q_count = q_len // q_step
    grad_q, grad_keys, grad_values = lax.map(
        per_query,
        (
            queries.reshape(q_count, q_step, head_count, HEAD),
            grad_mixed.reshape(q_count, q_step, head_count, HEAD),
            log_total,
            q_pos.reshape(q_count, q_step),
            q_seg.reshape(q_count, q_step),
        ),
    )
    return (
        grad_q.reshape(q_len, row_width),
        jnp.sum(grad_keys, axis=0),
        jnp.sum(grad_values, axis=0),
    )


def make_attention(q_pos, k_pos, q_seg, k_seg):

    def attend_fn(projected):
        key_all, value_all = gather_keys(projected)
        mixed_full, log_total = lax.map(
            lambda a: attend_one(*a), (projected[0], key_all, value_all, q_pos, k_pos, q_seg, k_seg)
        )
        return (mixed_full, (key_all, value_all, log_total))

    def attend_grad(projected, kept, grad_mixed):
        key_all, value_all, log_total = kept
        grad_q, grad_k, grad_v = lax.map(
            lambda a: attend_back(*a),
            (projected[0], key_all, value_all, grad_mixed, log_total, q_pos, k_pos, q_seg, k_seg),
        )
        grad_k, grad_v = scatter_key_grads(grad_k, grad_v)
        return jnp.stack(
            [grad_q.astype(jnp.bfloat16), grad_k.astype(jnp.bfloat16), grad_v.astype(jnp.bfloat16)]
        )

    return (attend_fn, attend_grad)


def block_forward(
    resid_in,
    gain_a,
    query_key_value_weight,
    output_weight_matrix,
    gain_m,
    up_weight_matrix,
    down_weight_matrix,
    attend_fn,
):
    attention_norm = rms_scale(resid_in, gain_a).astype(jnp.bfloat16)
    projected = jnp.einsum(
        "oym,qmh->qoyh", attention_norm, query_key_value_weight, preferred_element_type=jnp.float32
    ).astype(jnp.bfloat16)
    mixed_full, kept = attend_fn(projected)
    mixed_state = mixed_full.astype(jnp.bfloat16)
    attention_portion = jnp.einsum(
        "xtu,ua->xta", mixed_state, output_weight_matrix, preferred_element_type=jnp.float32
    )
    attn_out = tensor_sum(attention_portion)
    middle = resid_in + attn_out
    feedforward_norm = rms_scale(middle, gain_m).astype(jnp.bfloat16)
    hidden_preactivation = jnp.einsum(
        "iqp,po->iqo", feedforward_norm, up_weight_matrix, preferred_element_type=jnp.float32
    )
    hidden_activation = gelu_tanh(hidden_preactivation).astype(jnp.bfloat16)
    mlp_part = jnp.einsum(
        "euq,qt->eut", hidden_activation, down_weight_matrix, preferred_element_type=jnp.float32
    )
    mlp_out = tensor_sum(mlp_part)
    saved = (
        resid_in,
        attention_norm,
        projected,
        mixed_state,
        kept,
        middle,
        feedforward_norm,
        hidden_preactivation,
        hidden_activation,
    )
    return (attn_out, mlp_out, saved)


def block_backward(
    saved,
    grad_top,
    gain_a,
    query_key_value_weight,
    output_weight_matrix,
    gain_m,
    up_weight_matrix,
    down_weight_matrix,
    attend_grad,
):
    (
        resid_in,
        attention_norm,
        projected,
        mixed_state,
        kept,
        middle,
        feedforward_norm,
        hidden_preactivation,
        hidden_activation,
    ) = saved
    top_reduced = grad_top.astype(jnp.bfloat16)
    down_weight_gradient = jnp.einsum(
        "pgr,pgw->rw", hidden_activation, top_reduced, preferred_element_type=jnp.float32
    )
    activation_gradient = jnp.einsum(
        "ayx,cx->ayc", top_reduced, down_weight_matrix, preferred_element_type=jnp.float32
    )
    preactivation_gradient = jax.vjp(gelu_tanh, hidden_preactivation)[1](activation_gradient)[
        0
    ].astype(jnp.bfloat16)
    up_weight_gradient = jnp.einsum(
        "uzb,uzv->bv", feedforward_norm, preactivation_gradient, preferred_element_type=jnp.float32
    )
    norm_portion = jnp.einsum(
        "vok,hk->voh", preactivation_gradient, up_weight_matrix, preferred_element_type=jnp.float32
    )
    grad_norm_m = tensor_sum(norm_portion)
    grad_middle, grad_gain_m = jax.vjp(rms_scale, middle, gain_m)[1](grad_norm_m)
    grad_attn = grad_top + grad_middle
    attention_reduced = grad_attn.astype(jnp.bfloat16)
    output_weight_gradient = jnp.einsum(
        "omi,omj->ij", mixed_state, attention_reduced, preferred_element_type=jnp.float32
    )
    grad_mixed = jnp.einsum(
        "bjw,gw->bjg", attention_reduced, output_weight_matrix, preferred_element_type=jnp.float32
    ).astype(jnp.bfloat16)
    projection_gradient = attend_grad(projected, kept, grad_mixed)
    query_key_value_gradient = jnp.einsum(
        "xgt,axgf->atf", attention_norm, projection_gradient, preferred_element_type=jnp.float32
    )
    input_part = jnp.einsum(
        "gurh,gih->uri",
        projection_gradient,
        query_key_value_weight,
        preferred_element_type=jnp.float32,
    )
    grad_norm_a = tensor_sum(input_part)
    grad_resid, grad_gain_a = jax.vjp(rms_scale, resid_in, gain_a)[1](grad_norm_a)
    return (
        grad_attn,
        grad_middle,
        grad_resid,
        (
            grad_gain_a,
            query_key_value_gradient,
            output_weight_gradient,
            grad_gain_m,
            up_weight_gradient,
            down_weight_gradient,
        ),
    )


def pack_grads(grad_list, dims, groups):
    flats = []
    shapes = []
    for grad_item, which_dim in zip(grad_list, dims):
        moved = jnp.moveaxis(grad_item, which_dim, 0)
        shapes.append(moved.shape)
        flats.append(moved.reshape(groups, -1))
    return (jnp.concatenate(flats, axis=1), shapes)


def unpack_grads(summed, shapes, dims, groups):
    results = []
    offset = 0
    for moved_shape, which_dim in zip(shapes, dims):
        share_shape = (moved_shape[0] // groups,) + tuple(moved_shape[1:])
        width = math_prod(share_shape)
        piece = summed[0, offset : offset + width].reshape(share_shape)
        results.append(jnp.moveaxis(piece, 0, which_dim))
        offset = offset + width
    return tuple(results)


def math_prod(shape):
    total = 1
    for extent in shape:
        total = total * extent
    return total


def spread_grads(grad_list, dims):
    groups = lax.axis_size("dp") * lax.axis_size("ctx")
    packed, shapes = pack_grads(grad_list, dims, groups)
    summed = lax.psum_scatter(packed, ("dp", "ctx"), scatter_dimension=0, tiled=True)
    return unpack_grads(summed, shapes, dims, groups)


def plain_local(
    hidden_in,
    teacher,
    seg_ids,
    valid,
    routed_idx,
    attn_gain,
    w_qkv,
    w_out,
    mlp_gain,
    w_up,
    w_down,
    w_router,
):
    seqs_local, local_len, model_width = hidden_in.shape
    seq_len = seg_ids.shape[1]
    routed = routed_idx.shape[1]
    ctx_count = lax.axis_size("ctx")
    ctx_place = lax.axis_index("ctx")
    routed_local = routed // ctx_count
    dense_qpos = jnp.broadcast_to(
        ctx_place * local_len + jnp.arange(local_len, dtype=jnp.int32), (seqs_local, local_len)
    )
    dense_kpos = jnp.broadcast_to(jnp.arange(seq_len, dtype=jnp.int32), (seqs_local, seq_len))
    dense_qseg = lax.dynamic_slice_in_dim(seg_ids, ctx_place * local_len, local_len, 1)
    routed_seg = take_rows(seg_ids, routed_idx)
    routed_qpos = lax.dynamic_slice_in_dim(routed_idx, ctx_place * routed_local, routed_local, 1)
    routed_qseg = lax.dynamic_slice_in_dim(routed_seg, ctx_place * routed_local, routed_local, 1)
    owner_mine = routed_idx // local_len == ctx_place
    owner_row = routed_idx % local_len
    dense_attend, dense_grad = make_attention(dense_qpos, dense_kpos, dense_qseg, seg_ids)
    routed_attend, routed_grad = make_attention(routed_qpos, routed_idx, routed_qseg, routed_seg)
    x_input = hidden_in.astype(jnp.float32)
    attn_d, mlp_d, saved_d = block_forward(
        x_input, attn_gain[0], w_qkv[0], w_out[0], mlp_gain[0], w_up[0], w_down[0], dense_attend
    )
    layer_mid = saved_d[5] + mlp_d
    picked = (
        jnp.where(owner_mine[..., None], take_rows(layer_mid, owner_row), 0.0)
        .astype(jnp.bfloat16)
        .astype(jnp.float32)
    )
    chosen = to_workers(picked).astype(jnp.bfloat16).astype(jnp.float32)
    gating = gating_fn(chosen, w_router)
    attn_r, mlp_r, saved_r = block_forward(
        chosen, attn_gain[1], w_qkv[1], w_out[1], mlp_gain[1], w_up[1], w_down[1], routed_attend
    )
    branch_sum = attn_r + mlp_r
    sent_rows = (gating[..., None] * branch_sum).astype(jnp.bfloat16)
    returned = to_owners(sent_rows).astype(jnp.float32)
    layer_out = add_rows(layer_mid, owner_row, jnp.where(owner_mine[..., None], returned, 0.0))
    valid_rows = valid.astype(jnp.float32)
    error_rows = layer_out - teacher.astype(jnp.float32)
    error_sum, valid_count = lax.psum(
        (jnp.sum(valid_rows[..., None] * error_rows * error_rows), jnp.sum(valid_rows)),
        ("dp", "ctx"),
    )
    loss_value = error_sum / (valid_count * model_width)
    token_total = float(seqs_local * seq_len * lax.axis_size("dp"))
    grad_final = token_total / valid_count * valid_rows[..., None] * error_rows
    picked_grad = (
        jnp.where(owner_mine[..., None], take_rows(grad_final, owner_row), 0.0)
        .astype(jnp.bfloat16)
        .astype(jnp.float32)
    )
    branch_grad = to_workers(picked_grad).astype(jnp.bfloat16).astype(jnp.float32)
    grad_top = gating[..., None] * branch_grad
    gating_share, gating_back = jax.vjp(gating_fn, chosen, w_router)
    grad_gating = jnp.sum(branch_grad * branch_sum, axis=-1)
    grad_chosen_gate, grad_router = gating_back(grad_gating)
    grad_attn_r, grad_middle_r, grad_resid_r, grads_r = block_backward(
        saved_r,
        grad_top,
        attn_gain[1],
        w_qkv[1],
        w_out[1],
        mlp_gain[1],
        w_up[1],
        w_down[1],
        routed_grad,
    )
    grad_chosen = (grad_middle_r + grad_resid_r + grad_chosen_gate).astype(jnp.bfloat16)
    grads_r = grads_r + (grad_router,)
    spread_r = spread_grads(grads_r, (0, 1, 1, 0, 0, 1, 0))
    grad_rows = to_owners(grad_chosen).astype(jnp.float32)
    grad_mid = add_rows(grad_final, owner_row, jnp.where(owner_mine[..., None], grad_rows, 0.0))
    grad_attn_d, grad_middle_d, grad_resid_d, grads_d = block_backward(
        saved_d,
        grad_mid,
        attn_gain[0],
        w_qkv[0],
        w_out[0],
        mlp_gain[0],
        w_up[0],
        w_down[0],
        dense_grad,
    )
    grad_input = grad_attn_d + grad_resid_d
    spread_d = spread_grads(grads_d, (0, 1, 1, 0, 0, 1))
    return (
        layer_out.astype(jnp.bfloat16),
        loss_value,
        grad_input,
        jnp.stack([spread_d[0], spread_r[0]]),
        jnp.stack([spread_d[1], spread_r[1]]),
        jnp.stack([spread_d[2], spread_r[2]]),
        jnp.stack([spread_d[3], spread_r[3]]),
        jnp.stack([spread_d[4], spread_r[4]]),
        jnp.stack([spread_d[5], spread_r[5]]),
        spread_r[6],
    )


def head_pair(rows):
    lane = lax.broadcasted_iota(jnp.int32, rows.shape, 1)
    zero = jnp.zeros_like(rows)
    return jnp.concatenate([jnp.where(lane < HEAD, rows, zero), jnp.where(lane >= HEAD, rows, zero)], axis=0)


def pair_join(stacked):
    half = stacked.shape[0] // 2
    lane = lax.broadcasted_iota(jnp.int32, (half, stacked.shape[1]), 1)
    return jnp.where(lane < HEAD, stacked[:half], stacked[half:])


FWD_LAGS = (1, 2, 3, 4, 5, 6)


def dense_forward_kernel(
    sizes,
    x_ref, again_ref, mgain_ref, segc_ref, segr_ref, cnt_ref, wqkv_h, wout_h, wup_h, wdn_h,
    x2_ref, q_ref, k_ref, v_ref, mix_ref, lse_ref, mid_ref, n2_ref, pre_ref, act_ref, cnt_out,
    wqkv, wout, wup, wdn, part, part2,
    sE, rE, sI, rI, sO, sE2, rE2, sX, rX, cbuf,
    wsem, kvs, kvr, cs, cr, ss, rs,
):
    NC, R, D, L, S, NT, NDP, NCTX = sizes
    ln = Line()
    ctx = lax.axis_index("ctx")
    dp = lax.axis_index("dp")
    half = R // 2
    loads = [
        pltpu.make_async_copy(wqkv_h.at[0], wqkv, wsem.at[0]),
        pltpu.make_async_copy(wout_h.at[0], wout, wsem.at[1]),
        pltpu.make_async_copy(wup_h.at[0], wup, wsem.at[2]),
        pltpu.make_async_copy(wdn_h.at[0], wdn, wsem.at[3]),
    ]
    for ld in loads:
        ld.start()
    tpeers = tensor_peers(NT)
    rpeers = row_peers(NDP, NCTX)
    greet(tpeers + rpeers)

    def count_slot(j):
        return cbuf.at[j]

    cbuf[0] = cnt_ref[...]
    sends = []
    for j, p in enumerate(rpeers):
        sends.append(rcopy(cnt_ref, cbuf.at[j + 1], cs.at[j], cr.at[j], p))
    for cp in sends:
        cp.start()

    @pl.when(ln.is_end)
    def _():
        def zero(k, _):
            rE[k] = jnp.zeros((R, D), BF)
            return 0

        lax.fori_loop(0, NC, zero, 0)

    for ld in loads[:1]:
        ld.wait()
    RB = 2 * R
    again = again_ref[0:1, :]

    def project(i, _):
        rows = pl.ds(pl.multiple_of(i * RB, RB), RB)
        xv = x_ref[rows, :].astype(F32)
        n1 = (rms_parts(xv)[1] * again).astype(BF)
        for c, ref in enumerate((q_ref, k_ref, v_ref)):
            y = dot_nn(n1, wqkv[c]).astype(BF)
            if c == 0:
                ref[rows, :] = y
            else:
                ref[pl.ds(pl.multiple_of(ctx * L + i * RB, RB), RB), :] = y
        return 0

    lax.fori_loop(0, L // RB, project, 0)

    own = pl.ds(pl.multiple_of(ctx * L, L), L)

    def kv_copy(ref, which, c_to):
        return rcopy(ref.at[own, :], ref.at[own, :], kvs.at[which, c_to], kvr.at[which, ctx], {"ctx": c_to})

    for c_to in range(1, NCTX):
        @pl.when(c_to > ctx)
        def _(c_to=c_to):
            kv_copy(k_ref, 0, c_to).start()
            kv_copy(v_ref, 1, c_to).start()

    for c_from in range(NCTX - 1):
        @pl.when(c_from < ctx)
        def _(c_from=c_from):
            theirs = pl.ds(c_from * L, L)
            for which, ref in enumerate((k_ref, v_ref)):
                rcopy(ref.at[theirs, :], ref.at[theirs, :], kvs.at[which, c_from], kvr.at[which, c_from], {"ctx": c_from}).wait_recv()

    for c_later in range(1, NCTX):
        @pl.when(c_later > ctx)
        def _(c_later=c_later):
            k_ref[pl.ds(c_later * L, L), :] = jnp.zeros((L, k_ref.shape[1]), BF)
            v_ref[pl.ds(c_later * L, L), :] = jnp.zeros((L, k_ref.shape[1]), BF)

    for ld in loads[1:]:
        ld.wait()
    mgain = mgain_ref[0:1, :]
    groups = q_ref.shape[1] // 128

    def attend(i, keys):
        rows = pl.ds(pl.multiple_of(i * R, R), R)
        qpos = ctx * L + i * R + lax.broadcasted_iota(jnp.int32, (R, 1), 0)
        kpos = lax.broadcasted_iota(jnp.int32, (1, keys), 1)
        visible = (kpos <= qpos) & (segr_ref[:, :keys] == segc_ref[i])
        bias = jnp.where(visible, 0.0, masked_value)
        lane = lax.broadcasted_iota(jnp.int32, (R, 128), 1)
        lse_tile = jnp.zeros((R, 128), F32)
        qi = q_ref[rows, :] * jnp.asarray(0.125, BF)
        for g in range(groups):
            cols = slice(128 * g, 128 * g + 128)
            q2 = head_pair(qi[:, cols])
            s = dot_nt(q2, k_ref[:keys, cols]).reshape(2, R, keys) + bias[None]
            top = jnp.max(s, axis=-1, keepdims=True)
            p = jnp.exp(s - top)
            total = jnp.sum(p, axis=-1, keepdims=True)
            pr = (p * (1.0 / total)).astype(BF).reshape(2 * R, keys)
            lse = top + jnp.log(total)
            lse_tile = jnp.where(lane == 2 * g, lse[0], jnp.where(lane == 2 * g + 1, lse[1], lse_tile))
            o = dot_nn(pr, v_ref[:keys, cols])
            mix_ref[rows, cols] = pair_join(o).astype(BF)
        lse_ref[rows, :] = lse_tile

    a1, a2, a3, a4, a5, a6 = FWD_LAGS
    lag3 = jnp.where(ln.is_end, a3, a2)
    my_rows = pl.ds(pl.multiple_of(ln.side * half, half), half)
    ot_rows = pl.ds(pl.multiple_of((1 - ln.side) * half, half), half)

    def got(buf, flow, j):
        rcopy(buf.at[j], buf.at[j], ss.at[flow, j], rs.at[flow, j], ln.mid).wait_recv()

    def got_half(rows, flow, j):
        rcopy(x2_ref.at[j, rows, :], x2_ref.at[j, rows, :], ss.at[flow, j], rs.at[flow, j], ln.mid).wait_recv()

    def body(i, _):
        @pl.when(i < NC)
        def _():
            @pl.when(ctx == 0)
            def _():
                attend(i, L)

            @pl.when(ctx > 0)
            def _():
                attend(i, S)

            p = dot_nn(mix_ref[pl.ds(pl.multiple_of(i * R, R), R), :], wout[...])
            part[i] = p

            @pl.when(ln.is_end)
            def _():
                sE[i] = p.astype(BF)
                rcopy(sE.at[i], rE.at[i], ss.at[0, i], rs.at[0, i], ln.mid).start()

        j1 = i - a1

        @pl.when(ln.is_mid & (j1 >= 0) & (j1 < NC))
        def _():
            got(rE, 0, j1)
            sI[j1] = (rE[j1].astype(F32) + part[j1]).astype(BF)
            rcopy(sI.at[j1], rI.at[j1], ss.at[1, j1], rs.at[1, j1], ln.other).start()

        j3 = i - lag3

        @pl.when((j3 >= 0) & (j3 < NC))
        def _():
            got(rI, 1, j3)
            inner = rI[j3].astype(F32) + part[j3]

            @pl.when(ln.is_mid)
            def _():
                sO[j3] = inner.astype(BF)
                rcopy(sO.at[j3], rI.at[j3], ss.at[2, j3], rs.at[1, j3], ln.end).start()

            rows = pl.ds(pl.multiple_of(j3 * R, R), R)
            mid = x_ref[rows, :].astype(F32) + (inner + rE[j3].astype(F32))
            mid_ref[rows, :] = mid
            n2 = (rms_parts(mid)[1] * mgain).astype(BF)
            n2_ref[rows, :] = n2
            pre = dot_nn(n2, wup[...])
            pre_ref[rows, :] = pre
            act = (0.5 * pre * (1.0 + gelu_pair(pre))).astype(BF)
            act_ref[rows, :] = act
            p2 = dot_nn(act, wdn[...])

            @pl.when(ln.is_end)
            def _():
                sE2[j3] = p2.astype(BF)
                rcopy(sE2.at[j3], rE2.at[j3], ss.at[3, j3], rs.at[3, j3], ln.mid).start()

            @pl.when(ln.is_mid)
            def _():
                part2[j3] = p2

        j4 = i - a4

        @pl.when(ln.is_mid & (j4 >= 0) & (j4 < NC))
        def _():
            got(rE2, 3, j4)
            sX[j4] = (rE2[j4, ot_rows, :].astype(F32) + part2[j4, ot_rows, :]).astype(BF)
            rcopy(sX.at[j4], rX.at[j4], ss.at[4, j4], rs.at[4, j4], ln.other).start()

        j5 = i - a5

        @pl.when(ln.is_mid & (j5 >= 0) & (j5 < NC))
        def _():
            rcopy(rX.at[j5], rX.at[j5], ss.at[4, j5], rs.at[4, j5], ln.mid).wait_recv()
            rows = pl.ds(pl.multiple_of(j5 * R + ln.side * half, half), half)
            mlp = part2[j5, my_rows, :] + rE2[j5, my_rows, :].astype(F32) + rX[j5].astype(F32)
            x2_ref[j5, my_rows, :] = (mid_ref[rows, :] + mlp).astype(BF)
            mine = x2_ref.at[j5, my_rows, :]
            rcopy(mine, mine, ss.at[5, j5], rs.at[5, j5], ln.other).start()
            rcopy(mine, mine, ss.at[6, j5], rs.at[6, j5], ln.end).start()

        j6 = i - a6

        @pl.when(ln.is_mid & (j6 >= 0) & (j6 < NC))
        def _():
            got_half(ot_rows, 5, j6)
            theirs = x2_ref.at[j6, ot_rows, :]
            rcopy(theirs, theirs, ss.at[7, j6], rs.at[7, j6], ln.end).start()

        return 0

    lax.fori_loop(0, NC + a6, body, 0)

    for j, p in enumerate(rpeers):
        sends[j].wait()
    total = cbuf[0]
    for j in range(1, len(rpeers) + 1):
        total = total + cbuf[j]
    cnt_out[...] = total

    for c_to in range(1, NCTX):
        @pl.when(c_to > ctx)
        def _(c_to=c_to):
            kv_copy(k_ref, 0, c_to).wait_send()
            kv_copy(v_ref, 1, c_to).wait_send()

    def drain(k, _):
        @pl.when(ln.is_end)
        def _():
            got_half(my_rows, 6, k)
            got_half(ot_rows, 7, k)
            rcopy(sE.at[k], rE.at[k], ss.at[0, k], rs.at[0, k], ln.mid).wait_send()
            rcopy(sE2.at[k], rE2.at[k], ss.at[3, k], rs.at[3, k], ln.mid).wait_send()

        @pl.when(ln.is_mid)
        def _():
            rcopy(sI.at[k], rI.at[k], ss.at[1, k], rs.at[1, k], ln.other).wait_send()
            rcopy(sO.at[k], rI.at[k], ss.at[2, k], rs.at[1, k], ln.end).wait_send()
            rcopy(sX.at[k], rX.at[k], ss.at[4, k], rs.at[4, k], ln.other).wait_send()
            mine = x2_ref.at[k, my_rows, :]
            theirs = x2_ref.at[k, ot_rows, :]
            rcopy(mine, mine, ss.at[5, k], rs.at[5, k], ln.other).wait_send()
            rcopy(mine, mine, ss.at[6, k], rs.at[6, k], ln.end).wait_send()
            rcopy(theirs, theirs, ss.at[7, k], rs.at[7, k], ln.end).wait_send()

        return 0

    lax.fori_loop(0, NC, drain, 0)


CHUNK = 64


def dense_forward(x, again, mgain, seg, cnt, w_qkv, w_out, w_up, w_down):
    L, D = x.shape
    S = seg.shape[0]
    NT, NDP, NCTX = lax.axis_size("tensor"), lax.axis_size("dp"), lax.axis_size("ctx")
    R = CHUNK
    NC = L // R
    Hd = w_out.shape[1]
    Fl = w_up.shape[2]
    ctx = lax.axis_index("ctx")
    segc = lax.dynamic_slice_in_dim(seg, ctx * L, L, 0).reshape(NC, R, 1)
    sizes = (NC, R, D, L, S, NT, NDP, NCTX)
    flows = 8
    dma = pltpu.SemaphoreType.DMA
    rows = NDP * NCTX
    sd = jax.ShapeDtypeStruct
    v = pl.BlockSpec(memory_space=VM)
    a = pl.BlockSpec(memory_space=ANY)
    out = pl.pallas_call(
        functools.partial(dense_forward_kernel, sizes),
        name="dense_forward",
        out_shape=(
            sd((NC, R, D), BF), sd((L, Hd), BF), sd((S, Hd), BF), sd((S, Hd), BF), sd((L, Hd), BF),
            sd((L, 128), F32), sd((L, D), F32), sd((L, D), BF), sd((L, Fl), F32), sd((L, Fl), BF), sd((8, 128), F32),
        ),
        in_specs=[v] * 6 + [a] * 4,
        out_specs=(v,) * 11,
        scratch_shapes=[
            VM((3, D, Hd), BF), VM((Hd, D), BF), VM((D, Fl), BF), VM((Fl, D), BF),
            VM((NC, R, D), F32), VM((NC, R, D), F32),
            VM((NC, R, D), BF), VM((NC, R, D), BF), VM((NC, R, D), BF), VM((NC, R, D), BF), VM((NC, R, D), BF),
            VM((NC, R, D), BF), VM((NC, R, D), BF), VM((NC, R // 2, D), BF), VM((NC, R // 2, D), BF),
            VM((rows, 8, 128), F32),
            dma((4,)), dma((2, NCTX)), dma((2, NCTX)), dma((rows,)), dma((rows,)), dma((flows, NC)), dma((flows, NC)),
        ],
        compiler_params=pltpu.CompilerParams(collective_id=1, has_side_effects=True, vmem_limit_bytes=58 << 20),
    )(x, again, mgain, segc, seg.reshape(1, S), cnt, w_qkv, w_out, w_up, w_down)
    return out


BWD_LAGS = (1, 2, 3)
TAIL_LAGS = (1, 2, 3)


def share_add(own, came, d):
    def add(j, _):
        own[j] = (own[j].astype(F32) + came[j].astype(F32)).astype(BF)
        return 0

    lax.fori_loop(0, own.shape[0], add, 0)


def share_total(own, came, d):
    total = own[d].astype(F32)
    for j in range(came.shape[0]):
        total = total + came[j].astype(F32)
    return total


def dense_backward_kernel(
    sizes,
    x_ref, x2_ref, teach_ref, valid_ref, cnt_ref, sent_ref, gch_ref, ridx_ref, small_ref,
    again_ref, mgain_ref, segc_ref, segr_ref,
    q_ref, k_ref, v_ref, mix_ref, lse_ref, mid_ref, n2_ref, act_ref, pre_ref,
    wqkv_h, wout_h, wup_h, wdn_h, rdn_h, rup_h, rout_h, rqkv_h,
    hid_ref, loss_ref, gin_ref, dn_o, up_o, out_o, qkv_o, small_o,
    wqkv, wout, wup, wdn, g_s, gm_s, gpre_s, ga_s, n1_s, part, gqkv, dk_s, dv_s, rdk, rdv,
    sE, rE, sI, rI, sO, rE2, rX,
    tdn, odn, udn, wdn_r, tup, oup, uup, wup_r, tout, oout, uout, wout_r, tqkv, oqkv, uqkv, wqkv_r,
    ldn, lup, lout, lqkv, xdn, xup, xout, xqkv,
    acc_m, acc_a, lacc, lbuf, vec, vbuf, hbuf,
    wsem, lsem, kvsem, s1, r1, s2, r2, s3, r3, cs, cr, ts, tr, ss, rs,
):
    NC, R, D, L, S, NT, NDP, NCTX, scale_total = sizes
    ln = Line()
    ctx = lax.axis_index("ctx")
    dp = lax.axis_index("dp")
    half = R // 2
    G = NDP * NCTX
    W = D // G
    loads = [
        pltpu.make_async_copy(wdn_h.at[0], wdn, wsem.at[0]),
        pltpu.make_async_copy(wup_h.at[0], wup, wsem.at[1]),
        pltpu.make_async_copy(wout_h.at[0], wout, wsem.at[2]),
        pltpu.make_async_copy(wqkv_h.at[0], wqkv, wsem.at[3]),
    ]
    for ld in loads:
        ld.start()
    tpeers = tensor_peers(NT)
    rpeers = row_peers(NDP, NCTX)
    greet(tpeers + rpeers)

    routed = ((rdn_h, ldn, xdn), (rup_h, lup, xup), (rout_h, lout, xout), (rqkv_h, lqkv, xqkv))

    def routed_copy(w, j):
        src, _, dst = routed[w]
        to = lax.rem(dp + j, NDP)
        return rcopy(src.at[to], dst.at[j - 1], s3.at[w, j - 1], r3.at[w, j - 1], {"dp": to})

    def routed_own(w):
        return pltpu.make_async_copy(routed[w][0].at[dp], routed[w][1], lsem.at[w])

    for w in range(4):
        routed_own(w).start()
        for j in range(1, NDP):
            routed_copy(w, j).start()

    @pl.when(ln.is_end)
    def _():
        def zero(k, _):
            rE[k] = jnp.zeros((R, D), BF)
            return 0

        lax.fori_loop(0, NC, zero, 0)

    for ref in (dk_s, dv_s):
        ref[...] = jnp.zeros(ref.shape, F32)
    for ref in (acc_m, acc_a, lacc):
        ref[...] = jnp.zeros(ref.shape, F32)
    again = again_ref[0:1, :]
    mgain = mgain_ref[0:1, :]
    scale = scale_total / cnt_ref[0:1, 0:1]
    for ld in loads:
        ld.wait()

    groups = q_ref.shape[1] // 128
    Hd = q_ref.shape[1]

    def attend_back(j, gmix, keys):
        rows = pl.ds(pl.multiple_of(j * R, R), R)
        qpos = ctx * L + j * R + lax.broadcasted_iota(jnp.int32, (R, 1), 0)
        kpos = lax.broadcasted_iota(jnp.int32, (1, keys), 1)
        visible = (kpos <= qpos) & (segr_ref[:, :keys] == segc_ref[j])
        bias = jnp.where(visible, 0.0, masked_value)
        qi = q_ref[rows, :] * jnp.asarray(0.125, BF)
        lse = lse_ref[rows, :]
        for g in range(groups):
            cols = slice(128 * g, 128 * g + 128)
            q2 = head_pair(qi[:, cols])
            g2 = head_pair(gmix[:, cols])
            kg = k_ref[:keys, cols]
            vg = v_ref[:keys, cols]
            l2 = jnp.concatenate([lse[:, 2 * g : 2 * g + 1], lse[:, 2 * g + 1 : 2 * g + 2]], axis=0)
            s = (dot_nt(q2, kg).reshape(2, R, keys) + bias[None]).reshape(2 * R, keys)
            p = jnp.exp(s - l2)
            dp_ = dot_nt(g2, vg)
            inner = jnp.sum(p * dp_, axis=-1, keepdims=True)
            ds = (p * (dp_ - inner)).astype(BF)
            gq = pair_join(dot_nn(ds, kg)) * 0.125
            gqkv[0, rows, cols] = gq.astype(BF)
            dk_s[:keys, cols] += dot_tn(ds, q2)
            dv_s[:keys, cols] += dot_tn(p.astype(BF), g2)

    a1, a2, a3 = BWD_LAGS
    lag3 = jnp.where(ln.is_end, a3, a2)
    my_rows = pl.ds(pl.multiple_of(ln.side * half, half), half)
    ot_rows = pl.ds(pl.multiple_of((1 - ln.side) * half, half), half)

    def got(buf, flow, j):
        rcopy(buf.at[j], buf.at[j], ss.at[flow, j], rs.at[flow, j], ln.mid).wait_recv()

    def got_half(rows, flow, j):
        rcopy(gin_ref.at[j, rows, :], gin_ref.at[j, rows, :], ss.at[flow, j], rs.at[flow, j], ln.mid).wait_recv()

    def by_share(piece, send, keep):
        for c in range(NCTX):
            def one(d, _, c=c):
                val = piece(d * NCTX + c)

                @pl.when(ctx == c)
                def _():
                    keep[d] = val

                @pl.when(ctx != c)
                def _():
                    send[d] = val

                return 0

            lax.fori_loop(0, NDP, one, 0)

    def cols_of(g):
        return pl.ds(pl.multiple_of(g * W, W), W)

    def piece_dn(g):
        return dot_tn(act_ref[...], gm_s[:, cols_of(g)]).astype(BF)

    def piece_up(g):
        return dot_tn(n2_ref[:, cols_of(g)], gpre_s[...]).astype(BF)

    def piece_out(g):
        return dot_tn(mix_ref[...], ga_s[:, cols_of(g)]).astype(BF)

    def piece_qkv(g):
        lhs = n1_s[:, cols_of(g)]
        return jnp.concatenate([dot_tn(lhs, gqkv[c]) for c in range(3)], axis=1).astype(BF)

    shares = (
        (piece_dn, tdn, odn, udn, wdn_r),
        (piece_up, tup, oup, uup, wup_r),
        (piece_out, tout, oout, uout, wout_r),
        (piece_qkv, tqkv, oqkv, uqkv, wqkv_r),
    )
    across = {"ctx": 1 - ctx}

    def pair_copy(w):
        return rcopy(shares[w][1], shares[w][3], s1.at[w], r1.at[w], across)

    def share_first(w):
        by_share(shares[w][0], shares[w][1], shares[w][2])
        pair_copy(w).start()

    def dp_copy(w, j):
        to = lax.rem(dp + j, NDP)
        return rcopy(shares[w][2].at[to], shares[w][4].at[j - 1], s2.at[w, j - 1], r2.at[w, j - 1], {"dp": to})

    def share_second(w):
        pair_copy(w).wait_recv()
        share_add(shares[w][2], shares[w][3], dp)
        for j in range(1, NDP):
            dp_copy(w, j).start()

    me = dp * NCTX + ctx

    def body(i, _):
        @pl.when(i < NC)
        def _():
            rows = pl.ds(pl.multiple_of(i * R, R), R)
            place = ctx * L + i * R + lax.broadcasted_iota(jnp.int32, (R, 1), 0)
            pick = (place == ridx_ref[...]).astype(F32).astype(BF)
            x3 = x2_ref[i].astype(F32) + dot_nn(pick, sent_ref[...])
            hid_ref[rows, :] = x3.astype(BF)
            err = x3 - teach_ref[rows, :].astype(F32)
            counted = valid_ref[i] * err
            lacc[...] += fold8(counted * err)
            g2 = scale * counted + dot_nn(pick, gch_ref[...])
            g_s[rows, :] = g2
            gm = g2.astype(BF)
            gm_s[rows, :] = gm
            gact = dot_nt(gm, wdn[...])
            u = pre_ref[rows, :]
            t = gelu_pair(u)
            slope = 0.5 * (1.0 + t) + 0.5 * u * (1.0 - t * t) * (0.7978845608028654 * (1.0 + 3.0 * 0.044715 * u * u))
            gpre = (gact * slope).astype(BF)
            gpre_s[rows, :] = gpre
            p3 = dot_nt(gpre, wup[...])
            part[i] = p3

            @pl.when(ln.is_end)
            def _():
                sE[i] = p3.astype(BF)
                rcopy(sE.at[i], rE.at[i], ss.at[0, i], rs.at[0, i], ln.mid).start()

            n1_s[rows, :] = (rms_parts(x_ref[rows, :].astype(F32))[1] * again).astype(BF)

        j1 = i - a1

        @pl.when(ln.is_mid & (j1 >= 0) & (j1 < NC))
        def _():
            got(rE, 0, j1)
            sI[j1] = (rE[j1].astype(F32) + part[j1]).astype(BF)
            rcopy(sI.at[j1], rI.at[j1], ss.at[1, j1], rs.at[1, j1], ln.other).start()

        j3 = i - lag3

        @pl.when((j3 >= 0) & (j3 < NC))
        def _():
            got(rI, 1, j3)
            inner = rI[j3].astype(F32) + part[j3]

            @pl.when(ln.is_mid)
            def _():
                sO[j3] = inner.astype(BF)
                rcopy(sO.at[j3], rI.at[j3], ss.at[2, j3], rs.at[1, j3], ln.end).start()

            rows = pl.ds(pl.multiple_of(j3 * R, R), R)
            gn2 = inner + rE[j3].astype(F32)
            gmid, gain_rows = rms_back(mid_ref[rows, :], mgain, gn2)
            acc_m[...] += fold8(gain_rows)
            gattn = g_s[rows, :] + gmid
            g_s[rows, :] = gattn
            ga = gattn.astype(BF)
            ga_s[rows, :] = ga
            gmix = dot_nt(ga, wout[...]).astype(BF)

            @pl.when(ctx == 0)
            def _():
                attend_back(j3, gmix, L)

            @pl.when(ctx > 0)
            def _():
                attend_back(j3, gmix, S)

        @pl.when(i == NC)
        def _():
            share_first(0)
            part_loss = jnp.sum(lacc[...])
            lbuf[me] = jnp.full((8, 128), part_loss, F32)
            for j, p in enumerate(rpeers):
                rcopy(lbuf.at[me], lbuf.at[me], cs.at[j], cr.at[j], p).start()

        @pl.when(i == NC + 1)
        def _():
            share_first(1)

        return 0

    lax.fori_loop(0, NC + max(a3, 2), body, 0)

    def kv_copy(which):
        src, dst = ((dk_s, rdk), (dv_s, rdv))[which]
        return rcopy(src.at[pl.ds(0, L), :], dst, kvsem.at[which, 0], kvsem.at[which, 1], {"ctx": 0})

    @pl.when(ctx > 0)
    def _():
        kv_copy(0).start()
        kv_copy(1).start()
        for which, ref in enumerate((dk_s, dv_s)):
            gqkv[1 + which] = ref[pl.ds(L, L), :].astype(BF)

    share_first(2)

    @pl.when(ctx == 0)
    def _():
        for which, (ref, came) in enumerate(((dk_s, rdk), (dv_s, rdv))):
            kv_copy(which).wait_recv()
            gqkv[1 + which] = (ref[pl.ds(0, L), :] + came[...]).astype(BF)

    def settle(k, _):
        @pl.when(ln.is_end)
        def _():
            rcopy(sE.at[k], rE.at[k], ss.at[0, k], rs.at[0, k], ln.mid).wait_send()

        @pl.when(ln.is_mid)
        def _():
            rcopy(sI.at[k], rI.at[k], ss.at[1, k], rs.at[1, k], ln.other).wait_send()
            rcopy(sO.at[k], rI.at[k], ss.at[2, k], rs.at[1, k], ln.end).wait_send()

        return 0

    lax.fori_loop(0, NC, settle, 0)

    b4, b5, b6 = TAIL_LAGS
    sX = sI

    def tail(i, _):
        @pl.when(i < NC)
        def _():
            rows = pl.ds(pl.multiple_of(i * R, R), R)
            p4 = dot_nt(gqkv[0, rows, :], wqkv[0])
            p4 = p4 + dot_nt(gqkv[1, rows, :], wqkv[1])
            p4 = p4 + dot_nt(gqkv[2, rows, :], wqkv[2])

            @pl.when(ln.is_end)
            def _():
                sE[i] = p4.astype(BF)
                rcopy(sE.at[i], rE2.at[i], ss.at[3, i], rs.at[3, i], ln.mid).start()

            @pl.when(ln.is_mid)
            def _():
                part[i] = p4

        j4 = i - b4

        @pl.when(ln.is_mid & (j4 >= 0) & (j4 < NC))
        def _():
            got(rE2, 3, j4)
            sX[j4, pl.ds(0, half), :] = (rE2[j4, ot_rows, :].astype(F32) + part[j4, ot_rows, :]).astype(BF)
            rcopy(sX.at[j4, pl.ds(0, half), :], rX.at[j4], ss.at[4, j4], rs.at[4, j4], ln.other).start()

        j5 = i - b5

        @pl.when(ln.is_mid & (j5 >= 0) & (j5 < NC))
        def _():
            got(rX, 4, j5)
            rows = pl.ds(pl.multiple_of(j5 * R + ln.side * half, half), half)
            gn1 = part[j5, my_rows, :] + rE2[j5, my_rows, :].astype(F32) + rX[j5].astype(F32)
            gin, gain_rows = rms_back(x_ref[rows, :].astype(F32), again, gn1)
            acc_a[...] += fold8(gain_rows)
            gin_ref[j5, my_rows, :] = (g_s[rows, :] + gin).astype(BF)
            mine = gin_ref.at[j5, my_rows, :]
            rcopy(mine, mine, ss.at[5, j5], rs.at[5, j5], ln.other).start()
            rcopy(mine, mine, ss.at[6, j5], rs.at[6, j5], ln.end).start()

        j6 = i - b6

        @pl.when(ln.is_mid & (j6 >= 0) & (j6 < NC))
        def _():
            got_half(ot_rows, 5, j6)
            theirs = gin_ref.at[j6, ot_rows, :]
            rcopy(theirs, theirs, ss.at[7, j6], rs.at[7, j6], ln.end).start()

        @pl.when(i == 1)
        def _():
            share_second(0)

        @pl.when(i == 2)
        def _():
            share_second(1)
            share_second(2)

        @pl.when(i == 3)
        def _():
            share_first(3)

        @pl.when(i == 5)
        def _():
            share_second(3)

        return 0

    lax.fori_loop(0, NC + b6, tail, 0)

    vec[...] = small_ref[...]
    vec[0:1, :] = vec[0:1, :] + jnp.sum(acc_a[...], axis=0, keepdims=True)
    vec[1:2, :] = vec[1:2, :] + jnp.sum(acc_m[...], axis=0, keepdims=True) * (1.0 / NT)

    def vec_copy(j, d2, c2):
        return rcopy(vec.at[:, cols_of(d2 * NCTX + c2)], vbuf.at[me], ts.at[j], tr.at[j], {"dp": d2, "ctx": c2})

    places = []
    for j in range(NDP):
        for k in range(NCTX):
            if j or k:
                places.append((lax.rem(dp + j, NDP), lax.rem(ctx + k, NCTX)))
    for n, (d2, c2) in enumerate(places):
        vec_copy(n, d2, c2).start()
    vbuf[me] = vec[:, cols_of(me)]

    for w, (out, _) in enumerate(((dn_o, 0), (up_o, 0), (out_o, 0), (qkv_o, 0))):
        routed_own(w).wait()
        for j in range(1, NDP):
            routed_copy(w, j).wait()
        total = routed[w][1][...].astype(F32)
        for j in range(NDP - 1):
            total = total + routed[w][2][j].astype(F32)
        if w < 3:
            out[1] = total
        else:
            for c in range(3):
                out[1, c] = total[:, Hd * c : Hd * c + Hd]
    for w, out in enumerate((dn_o, up_o, out_o, qkv_o)):
        for j in range(1, NDP):
            dp_copy(w, j).wait()
        total = share_total(shares[w][2], shares[w][4], dp)
        if w < 3:
            out[0] = total
        else:
            for c in range(3):
                out[0, c] = total[:, Hd * c : Hd * c + Hd]

    for n, (d2, c2) in enumerate(places):
        vec_copy(n, d2, c2).wait()
    rows_sum = vbuf[0]
    for j in range(1, G):
        rows_sum = rows_sum + vbuf[j]
    hbuf[ln.t] = rows_sum

    def line_copy(n, p):
        return rcopy(hbuf.at[ln.t], hbuf.at[ln.t], ts.at[G - 1 + n], tr.at[G - 1 + n], p)

    for n, p in enumerate(tpeers):
        line_copy(n, p).start()
    for n, p in enumerate(tpeers):
        line_copy(n, p).wait()
    line_sum = hbuf[0]
    for j in range(1, NT):
        line_sum = line_sum + hbuf[j]
    small_o[...] = line_sum

    for j, p in enumerate(rpeers):
        rcopy(lbuf.at[me], lbuf.at[me], cs.at[j], cr.at[j], p).wait()
    loss = lbuf[0]
    for j in range(1, G):
        loss = loss + lbuf[j]
    loss_ref[...] = loss / (cnt_ref[...] * D)

    for w in range(4):
        pair_copy(w).wait_send()

    @pl.when(ctx > 0)
    def _():
        kv_copy(0).wait_send()
        kv_copy(1).wait_send()

    def drain(k, _):
        @pl.when(ln.is_end)
        def _():
            got_half(my_rows, 6, k)
            got_half(ot_rows, 7, k)
            rcopy(sE.at[k], rE2.at[k], ss.at[3, k], rs.at[3, k], ln.mid).wait_send()

        @pl.when(ln.is_mid)
        def _():
            rcopy(sX.at[k, pl.ds(0, half), :], rX.at[k], ss.at[4, k], rs.at[4, k], ln.other).wait_send()
            mine = gin_ref.at[k, my_rows, :]
            theirs = gin_ref.at[k, ot_rows, :]
            rcopy(mine, mine, ss.at[5, k], rs.at[5, k], ln.other).wait_send()
            rcopy(mine, mine, ss.at[6, k], rs.at[6, k], ln.end).wait_send()
            rcopy(theirs, theirs, ss.at[7, k], rs.at[7, k], ln.end).wait_send()

        return 0

    lax.fori_loop(0, NC, drain, 0)


BCHUNK = 64


def dense_backward(x, teacher, valid, cnt, sent, gchosen, ridx, small, again, mgain, seg, fwd, w_qkv, w_out, w_up, w_down, routed):
    L, D = x.shape
    S = seg.shape[0]
    NT, NDP, NCTX = lax.axis_size("tensor"), lax.axis_size("dp"), lax.axis_size("ctx")
    x2, q, k, v, mix, lse, mid, n2, pre, act = fwd
    R = BCHUNK
    NC = L // R
    Hd = w_out.shape[1]
    Fl = w_up.shape[2]
    G = NDP * NCTX
    W = D // G
    ctx = lax.axis_index("ctx")
    segc = lax.dynamic_slice_in_dim(seg, ctx * L, L, 0).reshape(NC, R, 1)
    validc = valid.astype(F32).reshape(NC, R, 1)
    sizes = (NC, R, D, L, S, NT, NDP, NCTX, float(S * NDP))
    dma = pltpu.SemaphoreType.DMA
    sd = jax.ShapeDtypeStruct
    v_ = pl.BlockSpec(memory_space=VM)
    a_ = pl.BlockSpec(memory_space=ANY)

    def four(shape):
        return [VM((NDP,) + shape, BF)] * 3 + [VM((NDP - 1,) + shape, BF)]

    wshape = ((Fl, W), (W, Fl), (Hd, W), (W, 3 * Hd))
    dense_shares = sum((four(s) for s in wshape), [])
    routed_scratch = [VM(s, BF) for s in wshape] + [VM((NDP - 1,) + s, BF) for s in wshape]
    big = VM((NC, R, D), BF)
    return pl.pallas_call(
        functools.partial(dense_backward_kernel, sizes),
        name="dense_backward",
        out_shape=(
            sd((L, D), BF), sd((8, 128), F32), sd((NC, R, D), BF),
            sd((2, Fl, W), F32), sd((2, W, Fl), F32), sd((2, Hd, W), F32), sd((2, 3, W, Hd), F32), sd((8, W), F32),
        ),
        in_specs=[v_] * 22 + [a_] * 8,
        out_specs=(v_,) * 8,
        scratch_shapes=[
            VM((3, D, Hd), BF), VM((Hd, D), BF), VM((D, Fl), BF), VM((Fl, D), BF),
            VM((L, D), F32), VM((L, D), BF), VM((L, Fl), BF), VM((L, D), BF), VM((L, D), BF),
            VM((NC, R, D), F32), VM((3, L, Hd), BF), VM((S, Hd), F32), VM((S, Hd), F32), VM((L, Hd), F32), VM((L, Hd), F32),
            big, big, big, big, big, big, VM((NC, R // 2, D), BF),
        ] + dense_shares + routed_scratch + [
            VM((8, D), F32), VM((8, D), F32), VM((8, D), F32), VM((G, 8, 128), F32),
            VM((8, D), F32), VM((G, 8, W), F32), VM((NT, 8, W), F32),
            dma((4,)), dma((4,)), dma((2, 2)), dma((4,)), dma((4,)), dma((4, NDP)), dma((4, NDP)), dma((4, NDP)), dma((4, NDP)),
            dma((G,)), dma((G,)), dma((G + NT,)), dma((G + NT,)), dma((8, NC)), dma((8, NC)),
        ],
        compiler_params=pltpu.CompilerParams(collective_id=3, has_side_effects=True, vmem_limit_bytes=62 << 20),
    )(
        x, x2.reshape(NC, R, D), teacher, validc, cnt, sent, gchosen, ridx, small, again, mgain, segc, seg.reshape(1, S),
        q, k, v, mix, lse, mid, n2, act, pre, w_qkv, w_out, w_up, w_down, *routed,
    )


def routed_by_xla(x2, teacher, valid, cnt, ridx, seg, again, mgain, w_qkv, w_out, w_up, w_down, w_router):
    L, D = teacher.shape
    ctx = lax.axis_index("ctx")
    NDP, NCTX = lax.axis_size("dp"), lax.axis_size("ctx")
    G = NDP * NCTX
    RL = ridx.shape[1] // NCTX
    routed_seg = take_rows(seg[None], ridx)
    qpos = lax.dynamic_slice_in_dim(ridx, ctx * RL, RL, 1)
    qseg = lax.dynamic_slice_in_dim(routed_seg, ctx * RL, RL, 1)
    owner_mine = ridx // L == ctx
    owner_row = ridx % L
    attend, attend_grad = make_attention(qpos, ridx, qseg, routed_seg)
    layer_mid = x2.reshape(1, L, D).astype(F32)
    picked = jnp.where(owner_mine[..., None], take_rows(layer_mid, owner_row), 0.0)
    chosen = to_workers(picked).astype(F32)
    gating = gating_fn(chosen, w_router)
    attn_r, mlp_r, saved = block_forward(
        chosen, again[1], w_qkv[1], w_out[1], mgain[1], w_up[1], w_down[1], attend
    )
    branch = attn_r + mlp_r
    sent_rows = (gating[..., None] * branch).astype(BF)
    sent = to_owners(sent_rows)
    layer_out = add_rows(layer_mid, owner_row, jnp.where(owner_mine[..., None], sent.astype(F32), 0.0))
    vr = valid.astype(F32)
    err = layer_out - teacher[None].astype(F32)
    gfinal = float(seg.shape[0] * NDP) / cnt[0, 0] * vr[..., None] * err
    pg = jnp.where(owner_mine[..., None], take_rows(gfinal, owner_row), 0.0)
    bgrad = to_workers(pg).astype(F32)
    top = gating[..., None] * bgrad
    _, gback = jax.vjp(gating_fn, chosen, w_router)
    gchoose, grouter = gback(jnp.sum(bgrad * branch, axis=-1))
    ga, gm, gr, grads = block_backward(
        saved, top, again[1], w_qkv[1], w_out[1], mgain[1], w_up[1], w_down[1], attend_grad
    )
    gch = to_owners((gm + gr + gchoose).astype(BF))
    g_gain_a, g_qkv, g_out, g_gain_m, g_up, g_dn = grads

    def pack(a, dim, lead):
        a = jnp.moveaxis(a.reshape(a.shape[:dim] + (NDP, NCTX, a.shape[dim] // G) + a.shape[dim + 1 :]), (dim, dim + 1), (1, 0))
        return lax.psum_scatter(a.astype(BF), "ctx", scatter_dimension=0, tiled=False)

    rdn = pack(g_dn, 1, 0)
    rup = pack(g_up, 0, 0)
    rout = pack(g_out, 1, 0)
    rqkv = pack(g_qkv, 1, 0)
    rqkv = jnp.moveaxis(rqkv, 1, 2).reshape(NDP, D // G, -1)
    own = jnp.where(lax.axis_index("tensor") == 0, 1.0, 0.0)
    z = jnp.zeros((D,), F32)
    small = jnp.stack([z, z, g_gain_a * own, g_gain_m * own, grouter * own, z, z, z])
    return sent[0], gch[0], small, (rdn, rup, rout, rqkv)


def fast_local(hidden_in, teacher, seg_ids, valid, routed_idx, attn_gain, w_qkv, w_out, mlp_gain, w_up, w_down, w_router):
    cnt = jnp.full((8, 128), jnp.sum(valid).astype(F32))
    seg = seg_ids[0]
    fwd = dense_forward(hidden_in[0], attn_gain, mlp_gain, seg, cnt, w_qkv, w_out, w_up, w_down)
    cnt = fwd[10]
    sent, gch, small, routed = routed_by_xla(
        fwd[0], teacher[0], valid, cnt, routed_idx, seg, attn_gain, mlp_gain, w_qkv, w_out, w_up, w_down, w_router
    )
    hid, loss, gin, dn, up, out, qkv, small = dense_backward(
        hidden_in[0], teacher[0], valid[0], cnt, sent, gch, routed_idx, small, attn_gain, mlp_gain, seg, fwd[:10],
        w_qkv, w_out, w_up, w_down, routed,
    )
    L, D = hidden_in.shape[1:]
    return (
        hid[None], loss[0, 0], gin.reshape(1, L, D).astype(F32),
        jnp.stack([small[0], small[2]]), qkv, out, jnp.stack([small[1], small[3]]), up, dn, small[4],
    )


def takes_kernels(mesh):
    shape = dict(mesh.shape)
    return shape["tensor"] == 4 and shape["ctx"] == 2


def solution(mesh):
    placed = (
        P("dp", "ctx", None),
        P("dp", "ctx", None),
        P("dp", None),
        P("dp", "ctx"),
        P("dp", None),
        P(),
        P(None, None, None, "tensor"),
        P(None, "tensor", None),
        P(),
        P(None, None, "tensor"),
        P(None, "tensor", None),
        P(),
    )
    return jax.shard_map(
        fast_local if takes_kernels(mesh) else plain_local,
        mesh=mesh,
        in_specs=placed,
        out_specs=(
            P("dp", "ctx", None),
            P(),
            P("dp", "ctx", None),
            P(None, ("dp", "ctx")),
            P(None, None, ("dp", "ctx"), "tensor"),
            P(None, "tensor", ("dp", "ctx")),
            P(None, ("dp", "ctx")),
            P(None, ("dp", "ctx"), "tensor"),
            P(None, "tensor", ("dp", "ctx")),
            P(("dp", "ctx")),
        ),
        check_vma=False,
    )
```

```python
import functools

import jax
import jax.numpy as jnp
from jax import lax
from jax.experimental import pallas as pl
from jax.experimental.pallas import tpu as pltpu
from jax.sharding import PartitionSpec as P

HEAD = 64
epsilon = 1e-06
masked_value = -1e30
MESH = pl.DeviceIdType.MESH
BF = jnp.bfloat16
F32 = jnp.float32
VM = pltpu.VMEM
ANY = pl.ANY


def rcopy(src, dst, send, recv, where):
    return pltpu.make_async_remote_copy(
        src_ref=src, dst_ref=dst, send_sem=send, recv_sem=recv, device_id=where, device_id_type=MESH
    )


def dot_nn(a, b):
    return lax.dot_general(a, b, (((1,), (0,)), ((), ())), preferred_element_type=F32)


def dot_nt(a, b):
    return lax.dot_general(a, b, (((1,), (1,)), ((), ())), preferred_element_type=F32)


def dot_tn(a, b):
    return lax.dot_general(a, b, (((0,), (0,)), ((), ())), preferred_element_type=F32)


def rms_parts(values):
    r = lax.rsqrt(jnp.mean(values * values, axis=-1, keepdims=True) + epsilon)
    return r, values * r


def rms_back(values, gain, grad):
    r, unit = rms_parts(values)
    scaled = grad * gain
    return r * (scaled - unit * jnp.mean(scaled * unit, axis=-1, keepdims=True)), grad * unit


def gelu_pair(u):
    c = 0.7978845608028654
    t = jnp.tanh(c * (u + 0.044715 * (u * u * u)))
    return t


def fold8(rows):
    return jnp.sum(rows.reshape(rows.shape[0] // 8, 8, rows.shape[1]), axis=0)


class Line:
    def __init__(self):
        t = lax.axis_index("tensor")
        self.t = t
        self.side = t // 2
        self.is_end = (t == 0) | (t == 3)
        self.is_mid = (t == 1) | (t == 2)
        self.end = {"tensor": self.side * 3}
        self.mid = {"tensor": 1 + self.side}
        self.other = {"tensor": 2 - self.side}


def greet(peers):
    bar = pltpu.get_barrier_semaphore()
    for p in peers:
        pl.semaphore_signal(bar, inc=1, device_id=p, device_id_type=MESH)
    pl.semaphore_wait(bar, len(peers))


def tensor_peers(n):
    t = lax.axis_index("tensor")
    return [{"tensor": lax.rem(t + j, n)} for j in range(1, n)]


def row_peers(n_dp, n_ctx):
    d, c = lax.axis_index("dp"), lax.axis_index("ctx")
    out = []
    for j in range(n_dp):
        for k in range(n_ctx):
            if j or k:
                out.append({"dp": lax.rem(d + j, n_dp), "ctx": lax.rem(c + k, n_ctx)})
    return out


def rms_scale(values, gain):
    return values * lax.rsqrt(jnp.mean(values * values, axis=-1, keepdims=True) + epsilon) * gain


def gelu_tanh(values):
    return jax.nn.gelu(values, approximate=True)


def gating_fn(chosen, router):
    return jax.nn.sigmoid(jnp.sum(chosen * router, axis=-1))


def tensor_sum(partial_sum):
    return lax.psum(partial_sum, "tensor")


def gather_keys(projected):
    return (
        lax.all_gather(projected[1], "ctx", axis=1, tiled=True),
        lax.all_gather(projected[2], "ctx", axis=1, tiled=True),
    )


def scatter_key_grads(grad_k, grad_v):
    stacked = jnp.stack([grad_k, grad_v])
    summed = lax.psum_scatter(stacked, "ctx", scatter_dimension=2, tiled=True)
    return (summed[0], summed[1])


def to_workers(picked):
    return lax.psum_scatter(
        picked.astype(jnp.bfloat16), "ctx", scatter_dimension=1, tiled=True
    ).astype(jnp.float32)


def to_owners(rows_low):
    return lax.all_gather(rows_low, "ctx", axis=1, tiled=True)


def take_rows(table, places):
    return jax.vmap(lambda t, i: t[i])(table, places)


def add_rows(table, places, addend):
    return jax.vmap(lambda t, i, a: t.at[i].add(a))(table, places, addend)


def tile_scores(q_tile, k_tile, qpos_tile, kpos_tile, qseg_tile, kseg_tile, score_scale):
    scores = (
        jnp.einsum("qhe,khe->hqk", q_tile, k_tile, preferred_element_type=jnp.float32) * score_scale
    )
    visible = (kpos_tile[None, :] <= qpos_tile[:, None]) & (
        kseg_tile[None, :] == qseg_tile[:, None]
    )
    return (scores, visible[None])


def tile_layout(queries, key_rows, value_rows, k_pos, k_seg):
    q_len, row_width = queries.shape
    k_len = key_rows.shape[0]
    head_count = row_width // HEAD
    q_step = min(512, q_len)
    k_step = min(2048, k_len)
    k_count = k_len // k_step
    key_tiles = key_rows.reshape(k_count, k_step, head_count, HEAD)
    value_tiles = value_rows.reshape(k_count, k_step, head_count, HEAD)
    kpos_tiles = k_pos.reshape(k_count, k_step)
    kseg_tiles = k_seg.reshape(k_count, k_step)
    return (
        q_len,
        row_width,
        k_len,
        head_count,
        q_step,
        (key_tiles, value_tiles, kpos_tiles, kseg_tiles),
    )


def attend_one(queries, key_rows, value_rows, q_pos, k_pos, q_seg, k_seg):
    q_len, row_width, k_len, head_count, q_step, tiles = tile_layout(
        queries, key_rows, value_rows, k_pos, k_seg
    )
    score_scale = 1.0 / HEAD**0.5

    def per_query(q_args):
        q_tile, qpos_tile, qseg_tile = q_args

        def total_step(carry, k_args):
            running, summed = carry
            k_tile, v_tile, kpos_tile, kseg_tile = k_args
            scores, visible = tile_scores(
                q_tile, k_tile, qpos_tile, kpos_tile, qseg_tile, kseg_tile, score_scale
            )
            raised = jnp.maximum(
                running, jnp.max(jnp.where(visible, scores, masked_value), axis=-1)
            )
            weights = jnp.where(visible, jnp.exp(scores - raised[..., None]), 0.0)
            return ((raised, summed * jnp.exp(running - raised) + jnp.sum(weights, axis=-1)), None)

        initial = (
            jnp.full((head_count, q_step), masked_value, jnp.float32),
            jnp.zeros((head_count, q_step), jnp.float32),
        )
        (running, summed), _ = lax.scan(total_step, initial, tiles)
        log_total = running + jnp.log(summed)

        def value_step(output, k_args):
            k_tile, v_tile, kpos_tile, kseg_tile = k_args
            scores, visible = tile_scores(
                q_tile, k_tile, qpos_tile, kpos_tile, qseg_tile, kseg_tile, score_scale
            )
            weights_low = jnp.where(visible, jnp.exp(scores - log_total[..., None]), 0.0).astype(
                jnp.bfloat16
            )
            return (
                output
                + jnp.einsum(
                    "hqk,khe->qhe", weights_low, v_tile, preferred_element_type=jnp.float32
                ),
                None,
            )

        output, _ = lax.scan(value_step, jnp.zeros((q_step, head_count, HEAD), jnp.float32), tiles)
        return (output, log_total)

    q_count = q_len // q_step
    output, log_total = lax.map(
        per_query,
        (
            queries.reshape(q_count, q_step, head_count, HEAD),
            q_pos.reshape(q_count, q_step),
            q_seg.reshape(q_count, q_step),
        ),
    )
    return (output.reshape(q_len, row_width), log_total)


def attend_back(queries, key_rows, value_rows, grad_mixed, log_total, q_pos, k_pos, q_seg, k_seg):
    q_len, row_width, k_len, head_count, q_step, tiles = tile_layout(
        queries, key_rows, value_rows, k_pos, k_seg
    )
    score_scale = 1.0 / HEAD**0.5

    def per_query(q_args):
        q_tile, g_tile, total_tile, qpos_tile, qseg_tile = q_args

        def tile_probs(k_tile, kpos_tile, kseg_tile):
            scores, visible = tile_scores(
                q_tile, k_tile, qpos_tile, kpos_tile, qseg_tile, kseg_tile, score_scale
            )
            return jnp.where(visible, jnp.exp(scores - total_tile[..., None]), 0.0)

        def inner_step(carry, k_args):
            k_tile, v_tile, kpos_tile, kseg_tile = k_args
            weights = tile_probs(k_tile, kpos_tile, kseg_tile)
            grad_weights = jnp.einsum(
                "qhe,khe->hqk", g_tile, v_tile, preferred_element_type=jnp.float32
            )
            return (carry + jnp.sum(weights * grad_weights, axis=-1), None)

        inner, _ = lax.scan(inner_step, jnp.zeros((head_count, q_step), jnp.float32), tiles)

        def grad_step(carry, k_args):
            k_tile, v_tile, kpos_tile, kseg_tile = k_args
            weights = tile_probs(k_tile, kpos_tile, kseg_tile)
            grad_weights = jnp.einsum(
                "qhe,khe->hqk", g_tile, v_tile, preferred_element_type=jnp.float32
            )
            grad_scores = (weights * (grad_weights - inner[..., None])).astype(jnp.bfloat16)
            carry = carry + jnp.einsum(
                "hqk,khe->qhe", grad_scores, k_tile, preferred_element_type=jnp.float32
            )
            grad_keys = jnp.einsum(
                "hqk,qhe->khe", grad_scores, q_tile, preferred_element_type=jnp.float32
            )
            grad_values = jnp.einsum(
                "hqk,qhe->khe",
                weights.astype(jnp.bfloat16),
                g_tile,
                preferred_element_type=jnp.float32,
            )
            return (carry, (grad_keys, grad_values))

        grad_q, (grad_keys, grad_values) = lax.scan(
            grad_step, jnp.zeros((q_step, head_count, HEAD), jnp.float32), tiles
        )
        return (
            grad_q * score_scale,
            grad_keys.reshape(k_len, row_width) * score_scale,
            grad_values.reshape(k_len, row_width),
        )

    q_count = q_len // q_step
    grad_q, grad_keys, grad_values = lax.map(
        per_query,
        (
            queries.reshape(q_count, q_step, head_count, HEAD),
            grad_mixed.reshape(q_count, q_step, head_count, HEAD),
            log_total,
            q_pos.reshape(q_count, q_step),
            q_seg.reshape(q_count, q_step),
        ),
    )
    return (
        grad_q.reshape(q_len, row_width),
        jnp.sum(grad_keys, axis=0),
        jnp.sum(grad_values, axis=0),
    )


def make_attention(q_pos, k_pos, q_seg, k_seg):

    def attend_fn(projected):
        key_all, value_all = gather_keys(projected)
        mixed_full, log_total = lax.map(
            lambda a: attend_one(*a), (projected[0], key_all, value_all, q_pos, k_pos, q_seg, k_seg)
        )
        return (mixed_full, (key_all, value_all, log_total))

    def attend_grad(projected, kept, grad_mixed):
        key_all, value_all, log_total = kept
        grad_q, grad_k, grad_v = lax.map(
            lambda a: attend_back(*a),
            (projected[0], key_all, value_all, grad_mixed, log_total, q_pos, k_pos, q_seg, k_seg),
        )
        grad_k, grad_v = scatter_key_grads(grad_k, grad_v)
        return jnp.stack(
            [grad_q.astype(jnp.bfloat16), grad_k.astype(jnp.bfloat16), grad_v.astype(jnp.bfloat16)]
        )

    return (attend_fn, attend_grad)


def block_forward(
    resid_in,
    gain_a,
    query_key_value_weight,
    output_weight_matrix,
    gain_m,
    up_weight_matrix,
    down_weight_matrix,
    attend_fn,
):
    attention_norm = rms_scale(resid_in, gain_a).astype(jnp.bfloat16)
    projected = jnp.einsum(
        "oym,qmh->qoyh", attention_norm, query_key_value_weight, preferred_element_type=jnp.float32
    ).astype(jnp.bfloat16)
    mixed_full, kept = attend_fn(projected)
    mixed_state = mixed_full.astype(jnp.bfloat16)
    attention_portion = jnp.einsum(
        "xtu,ua->xta", mixed_state, output_weight_matrix, preferred_element_type=jnp.float32
    )
    attn_out = tensor_sum(attention_portion)
    middle = resid_in + attn_out
    feedforward_norm = rms_scale(middle, gain_m).astype(jnp.bfloat16)
    hidden_preactivation = jnp.einsum(
        "iqp,po->iqo", feedforward_norm, up_weight_matrix, preferred_element_type=jnp.float32
    )
    hidden_activation = gelu_tanh(hidden_preactivation).astype(jnp.bfloat16)
    mlp_part = jnp.einsum(
        "euq,qt->eut", hidden_activation, down_weight_matrix, preferred_element_type=jnp.float32
    )
    mlp_out = tensor_sum(mlp_part)
    saved = (
        resid_in,
        attention_norm,
        projected,
        mixed_state,
        kept,
        middle,
        feedforward_norm,
        hidden_preactivation,
        hidden_activation,
    )
    return (attn_out, mlp_out, saved)


def block_backward(
    saved,
    grad_top,
    gain_a,
    query_key_value_weight,
    output_weight_matrix,
    gain_m,
    up_weight_matrix,
    down_weight_matrix,
    attend_grad,
):
    (
        resid_in,
        attention_norm,
        projected,
        mixed_state,
        kept,
        middle,
        feedforward_norm,
        hidden_preactivation,
        hidden_activation,
    ) = saved
    top_reduced = grad_top.astype(jnp.bfloat16)
    down_weight_gradient = jnp.einsum(
        "pgr,pgw->rw", hidden_activation, top_reduced, preferred_element_type=jnp.float32
    )
    activation_gradient = jnp.einsum(
        "ayx,cx->ayc", top_reduced, down_weight_matrix, preferred_element_type=jnp.float32
    )
    preactivation_gradient = jax.vjp(gelu_tanh, hidden_preactivation)[1](activation_gradient)[
        0
    ].astype(jnp.bfloat16)
    up_weight_gradient = jnp.einsum(
        "uzb,uzv->bv", feedforward_norm, preactivation_gradient, preferred_element_type=jnp.float32
    )
    norm_portion = jnp.einsum(
        "vok,hk->voh", preactivation_gradient, up_weight_matrix, preferred_element_type=jnp.float32
    )
    grad_norm_m = tensor_sum(norm_portion)
    grad_middle, grad_gain_m = jax.vjp(rms_scale, middle, gain_m)[1](grad_norm_m)
    grad_attn = grad_top + grad_middle
    attention_reduced = grad_attn.astype(jnp.bfloat16)
    output_weight_gradient = jnp.einsum(
        "omi,omj->ij", mixed_state, attention_reduced, preferred_element_type=jnp.float32
    )
    grad_mixed = jnp.einsum(
        "bjw,gw->bjg", attention_reduced, output_weight_matrix, preferred_element_type=jnp.float32
    ).astype(jnp.bfloat16)
    projection_gradient = attend_grad(projected, kept, grad_mixed)
    query_key_value_gradient = jnp.einsum(
        "xgt,axgf->atf", attention_norm, projection_gradient, preferred_element_type=jnp.float32
    )
    input_part = jnp.einsum(
        "gurh,gih->uri",
        projection_gradient,
        query_key_value_weight,
        preferred_element_type=jnp.float32,
    )
    grad_norm_a = tensor_sum(input_part)
    grad_resid, grad_gain_a = jax.vjp(rms_scale, resid_in, gain_a)[1](grad_norm_a)
    return (
        grad_attn,
        grad_middle,
        grad_resid,
        (
            grad_gain_a,
            query_key_value_gradient,
            output_weight_gradient,
            grad_gain_m,
            up_weight_gradient,
            down_weight_gradient,
        ),
    )


def pack_grads(grad_list, dims, groups):
    flats = []
    shapes = []
    for grad_item, which_dim in zip(grad_list, dims):
        moved = jnp.moveaxis(grad_item, which_dim, 0)
        shapes.append(moved.shape)
        flats.append(moved.reshape(groups, -1))
    return (jnp.concatenate(flats, axis=1), shapes)


def unpack_grads(summed, shapes, dims, groups):
    results = []
    offset = 0
    for moved_shape, which_dim in zip(shapes, dims):
        share_shape = (moved_shape[0] // groups,) + tuple(moved_shape[1:])
        width = math_prod(share_shape)
        piece = summed[0, offset : offset + width].reshape(share_shape)
        results.append(jnp.moveaxis(piece, 0, which_dim))
        offset = offset + width
    return tuple(results)


def math_prod(shape):
    total = 1
    for extent in shape:
        total = total * extent
    return total


def spread_grads(grad_list, dims):
    groups = lax.axis_size("dp") * lax.axis_size("ctx")
    packed, shapes = pack_grads(grad_list, dims, groups)
    summed = lax.psum_scatter(packed, ("dp", "ctx"), scatter_dimension=0, tiled=True)
    return unpack_grads(summed, shapes, dims, groups)


def plain_local(
    hidden_in,
    teacher,
    seg_ids,
    valid,
    routed_idx,
    attn_gain,
    w_qkv,
    w_out,
    mlp_gain,
    w_up,
    w_down,
    w_router,
):
    seqs_local, local_len, model_width = hidden_in.shape
    seq_len = seg_ids.shape[1]
    routed = routed_idx.shape[1]
    ctx_count = lax.axis_size("ctx")
    ctx_place = lax.axis_index("ctx")
    routed_local = routed // ctx_count
    dense_qpos = jnp.broadcast_to(
        ctx_place * local_len + jnp.arange(local_len, dtype=jnp.int32), (seqs_local, local_len)
    )
    dense_kpos = jnp.broadcast_to(jnp.arange(seq_len, dtype=jnp.int32), (seqs_local, seq_len))
    dense_qseg = lax.dynamic_slice_in_dim(seg_ids, ctx_place * local_len, local_len, 1)
    routed_seg = take_rows(seg_ids, routed_idx)
    routed_qpos = lax.dynamic_slice_in_dim(routed_idx, ctx_place * routed_local, routed_local, 1)
    routed_qseg = lax.dynamic_slice_in_dim(routed_seg, ctx_place * routed_local, routed_local, 1)
    owner_mine = routed_idx // local_len == ctx_place
    owner_row = routed_idx % local_len
    dense_attend, dense_grad = make_attention(dense_qpos, dense_kpos, dense_qseg, seg_ids)
    routed_attend, routed_grad = make_attention(routed_qpos, routed_idx, routed_qseg, routed_seg)
    x_input = hidden_in.astype(jnp.float32)
    attn_d, mlp_d, saved_d = block_forward(
        x_input, attn_gain[0], w_qkv[0], w_out[0], mlp_gain[0], w_up[0], w_down[0], dense_attend
    )
    layer_mid = saved_d[5] + mlp_d
    picked = (
        jnp.where(owner_mine[..., None], take_rows(layer_mid, owner_row), 0.0)
        .astype(jnp.bfloat16)
        .astype(jnp.float32)
    )
    chosen = to_workers(picked).astype(jnp.bfloat16).astype(jnp.float32)
    gating = gating_fn(chosen, w_router)
    attn_r, mlp_r, saved_r = block_forward(
        chosen, attn_gain[1], w_qkv[1], w_out[1], mlp_gain[1], w_up[1], w_down[1], routed_attend
    )
    branch_sum = attn_r + mlp_r
    sent_rows = (gating[..., None] * branch_sum).astype(jnp.bfloat16)
    returned = to_owners(sent_rows).astype(jnp.float32)
    layer_out = add_rows(layer_mid, owner_row, jnp.where(owner_mine[..., None], returned, 0.0))
    valid_rows = valid.astype(jnp.float32)
    error_rows = layer_out - teacher.astype(jnp.float32)
    error_sum, valid_count = lax.psum(
        (jnp.sum(valid_rows[..., None] * error_rows * error_rows), jnp.sum(valid_rows)),
        ("dp", "ctx"),
    )
    loss_value = error_sum / (valid_count * model_width)
    token_total = float(seqs_local * seq_len * lax.axis_size("dp"))
    grad_final = token_total / valid_count * valid_rows[..., None] * error_rows
    picked_grad = (
        jnp.where(owner_mine[..., None], take_rows(grad_final, owner_row), 0.0)
        .astype(jnp.bfloat16)
        .astype(jnp.float32)
    )
    branch_grad = to_workers(picked_grad).astype(jnp.bfloat16).astype(jnp.float32)
    grad_top = gating[..., None] * branch_grad
    gating_share, gating_back = jax.vjp(gating_fn, chosen, w_router)
    grad_gating = jnp.sum(branch_grad * branch_sum, axis=-1)
    grad_chosen_gate, grad_router = gating_back(grad_gating)
    grad_attn_r, grad_middle_r, grad_resid_r, grads_r = block_backward(
        saved_r,
        grad_top,
        attn_gain[1],
        w_qkv[1],
        w_out[1],
        mlp_gain[1],
        w_up[1],
        w_down[1],
        routed_grad,
    )
    grad_chosen = (grad_middle_r + grad_resid_r + grad_chosen_gate).astype(jnp.bfloat16)
    grads_r = grads_r + (grad_router,)
    spread_r = spread_grads(grads_r, (0, 1, 1, 0, 0, 1, 0))
    grad_rows = to_owners(grad_chosen).astype(jnp.float32)
    grad_mid = add_rows(grad_final, owner_row, jnp.where(owner_mine[..., None], grad_rows, 0.0))
    grad_attn_d, grad_middle_d, grad_resid_d, grads_d = block_backward(
        saved_d,
        grad_mid,
        attn_gain[0],
        w_qkv[0],
        w_out[0],
        mlp_gain[0],
        w_up[0],
        w_down[0],
        dense_grad,
    )
    grad_input = grad_attn_d + grad_resid_d
    spread_d = spread_grads(grads_d, (0, 1, 1, 0, 0, 1))
    return (
        layer_out.astype(jnp.bfloat16),
        loss_value,
        grad_input,
        jnp.stack([spread_d[0], spread_r[0]]),
        jnp.stack([spread_d[1], spread_r[1]]),
        jnp.stack([spread_d[2], spread_r[2]]),
        jnp.stack([spread_d[3], spread_r[3]]),
        jnp.stack([spread_d[4], spread_r[4]]),
        jnp.stack([spread_d[5], spread_r[5]]),
        spread_r[6],
    )


def head_pair(rows):
    lane = lax.broadcasted_iota(jnp.int32, rows.shape, 1)
    zero = jnp.zeros_like(rows)
    return jnp.concatenate([jnp.where(lane < HEAD, rows, zero), jnp.where(lane >= HEAD, rows, zero)], axis=0)


def pair_join(stacked):
    half = stacked.shape[0] // 2
    lane = lax.broadcasted_iota(jnp.int32, (half, stacked.shape[1]), 1)
    return jnp.where(lane < HEAD, stacked[:half], stacked[half:])


FWD_LAGS = (1, 2, 3, 4, 5, 6)


def dense_forward_kernel(
    sizes,
    x_ref, again_ref, mgain_ref, segc_ref, segr_ref, cnt_ref, wqkv_h, wout_h, wup_h, wdn_h,
    x2_ref, q_ref, k_ref, v_ref, mix_ref, lse_ref, mid_ref, n2_ref, pre_ref, act_ref, cnt_out,
    wqkv, wout, wup, wdn, part, part2,
    sE, rE, sI, rI, sO, sE2, rE2, sX, rX, cbuf,
    wsem, kvs, kvr, cs, cr, ss, rs,
):
    NC, R, D, L, S, NT, NDP, NCTX = sizes
    ln = Line()
    ctx = lax.axis_index("ctx")
    dp = lax.axis_index("dp")
    half = R // 2
    loads = [
        pltpu.make_async_copy(wqkv_h.at[0], wqkv, wsem.at[0]),
        pltpu.make_async_copy(wout_h.at[0], wout, wsem.at[1]),
        pltpu.make_async_copy(wup_h.at[0], wup, wsem.at[2]),
        pltpu.make_async_copy(wdn_h.at[0], wdn, wsem.at[3]),
    ]
    for ld in loads:
        ld.start()
    tpeers = tensor_peers(NT)
    rpeers = row_peers(NDP, NCTX)
    greet(tpeers + rpeers)

    def count_slot(j):
        return cbuf.at[j]

    cbuf[0] = cnt_ref[...]
    sends = []
    for j, p in enumerate(rpeers):
        sends.append(rcopy(cnt_ref, cbuf.at[j + 1], cs.at[j], cr.at[j], p))
    for cp in sends:
        cp.start()

    @pl.when(ln.is_end)
    def _():
        def zero(k, _):
            rE[k] = jnp.zeros((R, D), BF)
            return 0

        lax.fori_loop(0, NC, zero, 0)

    for ld in loads[:1]:
        ld.wait()
    RB = 2 * R
    again = again_ref[0:1, :]

    def project(i, _):
        rows = pl.ds(pl.multiple_of(i * RB, RB), RB)
        xv = x_ref[rows, :].astype(F32)
        n1 = (rms_parts(xv)[1] * again).astype(BF)
        for c, ref in enumerate((q_ref, k_ref, v_ref)):
            y = dot_nn(n1, wqkv[c]).astype(BF)
            if c == 0:
                ref[rows, :] = y
            else:
                ref[pl.ds(pl.multiple_of(ctx * L + i * RB, RB), RB), :] = y
        return 0

    lax.fori_loop(0, L // RB, project, 0)

    own = pl.ds(pl.multiple_of(ctx * L, L), L)

    def kv_copy(ref, which, c_to):
        return rcopy(ref.at[own, :], ref.at[own, :], kvs.at[which, c_to], kvr.at[which, ctx], {"ctx": c_to})

    for c_to in range(1, NCTX):
        @pl.when(c_to > ctx)
        def _(c_to=c_to):
            kv_copy(k_ref, 0, c_to).start()
            kv_copy(v_ref, 1, c_to).start()

    for c_from in range(NCTX - 1):
        @pl.when(c_from < ctx)
        def _(c_from=c_from):
            theirs = pl.ds(c_from * L, L)
            for which, ref in enumerate((k_ref, v_ref)):
                rcopy(ref.at[theirs, :], ref.at[theirs, :], kvs.at[which, c_from], kvr.at[which, c_from], {"ctx": c_from}).wait_recv()

    for c_later in range(1, NCTX):
        @pl.when(c_later > ctx)
        def _(c_later=c_later):
            k_ref[pl.ds(c_later * L, L), :] = jnp.zeros((L, k_ref.shape[1]), BF)
            v_ref[pl.ds(c_later * L, L), :] = jnp.zeros((L, k_ref.shape[1]), BF)

    for ld in loads[1:]:
        ld.wait()
    mgain = mgain_ref[0:1, :]
    groups = q_ref.shape[1] // 128

    def attend(i, keys):
        rows = pl.ds(pl.multiple_of(i * R, R), R)
        qpos = ctx * L + i * R + lax.broadcasted_iota(jnp.int32, (R, 1), 0)
        kpos = lax.broadcasted_iota(jnp.int32, (1, keys), 1)
        visible = (kpos <= qpos) & (segr_ref[:, :keys] == segc_ref[i])
        bias = jnp.where(visible, 0.0, masked_value)
        lane = lax.broadcasted_iota(jnp.int32, (R, 128), 1)
        lse_tile = jnp.zeros((R, 128), F32)
        qi = q_ref[rows, :] * jnp.asarray(0.125, BF)
        for g in range(groups):
            cols = slice(128 * g, 128 * g + 128)
            q2 = head_pair(qi[:, cols])
            s = dot_nt(q2, k_ref[:keys, cols]).reshape(2, R, keys) + bias[None]
            top = jnp.max(s, axis=-1, keepdims=True)
            p = jnp.exp(s - top)
            total = jnp.sum(p, axis=-1, keepdims=True)
            pr = (p * (1.0 / total)).astype(BF).reshape(2 * R, keys)
            lse = top + jnp.log(total)
            lse_tile = jnp.where(lane == 2 * g, lse[0], jnp.where(lane == 2 * g + 1, lse[1], lse_tile))
            o = dot_nn(pr, v_ref[:keys, cols])
            mix_ref[rows, cols] = pair_join(o).astype(BF)
        lse_ref[rows, :] = lse_tile

    a1, a2, a3, a4, a5, a6 = FWD_LAGS
    lag3 = jnp.where(ln.is_end, a3, a2)
    my_rows = pl.ds(pl.multiple_of(ln.side * half, half), half)
    ot_rows = pl.ds(pl.multiple_of((1 - ln.side) * half, half), half)

    def got(buf, flow, j):
        rcopy(buf.at[j], buf.at[j], ss.at[flow, j], rs.at[flow, j], ln.mid).wait_recv()

    def got_half(rows, flow, j):
        rcopy(x2_ref.at[j, rows, :], x2_ref.at[j, rows, :], ss.at[flow, j], rs.at[flow, j], ln.mid).wait_recv()

    def body(i, _):
        @pl.when(i < NC)
        def _():
            @pl.when(ctx == 0)
            def _():
                attend(i, L)

            @pl.when(ctx > 0)
            def _():
                attend(i, S)

            p = dot_nn(mix_ref[pl.ds(pl.multiple_of(i * R, R), R), :], wout[...])
            part[i] = p

            @pl.when(ln.is_end)
            def _():
                sE[i] = p.astype(BF)
                rcopy(sE.at[i], rE.at[i], ss.at[0, i], rs.at[0, i], ln.mid).start()

        j1 = i - a1

        @pl.when(ln.is_mid & (j1 >= 0) & (j1 < NC))
        def _():
            got(rE, 0, j1)
            sI[j1] = (rE[j1].astype(F32) + part[j1]).astype(BF)
            rcopy(sI.at[j1], rI.at[j1], ss.at[1, j1], rs.at[1, j1], ln.other).start()

        j3 = i - lag3

        @pl.when((j3 >= 0) & (j3 < NC))
        def _():
            got(rI, 1, j3)
            inner = rI[j3].astype(F32) + part[j3]

            @pl.when(ln.is_mid)
            def _():
                sO[j3] = inner.astype(BF)
                rcopy(sO.at[j3], rI.at[j3], ss.at[2, j3], rs.at[1, j3], ln.end).start()

            rows = pl.ds(pl.multiple_of(j3 * R, R), R)
            mid = x_ref[rows, :].astype(F32) + (inner + rE[j3].astype(F32))
            mid_ref[rows, :] = mid
            n2 = (rms_parts(mid)[1] * mgain).astype(BF)
            n2_ref[rows, :] = n2
            pre = dot_nn(n2, wup[...])
            pre_ref[rows, :] = pre
            act = (0.5 * pre * (1.0 + gelu_pair(pre))).astype(BF)
            act_ref[rows, :] = act
            p2 = dot_nn(act, wdn[...])

            @pl.when(ln.is_end)
            def _():
                sE2[j3] = p2.astype(BF)
                rcopy(sE2.at[j3], rE2.at[j3], ss.at[3, j3], rs.at[3, j3], ln.mid).start()

            @pl.when(ln.is_mid)
            def _():
                part2[j3] = p2

        j4 = i - a4

        @pl.when(ln.is_mid & (j4 >= 0) & (j4 < NC))
        def _():
            got(rE2, 3, j4)
            sX[j4] = (rE2[j4, ot_rows, :].astype(F32) + part2[j4, ot_rows, :]).astype(BF)
            rcopy(sX.at[j4], rX.at[j4], ss.at[4, j4], rs.at[4, j4], ln.other).start()

        j5 = i - a5

        @pl.when(ln.is_mid & (j5 >= 0) & (j5 < NC))
        def _():
            rcopy(rX.at[j5], rX.at[j5], ss.at[4, j5], rs.at[4, j5], ln.mid).wait_recv()
            rows = pl.ds(pl.multiple_of(j5 * R + ln.side * half, half), half)
            mlp = part2[j5, my_rows, :] + rE2[j5, my_rows, :].astype(F32) + rX[j5].astype(F32)
            x2_ref[j5, my_rows, :] = (mid_ref[rows, :] + mlp).astype(BF)
            mine = x2_ref.at[j5, my_rows, :]
            rcopy(mine, mine, ss.at[5, j5], rs.at[5, j5], ln.other).start()
            rcopy(mine, mine, ss.at[6, j5], rs.at[6, j5], ln.end).start()

        j6 = i - a6

        @pl.when(ln.is_mid & (j6 >= 0) & (j6 < NC))
        def _():
            got_half(ot_rows, 5, j6)
            theirs = x2_ref.at[j6, ot_rows, :]
            rcopy(theirs, theirs, ss.at[7, j6], rs.at[7, j6], ln.end).start()

        return 0

    lax.fori_loop(0, NC + a6, body, 0)

    for j, p in enumerate(rpeers):
        sends[j].wait()
    total = cbuf[0]
    for j in range(1, len(rpeers) + 1):
        total = total + cbuf[j]
    cnt_out[...] = total

    for c_to in range(1, NCTX):
        @pl.when(c_to > ctx)
        def _(c_to=c_to):
            kv_copy(k_ref, 0, c_to).wait_send()
            kv_copy(v_ref, 1, c_to).wait_send()

    def drain(k, _):
        @pl.when(ln.is_end)
        def _():
            got_half(my_rows, 6, k)
            got_half(ot_rows, 7, k)
            rcopy(sE.at[k], rE.at[k], ss.at[0, k], rs.at[0, k], ln.mid).wait_send()
            rcopy(sE2.at[k], rE2.at[k], ss.at[3, k], rs.at[3, k], ln.mid).wait_send()

        @pl.when(ln.is_mid)
        def _():
            rcopy(sI.at[k], rI.at[k], ss.at[1, k], rs.at[1, k], ln.other).wait_send()
            rcopy(sO.at[k], rI.at[k], ss.at[2, k], rs.at[1, k], ln.end).wait_send()
            rcopy(sX.at[k], rX.at[k], ss.at[4, k], rs.at[4, k], ln.other).wait_send()
            mine = x2_ref.at[k, my_rows, :]
            theirs = x2_ref.at[k, ot_rows, :]
            rcopy(mine, mine, ss.at[5, k], rs.at[5, k], ln.other).wait_send()
            rcopy(mine, mine, ss.at[6, k], rs.at[6, k], ln.end).wait_send()
            rcopy(theirs, theirs, ss.at[7, k], rs.at[7, k], ln.end).wait_send()

        return 0

    lax.fori_loop(0, NC, drain, 0)


CHUNK = 64


def dense_forward(x, again, mgain, seg, cnt, w_qkv, w_out, w_up, w_down):
    L, D = x.shape
    S = seg.shape[0]
    NT, NDP, NCTX = lax.axis_size("tensor"), lax.axis_size("dp"), lax.axis_size("ctx")
    R = CHUNK
    NC = L // R
    Hd = w_out.shape[1]
    Fl = w_up.shape[2]
    ctx = lax.axis_index("ctx")
    segc = lax.dynamic_slice_in_dim(seg, ctx * L, L, 0).reshape(NC, R, 1)
    sizes = (NC, R, D, L, S, NT, NDP, NCTX)
    flows = 8
    dma = pltpu.SemaphoreType.DMA
    rows = NDP * NCTX
    sd = jax.ShapeDtypeStruct
    v = pl.BlockSpec(memory_space=VM)
    a = pl.BlockSpec(memory_space=ANY)
    out = pl.pallas_call(
        functools.partial(dense_forward_kernel, sizes),
        name="dense_forward",
        out_shape=(
            sd((NC, R, D), BF), sd((L, Hd), BF), sd((S, Hd), BF), sd((S, Hd), BF), sd((L, Hd), BF),
            sd((L, 128), F32), sd((L, D), F32), sd((L, D), BF), sd((L, Fl), F32), sd((L, Fl), BF), sd((8, 128), F32),
        ),
        in_specs=[v] * 6 + [a] * 4,
        out_specs=(v,) * 11,
        scratch_shapes=[
            VM((3, D, Hd), BF), VM((Hd, D), BF), VM((D, Fl), BF), VM((Fl, D), BF),
            VM((NC, R, D), F32), VM((NC, R, D), F32),
            VM((NC, R, D), BF), VM((NC, R, D), BF), VM((NC, R, D), BF), VM((NC, R, D), BF), VM((NC, R, D), BF),
            VM((NC, R, D), BF), VM((NC, R, D), BF), VM((NC, R // 2, D), BF), VM((NC, R // 2, D), BF),
            VM((rows, 8, 128), F32),
            dma((4,)), dma((2, NCTX)), dma((2, NCTX)), dma((rows,)), dma((rows,)), dma((flows, NC)), dma((flows, NC)),
        ],
        compiler_params=pltpu.CompilerParams(collective_id=1, has_side_effects=True, vmem_limit_bytes=58 << 20),
    )(x, again, mgain, segc, seg.reshape(1, S), cnt, w_qkv, w_out, w_up, w_down)
    return out


BWD_LAGS = (1, 2, 3)
TAIL_LAGS = (1, 2, 3)


def share_add(own, came, d):
    def add(j, _):
        own[j] = (own[j].astype(F32) + came[j].astype(F32)).astype(BF)
        return 0

    lax.fori_loop(0, own.shape[0], add, 0)


def share_total(own, came, d):
    total = own[d].astype(F32)
    for j in range(came.shape[0]):
        total = total + came[j].astype(F32)
    return total


def dense_backward_kernel(
    sizes,
    x_ref, x2_ref, teach_ref, valid_ref, cnt_ref, sent_ref, gch_ref, ridx_ref, small_ref,
    again_ref, mgain_ref, segc_ref, segr_ref,
    q_ref, k_ref, v_ref, mix_ref, lse_ref, mid_ref, n2_ref, act_ref, pre_ref,
    wqkv_h, wout_h, wup_h, wdn_h, rdn_h, rup_h, rout_h, rqkv_h,
    hid_ref, loss_ref, gin_ref, dn_o, up_o, out_o, qkv_o, small_o,
    wqkv, wout, wup, wdn, g_s, gm_s, gpre_s, ga_s, n1_s, part, gqkv, dk_s, dv_s, rdk, rdv,
    sE, rE, sI, rI, sO, rE2, rX,
    tdn, odn, udn, wdn_r, tup, oup, uup, wup_r, tout, oout, uout, wout_r, tqkv, oqkv, uqkv, wqkv_r,
    ldn, lup, lout, lqkv, xdn, xup, xout, xqkv,
    acc_m, acc_a, lacc, lbuf, vec, vbuf, hbuf,
    wsem, lsem, kvsem, s1, r1, s2, r2, s3, r3, cs, cr, ts, tr, ss, rs,
):
    NC, R, D, L, S, NT, NDP, NCTX, scale_total = sizes
    ln = Line()
    ctx = lax.axis_index("ctx")
    dp = lax.axis_index("dp")
    half = R // 2
    G = NDP * NCTX
    W = D // G
    loads = [
        pltpu.make_async_copy(wdn_h.at[0], wdn, wsem.at[0]),
        pltpu.make_async_copy(wup_h.at[0], wup, wsem.at[1]),
        pltpu.make_async_copy(wout_h.at[0], wout, wsem.at[2]),
        pltpu.make_async_copy(wqkv_h.at[0], wqkv, wsem.at[3]),
    ]
    for ld in loads:
        ld.start()
    tpeers = tensor_peers(NT)
    rpeers = row_peers(NDP, NCTX)
    greet(tpeers + rpeers)

    routed = ((rdn_h, ldn, xdn), (rup_h, lup, xup), (rout_h, lout, xout), (rqkv_h, lqkv, xqkv))

    def routed_copy(w, j):
        src, _, dst = routed[w]
        to = lax.rem(dp + j, NDP)
        return rcopy(src.at[to], dst.at[j - 1], s3.at[w, j - 1], r3.at[w, j - 1], {"dp": to})

    def routed_own(w):
        return pltpu.make_async_copy(routed[w][0].at[dp], routed[w][1], lsem.at[w])

    for w in range(4):
        routed_own(w).start()
        for j in range(1, NDP):
            routed_copy(w, j).start()

    @pl.when(ln.is_end)
    def _():
        def zero(k, _):
            rE[k] = jnp.zeros((R, D), BF)
            return 0

        lax.fori_loop(0, NC, zero, 0)

    for ref in (dk_s, dv_s):
        ref[...] = jnp.zeros(ref.shape, F32)
    for ref in (acc_m, acc_a, lacc):
        ref[...] = jnp.zeros(ref.shape, F32)
    again = again_ref[0:1, :]
    mgain = mgain_ref[0:1, :]
    scale = scale_total / cnt_ref[0:1, 0:1]
    for ld in loads:
        ld.wait()

    groups = q_ref.shape[1] // 128
    Hd = q_ref.shape[1]

    def attend_back(j, gmix, keys):
        rows = pl.ds(pl.multiple_of(j * R, R), R)
        qpos = ctx * L + j * R + lax.broadcasted_iota(jnp.int32, (R, 1), 0)
        kpos = lax.broadcasted_iota(jnp.int32, (1, keys), 1)
        visible = (kpos <= qpos) & (segr_ref[:, :keys] == segc_ref[j])
        bias = jnp.where(visible, 0.0, masked_value)
        qi = q_ref[rows, :] * jnp.asarray(0.125, BF)
        lse = lse_ref[rows, :]
        for g in range(groups):
            cols = slice(128 * g, 128 * g + 128)
            q2 = head_pair(qi[:, cols])
            g2 = head_pair(gmix[:, cols])
            kg = k_ref[:keys, cols]
            vg = v_ref[:keys, cols]
            l2 = jnp.concatenate([lse[:, 2 * g : 2 * g + 1], lse[:, 2 * g + 1 : 2 * g + 2]], axis=0)
            s = (dot_nt(q2, kg).reshape(2, R, keys) + bias[None]).reshape(2 * R, keys)
            p = jnp.exp(s - l2)
            dp_ = dot_nt(g2, vg)
            inner = jnp.sum(p * dp_, axis=-1, keepdims=True)
            ds = (p * (dp_ - inner)).astype(BF)
            gq = pair_join(dot_nn(ds, kg)) * 0.125
            gqkv[0, rows, cols] = gq.astype(BF)
            dk_s[:keys, cols] += dot_tn(ds, q2)
            dv_s[:keys, cols] += dot_tn(p.astype(BF), g2)

    a1, a2, a3 = BWD_LAGS
    lag3 = jnp.where(ln.is_end, a3, a2)
    my_rows = pl.ds(pl.multiple_of(ln.side * half, half), half)
    ot_rows = pl.ds(pl.multiple_of((1 - ln.side) * half, half), half)

    def got(buf, flow, j):
        rcopy(buf.at[j], buf.at[j], ss.at[flow, j], rs.at[flow, j], ln.mid).wait_recv()

    def got_half(rows, flow, j):
        rcopy(gin_ref.at[j, rows, :], gin_ref.at[j, rows, :], ss.at[flow, j], rs.at[flow, j], ln.mid).wait_recv()

    def by_share(piece, send, keep):
        for c in range(NCTX):
            def one(d, _, c=c):
                val = piece(d * NCTX + c)

                @pl.when(ctx == c)
                def _():
                    keep[d] = val

                @pl.when(ctx != c)
                def _():
                    send[d] = val

                return 0

            lax.fori_loop(0, NDP, one, 0)

    def cols_of(g):
        return pl.ds(pl.multiple_of(g * W, W), W)

    def piece_dn(g):
        return dot_tn(act_ref[...], gm_s[:, cols_of(g)]).astype(BF)

    def piece_up(g):
        return dot_tn(n2_ref[:, cols_of(g)], gpre_s[...]).astype(BF)

    def piece_out(g):
        return dot_tn(mix_ref[...], ga_s[:, cols_of(g)]).astype(BF)

    def piece_qkv(g):
        lhs = n1_s[:, cols_of(g)]
        return jnp.concatenate([dot_tn(lhs, gqkv[c]) for c in range(3)], axis=1).astype(BF)

    shares = (
        (piece_dn, tdn, odn, udn, wdn_r),
        (piece_up, tup, oup, uup, wup_r),
        (piece_out, tout, oout, uout, wout_r),
        (piece_qkv, tqkv, oqkv, uqkv, wqkv_r),
    )
    across = {"ctx": 1 - ctx}

    def pair_copy(w):
        return rcopy(shares[w][1], shares[w][3], s1.at[w], r1.at[w], across)

    def share_first(w):
        by_share(shares[w][0], shares[w][1], shares[w][2])
        pair_copy(w).start()

    def dp_copy(w, j):
        to = lax.rem(dp + j, NDP)
        return rcopy(shares[w][2].at[to], shares[w][4].at[j - 1], s2.at[w, j - 1], r2.at[w, j - 1], {"dp": to})

    def share_second(w):
        pair_copy(w).wait_recv()
        share_add(shares[w][2], shares[w][3], dp)
        for j in range(1, NDP):
            dp_copy(w, j).start()

    me = dp * NCTX + ctx

    def body(i, _):
        @pl.when(i < NC)
        def _():
            rows = pl.ds(pl.multiple_of(i * R, R), R)
            place = ctx * L + i * R + lax.broadcasted_iota(jnp.int32, (R, 1), 0)
            pick = (place == ridx_ref[...]).astype(F32).astype(BF)
            x3 = x2_ref[i].astype(F32) + dot_nn(pick, sent_ref[...])
            hid_ref[rows, :] = x3.astype(BF)
            err = x3 - teach_ref[rows, :].astype(F32)
            counted = valid_ref[i] * err
            lacc[...] += fold8(counted * err)
            g2 = scale * counted + dot_nn(pick, gch_ref[...])
            g_s[rows, :] = g2
            gm = g2.astype(BF)
            gm_s[rows, :] = gm
            gact = dot_nt(gm, wdn[...])
            u = pre_ref[rows, :]
            t = gelu_pair(u)
            slope = 0.5 * (1.0 + t) + 0.5 * u * (1.0 - t * t) * (0.7978845608028654 * (1.0 + 3.0 * 0.044715 * u * u))
            gpre = (gact * slope).astype(BF)
            gpre_s[rows, :] = gpre
            p3 = dot_nt(gpre, wup[...])
            part[i] = p3

            @pl.when(ln.is_end)
            def _():
                sE[i] = p3.astype(BF)
                rcopy(sE.at[i], rE.at[i], ss.at[0, i], rs.at[0, i], ln.mid).start()

            n1_s[rows, :] = (rms_parts(x_ref[rows, :].astype(F32))[1] * again).astype(BF)

        j1 = i - a1

        @pl.when(ln.is_mid & (j1 >= 0) & (j1 < NC))
        def _():
            got(rE, 0, j1)
            sI[j1] = (rE[j1].astype(F32) + part[j1]).astype(BF)
            rcopy(sI.at[j1], rI.at[j1], ss.at[1, j1], rs.at[1, j1], ln.other).start()

        j3 = i - lag3

        @pl.when((j3 >= 0) & (j3 < NC))
        def _():
            got(rI, 1, j3)
            inner = rI[j3].astype(F32) + part[j3]

            @pl.when(ln.is_mid)
            def _():
                sO[j3] = inner.astype(BF)
                rcopy(sO.at[j3], rI.at[j3], ss.at[2, j3], rs.at[1, j3], ln.end).start()

            rows = pl.ds(pl.multiple_of(j3 * R, R), R)
            gn2 = inner + rE[j3].astype(F32)
            gmid, gain_rows = rms_back(mid_ref[rows, :], mgain, gn2)
            acc_m[...] += fold8(gain_rows)
            gattn = g_s[rows, :] + gmid
            g_s[rows, :] = gattn
            ga = gattn.astype(BF)
            ga_s[rows, :] = ga
            gmix = dot_nt(ga, wout[...]).astype(BF)

            @pl.when(ctx == 0)
            def _():
                attend_back(j3, gmix, L)

            @pl.when(ctx > 0)
            def _():
                attend_back(j3, gmix, S)

        @pl.when(i == NC)
        def _():
            share_first(0)
            part_loss = jnp.sum(lacc[...])
            lbuf[me] = jnp.full((8, 128), part_loss, F32)
            for j, p in enumerate(rpeers):
                rcopy(lbuf.at[me], lbuf.at[me], cs.at[j], cr.at[j], p).start()

        @pl.when(i == NC + 1)
        def _():
            share_first(1)

        return 0

    lax.fori_loop(0, NC + max(a3, 2), body, 0)

    def kv_copy(which):
        src, dst = ((dk_s, rdk), (dv_s, rdv))[which]
        return rcopy(src.at[pl.ds(0, L), :], dst, kvsem.at[which, 0], kvsem.at[which, 1], {"ctx": 0})

    @pl.when(ctx > 0)
    def _():
        kv_copy(0).start()
        kv_copy(1).start()
        for which, ref in enumerate((dk_s, dv_s)):
            gqkv[1 + which] = ref[pl.ds(L, L), :].astype(BF)

    share_first(2)

    @pl.when(ctx == 0)
    def _():
        for which, (ref, came) in enumerate(((dk_s, rdk), (dv_s, rdv))):
            kv_copy(which).wait_recv()
            gqkv[1 + which] = (ref[pl.ds(0, L), :] + came[...]).astype(BF)

    def settle(k, _):
        @pl.when(ln.is_end)
        def _():
            rcopy(sE.at[k], rE.at[k], ss.at[0, k], rs.at[0, k], ln.mid).wait_send()

        @pl.when(ln.is_mid)
        def _():
            rcopy(sI.at[k], rI.at[k], ss.at[1, k], rs.at[1, k], ln.other).wait_send()
            rcopy(sO.at[k], rI.at[k], ss.at[2, k], rs.at[1, k], ln.end).wait_send()

        return 0

    lax.fori_loop(0, NC, settle, 0)

    b4, b5, b6 = TAIL_LAGS
    sX = sI

    def tail(i, _):
        @pl.when(i < NC)
        def _():
            rows = pl.ds(pl.multiple_of(i * R, R), R)
            p4 = dot_nt(gqkv[0, rows, :], wqkv[0])
            p4 = p4 + dot_nt(gqkv[1, rows, :], wqkv[1])
            p4 = p4 + dot_nt(gqkv[2, rows, :], wqkv[2])

            @pl.when(ln.is_end)
            def _():
                sE[i] = p4.astype(BF)
                rcopy(sE.at[i], rE2.at[i], ss.at[3, i], rs.at[3, i], ln.mid).start()

            @pl.when(ln.is_mid)
            def _():
                part[i] = p4

        j4 = i - b4

        @pl.when(ln.is_mid & (j4 >= 0) & (j4 < NC))
        def _():
            got(rE2, 3, j4)
            sX[j4, pl.ds(0, half), :] = (rE2[j4, ot_rows, :].astype(F32) + part[j4, ot_rows, :]).astype(BF)
            rcopy(sX.at[j4, pl.ds(0, half), :], rX.at[j4], ss.at[4, j4], rs.at[4, j4], ln.other).start()

        j5 = i - b5

        @pl.when(ln.is_mid & (j5 >= 0) & (j5 < NC))
        def _():
            got(rX, 4, j5)
            rows = pl.ds(pl.multiple_of(j5 * R + ln.side * half, half), half)
            gn1 = part[j5, my_rows, :] + rE2[j5, my_rows, :].astype(F32) + rX[j5].astype(F32)
            gin, gain_rows = rms_back(x_ref[rows, :].astype(F32), again, gn1)
            acc_a[...] += fold8(gain_rows)
            gin_ref[j5, my_rows, :] = (g_s[rows, :] + gin).astype(BF)
            mine = gin_ref.at[j5, my_rows, :]
            rcopy(mine, mine, ss.at[5, j5], rs.at[5, j5], ln.other).start()
            rcopy(mine, mine, ss.at[6, j5], rs.at[6, j5], ln.end).start()

        j6 = i - b6

        @pl.when(ln.is_mid & (j6 >= 0) & (j6 < NC))
        def _():
            got_half(ot_rows, 5, j6)
            theirs = gin_ref.at[j6, ot_rows, :]
            rcopy(theirs, theirs, ss.at[7, j6], rs.at[7, j6], ln.end).start()

        @pl.when(i == 1)
        def _():
            share_second(0)

        @pl.when(i == 2)
        def _():
            share_second(1)
            share_second(2)

        @pl.when(i == 3)
        def _():
            share_first(3)

        @pl.when(i == 5)
        def _():
            share_second(3)

        return 0

    lax.fori_loop(0, NC + b6, tail, 0)

    vec[...] = small_ref[...]
    vec[0:1, :] = vec[0:1, :] + jnp.sum(acc_a[...], axis=0, keepdims=True)
    vec[1:2, :] = vec[1:2, :] + jnp.sum(acc_m[...], axis=0, keepdims=True) * (1.0 / NT)

    def vec_copy(j, d2, c2):
        return rcopy(vec.at[:, cols_of(d2 * NCTX + c2)], vbuf.at[me], ts.at[j], tr.at[j], {"dp": d2, "ctx": c2})

    places = []
    for j in range(NDP):
        for k in range(NCTX):
            if j or k:
                places.append((lax.rem(dp + j, NDP), lax.rem(ctx + k, NCTX)))
    for n, (d2, c2) in enumerate(places):
        vec_copy(n, d2, c2).start()
    vbuf[me] = vec[:, cols_of(me)]

    for w, (out, _) in enumerate(((dn_o, 0), (up_o, 0), (out_o, 0), (qkv_o, 0))):
        routed_own(w).wait()
        for j in range(1, NDP):
            routed_copy(w, j).wait()
        total = routed[w][1][...].astype(F32)
        for j in range(NDP - 1):
            total = total + routed[w][2][j].astype(F32)
        if w < 3:
            out[1] = total
        else:
            for c in range(3):
                out[1, c] = total[:, Hd * c : Hd * c + Hd]
    for w, out in enumerate((dn_o, up_o, out_o, qkv_o)):
        for j in range(1, NDP):
            dp_copy(w, j).wait()
        total = share_total(shares[w][2], shares[w][4], dp)
        if w < 3:
            out[0] = total
        else:
            for c in range(3):
                out[0, c] = total[:, Hd * c : Hd * c + Hd]

    for n, (d2, c2) in enumerate(places):
        vec_copy(n, d2, c2).wait()
    rows_sum = vbuf[0]
    for j in range(1, G):
        rows_sum = rows_sum + vbuf[j]
    hbuf[ln.t] = rows_sum

    def line_copy(n, p):
        return rcopy(hbuf.at[ln.t], hbuf.at[ln.t], ts.at[G - 1 + n], tr.at[G - 1 + n], p)

    for n, p in enumerate(tpeers):
        line_copy(n, p).start()
    for n, p in enumerate(tpeers):
        line_copy(n, p).wait()
    line_sum = hbuf[0]
    for j in range(1, NT):
        line_sum = line_sum + hbuf[j]
    small_o[...] = line_sum

    for j, p in enumerate(rpeers):
        rcopy(lbuf.at[me], lbuf.at[me], cs.at[j], cr.at[j], p).wait()
    loss = lbuf[0]
    for j in range(1, G):
        loss = loss + lbuf[j]
    loss_ref[...] = loss / (cnt_ref[...] * D)

    for w in range(4):
        pair_copy(w).wait_send()

    @pl.when(ctx > 0)
    def _():
        kv_copy(0).wait_send()
        kv_copy(1).wait_send()

    def drain(k, _):
        @pl.when(ln.is_end)
        def _():
            got_half(my_rows, 6, k)
            got_half(ot_rows, 7, k)
            rcopy(sE.at[k], rE2.at[k], ss.at[3, k], rs.at[3, k], ln.mid).wait_send()

        @pl.when(ln.is_mid)
        def _():
            rcopy(sX.at[k, pl.ds(0, half), :], rX.at[k], ss.at[4, k], rs.at[4, k], ln.other).wait_send()
            mine = gin_ref.at[k, my_rows, :]
            theirs = gin_ref.at[k, ot_rows, :]
            rcopy(mine, mine, ss.at[5, k], rs.at[5, k], ln.other).wait_send()
            rcopy(mine, mine, ss.at[6, k], rs.at[6, k], ln.end).wait_send()
            rcopy(theirs, theirs, ss.at[7, k], rs.at[7, k], ln.end).wait_send()

        return 0

    lax.fori_loop(0, NC, drain, 0)


BCHUNK = 64


def dense_backward(x, teacher, valid, cnt, sent, gchosen, ridx, small, again, mgain, seg, fwd, w_qkv, w_out, w_up, w_down, routed):
    L, D = x.shape
    S = seg.shape[0]
    NT, NDP, NCTX = lax.axis_size("tensor"), lax.axis_size("dp"), lax.axis_size("ctx")
    x2, q, k, v, mix, lse, mid, n2, pre, act = fwd
    R = BCHUNK
    NC = L // R
    Hd = w_out.shape[1]
    Fl = w_up.shape[2]
    G = NDP * NCTX
    W = D // G
    ctx = lax.axis_index("ctx")
    segc = lax.dynamic_slice_in_dim(seg, ctx * L, L, 0).reshape(NC, R, 1)
    validc = valid.astype(F32).reshape(NC, R, 1)
    sizes = (NC, R, D, L, S, NT, NDP, NCTX, float(S * NDP))
    dma = pltpu.SemaphoreType.DMA
    sd = jax.ShapeDtypeStruct
    v_ = pl.BlockSpec(memory_space=VM)
    a_ = pl.BlockSpec(memory_space=ANY)

    def four(shape):
        return [VM((NDP,) + shape, BF)] * 3 + [VM((NDP - 1,) + shape, BF)]

    wshape = ((Fl, W), (W, Fl), (Hd, W), (W, 3 * Hd))
    dense_shares = sum((four(s) for s in wshape), [])
    routed_scratch = [VM(s, BF) for s in wshape] + [VM((NDP - 1,) + s, BF) for s in wshape]
    big = VM((NC, R, D), BF)
    return pl.pallas_call(
        functools.partial(dense_backward_kernel, sizes),
        name="dense_backward",
        out_shape=(
            sd((L, D), BF), sd((8, 128), F32), sd((NC, R, D), BF),
            sd((2, Fl, W), F32), sd((2, W, Fl), F32), sd((2, Hd, W), F32), sd((2, 3, W, Hd), F32), sd((8, W), F32),
        ),
        in_specs=[v_] * 22 + [a_] * 8,
        out_specs=(v_,) * 8,
        scratch_shapes=[
            VM((3, D, Hd), BF), VM((Hd, D), BF), VM((D, Fl), BF), VM((Fl, D), BF),
            VM((L, D), F32), VM((L, D), BF), VM((L, Fl), BF), VM((L, D), BF), VM((L, D), BF),
            VM((NC, R, D), F32), VM((3, L, Hd), BF), VM((S, Hd), F32), VM((S, Hd), F32), VM((L, Hd), F32), VM((L, Hd), F32),
            big, big, big, big, big, big, VM((NC, R // 2, D), BF),
        ] + dense_shares + routed_scratch + [
            VM((8, D), F32), VM((8, D), F32), VM((8, D), F32), VM((G, 8, 128), F32),
            VM((8, D), F32), VM((G, 8, W), F32), VM((NT, 8, W), F32),
            dma((4,)), dma((4,)), dma((2, 2)), dma((4,)), dma((4,)), dma((4, NDP)), dma((4, NDP)), dma((4, NDP)), dma((4, NDP)),
            dma((G,)), dma((G,)), dma((G + NT,)), dma((G + NT,)), dma((8, NC)), dma((8, NC)),
        ],
        compiler_params=pltpu.CompilerParams(collective_id=3, has_side_effects=True, vmem_limit_bytes=62 << 20),
    )(
        x, x2.reshape(NC, R, D), teacher, validc, cnt, sent, gchosen, ridx, small, again, mgain, segc, seg.reshape(1, S),
        q, k, v, mix, lse, mid, n2, act, pre, w_qkv, w_out, w_up, w_down, *routed,
    )


def routed_kernel(
    sizes,
    x2_ref, teach_ref, valid_ref, cnt_ref, idxc_ref, idxr_ref, segc_ref, segr_ref, again_ref, mgain_ref, router_ref,
    wqkv_h, wout_h, wup_h, wdn_h,
    sent_ref, gch_ref, small_ref, dn_o, up_o, out_o, qkv_o,
    wqkv, wout, wup, wdn, xs, xc, tsel, tc, vsel, vc, n1_s, k_s, v_s, part, mix_s, n2_s, act_s, gpre_s, gm_s, ga_s, gqkv, dkv, dkvc,
    posc, segq, sbuf, rbuf, tdn, udn, tup, uup, tout, uout, tqkv, uqkv,
    wsem, xsem, xrem, dsem, drem, s1, r1, ps, pr_, gs, gr,
):
    L, D, S, RT, NT, NDP, NCTX, scale_total = sizes
    RL = RT // NCTX
    Q = RL // NT
    G = NDP * NCTX
    W = D // G
    t = lax.axis_index("tensor")
    ctx = lax.axis_index("ctx")
    across = {"ctx": 1 - ctx}
    loads = [
        pltpu.make_async_copy(wqkv_h.at[1], wqkv, wsem.at[0]),
        pltpu.make_async_copy(wout_h.at[1], wout, wsem.at[1]),
        pltpu.make_async_copy(wup_h.at[1], wup, wsem.at[2]),
        pltpu.make_async_copy(wdn_h.at[1], wdn, wsem.at[3]),
    ]
    for ld in loads:
        ld.start()
    greet(tensor_peers(NT) + [across])
    my = pl.ds(pl.multiple_of(ctx * RL, RL), RL)
    theirs = pl.ds(pl.multiple_of((1 - ctx) * RL, RL), RL)
    own = pl.ds(pl.multiple_of(t * Q, Q), Q)

    idxc = idxc_ref[...]
    held = idxc - ctx * L == lax.broadcasted_iota(jnp.int32, (RT, L), 1)
    pick = held.astype(F32).astype(BF)
    xs[...] = dot_nn(pick, x2_ref[...]).astype(BF)
    first = [rcopy(xs, xc, xsem.at[0], xrem.at[0], across)]
    first[0].start()
    tsel[...] = dot_nn(pick, teach_ref[...]).astype(BF)
    vsel[...] = jnp.broadcast_to(jnp.sum(jnp.where(held, valid_ref[...], 0.0), axis=-1, keepdims=True), (RT, 128))
    first.append(rcopy(tsel.at[theirs, :], tc, xsem.at[1], xrem.at[1], across))
    first.append(rcopy(vsel.at[theirs, :], vc, xsem.at[2], xrem.at[2], across))
    first[1].start()
    first[2].start()

    at = idxc == lax.broadcasted_iota(jnp.int32, (RT, S), 1)
    posc[...] = jnp.broadcast_to(idxc, (RT, 128))
    segq[...] = jnp.broadcast_to(jnp.sum(jnp.where(at, segr_ref[...], 0), axis=-1, keepdims=True), (RT, 128))
    down = lax.broadcasted_iota(jnp.int32, (S, RT), 0) == idxr_ref[...]
    seg_row = jnp.sum(jnp.where(down, segc_ref[...], 0), axis=0, keepdims=True)
    visible = (idxr_ref[...] <= posc[my, 0:1]) & (seg_row == segq[my, 0:1])
    bias = jnp.where(visible, 0.0, masked_value)
    again = again_ref[1:2, :]
    mgain = mgain_ref[1:2, :]
    router = router_ref[...]
    Hd = wout.shape[0]
    groups = Hd // 128

    for ld in loads:
        ld.wait()
    first[0].wait_recv()
    chosen = xs[...].astype(F32) + xc[...].astype(F32)
    xs_all = chosen.astype(BF)
    n1 = (rms_parts(chosen)[1] * again).astype(BF)
    n1_s[...] = n1
    first[0].wait_send()
    xs[...] = xs_all
    k_s[...] = dot_nn(n1, wqkv[1]).astype(BF)
    v_s[...] = dot_nn(n1, wqkv[2]).astype(BF)
    n1m = n1_s[my, :]
    q = (dot_nn(n1m, wqkv[0]).astype(BF) * jnp.asarray(0.125, BF))
    probs = []
    for g in range(groups):
        cols = slice(128 * g, 128 * g + 128)
        q2 = head_pair(q[:, cols])
        s = dot_nt(q2, k_s[:, cols]).reshape(2, RL, RT) + bias[None]
        p = jnp.exp(s - jnp.max(s, axis=-1, keepdims=True))
        p = (p * (1.0 / jnp.sum(p, axis=-1, keepdims=True))).reshape(2 * RL, RT)
        probs.append((q2, p))
        mix_s[:, cols] = pair_join(dot_nn(p.astype(BF), v_s[:, cols])).astype(BF)

    def piece_copy(step, j):
        to = lax.rem(t + j, NT)
        rows = pl.ds(pl.multiple_of(to * Q, Q), Q)
        return rcopy(sbuf.at[step, rows, :], rbuf.at[step, j - 1], ps.at[step, j - 1], pr_.at[step, j - 1], {"tensor": to})

    def spread(step, value):
        part[...] = value
        sbuf[step] = value.astype(BF)
        for j in range(1, NT):
            piece_copy(step, j).start()

    def collect(step):
        total = part[own, :]
        for j in range(1, NT):
            piece_copy(step, j).wait_recv()
            total = total + rbuf[step, j - 1].astype(F32)
        return total

    def gather_copy(step, ref, base_row, j):
        to = lax.rem(t + j, NT)
        rows = pl.ds(pl.multiple_of(base_row + t * Q, Q), Q)
        return rcopy(ref.at[rows, :], ref.at[rows, :], gs.at[step, j - 1], gr.at[step, j - 1], {"tensor": to})

    def gather(step, ref, base_row):
        for j in range(1, NT):
            gather_copy(step, ref, base_row, j).start()

    def gathered(step, ref, base_row):
        for j in range(1, NT):
            gather_copy(step, ref, base_row, j).wait()

    mine16 = pl.ds(pl.multiple_of(ctx * RL + t * Q, Q), Q)
    spread(0, dot_nn(mix_s[...], wout[...]))
    chosen_o = xs[mine16, :].astype(F32)
    gate_o = jax.nn.sigmoid(jnp.sum(chosen_o * router, axis=-1, keepdims=True))
    chosen_m = xs[my, :].astype(F32)
    gate_m = jax.nn.sigmoid(jnp.sum(chosen_m * router, axis=-1, keepdims=True))
    attn_o = collect(0)
    mid_o = chosen_o + attn_o
    n2_s[own, :] = (rms_parts(mid_o)[1] * mgain).astype(BF)
    gather(0, n2_s, 0)
    gathered(0, n2_s, 0)

    pre = dot_nn(n2_s[...], wup[...])
    th = gelu_pair(pre)
    act_s[...] = (0.5 * pre * (1.0 + th)).astype(BF)
    spread(1, dot_nn(act_s[...], wdn[...]))
    slope = 0.5 * (1.0 + th) + 0.5 * pre * (1.0 - th * th) * (0.7978845608028654 * (1.0 + 3.0 * 0.044715 * pre * pre))
    first[1].wait()
    first[2].wait()
    teach = tsel[my, :].astype(F32) + tc[...].astype(F32)
    counted = vsel[my, 0:1] + vc[:, 0:1]
    scale = scale_total / cnt_ref[0:1, 0:1]
    branch_o = attn_o + collect(1)
    sent_ref[mine16, :] = (gate_o * branch_o).astype(BF)
    gather(1, sent_ref, ctx * RL)
    gathered(1, sent_ref, ctx * RL)

    sent_pair = rcopy(sent_ref.at[my, :], sent_ref.at[my, :], dsem.at[0], drem.at[0], across)
    sent_pair.start()
    gsent = (scale * counted * (chosen_m + sent_ref[my, :].astype(F32) - teach)).astype(BF).astype(F32)
    top = gate_m * gsent
    part[...] = gsent
    gsent_o = part[own, :]
    gm = top.astype(BF)
    gm_s[...] = gm
    gpre = (dot_nt(gm, wdn[...]) * slope).astype(BF)
    gpre_s[...] = gpre
    spread(2, dot_nt(gpre, wup[...]))

    def by_share(piece, send, keep):
        for c in range(NCTX):
            def one(d, _, c=c):
                val = piece(d * NCTX + c)

                @pl.when(ctx == c)
                def _():
                    keep[d] = val

                @pl.when(ctx != c)
                def _():
                    send[d] = val

                return 0

            lax.fori_loop(0, NDP, one, 0)

    def cols_of(g):
        return pl.ds(pl.multiple_of(g * W, W), W)

    def piece_dn(g):
        return dot_tn(act_s[...], gm_s[:, cols_of(g)]).astype(BF)

    def piece_up(g):
        return dot_tn(n2_s[:, cols_of(g)], gpre_s[...]).astype(BF)

    def piece_out(g):
        return dot_tn(mix_s[...], ga_s[:, cols_of(g)]).astype(BF)

    def piece_qkv(g):
        lhs = n1_s[my, cols_of(g)]
        return jnp.concatenate([dot_tn(lhs, gqkv[c]) for c in range(3)], axis=1).astype(BF)

    shares = ((piece_dn, tdn, dn_o, udn), (piece_up, tup, up_o, uup), (piece_out, tout, out_o, uout), (piece_qkv, tqkv, qkv_o, uqkv))

    def pair_copy(w):
        return rcopy(shares[w][1], shares[w][3], s1.at[w], r1.at[w], across)

    def share_first(w):
        by_share(shares[w][0], shares[w][1], shares[w][2])
        pair_copy(w).start()

    ggate_o = jnp.sum(gsent_o * branch_o, axis=-1, keepdims=True) * gate_o * (1.0 - gate_o)
    small_ref[...] = jnp.zeros(small_ref.shape, F32)
    small_ref[4:5, :] = jnp.sum(ggate_o * chosen_o, axis=0, keepdims=True)
    top_o = gate_o * gsent_o
    share_first(0)
    gmid_o, gain_rows = rms_back(mid_o, mgain, collect(2))
    small_ref[3:4, :] = jnp.sum(gain_rows, axis=0, keepdims=True)
    ga_s[own, :] = (top_o + gmid_o).astype(BF)
    gather(2, ga_s, 0)
    share_first(1)
    gathered(2, ga_s, 0)

    gmix = dot_nt(ga_s[...], wout[...]).astype(BF)
    for g in range(groups):
        cols = slice(128 * g, 128 * g + 128)
        q2, p = probs[g]
        g2 = head_pair(gmix[:, cols])
        dp_ = dot_nt(g2, v_s[:, cols])
        ds = (p * (dp_ - jnp.sum(p * dp_, axis=-1, keepdims=True))).astype(BF)
        gqkv[0, :, cols] = (pair_join(dot_nn(ds, k_s[:, cols])) * 0.125).astype(BF)
        dkv[0, :, cols] = dot_tn(ds, q2)
        dkv[1, :, cols] = dot_tn(p.astype(BF), g2)
    kv_pair = [rcopy(dkv.at[c, theirs, :], dkvc.at[c], dsem.at[1 + c], drem.at[1 + c], across) for c in range(2)]
    for cp in kv_pair:
        cp.start()
    p4 = dot_nt(gqkv[0], wqkv[0])
    for c in range(2):
        kv_pair[c].wait()
        gqkv[1 + c] = (dkv[c, my, :] + dkvc[c]).astype(BF)
        p4 = p4 + dot_nt(gqkv[1 + c], wqkv[1 + c])
    spread(3, p4)
    share_first(2)
    gin_o, gain_rows = rms_back(chosen_o, again, collect(3))
    small_ref[2:3, :] = jnp.sum(gain_rows, axis=0, keepdims=True)
    gch_ref[mine16, :] = (gmid_o + gin_o + ggate_o * router).astype(BF)
    gather(3, gch_ref, ctx * RL)
    share_first(3)
    gathered(3, gch_ref, ctx * RL)
    gch_pair = rcopy(gch_ref.at[my, :], gch_ref.at[my, :], dsem.at[3], drem.at[3], across)
    gch_pair.start()

    for w, (_, _, keep, came) in enumerate(shares):
        pair_copy(w).wait()

        def add(j, _, keep=keep, came=came):
            keep[j] = (keep[j].astype(F32) + came[j].astype(F32)).astype(BF)
            return 0

        lax.fori_loop(0, NDP, add, 0)
    for step in range(4):
        for j in range(1, NT):
            piece_copy(step, j).wait_send()
    sent_pair.wait()
    gch_pair.wait()


def routed_block(x2, teacher, valid, cnt, ridx, seg, again, mgain, w_router, w_qkv, w_out, w_up, w_down):
    L, D = teacher.shape
    S = seg.shape[0]
    RT = ridx.shape[0]
    NT, NDP, NCTX = lax.axis_size("tensor"), lax.axis_size("dp"), lax.axis_size("ctx")
    Hd = w_out.shape[1]
    Fl = w_up.shape[2]
    RL = RT // NCTX
    Q = RL // NT
    G = NDP * NCTX
    W = D // G
    sizes = (L, D, S, RT, NT, NDP, NCTX, float(S * NDP))
    dma = pltpu.SemaphoreType.DMA
    sd = jax.ShapeDtypeStruct
    v_ = pl.BlockSpec(memory_space=VM)
    a_ = pl.BlockSpec(memory_space=ANY)
    wshape = ((Fl, W), (W, Fl), (Hd, W), (W, 3 * Hd))
    return pl.pallas_call(
        functools.partial(routed_kernel, sizes),
        name="routed_block",
        out_shape=(
            sd((RT, D), BF), sd((RT, D), BF), sd((8, D), F32),
            *[sd((NDP,) + s, BF) for s in wshape],
        ),
        in_specs=[v_] * 11 + [a_] * 4,
        out_specs=(v_,) * 7,
        scratch_shapes=[
            VM((3, D, Hd), BF), VM((Hd, D), BF), VM((D, Fl), BF), VM((Fl, D), BF),
            VM((RT, D), BF), VM((RT, D), BF), VM((RT, D), BF), VM((RL, D), BF), VM((RT, 128), F32), VM((RL, 128), F32),
            VM((RT, D), BF), VM((RT, Hd), BF), VM((RT, Hd), BF), VM((RL, D), F32), VM((RL, Hd), BF), VM((RL, D), BF),
            VM((RL, Fl), BF), VM((RL, Fl), BF), VM((RL, D), BF), VM((RL, D), BF), VM((3, RL, Hd), BF),
            VM((2, RT, Hd), F32), VM((2, RL, Hd), F32),
            VM((RT, 128), jnp.int32), VM((RT, 128), jnp.int32),
            VM((4, RL, D), BF), VM((4, NT - 1, Q, D), BF),
            *sum(([VM((NDP,) + s, BF)] * 2 for s in wshape), []),
            dma((4,)), dma((3,)), dma((3,)), dma((4,)), dma((4,)), dma((4,)), dma((4,)),
            dma((4, NT)), dma((4, NT)), dma((4, NT)), dma((4, NT)),
        ],
        compiler_params=pltpu.CompilerParams(collective_id=2, has_side_effects=True, vmem_limit_bytes=60 << 20),
    )(
        x2.reshape(L, D), teacher, valid.astype(F32).reshape(1, L), cnt, ridx.reshape(RT, 1), ridx.reshape(1, RT),
        seg.reshape(S, 1), seg.reshape(1, S), again, mgain, w_router.reshape(1, D), w_qkv, w_out, w_up, w_down,
    )


def fast_local(hidden_in, teacher, seg_ids, valid, routed_idx, attn_gain, w_qkv, w_out, mlp_gain, w_up, w_down, w_router):
    L, D = hidden_in.shape[1:]
    cnt = jnp.full((8, 128), jnp.sum(valid).astype(F32))
    seg = seg_ids[0]
    fwd = dense_forward(hidden_in[0], attn_gain, mlp_gain, seg, cnt, w_qkv, w_out, w_up, w_down)
    cnt = fwd[10]
    sent, gch, small, *routed = routed_block(
        fwd[0], teacher[0], valid[0], cnt, routed_idx[0], seg, attn_gain, mlp_gain, w_router, w_qkv, w_out, w_up, w_down
    )
    hid, loss, gin, dn, up, out, qkv, small = dense_backward(
        hidden_in[0], teacher[0], valid[0], cnt, sent, gch, routed_idx, small, attn_gain, mlp_gain, seg, fwd[:10],
        w_qkv, w_out, w_up, w_down, routed,
    )
    return (
        hid[None], loss[0, 0], gin.reshape(1, L, D).astype(F32),
        jnp.stack([small[0], small[2]]), qkv, out, jnp.stack([small[1], small[3]]), up, dn, small[4],
    )


def takes_kernels(mesh):
    shape = dict(mesh.shape)
    return shape["tensor"] == 4 and shape["ctx"] == 2


def solution(mesh):
    placed = (
        P("dp", "ctx", None),
        P("dp", "ctx", None),
        P("dp", None),
        P("dp", "ctx"),
        P("dp", None),
        P(),
        P(None, None, None, "tensor"),
        P(None, "tensor", None),
        P(),
        P(None, None, "tensor"),
        P(None, "tensor", None),
        P(),
    )
    return jax.shard_map(
        fast_local if takes_kernels(mesh) else plain_local,
        mesh=mesh,
        in_specs=placed,
        out_specs=(
            P("dp", "ctx", None),
            P(),
            P("dp", "ctx", None),
            P(None, ("dp", "ctx")),
            P(None, None, ("dp", "ctx"), "tensor"),
            P(None, "tensor", ("dp", "ctx")),
            P(None, ("dp", "ctx")),
            P(None, ("dp", "ctx"), "tensor"),
            P(None, "tensor", ("dp", "ctx")),
            P(("dp", "ctx")),
        ),
        check_vma=False,
    )
```

```python
import functools

import jax
import jax.numpy as jnp
from jax import lax
from jax.experimental import pallas as pl
from jax.experimental.pallas import tpu as pltpu
from jax.sharding import PartitionSpec as P

HEAD = 64
epsilon = 1e-06
masked_value = -1e30
MESH = pl.DeviceIdType.MESH
BF = jnp.bfloat16
F32 = jnp.float32
VM = pltpu.VMEM
ANY = pl.ANY


def rcopy(src, dst, send, recv, where):
    return pltpu.make_async_remote_copy(
        src_ref=src, dst_ref=dst, send_sem=send, recv_sem=recv, device_id=where, device_id_type=MESH
    )


def dot_nn(a, b):
    return lax.dot_general(a, b, (((1,), (0,)), ((), ())), preferred_element_type=F32)


def dot_nt(a, b):
    return lax.dot_general(a, b, (((1,), (1,)), ((), ())), preferred_element_type=F32)


def dot_tn(a, b):
    return lax.dot_general(a, b, (((0,), (0,)), ((), ())), preferred_element_type=F32)


def rms_parts(values):
    r = lax.rsqrt(jnp.mean(values * values, axis=-1, keepdims=True) + epsilon)
    return r, values * r


def rms_back(values, gain, grad):
    r, unit = rms_parts(values)
    scaled = grad * gain
    return r * (scaled - unit * jnp.mean(scaled * unit, axis=-1, keepdims=True)), grad * unit


def gelu_pair(u):
    c = 0.7978845608028654
    t = jnp.tanh(c * (u + 0.044715 * (u * u * u)))
    return t


def fold8(rows):
    return jnp.sum(rows.reshape(rows.shape[0] // 8, 8, rows.shape[1]), axis=0)


class Line:
    def __init__(self):
        t = lax.axis_index("tensor")
        self.t = t
        self.side = t // 2
        self.is_end = (t == 0) | (t == 3)
        self.is_mid = (t == 1) | (t == 2)
        self.end = {"tensor": self.side * 3}
        self.mid = {"tensor": 1 + self.side}
        self.other = {"tensor": 2 - self.side}


def greet(peers):
    bar = pltpu.get_barrier_semaphore()
    for p in peers:
        pl.semaphore_signal(bar, inc=1, device_id=p, device_id_type=MESH)
    pl.semaphore_wait(bar, len(peers))


def tensor_peers(n):
    t = lax.axis_index("tensor")
    return [{"tensor": lax.rem(t + j, n)} for j in range(1, n)]


def row_peers(n_dp, n_ctx):
    d, c = lax.axis_index("dp"), lax.axis_index("ctx")
    out = []
    for j in range(n_dp):
        for k in range(n_ctx):
            if j or k:
                out.append({"dp": lax.rem(d + j, n_dp), "ctx": lax.rem(c + k, n_ctx)})
    return out


def rms_scale(values, gain):
    return values * lax.rsqrt(jnp.mean(values * values, axis=-1, keepdims=True) + epsilon) * gain


def gelu_tanh(values):
    return jax.nn.gelu(values, approximate=True)


def gating_fn(chosen, router):
    return jax.nn.sigmoid(jnp.sum(chosen * router, axis=-1))


def tensor_sum(partial_sum):
    return lax.psum(partial_sum, "tensor")


def gather_keys(projected):
    return (
        lax.all_gather(projected[1], "ctx", axis=1, tiled=True),
        lax.all_gather(projected[2], "ctx", axis=1, tiled=True),
    )


def scatter_key_grads(grad_k, grad_v):
    stacked = jnp.stack([grad_k, grad_v])
    summed = lax.psum_scatter(stacked, "ctx", scatter_dimension=2, tiled=True)
    return (summed[0], summed[1])


def to_workers(picked):
    return lax.psum_scatter(
        picked.astype(jnp.bfloat16), "ctx", scatter_dimension=1, tiled=True
    ).astype(jnp.float32)


def to_owners(rows_low):
    return lax.all_gather(rows_low, "ctx", axis=1, tiled=True)


def take_rows(table, places):
    return jax.vmap(lambda t, i: t[i])(table, places)


def add_rows(table, places, addend):
    return jax.vmap(lambda t, i, a: t.at[i].add(a))(table, places, addend)


def tile_scores(q_tile, k_tile, qpos_tile, kpos_tile, qseg_tile, kseg_tile, score_scale):
    scores = (
        jnp.einsum("qhe,khe->hqk", q_tile, k_tile, preferred_element_type=jnp.float32) * score_scale
    )
    visible = (kpos_tile[None, :] <= qpos_tile[:, None]) & (
        kseg_tile[None, :] == qseg_tile[:, None]
    )
    return (scores, visible[None])


def tile_layout(queries, key_rows, value_rows, k_pos, k_seg):
    q_len, row_width = queries.shape
    k_len = key_rows.shape[0]
    head_count = row_width // HEAD
    q_step = min(512, q_len)
    k_step = min(2048, k_len)
    k_count = k_len // k_step
    key_tiles = key_rows.reshape(k_count, k_step, head_count, HEAD)
    value_tiles = value_rows.reshape(k_count, k_step, head_count, HEAD)
    kpos_tiles = k_pos.reshape(k_count, k_step)
    kseg_tiles = k_seg.reshape(k_count, k_step)
    return (
        q_len,
        row_width,
        k_len,
        head_count,
        q_step,
        (key_tiles, value_tiles, kpos_tiles, kseg_tiles),
    )


def attend_one(queries, key_rows, value_rows, q_pos, k_pos, q_seg, k_seg):
    q_len, row_width, k_len, head_count, q_step, tiles = tile_layout(
        queries, key_rows, value_rows, k_pos, k_seg
    )
    score_scale = 1.0 / HEAD**0.5

    def per_query(q_args):
        q_tile, qpos_tile, qseg_tile = q_args

        def total_step(carry, k_args):
            running, summed = carry
            k_tile, v_tile, kpos_tile, kseg_tile = k_args
            scores, visible = tile_scores(
                q_tile, k_tile, qpos_tile, kpos_tile, qseg_tile, kseg_tile, score_scale
            )
            raised = jnp.maximum(
                running, jnp.max(jnp.where(visible, scores, masked_value), axis=-1)
            )
            weights = jnp.where(visible, jnp.exp(scores - raised[..., None]), 0.0)
            return ((raised, summed * jnp.exp(running - raised) + jnp.sum(weights, axis=-1)), None)

        initial = (
            jnp.full((head_count, q_step), masked_value, jnp.float32),
            jnp.zeros((head_count, q_step), jnp.float32),
        )
        (running, summed), _ = lax.scan(total_step, initial, tiles)
        log_total = running + jnp.log(summed)

        def value_step(output, k_args):
            k_tile, v_tile, kpos_tile, kseg_tile = k_args
            scores, visible = tile_scores(
                q_tile, k_tile, qpos_tile, kpos_tile, qseg_tile, kseg_tile, score_scale
            )
            weights_low = jnp.where(visible, jnp.exp(scores - log_total[..., None]), 0.0).astype(
                jnp.bfloat16
            )
            return (
                output
                + jnp.einsum(
                    "hqk,khe->qhe", weights_low, v_tile, preferred_element_type=jnp.float32
                ),
                None,
            )

        output, _ = lax.scan(value_step, jnp.zeros((q_step, head_count, HEAD), jnp.float32), tiles)
        return (output, log_total)

    q_count = q_len // q_step
    output, log_total = lax.map(
        per_query,
        (
            queries.reshape(q_count, q_step, head_count, HEAD),
            q_pos.reshape(q_count, q_step),
            q_seg.reshape(q_count, q_step),
        ),
    )
    return (output.reshape(q_len, row_width), log_total)


def attend_back(queries, key_rows, value_rows, grad_mixed, log_total, q_pos, k_pos, q_seg, k_seg):
    q_len, row_width, k_len, head_count, q_step, tiles = tile_layout(
        queries, key_rows, value_rows, k_pos, k_seg
    )
    score_scale = 1.0 / HEAD**0.5

    def per_query(q_args):
        q_tile, g_tile, total_tile, qpos_tile, qseg_tile = q_args

        def tile_probs(k_tile, kpos_tile, kseg_tile):
            scores, visible = tile_scores(
                q_tile, k_tile, qpos_tile, kpos_tile, qseg_tile, kseg_tile, score_scale
            )
            return jnp.where(visible, jnp.exp(scores - total_tile[..., None]), 0.0)

        def inner_step(carry, k_args):
            k_tile, v_tile, kpos_tile, kseg_tile = k_args
            weights = tile_probs(k_tile, kpos_tile, kseg_tile)
            grad_weights = jnp.einsum(
                "qhe,khe->hqk", g_tile, v_tile, preferred_element_type=jnp.float32
            )
            return (carry + jnp.sum(weights * grad_weights, axis=-1), None)

        inner, _ = lax.scan(inner_step, jnp.zeros((head_count, q_step), jnp.float32), tiles)

        def grad_step(carry, k_args):
            k_tile, v_tile, kpos_tile, kseg_tile = k_args
            weights = tile_probs(k_tile, kpos_tile, kseg_tile)
            grad_weights = jnp.einsum(
                "qhe,khe->hqk", g_tile, v_tile, preferred_element_type=jnp.float32
            )
            grad_scores = (weights * (grad_weights - inner[..., None])).astype(jnp.bfloat16)
            carry = carry + jnp.einsum(
                "hqk,khe->qhe", grad_scores, k_tile, preferred_element_type=jnp.float32
            )
            grad_keys = jnp.einsum(
                "hqk,qhe->khe", grad_scores, q_tile, preferred_element_type=jnp.float32
            )
            grad_values = jnp.einsum(
                "hqk,qhe->khe",
                weights.astype(jnp.bfloat16),
                g_tile,
                preferred_element_type=jnp.float32,
            )
            return (carry, (grad_keys, grad_values))

        grad_q, (grad_keys, grad_values) = lax.scan(
            grad_step, jnp.zeros((q_step, head_count, HEAD), jnp.float32), tiles
        )
        return (
            grad_q * score_scale,
            grad_keys.reshape(k_len, row_width) * score_scale,
            grad_values.reshape(k_len, row_width),
        )

    q_count = q_len // q_step
    grad_q, grad_keys, grad_values = lax.map(
        per_query,
        (
            queries.reshape(q_count, q_step, head_count, HEAD),
            grad_mixed.reshape(q_count, q_step, head_count, HEAD),
            log_total,
            q_pos.reshape(q_count, q_step),
            q_seg.reshape(q_count, q_step),
        ),
    )
    return (
        grad_q.reshape(q_len, row_width),
        jnp.sum(grad_keys, axis=0),
        jnp.sum(grad_values, axis=0),
    )


def make_attention(q_pos, k_pos, q_seg, k_seg):

    def attend_fn(projected):
        key_all, value_all = gather_keys(projected)
        mixed_full, log_total = lax.map(
            lambda a: attend_one(*a), (projected[0], key_all, value_all, q_pos, k_pos, q_seg, k_seg)
        )
        return (mixed_full, (key_all, value_all, log_total))

    def attend_grad(projected, kept, grad_mixed):
        key_all, value_all, log_total = kept
        grad_q, grad_k, grad_v = lax.map(
            lambda a: attend_back(*a),
            (projected[0], key_all, value_all, grad_mixed, log_total, q_pos, k_pos, q_seg, k_seg),
        )
        grad_k, grad_v = scatter_key_grads(grad_k, grad_v)
        return jnp.stack(
            [grad_q.astype(jnp.bfloat16), grad_k.astype(jnp.bfloat16), grad_v.astype(jnp.bfloat16)]
        )

    return (attend_fn, attend_grad)


def block_forward(
    resid_in,
    gain_a,
    query_key_value_weight,
    output_weight_matrix,
    gain_m,
    up_weight_matrix,
    down_weight_matrix,
    attend_fn,
):
    attention_norm = rms_scale(resid_in, gain_a).astype(jnp.bfloat16)
    projected = jnp.einsum(
        "oym,qmh->qoyh", attention_norm, query_key_value_weight, preferred_element_type=jnp.float32
    ).astype(jnp.bfloat16)
    mixed_full, kept = attend_fn(projected)
    mixed_state = mixed_full.astype(jnp.bfloat16)
    attention_portion = jnp.einsum(
        "xtu,ua->xta", mixed_state, output_weight_matrix, preferred_element_type=jnp.float32
    )
    attn_out = tensor_sum(attention_portion)
    middle = resid_in + attn_out
    feedforward_norm = rms_scale(middle, gain_m).astype(jnp.bfloat16)
    hidden_preactivation = jnp.einsum(
        "iqp,po->iqo", feedforward_norm, up_weight_matrix, preferred_element_type=jnp.float32
    )
    hidden_activation = gelu_tanh(hidden_preactivation).astype(jnp.bfloat16)
    mlp_part = jnp.einsum(
        "euq,qt->eut", hidden_activation, down_weight_matrix, preferred_element_type=jnp.float32
    )
    mlp_out = tensor_sum(mlp_part)
    saved = (
        resid_in,
        attention_norm,
        projected,
        mixed_state,
        kept,
        middle,
        feedforward_norm,
        hidden_preactivation,
        hidden_activation,
    )
    return (attn_out, mlp_out, saved)


def block_backward(
    saved,
    grad_top,
    gain_a,
    query_key_value_weight,
    output_weight_matrix,
    gain_m,
    up_weight_matrix,
    down_weight_matrix,
    attend_grad,
):
    (
        resid_in,
        attention_norm,
        projected,
        mixed_state,
        kept,
        middle,
        feedforward_norm,
        hidden_preactivation,
        hidden_activation,
    ) = saved
    top_reduced = grad_top.astype(jnp.bfloat16)
    down_weight_gradient = jnp.einsum(
        "pgr,pgw->rw", hidden_activation, top_reduced, preferred_element_type=jnp.float32
    )
    activation_gradient = jnp.einsum(
        "ayx,cx->ayc", top_reduced, down_weight_matrix, preferred_element_type=jnp.float32
    )
    preactivation_gradient = jax.vjp(gelu_tanh, hidden_preactivation)[1](activation_gradient)[
        0
    ].astype(jnp.bfloat16)
    up_weight_gradient = jnp.einsum(
        "uzb,uzv->bv", feedforward_norm, preactivation_gradient, preferred_element_type=jnp.float32
    )
    norm_portion = jnp.einsum(
        "vok,hk->voh", preactivation_gradient, up_weight_matrix, preferred_element_type=jnp.float32
    )
    grad_norm_m = tensor_sum(norm_portion)
    grad_middle, grad_gain_m = jax.vjp(rms_scale, middle, gain_m)[1](grad_norm_m)
    grad_attn = grad_top + grad_middle
    attention_reduced = grad_attn.astype(jnp.bfloat16)
    output_weight_gradient = jnp.einsum(
        "omi,omj->ij", mixed_state, attention_reduced, preferred_element_type=jnp.float32
    )
    grad_mixed = jnp.einsum(
        "bjw,gw->bjg", attention_reduced, output_weight_matrix, preferred_element_type=jnp.float32
    ).astype(jnp.bfloat16)
    projection_gradient = attend_grad(projected, kept, grad_mixed)
    query_key_value_gradient = jnp.einsum(
        "xgt,axgf->atf", attention_norm, projection_gradient, preferred_element_type=jnp.float32
    )
    input_part = jnp.einsum(
        "gurh,gih->uri",
        projection_gradient,
        query_key_value_weight,
        preferred_element_type=jnp.float32,
    )
    grad_norm_a = tensor_sum(input_part)
    grad_resid, grad_gain_a = jax.vjp(rms_scale, resid_in, gain_a)[1](grad_norm_a)
    return (
        grad_attn,
        grad_middle,
        grad_resid,
        (
            grad_gain_a,
            query_key_value_gradient,
            output_weight_gradient,
            grad_gain_m,
            up_weight_gradient,
            down_weight_gradient,
        ),
    )


def pack_grads(grad_list, dims, groups):
    flats = []
    shapes = []
    for grad_item, which_dim in zip(grad_list, dims):
        moved = jnp.moveaxis(grad_item, which_dim, 0)
        shapes.append(moved.shape)
        flats.append(moved.reshape(groups, -1))
    return (jnp.concatenate(flats, axis=1), shapes)


def unpack_grads(summed, shapes, dims, groups):
    results = []
    offset = 0
    for moved_shape, which_dim in zip(shapes, dims):
        share_shape = (moved_shape[0] // groups,) + tuple(moved_shape[1:])
        width = math_prod(share_shape)
        piece = summed[0, offset : offset + width].reshape(share_shape)
        results.append(jnp.moveaxis(piece, 0, which_dim))
        offset = offset + width
    return tuple(results)


def math_prod(shape):
    total = 1
    for extent in shape:
        total = total * extent
    return total


def spread_grads(grad_list, dims):
    groups = lax.axis_size("dp") * lax.axis_size("ctx")
    packed, shapes = pack_grads(grad_list, dims, groups)
    summed = lax.psum_scatter(packed, ("dp", "ctx"), scatter_dimension=0, tiled=True)
    return unpack_grads(summed, shapes, dims, groups)


def plain_local(
    hidden_in,
    teacher,
    seg_ids,
    valid,
    routed_idx,
    attn_gain,
    w_qkv,
    w_out,
    mlp_gain,
    w_up,
    w_down,
    w_router,
):
    seqs_local, local_len, model_width = hidden_in.shape
    seq_len = seg_ids.shape[1]
    routed = routed_idx.shape[1]
    ctx_count = lax.axis_size("ctx")
    ctx_place = lax.axis_index("ctx")
    routed_local = routed // ctx_count
    dense_qpos = jnp.broadcast_to(
        ctx_place * local_len + jnp.arange(local_len, dtype=jnp.int32), (seqs_local, local_len)
    )
    dense_kpos = jnp.broadcast_to(jnp.arange(seq_len, dtype=jnp.int32), (seqs_local, seq_len))
    dense_qseg = lax.dynamic_slice_in_dim(seg_ids, ctx_place * local_len, local_len, 1)
    routed_seg = take_rows(seg_ids, routed_idx)
    routed_qpos = lax.dynamic_slice_in_dim(routed_idx, ctx_place * routed_local, routed_local, 1)
    routed_qseg = lax.dynamic_slice_in_dim(routed_seg, ctx_place * routed_local, routed_local, 1)
    owner_mine = routed_idx // local_len == ctx_place
    owner_row = routed_idx % local_len
    dense_attend, dense_grad = make_attention(dense_qpos, dense_kpos, dense_qseg, seg_ids)
    routed_attend, routed_grad = make_attention(routed_qpos, routed_idx, routed_qseg, routed_seg)
    x_input = hidden_in.astype(jnp.float32)
    attn_d, mlp_d, saved_d = block_forward(
        x_input, attn_gain[0], w_qkv[0], w_out[0], mlp_gain[0], w_up[0], w_down[0], dense_attend
    )
    layer_mid = saved_d[5] + mlp_d
    picked = (
        jnp.where(owner_mine[..., None], take_rows(layer_mid, owner_row), 0.0)
        .astype(jnp.bfloat16)
        .astype(jnp.float32)
    )
    chosen = to_workers(picked).astype(jnp.bfloat16).astype(jnp.float32)
    gating = gating_fn(chosen, w_router)
    attn_r, mlp_r, saved_r = block_forward(
        chosen, attn_gain[1], w_qkv[1], w_out[1], mlp_gain[1], w_up[1], w_down[1], routed_attend
    )
    branch_sum = attn_r + mlp_r
    sent_rows = (gating[..., None] * branch_sum).astype(jnp.bfloat16)
    returned = to_owners(sent_rows).astype(jnp.float32)
    layer_out = add_rows(layer_mid, owner_row, jnp.where(owner_mine[..., None], returned, 0.0))
    valid_rows = valid.astype(jnp.float32)
    error_rows = layer_out - teacher.astype(jnp.float32)
    error_sum, valid_count = lax.psum(
        (jnp.sum(valid_rows[..., None] * error_rows * error_rows), jnp.sum(valid_rows)),
        ("dp", "ctx"),
    )
    loss_value = error_sum / (valid_count * model_width)
    token_total = float(seqs_local * seq_len * lax.axis_size("dp"))
    grad_final = token_total / valid_count * valid_rows[..., None] * error_rows
    picked_grad = (
        jnp.where(owner_mine[..., None], take_rows(grad_final, owner_row), 0.0)
        .astype(jnp.bfloat16)
        .astype(jnp.float32)
    )
    branch_grad = to_workers(picked_grad).astype(jnp.bfloat16).astype(jnp.float32)
    grad_top = gating[..., None] * branch_grad
    gating_share, gating_back = jax.vjp(gating_fn, chosen, w_router)
    grad_gating = jnp.sum(branch_grad * branch_sum, axis=-1)
    grad_chosen_gate, grad_router = gating_back(grad_gating)
    grad_attn_r, grad_middle_r, grad_resid_r, grads_r = block_backward(
        saved_r,
        grad_top,
        attn_gain[1],
        w_qkv[1],
        w_out[1],
        mlp_gain[1],
        w_up[1],
        w_down[1],
        routed_grad,
    )
    grad_chosen = (grad_middle_r + grad_resid_r + grad_chosen_gate).astype(jnp.bfloat16)
    grads_r = grads_r + (grad_router,)
    spread_r = spread_grads(grads_r, (0, 1, 1, 0, 0, 1, 0))
    grad_rows = to_owners(grad_chosen).astype(jnp.float32)
    grad_mid = add_rows(grad_final, owner_row, jnp.where(owner_mine[..., None], grad_rows, 0.0))
    grad_attn_d, grad_middle_d, grad_resid_d, grads_d = block_backward(
        saved_d,
        grad_mid,
        attn_gain[0],
        w_qkv[0],
        w_out[0],
        mlp_gain[0],
        w_up[0],
        w_down[0],
        dense_grad,
    )
    grad_input = grad_attn_d + grad_resid_d
    spread_d = spread_grads(grads_d, (0, 1, 1, 0, 0, 1))
    return (
        layer_out.astype(jnp.bfloat16),
        loss_value,
        grad_input,
        jnp.stack([spread_d[0], spread_r[0]]),
        jnp.stack([spread_d[1], spread_r[1]]),
        jnp.stack([spread_d[2], spread_r[2]]),
        jnp.stack([spread_d[3], spread_r[3]]),
        jnp.stack([spread_d[4], spread_r[4]]),
        jnp.stack([spread_d[5], spread_r[5]]),
        spread_r[6],
    )


def column(row, start, length):
    wanted = start + lax.broadcasted_iota(jnp.int32, (length, 1), 0)
    hit = lax.broadcasted_iota(jnp.int32, (length, row.shape[1]), 1) == wanted
    return jnp.sum(jnp.where(hit, row, jnp.zeros_like(row)), axis=-1, keepdims=True)


def head_pair(rows):
    lane = lax.broadcasted_iota(jnp.int32, rows.shape, 1)
    zero = jnp.zeros_like(rows)
    return jnp.concatenate([jnp.where(lane < HEAD, rows, zero), jnp.where(lane >= HEAD, rows, zero)], axis=0)


def pair_join(stacked):
    half = stacked.shape[0] // 2
    lane = lax.broadcasted_iota(jnp.int32, (half, stacked.shape[1]), 1)
    return jnp.where(lane < HEAD, stacked[:half], stacked[half:])


FWD_LAGS = (1, 2, 3, 4, 5, 6)
CHUNK = 128
SUB = 2


def dense_forward_kernel(
    sizes,
    x_ref, again_ref, mgain_ref, seg_ref, valid_ref, wqkv_h, wout_h, wup_h, wdn_h,
    x2_ref, q_h, k_h, v_h, mix_h, lse_h, mid_h, pre_h, cnt_out,
    q_ref, k_ref, v_ref, mix_ref, lse_ref, mid_ref, pre_ref,
    wqkv, wout, wup, wdn, part, part2,
    sE, rE, sI, rI, sO, sE2, rE2, sX, rX, cbuf,
    wsem, osem, kvs, kvr, cs, cr, ss, rs,
):
    NC, SUBS, R, D, L, S, NT, NDP, NCTX = sizes
    RS = R // SUBS
    NM = NC * SUBS
    ln = Line()
    ctx = lax.axis_index("ctx")
    half = RS // 2
    loads = [
        pltpu.make_async_copy(wqkv_h.at[0], wqkv, wsem.at[0]),
        pltpu.make_async_copy(wout_h.at[0], wout, wsem.at[1]),
        pltpu.make_async_copy(wup_h.at[0], wup, wsem.at[2]),
        pltpu.make_async_copy(wdn_h.at[0], wdn, wsem.at[3]),
    ]
    for ld in loads:
        ld.start()
    tpeers = tensor_peers(NT)
    rpeers = row_peers(NDP, NCTX)
    greet(tpeers + rpeers)

    cbuf[0] = jnp.full((8, 128), jnp.sum(valid_ref[...].astype(F32)))
    counts = [rcopy(cbuf.at[0], cbuf.at[j + 1], cs.at[j], cr.at[j], p) for j, p in enumerate(rpeers)]
    for cp in counts:
        cp.start()

    @pl.when(ln.is_end)
    def _():
        def zero(k, _):
            rE[k] = jnp.zeros((RS, D), BF)
            return 0

        lax.fori_loop(0, NM, zero, 0)

    loads[0].wait()
    RB = 128
    again = again_ref[0:1, :]

    def project(i, _):
        rows = pl.ds(pl.multiple_of(i * RB, RB), RB)
        xv = x_ref[rows, :].astype(F32)
        n1 = (rms_parts(xv)[1] * again).astype(BF)
        for c, ref in enumerate((q_ref, k_ref, v_ref)):
            y = dot_nn(n1, wqkv[c]).astype(BF)
            if c == 0:
                ref[rows, :] = y * jnp.asarray(0.125, BF)
            else:
                ref[pl.ds(pl.multiple_of(ctx * L + i * RB, RB), RB), :] = y
        return 0

    lax.fori_loop(0, L // RB, project, 0)

    own = pl.ds(pl.multiple_of(ctx * L, L), L)

    def kv_copy(ref, which, c_to):
        return rcopy(ref.at[own, :], ref.at[own, :], kvs.at[which, c_to], kvr.at[which, ctx], {"ctx": c_to})

    for c_to in range(1, NCTX):
        @pl.when(c_to > ctx)
        def _(c_to=c_to):
            kv_copy(k_ref, 0, c_to).start()
            kv_copy(v_ref, 1, c_to).start()

    for c_later in range(1, NCTX):
        @pl.when(c_later > ctx)
        def _(c_later=c_later):
            k_ref[pl.ds(c_later * L, L), :] = jnp.zeros((L, k_ref.shape[1]), BF)
            v_ref[pl.ds(c_later * L, L), :] = jnp.zeros((L, k_ref.shape[1]), BF)

    loads[1].wait()
    loads[2].wait()
    loads[3].wait()
    for c_from in range(NCTX - 1):
        @pl.when(c_from < ctx)
        def _(c_from=c_from):
            theirs = pl.ds(c_from * L, L)
            for which, ref in enumerate((k_ref, v_ref)):
                rcopy(ref.at[theirs, :], ref.at[theirs, :], kvs.at[which, c_from], kvr.at[which, c_from], {"ctx": c_from}).wait_recv()

    whole = [pltpu.make_async_copy(a, b, osem.at[n, 0]) for n, (a, b) in enumerate(((q_ref, q_h), (k_ref, k_h), (v_ref, v_h)))]
    for cp in whole:
        cp.start()
    mgain = mgain_ref[0:1, :]
    groups = q_ref.shape[1] // 128

    def keep_copy(n, src, dst, i):
        rows = pl.ds(pl.multiple_of(i * R, R), R)
        return pltpu.make_async_copy(src.at[rows, :], dst.at[rows, :], osem.at[n, i])

    def keep_early(i):
        return (keep_copy(3, mix_ref, mix_h, i), keep_copy(4, lse_ref, lse_h, i))

    def keep_late(i):
        return (keep_copy(5, mid_ref, mid_h, i), keep_copy(6, pre_ref, pre_h, i))

    def attend(i, keys):
        rows = pl.ds(pl.multiple_of(i * R, R), R)
        qpos = ctx * L + i * R + lax.broadcasted_iota(jnp.int32, (R, 1), 0)
        qseg = column(seg_ref[...], ctx * L + i * R, R)
        kpos = lax.broadcasted_iota(jnp.int32, (1, keys), 1)
        visible = (kpos <= qpos) & (seg_ref[:, :keys] == qseg)
        bias = jnp.where(visible, 0.0, masked_value)
        lane = lax.broadcasted_iota(jnp.int32, (R, 128), 1)
        lse_tile = jnp.zeros((R, 128), F32)
        for g in range(groups):
            cols = slice(128 * g, 128 * g + 128)
            q2 = head_pair(q_ref[rows, cols])
            s = dot_nt(q2, k_ref[:keys, cols]).reshape(2, R, keys) + bias[None]
            top = jnp.max(s, axis=-1, keepdims=True)
            p = jnp.exp(s - top)
            total = jnp.sum(p, axis=-1, keepdims=True)
            pr = (p * (1.0 / total)).astype(BF).reshape(2 * R, keys)
            lse = top + jnp.log(total)
            lse_tile = jnp.where(lane == 2 * g, lse[0], jnp.where(lane == 2 * g + 1, lse[1], lse_tile))
            o = dot_nn(pr, v_ref[:keys, cols])
            mix_ref[rows, cols] = pair_join(o).astype(BF)
        lse_ref[rows, :] = lse_tile

    a1, a2, a3, a4, a5, a6 = FWD_LAGS
    lag3 = jnp.where(ln.is_end, a3, a2)
    my_rows = pl.ds(pl.multiple_of(ln.side * half, half), half)
    ot_rows = pl.ds(pl.multiple_of((1 - ln.side) * half, half), half)

    def got(buf, flow, j):
        rcopy(buf.at[j], buf.at[j], ss.at[flow, j], rs.at[flow, j], ln.mid).wait_recv()

    def got_half(rows, flow, j):
        rcopy(x2_ref.at[j, rows, :], x2_ref.at[j, rows, :], ss.at[flow, j], rs.at[flow, j], ln.mid).wait_recv()

    def each(j, fn):
        for s in range(SUBS):
            fn(j * SUBS + s)

    def body(i, _):
        @pl.when(i < NC)
        def _():
            @pl.when(ctx == 0)
            def _():
                attend(i, L)

            @pl.when(ctx > 0)
            def _():
                attend(i, S)

            for s in range(SUBS):
                m = i * SUBS + s
                p = dot_nn(mix_ref[pl.ds(pl.multiple_of(i * R + s * RS, RS), RS), :], wout[...])
                part[m] = p

                @pl.when(ln.is_end)
                def _(m=m, p=p):
                    sE[m] = p.astype(BF)
                    rcopy(sE.at[m], rE.at[m], ss.at[0, m], rs.at[0, m], ln.mid).start()

            for cp in keep_early(i):
                cp.start()

        j1 = i - a1

        @pl.when(ln.is_mid & (j1 >= 0) & (j1 < NC))
        def _():
            def forward(m):
                got(rE, 0, m)
                sI[m] = (rE[m].astype(F32) + part[m]).astype(BF)
                rcopy(sI.at[m], rI.at[m], ss.at[1, m], rs.at[1, m], ln.other).start()

            each(j1, forward)

        j3 = i - lag3

        @pl.when((j3 >= 0) & (j3 < NC))
        def _():
            def arrive(m):
                got(rI, 1, m)

                @pl.when(ln.is_mid)
                def _():
                    sO[m] = (rI[m].astype(F32) + part[m]).astype(BF)
                    rcopy(sO.at[m], rI.at[m], ss.at[2, m], rs.at[1, m], ln.end).start()

            each(j3, arrive)
            ms = pl.ds(j3 * SUBS, SUBS)
            rows = pl.ds(pl.multiple_of(j3 * R, R), R)
            total = (rI[ms].astype(F32) + part[ms] + rE[ms].astype(F32)).reshape(R, D)
            mid = x_ref[rows, :].astype(F32) + total
            mid_ref[rows, :] = mid
            n2 = (rms_parts(mid)[1] * mgain).astype(BF)
            pre = dot_nn(n2, wup[...])
            pre_ref[rows, :] = pre
            for cp in keep_late(j3):
                cp.start()
            act = (0.5 * pre * (1.0 + gelu_pair(pre))).astype(BF)
            for s in range(SUBS):
                m = j3 * SUBS + s
                p2 = dot_nn(act[s * RS : (s + 1) * RS], wdn[...])

                @pl.when(ln.is_end)
                def _(m=m, p2=p2):
                    sE2[m] = p2.astype(BF)
                    rcopy(sE2.at[m], rE2.at[m], ss.at[3, m], rs.at[3, m], ln.mid).start()

                @pl.when(ln.is_mid)
                def _(m=m, p2=p2):
                    part2[m] = p2

        j4 = i - a4

        @pl.when(ln.is_mid & (j4 >= 0) & (j4 < NC))
        def _():
            def cross(m):
                got(rE2, 3, m)
                sX[m] = (rE2[m, ot_rows, :].astype(F32) + part2[m, ot_rows, :]).astype(BF)
                rcopy(sX.at[m], rX.at[m], ss.at[4, m], rs.at[4, m], ln.other).start()

            each(j4, cross)

        j5 = i - a5

        @pl.when(ln.is_mid & (j5 >= 0) & (j5 < NC))
        def _():
            def settle(m):
                got(rX, 4, m)
                rows = pl.ds(pl.multiple_of(m * RS + ln.side * half, half), half)
                mlp = part2[m, my_rows, :] + rE2[m, my_rows, :].astype(F32) + rX[m].astype(F32)
                x2_ref[m, my_rows, :] = (mid_ref[rows, :] + mlp).astype(BF)
                mine = x2_ref.at[m, my_rows, :]
                rcopy(mine, mine, ss.at[5, m], rs.at[5, m], ln.other).start()
                rcopy(mine, mine, ss.at[6, m], rs.at[6, m], ln.end).start()

            each(j5, settle)

        j6 = i - a6

        @pl.when(ln.is_mid & (j6 >= 0) & (j6 < NC))
        def _():
            def relay(m):
                got_half(ot_rows, 5, m)
                theirs = x2_ref.at[m, ot_rows, :]
                rcopy(theirs, theirs, ss.at[7, m], rs.at[7, m], ln.end).start()

            each(j6, relay)

        return 0

    lax.fori_loop(0, NC + a6, body, 0)

    for cp in counts:
        cp.wait()
    total = cbuf[0]
    for j in range(1, len(rpeers) + 1):
        total = total + cbuf[j]
    cnt_out[...] = total

    for c_to in range(1, NCTX):
        @pl.when(c_to > ctx)
        def _(c_to=c_to):
            kv_copy(k_ref, 0, c_to).wait_send()
            kv_copy(v_ref, 1, c_to).wait_send()

    for cp in whole:
        cp.wait()

    def kept(i, _):
        for cp in keep_early(i) + keep_late(i):
            cp.wait()
        return 0

    lax.fori_loop(0, NC, kept, 0)

    def drain(m, _):
        @pl.when(ln.is_end)
        def _():
            got_half(my_rows, 6, m)
            got_half(ot_rows, 7, m)
            rcopy(sE.at[m], rE.at[m], ss.at[0, m], rs.at[0, m], ln.mid).wait_send()
            rcopy(sE2.at[m], rE2.at[m], ss.at[3, m], rs.at[3, m], ln.mid).wait_send()

        @pl.when(ln.is_mid)
        def _():
            rcopy(sI.at[m], rI.at[m], ss.at[1, m], rs.at[1, m], ln.other).wait_send()
            rcopy(sO.at[m], rI.at[m], ss.at[2, m], rs.at[1, m], ln.end).wait_send()
            rcopy(sX.at[m], rX.at[m], ss.at[4, m], rs.at[4, m], ln.other).wait_send()
            mine = x2_ref.at[m, my_rows, :]
            theirs = x2_ref.at[m, ot_rows, :]
            rcopy(mine, mine, ss.at[5, m], rs.at[5, m], ln.other).wait_send()
            rcopy(mine, mine, ss.at[6, m], rs.at[6, m], ln.end).wait_send()
            rcopy(theirs, theirs, ss.at[7, m], rs.at[7, m], ln.end).wait_send()

        return 0

    lax.fori_loop(0, NM, drain, 0)


def dense_forward(x, again, mgain, seg, valid, w_qkv, w_out, w_up, w_down):
    L, D = x.shape
    S = seg.shape[1]
    NT, NDP, NCTX = lax.axis_size("tensor"), lax.axis_size("dp"), lax.axis_size("ctx")
    R = min(CHUNK, L)
    NC = L // R
    RS = R // SUB
    NM = NC * SUB
    Hd = w_out.shape[1]
    Fl = w_up.shape[2]
    sizes = (NC, SUB, R, D, L, S, NT, NDP, NCTX)
    flows = 8
    dma = pltpu.SemaphoreType.DMA
    rows = NDP * NCTX
    sd = jax.ShapeDtypeStruct
    v = pl.BlockSpec(memory_space=VM)
    a = pl.BlockSpec(memory_space=ANY)
    big = VM((NM, RS, D), BF)
    return pl.pallas_call(
        functools.partial(dense_forward_kernel, sizes),
        name="dense_forward",
        out_shape=(
            sd((NM, RS, D), BF), sd((L, Hd), BF), sd((S, Hd), BF), sd((S, Hd), BF), sd((L, Hd), BF),
            sd((L, 128), F32), sd((L, D), F32), sd((L, Fl), F32), sd((8, 128), F32),
        ),
        in_specs=[v] * 5 + [a] * 4,
        out_specs=(v,) + (a,) * 7 + (v,),
        scratch_shapes=[
            VM((L, Hd), BF), VM((S, Hd), BF), VM((S, Hd), BF), VM((L, Hd), BF), VM((L, 128), F32), VM((L, D), F32), VM((L, Fl), F32),
            VM((3, D, Hd), BF), VM((Hd, D), BF), VM((D, Fl), BF), VM((Fl, D), BF),
            VM((NM, RS, D), F32), VM((NM, RS, D), F32),
            big, big, big, big, big, big, big, VM((NM, RS // 2, D), BF), VM((NM, RS // 2, D), BF),
            VM((rows, 8, 128), F32),
            dma((4,)), dma((7, NC)), dma((2, NCTX)), dma((2, NCTX)), dma((rows,)), dma((rows,)), dma((flows, NM)), dma((flows, NM)),
        ],
        compiler_params=pltpu.CompilerParams(collective_id=1, has_side_effects=True, vmem_limit_bytes=58 << 20),
    )(x, again, mgain, seg, valid, w_qkv, w_out, w_up, w_down)


BWD_LAGS = (1, 2, 3)
TAIL_LAGS = (1, 2, 3)
BCHUNK = 128


def share_add(own, came):
    def add(j, _):
        own[j] = (own[j].astype(F32) + came[j].astype(F32)).astype(BF)
        return 0

    lax.fori_loop(0, own.shape[0], add, 0)


def dense_backward_kernel(
    sizes,
    x_ref, x2_ref, teach_ref, valid_ref, cnt_ref, sent_ref, gch_ref, ridx_ref, small_ref, again_ref, mgain_ref, seg_ref,
    q_h, k_h, v_h, mix_h, lse_h, mid_h, pre_h, wqkv_h, wout_h, wup_h, wdn_h, rdn_h, rup_h, rout_h, rqkv_h,
    hid_ref, loss_ref, gin_ref, dn_o, up_o, out_o, qkv_o, small_o,
    q_ref, k_ref, v_ref, mix_ref, lse_ref, mid_ref, pre_ref,
    wqkv, wout, wup, wdn, g_s, gm_s, act_s, gpre_s, n2_s, ga_s, n1_s, part, gqkv, dk_s, dv_s, rdk, rdv,
    sE, rE, sI, rI, sO, rE2, rX,
    tdn, odn, udn, wdn_r, tup, oup, uup, wup_r, tout, oout, uout, wout_r, tqkv, oqkv, uqkv, wqkv_r,
    ldn, lup, lout, lqkv, xdn, xup, xout, xqkv,
    acc_m, acc_a, lacc, lbuf, vec, vbuf, hbuf,
    isem, lsem, kvsem, s1, r1, s2, r2, s3, r3, cs, cr, ts, tr, ss, rs,
):
    NC, SUBS, R, D, L, S, NT, NDP, NCTX, scale_total = sizes
    RS = R // SUBS
    NM = NC * SUBS
    ln = Line()
    ctx = lax.axis_index("ctx")
    dp = lax.axis_index("dp")
    half = RS // 2
    G = NDP * NCTX
    W = D // G
    order = (
        (wdn_h.at[0], wdn), (pre_h, pre_ref), (wup_h.at[0], wup), (mid_h, mid_ref), (wout_h.at[0], wout), (q_h, q_ref),
        (k_h, k_ref), (v_h, v_ref), (lse_h, lse_ref), (mix_h, mix_ref), (wqkv_h.at[0], wqkv),
    )
    loads = [pltpu.make_async_copy(a, b, isem.at[n]) for n, (a, b) in enumerate(order)]
    for ld in loads:
        ld.start()
    tpeers = tensor_peers(NT)
    rpeers = row_peers(NDP, NCTX)
    greet(tpeers + rpeers)

    routed = ((rdn_h, ldn, xdn), (rup_h, lup, xup), (rout_h, lout, xout), (rqkv_h, lqkv, xqkv))

    def routed_copy(w, j):
        src, _, dst = routed[w]
        to = lax.rem(dp + j, NDP)
        return rcopy(src.at[to], dst.at[j - 1], s3.at[w, j - 1], r3.at[w, j - 1], {"dp": to})

    def routed_own(w):
        return pltpu.make_async_copy(routed[w][0].at[dp], routed[w][1], lsem.at[w])

    for w in range(4):
        routed_own(w).start()
        for j in range(1, NDP):
            routed_copy(w, j).start()

    @pl.when(ln.is_end)
    def _():
        def zero(m, _):
            rE[m] = jnp.zeros((RS, D), BF)
            return 0

        lax.fori_loop(0, NM, zero, 0)

    for ref in (dk_s, dv_s, acc_m, acc_a, lacc):
        ref[...] = jnp.zeros(ref.shape, F32)
    again = again_ref[0:1, :]
    mgain = mgain_ref[0:1, :]
    scale = scale_total / cnt_ref[0:1, 0:1]
    for ld in loads:
        ld.wait()

    Hd = q_ref.shape[1]
    groups = Hd // 128

    def attend_back(j, gmix, keys):
        rows = pl.ds(pl.multiple_of(j * R, R), R)
        qpos = ctx * L + j * R + lax.broadcasted_iota(jnp.int32, (R, 1), 0)
        qseg = column(seg_ref[...], ctx * L + j * R, R)
        kpos = lax.broadcasted_iota(jnp.int32, (1, keys), 1)
        visible = (kpos <= qpos) & (seg_ref[:, :keys] == qseg)
        bias = jnp.where(visible, 0.0, masked_value)
        lse = lse_ref[rows, :]
        for g in range(groups):
            cols = slice(128 * g, 128 * g + 128)
            q2 = head_pair(q_ref[rows, cols])
            g2 = head_pair(gmix[:, cols])
            kg = k_ref[:keys, cols]
            vg = v_ref[:keys, cols]
            l2 = jnp.concatenate([lse[:, 2 * g : 2 * g + 1], lse[:, 2 * g + 1 : 2 * g + 2]], axis=0)
            s = (dot_nt(q2, kg).reshape(2, R, keys) + bias[None]).reshape(2 * R, keys)
            p = jnp.exp(s - l2)
            dp_ = dot_nt(g2, vg)
            inner = jnp.sum(p * dp_, axis=-1, keepdims=True)
            ds = (p * (dp_ - inner)).astype(BF)
            gqkv[0, rows, cols] = (pair_join(dot_nn(ds, kg)) * 0.125).astype(BF)
            dk_s[:keys, cols] += dot_tn(ds, q2)
            dv_s[:keys, cols] += dot_tn(p.astype(BF), g2)

    a1, a2, a3 = BWD_LAGS
    lag3 = jnp.where(ln.is_end, a3, a2)
    my_rows = pl.ds(pl.multiple_of(ln.side * half, half), half)
    ot_rows = pl.ds(pl.multiple_of((1 - ln.side) * half, half), half)

    def got(buf, flow, j):
        rcopy(buf.at[j], buf.at[j], ss.at[flow, j], rs.at[flow, j], ln.mid).wait_recv()

    def got_half(rows, flow, j):
        rcopy(gin_ref.at[j, rows, :], gin_ref.at[j, rows, :], ss.at[flow, j], rs.at[flow, j], ln.mid).wait_recv()

    def each(j, fn):
        for s in range(SUBS):
            fn(j * SUBS + s)

    def both_of(d):
        return pl.ds(pl.multiple_of(d * NCTX * W, NCTX * W), NCTX * W)

    def by_share(piece, send, keep):
        def one(d, _):
            for lo, width, val in piece(both_of(d)):
                for c in range(NCTX):
                    rows = val[c * W : (c + 1) * W].astype(BF)

                    @pl.when(ctx == c)
                    def _(rows=rows, lo=lo, width=width):
                        keep[d, :, lo : lo + width] = rows

                    @pl.when(ctx != c)
                    def _(rows=rows, lo=lo, width=width):
                        send[d, :, lo : lo + width] = rows

            return 0

        lax.fori_loop(0, NDP, one, 0)

    def piece_dn(cols):
        return [(0, act_s.shape[1], dot_tn(gm_s[:, cols], act_s[...]))]

    def piece_up(cols):
        return [(0, gpre_s.shape[1], dot_tn(n2_s[:, cols], gpre_s[...]))]

    def piece_out(cols):
        return [(0, Hd, dot_tn(ga_s[:, cols], mix_ref[...]))]

    def piece_qkv(cols):
        lhs = n1_s[:, cols]
        return [(Hd * c, Hd, dot_tn(lhs, gqkv[c])) for c in range(3)]

    shares = (
        (piece_dn, tdn, odn, udn, wdn_r, dn_o),
        (piece_up, tup, oup, uup, wup_r, up_o),
        (piece_out, tout, oout, uout, wout_r, out_o),
        (piece_qkv, tqkv, oqkv, uqkv, wqkv_r, qkv_o),
    )
    across = {"ctx": 1 - ctx}

    def pair_copy(w):
        return rcopy(shares[w][1], shares[w][3], s1.at[w], r1.at[w], across)

    def share_first(w):
        by_share(shares[w][0], shares[w][1], shares[w][2])
        pair_copy(w).start()

    def dp_copy(w, j):
        to = lax.rem(dp + j, NDP)
        return rcopy(shares[w][2].at[to], shares[w][4].at[j - 1], s2.at[w, j - 1], r2.at[w, j - 1], {"dp": to})

    def share_second(w):
        pair_copy(w).wait_recv()
        share_add(shares[w][2], shares[w][3])
        for j in range(1, NDP):
            dp_copy(w, j).start()

    def put_total(w, layer, total):
        out = shares[w][5]
        if w == 3:
            for c in range(3):
                out[layer, c] = total[:, Hd * c : Hd * c + Hd]
        elif w == 1:
            out[layer] = total
        else:
            out[layer] = total.T

    def dense_total(w):
        for j in range(1, NDP):
            dp_copy(w, j).wait()
        total = shares[w][2][dp].astype(F32)
        for j in range(NDP - 1):
            total = total + shares[w][4][j].astype(F32)
        put_total(w, 0, total)

    def routed_total(w):
        routed_own(w).wait()
        for j in range(1, NDP):
            routed_copy(w, j).wait()
        total = routed[w][1][...].astype(F32)
        for j in range(NDP - 1):
            total = total + routed[w][2][j].astype(F32)
        put_total(w, 1, total)

    me = dp * NCTX + ctx

    def body(i, _):
        @pl.when(i < NC)
        def _():
            rows = pl.ds(pl.multiple_of(i * R, R), R)
            place = ctx * L + i * R + lax.broadcasted_iota(jnp.int32, (R, 1), 0)
            pick = (place == ridx_ref[...]).astype(F32).astype(BF)
            ms = pl.ds(i * SUBS, SUBS)
            x3 = x2_ref[ms].astype(F32).reshape(R, D) + dot_nn(pick, sent_ref[...])
            hid_ref[rows, :] = x3.astype(BF)
            err = x3 - teach_ref[rows, :].astype(F32)
            counted = column(valid_ref[...].astype(F32), i * R, R) * err
            lacc[...] += fold8(counted * err)
            g2 = scale * counted + dot_nn(pick, gch_ref[...])
            g_s[rows, :] = g2
            gm = g2.astype(BF)
            gm_s[rows, :] = gm
            gact = dot_nt(gm, wdn[...])
            u = pre_ref[rows, :]
            t = gelu_pair(u)
            act_s[rows, :] = (0.5 * u * (1.0 + t)).astype(BF)
            slope = 0.5 * (1.0 + t) + 0.5 * u * (1.0 - t * t) * (0.7978845608028654 * (1.0 + 3.0 * 0.044715 * u * u))
            gpre = (gact * slope).astype(BF)
            gpre_s[rows, :] = gpre
            for s in range(SUBS):
                m = i * SUBS + s
                p3 = dot_nt(gpre[s * RS : (s + 1) * RS], wup[...])
                part[m] = p3

                @pl.when(ln.is_end)
                def _(m=m, p3=p3):
                    sE[m] = p3.astype(BF)
                    rcopy(sE.at[m], rE.at[m], ss.at[0, m], rs.at[0, m], ln.mid).start()

            n1_s[rows, :] = (rms_parts(x_ref[rows, :].astype(F32))[1] * again).astype(BF)

        j1 = i - a1

        @pl.when(ln.is_mid & (j1 >= 0) & (j1 < NC))
        def _():
            def forward(m):
                got(rE, 0, m)
                sI[m] = (rE[m].astype(F32) + part[m]).astype(BF)
                rcopy(sI.at[m], rI.at[m], ss.at[1, m], rs.at[1, m], ln.other).start()

            each(j1, forward)

        j3 = i - lag3

        @pl.when((j3 >= 0) & (j3 < NC))
        def _():
            def arrive(m):
                got(rI, 1, m)

                @pl.when(ln.is_mid)
                def _():
                    sO[m] = (rI[m].astype(F32) + part[m]).astype(BF)
                    rcopy(sO.at[m], rI.at[m], ss.at[2, m], rs.at[1, m], ln.end).start()

            each(j3, arrive)
            ms = pl.ds(j3 * SUBS, SUBS)
            rows = pl.ds(pl.multiple_of(j3 * R, R), R)
            gn2 = (rI[ms].astype(F32) + part[ms] + rE[ms].astype(F32)).reshape(R, D)
            r, unit = rms_parts(mid_ref[rows, :])
            n2_s[rows, :] = (unit * mgain).astype(BF)
            scaled = gn2 * mgain
            gmid = r * (scaled - unit * jnp.mean(scaled * unit, axis=-1, keepdims=True))
            acc_m[...] += fold8(gn2 * unit)
            gattn = g_s[rows, :] + gmid
            g_s[rows, :] = gattn
            ga = gattn.astype(BF)
            ga_s[rows, :] = ga
            gmix = dot_nt(ga, wout[...]).astype(BF)

            @pl.when(ctx == 0)
            def _():
                attend_back(j3, gmix, L)

            @pl.when(ctx > 0)
            def _():
                attend_back(j3, gmix, S)

        @pl.when(i == NC)
        def _():
            lbuf[me] = jnp.full((8, 128), jnp.sum(lacc[...]))
            for j, p in enumerate(rpeers):
                rcopy(lbuf.at[me], lbuf.at[me], cs.at[j], cr.at[j], p).start()
            share_first(0)

        return 0

    lax.fori_loop(0, NC + a3, body, 0)

    def kv_copy(which):
        src, dst = ((dk_s, rdk), (dv_s, rdv))[which]
        return rcopy(src.at[pl.ds(0, L), :], dst, kvsem.at[which, 0], kvsem.at[which, 1], {"ctx": 0})

    @pl.when(ctx > 0)
    def _():
        kv_copy(0).start()
        kv_copy(1).start()
        for which, ref in enumerate((dk_s, dv_s)):
            gqkv[1 + which] = ref[pl.ds(L, L), :].astype(BF)

    def settle_sends(m, _):
        @pl.when(ln.is_end)
        def _():
            rcopy(sE.at[m], rE.at[m], ss.at[0, m], rs.at[0, m], ln.mid).wait_send()

        @pl.when(ln.is_mid)
        def _():
            rcopy(sI.at[m], rI.at[m], ss.at[1, m], rs.at[1, m], ln.other).wait_send()
            rcopy(sO.at[m], rI.at[m], ss.at[2, m], rs.at[1, m], ln.end).wait_send()

        return 0

    lax.fori_loop(0, NM, settle_sends, 0)

    @pl.when(ctx == 0)
    def _():
        for which, (ref, came) in enumerate(((dk_s, rdk), (dv_s, rdv))):
            kv_copy(which).wait_recv()
            gqkv[1 + which] = (ref[pl.ds(0, L), :] + came[...]).astype(BF)

    b4, b5, b6 = TAIL_LAGS
    sX = sI

    def tail(i, _):
        @pl.when(i < NC)
        def _():
            for s in range(SUBS):
                m = i * SUBS + s
                rows = pl.ds(pl.multiple_of(i * R + s * RS, RS), RS)
                p4 = dot_nt(gqkv[0, rows, :], wqkv[0])
                p4 = p4 + dot_nt(gqkv[1, rows, :], wqkv[1])
                p4 = p4 + dot_nt(gqkv[2, rows, :], wqkv[2])

                @pl.when(ln.is_end)
                def _(m=m, p4=p4):
                    sE[m] = p4.astype(BF)
                    rcopy(sE.at[m], rE2.at[m], ss.at[3, m], rs.at[3, m], ln.mid).start()

                @pl.when(ln.is_mid)
                def _(m=m, p4=p4):
                    part[m] = p4

        j4 = i - b4

        @pl.when(ln.is_mid & (j4 >= 0) & (j4 < NC))
        def _():
            def cross(m):
                got(rE2, 3, m)
                sX[m, pl.ds(0, half), :] = (rE2[m, ot_rows, :].astype(F32) + part[m, ot_rows, :]).astype(BF)
                rcopy(sX.at[m, pl.ds(0, half), :], rX.at[m], ss.at[4, m], rs.at[4, m], ln.other).start()

            each(j4, cross)

        j5 = i - b5

        @pl.when(ln.is_mid & (j5 >= 0) & (j5 < NC))
        def _():
            def settle(m):
                got(rX, 4, m)
                rows = pl.ds(pl.multiple_of(m * RS + ln.side * half, half), half)
                gn1 = part[m, my_rows, :] + rE2[m, my_rows, :].astype(F32) + rX[m].astype(F32)
                gin, gain_rows = rms_back(x_ref[rows, :].astype(F32), again, gn1)
                acc_a[...] += fold8(gain_rows)
                gin_ref[m, my_rows, :] = (g_s[rows, :] + gin).astype(BF)
                mine = gin_ref.at[m, my_rows, :]
                rcopy(mine, mine, ss.at[5, m], rs.at[5, m], ln.other).start()
                rcopy(mine, mine, ss.at[6, m], rs.at[6, m], ln.end).start()

            each(j5, settle)

        j6 = i - b6

        @pl.when(ln.is_mid & (j6 >= 0) & (j6 < NC))
        def _():
            def relay(m):
                got_half(ot_rows, 5, m)
                theirs = gin_ref.at[m, ot_rows, :]
                rcopy(theirs, theirs, ss.at[7, m], rs.at[7, m], ln.end).start()

            each(j6, relay)

        @pl.when(i == 0)
        def _():
            share_second(0)
            share_first(3)

        @pl.when(i == 1)
        def _():
            share_first(1)

        @pl.when(i == 2)
        def _():
            share_second(3)
            share_first(2)

        @pl.when(i == 3)
        def _():
            share_second(1)
            share_second(2)

        @pl.when(i == NC)
        def _():
            for w in range(4):
                routed_total(w)

        @pl.when(i == NC + 1)
        def _():
            dense_total(0)

        return 0

    lax.fori_loop(0, NC + b6, tail, 0)

    vec[...] = small_ref[...]
    vec[0:1, :] = vec[0:1, :] + jnp.sum(acc_a[...], axis=0, keepdims=True)
    vec[1:2, :] = vec[1:2, :] + jnp.sum(acc_m[...], axis=0, keepdims=True) * (1.0 / NT)
    places = []
    for j in range(NDP):
        for k in range(NCTX):
            if j or k:
                places.append((lax.rem(dp + j, NDP), lax.rem(ctx + k, NCTX)))

    def cols_of(g):
        return pl.ds(pl.multiple_of(g * W, W), W)

    def vec_copy(n):
        d2, c2 = places[n]
        return rcopy(vec.at[:, cols_of(d2 * NCTX + c2)], vbuf.at[me], ts.at[n], tr.at[n], {"dp": d2, "ctx": c2})

    for n in range(G - 1):
        vec_copy(n).start()
    vbuf[me] = vec[:, cols_of(me)]
    dense_total(3)
    for n in range(G - 1):
        vec_copy(n).wait()
    rows_sum = vbuf[0]
    for j in range(1, G):
        rows_sum = rows_sum + vbuf[j]
    hbuf[ln.t] = rows_sum

    def line_copy(n):
        return rcopy(hbuf.at[ln.t], hbuf.at[ln.t], ts.at[G - 1 + n], tr.at[G - 1 + n], tpeers[n])

    for n in range(NT - 1):
        line_copy(n).start()
    dense_total(1)
    dense_total(2)
    for j, p in enumerate(rpeers):
        rcopy(lbuf.at[me], lbuf.at[me], cs.at[j], cr.at[j], p).wait()
    loss = lbuf[0]
    for j in range(1, G):
        loss = loss + lbuf[j]
    loss_ref[...] = loss / (cnt_ref[...] * D)
    for n in range(NT - 1):
        line_copy(n).wait()
    line_sum = hbuf[0]
    for j in range(1, NT):
        line_sum = line_sum + hbuf[j]
    small_o[...] = line_sum

    for w in range(4):
        pair_copy(w).wait_send()

    @pl.when(ctx > 0)
    def _():
        kv_copy(0).wait_send()
        kv_copy(1).wait_send()

    def drain(m, _):
        @pl.when(ln.is_end)
        def _():
            got_half(my_rows, 6, m)
            got_half(ot_rows, 7, m)
            rcopy(sE.at[m], rE2.at[m], ss.at[3, m], rs.at[3, m], ln.mid).wait_send()

        @pl.when(ln.is_mid)
        def _():
            rcopy(sX.at[m, pl.ds(0, half), :], rX.at[m], ss.at[4, m], rs.at[4, m], ln.other).wait_send()
            mine = gin_ref.at[m, my_rows, :]
            theirs = gin_ref.at[m, ot_rows, :]
            rcopy(mine, mine, ss.at[5, m], rs.at[5, m], ln.other).wait_send()
            rcopy(mine, mine, ss.at[6, m], rs.at[6, m], ln.end).wait_send()
            rcopy(theirs, theirs, ss.at[7, m], rs.at[7, m], ln.end).wait_send()

        return 0

    lax.fori_loop(0, NM, drain, 0)


def dense_backward(x, x2, teacher, valid, cnt, sent, gchosen, ridx, small, again, mgain, seg, saved, w_qkv, w_out, w_up, w_down, routed):
    L, D = x.shape
    S = seg.shape[1]
    NT, NDP, NCTX = lax.axis_size("tensor"), lax.axis_size("dp"), lax.axis_size("ctx")
    R = min(BCHUNK, L)
    NC = L // R
    RS = R // SUB
    NM = NC * SUB
    Hd = w_out.shape[1]
    Fl = w_up.shape[2]
    G = NDP * NCTX
    W = D // G
    sizes = (NC, SUB, R, D, L, S, NT, NDP, NCTX, float(S * NDP))
    dma = pltpu.SemaphoreType.DMA
    sd = jax.ShapeDtypeStruct
    v_ = pl.BlockSpec(memory_space=VM)
    a_ = pl.BlockSpec(memory_space=ANY)

    def four(shape):
        return [VM((NDP,) + shape, BF)] * 3 + [VM((NDP - 1,) + shape, BF)]

    wshape = ((W, Fl), (W, Fl), (W, Hd), (W, 3 * Hd))
    dense_shares = sum((four(s) for s in wshape), [])
    routed_scratch = [VM(s, BF) for s in wshape] + [VM((NDP - 1,) + s, BF) for s in wshape]
    big = VM((NM, RS, D), BF)
    return pl.pallas_call(
        functools.partial(dense_backward_kernel, sizes),
        name="dense_backward",
        out_shape=(
            sd((L, D), BF), sd((8, 128), F32), sd((NM, RS, D), BF),
            sd((2, Fl, W), F32), sd((2, W, Fl), F32), sd((2, Hd, W), F32), sd((2, 3, W, Hd), F32), sd((8, W), F32),
        ),
        in_specs=[v_] * 12 + [a_] * 15,
        out_specs=(v_,) * 8,
        scratch_shapes=[
            VM((L, Hd), BF), VM((S, Hd), BF), VM((S, Hd), BF), VM((L, Hd), BF), VM((L, 128), F32), VM((L, D), F32), VM((L, Fl), F32),
            VM((3, D, Hd), BF), VM((Hd, D), BF), VM((D, Fl), BF), VM((Fl, D), BF),
            VM((L, D), F32), VM((L, D), BF), VM((L, Fl), BF), VM((L, Fl), BF), VM((L, D), BF), VM((L, D), BF), VM((L, D), BF),
            VM((NM, RS, D), F32), VM((3, L, Hd), BF), VM((S, Hd), F32), VM((S, Hd), F32), VM((L, Hd), F32), VM((L, Hd), F32),
            big, big, big, big, big, big, VM((NM, RS // 2, D), BF),
        ] + dense_shares + routed_scratch + [
            VM((8, D), F32), VM((8, D), F32), VM((8, D), F32), VM((G, 8, 128), F32),
            VM((8, D), F32), VM((G, 8, W), F32), VM((NT, 8, W), F32),
            dma((11,)), dma((4,)), dma((2, 2)), dma((4,)), dma((4,)), dma((4, NDP)), dma((4, NDP)), dma((4, NDP)), dma((4, NDP)),
            dma((G,)), dma((G,)), dma((G + NT,)), dma((G + NT,)), dma((8, NM)), dma((8, NM)),
        ],
        compiler_params=pltpu.CompilerParams(collective_id=3, has_side_effects=True, vmem_limit_bytes=62 << 20),
    )(
        x, x2, teacher, valid, cnt, sent, gchosen, ridx, small, again, mgain, seg, *saved, w_qkv, w_out, w_up, w_down, *routed,
    )


def routed_kernel(
    sizes,
    x2_ref, teach_ref, valid_ref, cnt_ref, idxr_ref, segr_ref, again_ref, mgain_ref, router_ref,
    wqkv_h, wout_h, wup_h, wdn_h,
    sent_ref, gch_ref, small_ref, dn_o, up_o, out_o, qkv_o,
    wqkv, wout, wup, wdn, xs, xc, tsel, tc, vsel, vc, n1_s, k_s, v_s, part, mix_s, n2_s, act_s, gpre_s, gm_s, ga_s, gqkv, dkv, dkvc,
    posc, segq, sbuf, rbuf, tdn, udn, tup, uup, tout, uout, tqkv, uqkv,
    wsem, xsem, xrem, dsem, drem, s1, r1, ps, pr_, gs, gr,
):
    L, D, S, RT, NT, NDP, NCTX, scale_total = sizes
    RL = RT // NCTX
    Q = RL // NT
    G = NDP * NCTX
    W = D // G
    t = lax.axis_index("tensor")
    ctx = lax.axis_index("ctx")
    across = {"ctx": 1 - ctx}
    loads = [
        pltpu.make_async_copy(wqkv_h.at[1], wqkv, wsem.at[0]),
        pltpu.make_async_copy(wout_h.at[1], wout, wsem.at[1]),
        pltpu.make_async_copy(wup_h.at[1], wup, wsem.at[2]),
        pltpu.make_async_copy(wdn_h.at[1], wdn, wsem.at[3]),
    ]
    for ld in loads:
        ld.start()
    greet(tensor_peers(NT) + [across])
    my = pl.ds(pl.multiple_of(ctx * RL, RL), RL)
    theirs = pl.ds(pl.multiple_of((1 - ctx) * RL, RL), RL)
    own = pl.ds(pl.multiple_of(t * Q, Q), Q)

    idxc = column(idxr_ref[...], 0, RT)
    held = idxc - ctx * L == lax.broadcasted_iota(jnp.int32, (RT, L), 1)
    pick = held.astype(F32).astype(BF)
    xs[...] = dot_nn(pick, x2_ref[...]).astype(BF)
    first = [rcopy(xs, xc, xsem.at[0], xrem.at[0], across)]
    first[0].start()
    tsel[...] = dot_nn(pick, teach_ref[...]).astype(BF)
    vsel[...] = jnp.broadcast_to(jnp.sum(jnp.where(held, valid_ref[...].astype(F32), 0.0), axis=-1, keepdims=True), (RT, 128))
    first.append(rcopy(tsel.at[theirs, :], tc, xsem.at[1], xrem.at[1], across))
    first.append(rcopy(vsel.at[theirs, :], vc, xsem.at[2], xrem.at[2], across))
    first[1].start()
    first[2].start()

    at = idxc == lax.broadcasted_iota(jnp.int32, (RT, S), 1)
    posc[...] = jnp.broadcast_to(idxc, (RT, 128))
    seg_col = jnp.sum(jnp.where(at, segr_ref[...], 0), axis=-1, keepdims=True)
    segq[...] = jnp.broadcast_to(seg_col, (RT, 128))
    same = lax.broadcasted_iota(jnp.int32, (RT, RT), 0) == lax.broadcasted_iota(jnp.int32, (RT, RT), 1)
    seg_row = jnp.sum(jnp.where(same, seg_col, 0), axis=0, keepdims=True)
    visible = (idxr_ref[...] <= posc[my, 0:1]) & (seg_row == segq[my, 0:1])
    bias = jnp.where(visible, 0.0, masked_value)
    again = again_ref[1:2, :]
    mgain = mgain_ref[1:2, :]
    router = router_ref[...]
    Hd = wout.shape[0]
    groups = Hd // 128

    for ld in loads:
        ld.wait()
    first[0].wait_recv()
    chosen = xs[...].astype(F32) + xc[...].astype(F32)
    xs_all = chosen.astype(BF)
    n1 = (rms_parts(chosen)[1] * again).astype(BF)
    n1_s[...] = n1
    first[0].wait_send()
    xs[...] = xs_all
    k_s[...] = dot_nn(n1, wqkv[1]).astype(BF)
    v_s[...] = dot_nn(n1, wqkv[2]).astype(BF)
    n1m = n1_s[my, :]
    q = (dot_nn(n1m, wqkv[0]).astype(BF) * jnp.asarray(0.125, BF))
    probs = []
    for g in range(groups):
        cols = slice(128 * g, 128 * g + 128)
        q2 = head_pair(q[:, cols])
        s = dot_nt(q2, k_s[:, cols]).reshape(2, RL, RT) + bias[None]
        p = jnp.exp(s - jnp.max(s, axis=-1, keepdims=True))
        p = (p * (1.0 / jnp.sum(p, axis=-1, keepdims=True))).reshape(2 * RL, RT)
        probs.append((q2, p))
        mix_s[:, cols] = pair_join(dot_nn(p.astype(BF), v_s[:, cols])).astype(BF)

    def piece_copy(step, j):
        to = lax.rem(t + j, NT)
        rows = pl.ds(pl.multiple_of(to * Q, Q), Q)
        return rcopy(sbuf.at[step, rows, :], rbuf.at[step, j - 1], ps.at[step, j - 1], pr_.at[step, j - 1], {"tensor": to})

    def spread(step, value):
        part[...] = value
        sbuf[step] = value.astype(BF)
        for j in range(1, NT):
            piece_copy(step, j).start()

    def collect(step):
        total = part[own, :]
        for j in range(1, NT):
            piece_copy(step, j).wait_recv()
            total = total + rbuf[step, j - 1].astype(F32)
        return total

    def gather_copy(step, ref, base_row, j):
        to = lax.rem(t + j, NT)
        rows = pl.ds(pl.multiple_of(base_row + t * Q, Q), Q)
        return rcopy(ref.at[rows, :], ref.at[rows, :], gs.at[step, j - 1], gr.at[step, j - 1], {"tensor": to})

    def gather(step, ref, base_row):
        for j in range(1, NT):
            gather_copy(step, ref, base_row, j).start()

    def gathered(step, ref, base_row):
        for j in range(1, NT):
            gather_copy(step, ref, base_row, j).wait()

    mine16 = pl.ds(pl.multiple_of(ctx * RL + t * Q, Q), Q)
    spread(0, dot_nn(mix_s[...], wout[...]))
    chosen_o = xs[mine16, :].astype(F32)
    gate_o = jax.nn.sigmoid(jnp.sum(chosen_o * router, axis=-1, keepdims=True))
    chosen_m = xs[my, :].astype(F32)
    gate_m = jax.nn.sigmoid(jnp.sum(chosen_m * router, axis=-1, keepdims=True))
    attn_o = collect(0)
    mid_o = chosen_o + attn_o
    n2_s[own, :] = (rms_parts(mid_o)[1] * mgain).astype(BF)
    gather(0, n2_s, 0)
    gathered(0, n2_s, 0)

    pre = dot_nn(n2_s[...], wup[...])
    th = gelu_pair(pre)
    act_s[...] = (0.5 * pre * (1.0 + th)).astype(BF)
    spread(1, dot_nn(act_s[...], wdn[...]))
    slope = 0.5 * (1.0 + th) + 0.5 * pre * (1.0 - th * th) * (0.7978845608028654 * (1.0 + 3.0 * 0.044715 * pre * pre))
    first[1].wait()
    first[2].wait()
    teach = tsel[my, :].astype(F32) + tc[...].astype(F32)
    counted = vsel[my, 0:1] + vc[:, 0:1]
    scale = scale_total / cnt_ref[0:1, 0:1]
    branch_o = attn_o + collect(1)
    sent_ref[mine16, :] = (gate_o * branch_o).astype(BF)
    gather(1, sent_ref, ctx * RL)
    gathered(1, sent_ref, ctx * RL)

    sent_pair = rcopy(sent_ref.at[my, :], sent_ref.at[my, :], dsem.at[0], drem.at[0], across)
    sent_pair.start()
    gsent = (scale * counted * (chosen_m + sent_ref[my, :].astype(F32) - teach)).astype(BF).astype(F32)
    top = gate_m * gsent
    part[...] = gsent
    gsent_o = part[own, :]
    gm = top.astype(BF)
    gm_s[...] = gm
    gpre = (dot_nt(gm, wdn[...]) * slope).astype(BF)
    gpre_s[...] = gpre
    spread(2, dot_nt(gpre, wup[...]))

    def both_of(d):
        return pl.ds(pl.multiple_of(d * NCTX * W, NCTX * W), NCTX * W)

    def by_share(piece, send, keep):
        def one(d, _):
            for lo, width, val in piece(both_of(d)):
                for c in range(NCTX):
                    rows = val[c * W : (c + 1) * W].astype(BF)

                    @pl.when(ctx == c)
                    def _(rows=rows, lo=lo, width=width):
                        keep[d, :, lo : lo + width] = rows

                    @pl.when(ctx != c)
                    def _(rows=rows, lo=lo, width=width):
                        send[d, :, lo : lo + width] = rows

            return 0

        lax.fori_loop(0, NDP, one, 0)

    def piece_dn(cols):
        return [(0, act_s.shape[1], dot_tn(gm_s[:, cols], act_s[...]))]

    def piece_up(cols):
        return [(0, gpre_s.shape[1], dot_tn(n2_s[:, cols], gpre_s[...]))]

    def piece_out(cols):
        return [(0, Hd, dot_tn(ga_s[:, cols], mix_s[...]))]

    def piece_qkv(cols):
        lhs = n1_s[my, cols]
        return [(Hd * c, Hd, dot_tn(lhs, gqkv[c])) for c in range(3)]

    shares = ((piece_dn, tdn, dn_o, udn), (piece_up, tup, up_o, uup), (piece_out, tout, out_o, uout), (piece_qkv, tqkv, qkv_o, uqkv))

    def pair_copy(w):
        return rcopy(shares[w][1], shares[w][3], s1.at[w], r1.at[w], across)

    def share_first(w):
        by_share(shares[w][0], shares[w][1], shares[w][2])
        pair_copy(w).start()

    ggate_o = jnp.sum(gsent_o * branch_o, axis=-1, keepdims=True) * gate_o * (1.0 - gate_o)
    small_ref[...] = jnp.zeros(small_ref.shape, F32)
    small_ref[4:5, :] = jnp.sum(ggate_o * chosen_o, axis=0, keepdims=True)
    top_o = gate_o * gsent_o
    share_first(0)
    gmid_o, gain_rows = rms_back(mid_o, mgain, collect(2))
    small_ref[3:4, :] = jnp.sum(gain_rows, axis=0, keepdims=True)
    ga_s[own, :] = (top_o + gmid_o).astype(BF)
    gather(2, ga_s, 0)
    share_first(1)
    gathered(2, ga_s, 0)

    gmix = dot_nt(ga_s[...], wout[...]).astype(BF)
    for g in range(groups):
        cols = slice(128 * g, 128 * g + 128)
        q2, p = probs[g]
        g2 = head_pair(gmix[:, cols])
        dp_ = dot_nt(g2, v_s[:, cols])
        ds = (p * (dp_ - jnp.sum(p * dp_, axis=-1, keepdims=True))).astype(BF)
        gqkv[0, :, cols] = (pair_join(dot_nn(ds, k_s[:, cols])) * 0.125).astype(BF)
        dkv[0, :, cols] = dot_tn(ds, q2)
        dkv[1, :, cols] = dot_tn(p.astype(BF), g2)
    kv_pair = [rcopy(dkv.at[c, theirs, :], dkvc.at[c], dsem.at[1 + c], drem.at[1 + c], across) for c in range(2)]
    for cp in kv_pair:
        cp.start()
    p4 = dot_nt(gqkv[0], wqkv[0])
    for c in range(2):
        kv_pair[c].wait()
        gqkv[1 + c] = (dkv[c, my, :] + dkvc[c]).astype(BF)
        p4 = p4 + dot_nt(gqkv[1 + c], wqkv[1 + c])
    spread(3, p4)
    share_first(2)
    gin_o, gain_rows = rms_back(chosen_o, again, collect(3))
    small_ref[2:3, :] = jnp.sum(gain_rows, axis=0, keepdims=True)
    gch_ref[mine16, :] = (gmid_o + gin_o + ggate_o * router).astype(BF)
    gather(3, gch_ref, ctx * RL)
    share_first(3)
    gathered(3, gch_ref, ctx * RL)
    gch_pair = rcopy(gch_ref.at[my, :], gch_ref.at[my, :], dsem.at[3], drem.at[3], across)
    gch_pair.start()

    for w, (_, _, keep, came) in enumerate(shares):
        pair_copy(w).wait()

        def add(j, _, keep=keep, came=came):
            keep[j] = (keep[j].astype(F32) + came[j].astype(F32)).astype(BF)
            return 0

        lax.fori_loop(0, NDP, add, 0)
    for step in range(4):
        for j in range(1, NT):
            piece_copy(step, j).wait_send()
    sent_pair.wait()
    gch_pair.wait()


def routed_block(x2, teacher, valid, cnt, ridx, seg, again, mgain, w_router, w_qkv, w_out, w_up, w_down):
    L, D = teacher.shape
    S = seg.shape[1]
    RT = ridx.shape[1]
    NT, NDP, NCTX = lax.axis_size("tensor"), lax.axis_size("dp"), lax.axis_size("ctx")
    Hd = w_out.shape[1]
    Fl = w_up.shape[2]
    RL = RT // NCTX
    Q = RL // NT
    G = NDP * NCTX
    W = D // G
    sizes = (L, D, S, RT, NT, NDP, NCTX, float(S * NDP))
    dma = pltpu.SemaphoreType.DMA
    sd = jax.ShapeDtypeStruct
    v_ = pl.BlockSpec(memory_space=VM)
    a_ = pl.BlockSpec(memory_space=ANY)
    wshape = ((W, Fl), (W, Fl), (W, Hd), (W, 3 * Hd))
    return pl.pallas_call(
        functools.partial(routed_kernel, sizes),
        name="routed_block",
        out_shape=(
            sd((RT, D), BF), sd((RT, D), BF), sd((8, D), F32),
            *[sd((NDP,) + s, BF) for s in wshape],
        ),
        in_specs=[v_] * 9 + [a_] * 4,
        out_specs=(v_,) * 7,
        scratch_shapes=[
            VM((3, D, Hd), BF), VM((Hd, D), BF), VM((D, Fl), BF), VM((Fl, D), BF),
            VM((RT, D), BF), VM((RT, D), BF), VM((RT, D), BF), VM((RL, D), BF), VM((RT, 128), F32), VM((RL, 128), F32),
            VM((RT, D), BF), VM((RT, Hd), BF), VM((RT, Hd), BF), VM((RL, D), F32), VM((RL, Hd), BF), VM((RL, D), BF),
            VM((RL, Fl), BF), VM((RL, Fl), BF), VM((RL, D), BF), VM((RL, D), BF), VM((3, RL, Hd), BF),
            VM((2, RT, Hd), F32), VM((2, RL, Hd), F32),
            VM((RT, 128), jnp.int32), VM((RT, 128), jnp.int32),
            VM((4, RL, D), BF), VM((4, NT - 1, Q, D), BF),
            *sum(([VM((NDP,) + s, BF)] * 2 for s in wshape), []),
            dma((4,)), dma((3,)), dma((3,)), dma((4,)), dma((4,)), dma((4,)), dma((4,)),
            dma((4, NT)), dma((4, NT)), dma((4, NT)), dma((4, NT)),
        ],
        compiler_params=pltpu.CompilerParams(collective_id=2, has_side_effects=True, vmem_limit_bytes=60 << 20),
    )(
        x2.reshape(L, D), teacher, valid, cnt, ridx, seg, again, mgain, w_router.reshape(1, D), w_qkv, w_out, w_up, w_down,
    )


def finish_kernel(hid_h, gin_ref, dn_h, up_h, out_h, qkv_h, small_ref, loss_ref, hid_o, loss_o, gin_o, ag_o, qkv_o, out_o, mg_o, up_o, dn_o, router_o, sem):
    moves = ((hid_h, hid_o), (dn_h, dn_o), (up_h, up_o), (out_h, out_o), (qkv_h, qkv_o))
    copies = [pltpu.make_async_copy(a, b, sem.at[n]) for n, (a, b) in enumerate(moves)]
    for cp in copies:
        cp.start()
    gin_o[...] = gin_ref[...].astype(F32)
    loss_o[...] = loss_ref[0:1, 0:1]
    for j in range(2):
        ag_o[j : j + 1, :] = small_ref[2 * j : 2 * j + 1, :]
        mg_o[j : j + 1, :] = small_ref[2 * j + 1 : 2 * j + 2, :]
    router_o[...] = small_ref[4:5, :]
    for cp in copies:
        cp.wait()


def finish(hid, gin, dn, up, out, qkv, small, loss):
    sd = jax.ShapeDtypeStruct
    v_ = pl.BlockSpec(memory_space=VM)
    a_ = pl.BlockSpec(memory_space=ANY)
    W = small.shape[1]

    def like(arr):
        return sd(arr.shape, arr.dtype)

    return pl.pallas_call(
        finish_kernel,
        name="finish",
        out_shape=(like(hid), sd((1, 1), F32), sd(gin.shape, F32), sd((2, W), F32), like(qkv), like(out), sd((2, W), F32), like(up), like(dn), sd((1, W), F32)),
        in_specs=[a_, v_, a_, a_, a_, a_, v_, v_],
        out_specs=(a_, v_, v_, v_, a_, a_, v_, a_, a_, v_),
        scratch_shapes=[pltpu.SemaphoreType.DMA((5,))],
        compiler_params=pltpu.CompilerParams(vmem_limit_bytes=40 << 20),
    )(hid, gin, dn, up, out, qkv, small, loss)


def fast_local(hidden_in, teacher, seg_ids, valid, routed_idx, attn_gain, w_qkv, w_out, mlp_gain, w_up, w_down, w_router):
    L, D = hidden_in.shape[1:]
    x2, *saved, cnt = dense_forward(hidden_in[0], attn_gain, mlp_gain, seg_ids, valid, w_qkv, w_out, w_up, w_down)
    sent, gch, small, *routed = routed_block(
        x2, teacher[0], valid, cnt, routed_idx, seg_ids, attn_gain, mlp_gain, w_router, w_qkv, w_out, w_up, w_down
    )
    hid, loss, gin, dn, up, out, qkv, small = dense_backward(
        hidden_in[0], x2, teacher[0], valid, cnt, sent, gch, routed_idx, small, attn_gain, mlp_gain, seg_ids, saved,
        w_qkv, w_out, w_up, w_down, routed,
    )
    hid, loss, gin, ag, qkv, out, mg, up, dn, router = finish(hid, gin, dn, up, out, qkv, small, loss)
    return (hid[None], loss[0, 0], gin.reshape(1, L, D), ag, qkv, out, mg, up, dn, router[0])


def takes_kernels(mesh):
    shape = dict(mesh.shape)
    return shape["tensor"] == 4 and shape["ctx"] == 2


def solution(mesh):
    placed = (
        P("dp", "ctx", None),
        P("dp", "ctx", None),
        P("dp", None),
        P("dp", "ctx"),
        P("dp", None),
        P(),
        P(None, None, None, "tensor"),
        P(None, "tensor", None),
        P(),
        P(None, None, "tensor"),
        P(None, "tensor", None),
        P(),
    )
    return jax.shard_map(
        fast_local if takes_kernels(mesh) else plain_local,
        mesh=mesh,
        in_specs=placed,
        out_specs=(
            P("dp", "ctx", None),
            P(),
            P("dp", "ctx", None),
            P(None, ("dp", "ctx")),
            P(None, None, ("dp", "ctx"), "tensor"),
            P(None, "tensor", ("dp", "ctx")),
            P(None, ("dp", "ctx")),
            P(None, ("dp", "ctx"), "tensor"),
            P(None, "tensor", ("dp", "ctx")),
            P(("dp", "ctx")),
        ),
        check_vma=False,
    )
```

```python
import functools

import jax
import jax.numpy as jnp
from jax import lax
from jax.experimental import pallas as pl
from jax.experimental.pallas import tpu as pltpu
from jax.sharding import PartitionSpec as P

HEAD = 64
epsilon = 1e-06
masked_value = -1e30
MESH = pl.DeviceIdType.MESH
BF = jnp.bfloat16
F32 = jnp.float32
VM = pltpu.VMEM
ANY = pl.ANY


def rcopy(src, dst, send, recv, where):
    return pltpu.make_async_remote_copy(
        src_ref=src, dst_ref=dst, send_sem=send, recv_sem=recv, device_id=where, device_id_type=MESH
    )


def dot_nn(a, b):
    return lax.dot_general(a, b, (((1,), (0,)), ((), ())), preferred_element_type=F32)


def dot_nt(a, b):
    return lax.dot_general(a, b, (((1,), (1,)), ((), ())), preferred_element_type=F32)


def dot_tn(a, b):
    return lax.dot_general(a, b, (((0,), (0,)), ((), ())), preferred_element_type=F32)


def rms_parts(values):
    r = lax.rsqrt(jnp.mean(values * values, axis=-1, keepdims=True) + epsilon)
    return r, values * r


def rms_back(values, gain, grad):
    r, unit = rms_parts(values)
    scaled = grad * gain
    return r * (scaled - unit * jnp.mean(scaled * unit, axis=-1, keepdims=True)), grad * unit


def gelu_pair(u):
    c = 0.7978845608028654
    t = jnp.tanh(c * (u + 0.044715 * (u * u * u)))
    return t


def fold8(rows):
    return jnp.sum(rows.reshape(rows.shape[0] // 8, 8, rows.shape[1]), axis=0)


class Line:
    def __init__(self):
        t = lax.axis_index("tensor")
        self.t = t
        self.side = t // 2
        self.is_end = (t == 0) | (t == 3)
        self.is_mid = (t == 1) | (t == 2)
        self.end = {"tensor": self.side * 3}
        self.mid = {"tensor": 1 + self.side}
        self.other = {"tensor": 2 - self.side}


def greet(peers):
    bar = pltpu.get_barrier_semaphore()
    for p in peers:
        pl.semaphore_signal(bar, inc=1, device_id=p, device_id_type=MESH)
    pl.semaphore_wait(bar, len(peers))


def tensor_peers(n):
    t = lax.axis_index("tensor")
    return [{"tensor": lax.rem(t + j, n)} for j in range(1, n)]


def row_peers(n_dp, n_ctx):
    d, c = lax.axis_index("dp"), lax.axis_index("ctx")
    out = []
    for j in range(n_dp):
        for k in range(n_ctx):
            if j or k:
                out.append({"dp": lax.rem(d + j, n_dp), "ctx": lax.rem(c + k, n_ctx)})
    return out


def rms_scale(values, gain):
    return values * lax.rsqrt(jnp.mean(values * values, axis=-1, keepdims=True) + epsilon) * gain


def gelu_tanh(values):
    return jax.nn.gelu(values, approximate=True)


def gating_fn(chosen, router):
    return jax.nn.sigmoid(jnp.sum(chosen * router, axis=-1))


def tensor_sum(partial_sum):
    return lax.psum(partial_sum, "tensor")


def gather_keys(projected):
    return (
        lax.all_gather(projected[1], "ctx", axis=1, tiled=True),
        lax.all_gather(projected[2], "ctx", axis=1, tiled=True),
    )


def scatter_key_grads(grad_k, grad_v):
    stacked = jnp.stack([grad_k, grad_v])
    summed = lax.psum_scatter(stacked, "ctx", scatter_dimension=2, tiled=True)
    return (summed[0], summed[1])


def to_workers(picked):
    return lax.psum_scatter(
        picked.astype(jnp.bfloat16), "ctx", scatter_dimension=1, tiled=True
    ).astype(jnp.float32)


def to_owners(rows_low):
    return lax.all_gather(rows_low, "ctx", axis=1, tiled=True)


def take_rows(table, places):
    return jax.vmap(lambda t, i: t[i])(table, places)


def add_rows(table, places, addend):
    return jax.vmap(lambda t, i, a: t.at[i].add(a))(table, places, addend)


def tile_scores(q_tile, k_tile, qpos_tile, kpos_tile, qseg_tile, kseg_tile, score_scale):
    scores = (
        jnp.einsum("qhe,khe->hqk", q_tile, k_tile, preferred_element_type=jnp.float32) * score_scale
    )
    visible = (kpos_tile[None, :] <= qpos_tile[:, None]) & (
        kseg_tile[None, :] == qseg_tile[:, None]
    )
    return (scores, visible[None])


def tile_layout(queries, key_rows, value_rows, k_pos, k_seg):
    q_len, row_width = queries.shape
    k_len = key_rows.shape[0]
    head_count = row_width // HEAD
    q_step = min(512, q_len)
    k_step = min(2048, k_len)
    k_count = k_len // k_step
    key_tiles = key_rows.reshape(k_count, k_step, head_count, HEAD)
    value_tiles = value_rows.reshape(k_count, k_step, head_count, HEAD)
    kpos_tiles = k_pos.reshape(k_count, k_step)
    kseg_tiles = k_seg.reshape(k_count, k_step)
    return (
        q_len,
        row_width,
        k_len,
        head_count,
        q_step,
        (key_tiles, value_tiles, kpos_tiles, kseg_tiles),
    )


def attend_one(queries, key_rows, value_rows, q_pos, k_pos, q_seg, k_seg):
    q_len, row_width, k_len, head_count, q_step, tiles = tile_layout(
        queries, key_rows, value_rows, k_pos, k_seg
    )
    score_scale = 1.0 / HEAD**0.5

    def per_query(q_args):
        q_tile, qpos_tile, qseg_tile = q_args

        def total_step(carry, k_args):
            running, summed = carry
            k_tile, v_tile, kpos_tile, kseg_tile = k_args
            scores, visible = tile_scores(
                q_tile, k_tile, qpos_tile, kpos_tile, qseg_tile, kseg_tile, score_scale
            )
            raised = jnp.maximum(
                running, jnp.max(jnp.where(visible, scores, masked_value), axis=-1)
            )
            weights = jnp.where(visible, jnp.exp(scores - raised[..., None]), 0.0)
            return ((raised, summed * jnp.exp(running - raised) + jnp.sum(weights, axis=-1)), None)

        initial = (
            jnp.full((head_count, q_step), masked_value, jnp.float32),
            jnp.zeros((head_count, q_step), jnp.float32),
        )
        (running, summed), _ = lax.scan(total_step, initial, tiles)
        log_total = running + jnp.log(summed)

        def value_step(output, k_args):
            k_tile, v_tile, kpos_tile, kseg_tile = k_args
            scores, visible = tile_scores(
                q_tile, k_tile, qpos_tile, kpos_tile, qseg_tile, kseg_tile, score_scale
            )
            weights_low = jnp.where(visible, jnp.exp(scores - log_total[..., None]), 0.0).astype(
                jnp.bfloat16
            )
            return (
                output
                + jnp.einsum(
                    "hqk,khe->qhe", weights_low, v_tile, preferred_element_type=jnp.float32
                ),
                None,
            )

        output, _ = lax.scan(value_step, jnp.zeros((q_step, head_count, HEAD), jnp.float32), tiles)
        return (output, log_total)

    q_count = q_len // q_step
    output, log_total = lax.map(
        per_query,
        (
            queries.reshape(q_count, q_step, head_count, HEAD),
            q_pos.reshape(q_count, q_step),
            q_seg.reshape(q_count, q_step),
        ),
    )
    return (output.reshape(q_len, row_width), log_total)


def attend_back(queries, key_rows, value_rows, grad_mixed, log_total, q_pos, k_pos, q_seg, k_seg):
    q_len, row_width, k_len, head_count, q_step, tiles = tile_layout(
        queries, key_rows, value_rows, k_pos, k_seg
    )
    score_scale = 1.0 / HEAD**0.5

    def per_query(q_args):
        q_tile, g_tile, total_tile, qpos_tile, qseg_tile = q_args

        def tile_probs(k_tile, kpos_tile, kseg_tile):
            scores, visible = tile_scores(
                q_tile, k_tile, qpos_tile, kpos_tile, qseg_tile, kseg_tile, score_scale
            )
            return jnp.where(visible, jnp.exp(scores - total_tile[..., None]), 0.0)

        def inner_step(carry, k_args):
            k_tile, v_tile, kpos_tile, kseg_tile = k_args
            weights = tile_probs(k_tile, kpos_tile, kseg_tile)
            grad_weights = jnp.einsum(
                "qhe,khe->hqk", g_tile, v_tile, preferred_element_type=jnp.float32
            )
            return (carry + jnp.sum(weights * grad_weights, axis=-1), None)

        inner, _ = lax.scan(inner_step, jnp.zeros((head_count, q_step), jnp.float32), tiles)

        def grad_step(carry, k_args):
            k_tile, v_tile, kpos_tile, kseg_tile = k_args
            weights = tile_probs(k_tile, kpos_tile, kseg_tile)
            grad_weights = jnp.einsum(
                "qhe,khe->hqk", g_tile, v_tile, preferred_element_type=jnp.float32
            )
            grad_scores = (weights * (grad_weights - inner[..., None])).astype(jnp.bfloat16)
            carry = carry + jnp.einsum(
                "hqk,khe->qhe", grad_scores, k_tile, preferred_element_type=jnp.float32
            )
            grad_keys = jnp.einsum(
                "hqk,qhe->khe", grad_scores, q_tile, preferred_element_type=jnp.float32
            )
            grad_values = jnp.einsum(
                "hqk,qhe->khe",
                weights.astype(jnp.bfloat16),
                g_tile,
                preferred_element_type=jnp.float32,
            )
            return (carry, (grad_keys, grad_values))

        grad_q, (grad_keys, grad_values) = lax.scan(
            grad_step, jnp.zeros((q_step, head_count, HEAD), jnp.float32), tiles
        )
        return (
            grad_q * score_scale,
            grad_keys.reshape(k_len, row_width) * score_scale,
            grad_values.reshape(k_len, row_width),
        )

    q_count = q_len // q_step
    grad_q, grad_keys, grad_values = lax.map(
        per_query,
        (
            queries.reshape(q_count, q_step, head_count, HEAD),
            grad_mixed.reshape(q_count, q_step, head_count, HEAD),
            log_total,
            q_pos.reshape(q_count, q_step),
            q_seg.reshape(q_count, q_step),
        ),
    )
    return (
        grad_q.reshape(q_len, row_width),
        jnp.sum(grad_keys, axis=0),
        jnp.sum(grad_values, axis=0),
    )


def make_attention(q_pos, k_pos, q_seg, k_seg):

    def attend_fn(projected):
        key_all, value_all = gather_keys(projected)
        mixed_full, log_total = lax.map(
            lambda a: attend_one(*a), (projected[0], key_all, value_all, q_pos, k_pos, q_seg, k_seg)
        )
        return (mixed_full, (key_all, value_all, log_total))

    def attend_grad(projected, kept, grad_mixed):
        key_all, value_all, log_total = kept
        grad_q, grad_k, grad_v = lax.map(
            lambda a: attend_back(*a),
            (projected[0], key_all, value_all, grad_mixed, log_total, q_pos, k_pos, q_seg, k_seg),
        )
        grad_k, grad_v = scatter_key_grads(grad_k, grad_v)
        return jnp.stack(
            [grad_q.astype(jnp.bfloat16), grad_k.astype(jnp.bfloat16), grad_v.astype(jnp.bfloat16)]
        )

    return (attend_fn, attend_grad)


def block_forward(
    resid_in,
    gain_a,
    query_key_value_weight,
    output_weight_matrix,
    gain_m,
    up_weight_matrix,
    down_weight_matrix,
    attend_fn,
):
    attention_norm = rms_scale(resid_in, gain_a).astype(jnp.bfloat16)
    projected = jnp.einsum(
        "oym,qmh->qoyh", attention_norm, query_key_value_weight, preferred_element_type=jnp.float32
    ).astype(jnp.bfloat16)
    mixed_full, kept = attend_fn(projected)
    mixed_state = mixed_full.astype(jnp.bfloat16)
    attention_portion = jnp.einsum(
        "xtu,ua->xta", mixed_state, output_weight_matrix, preferred_element_type=jnp.float32
    )
    attn_out = tensor_sum(attention_portion)
    middle = resid_in + attn_out
    feedforward_norm = rms_scale(middle, gain_m).astype(jnp.bfloat16)
    hidden_preactivation = jnp.einsum(
        "iqp,po->iqo", feedforward_norm, up_weight_matrix, preferred_element_type=jnp.float32
    )
    hidden_activation = gelu_tanh(hidden_preactivation).astype(jnp.bfloat16)
    mlp_part = jnp.einsum(
        "euq,qt->eut", hidden_activation, down_weight_matrix, preferred_element_type=jnp.float32
    )
    mlp_out = tensor_sum(mlp_part)
    saved = (
        resid_in,
        attention_norm,
        projected,
        mixed_state,
        kept,
        middle,
        feedforward_norm,
        hidden_preactivation,
        hidden_activation,
    )
    return (attn_out, mlp_out, saved)


def block_backward(
    saved,
    grad_top,
    gain_a,
    query_key_value_weight,
    output_weight_matrix,
    gain_m,
    up_weight_matrix,
    down_weight_matrix,
    attend_grad,
):
    (
        resid_in,
        attention_norm,
        projected,
        mixed_state,
        kept,
        middle,
        feedforward_norm,
        hidden_preactivation,
        hidden_activation,
    ) = saved
    top_reduced = grad_top.astype(jnp.bfloat16)
    down_weight_gradient = jnp.einsum(
        "pgr,pgw->rw", hidden_activation, top_reduced, preferred_element_type=jnp.float32
    )
    activation_gradient = jnp.einsum(
        "ayx,cx->ayc", top_reduced, down_weight_matrix, preferred_element_type=jnp.float32
    )
    preactivation_gradient = jax.vjp(gelu_tanh, hidden_preactivation)[1](activation_gradient)[
        0
    ].astype(jnp.bfloat16)
    up_weight_gradient = jnp.einsum(
        "uzb,uzv->bv", feedforward_norm, preactivation_gradient, preferred_element_type=jnp.float32
    )
    norm_portion = jnp.einsum(
        "vok,hk->voh", preactivation_gradient, up_weight_matrix, preferred_element_type=jnp.float32
    )
    grad_norm_m = tensor_sum(norm_portion)
    grad_middle, grad_gain_m = jax.vjp(rms_scale, middle, gain_m)[1](grad_norm_m)
    grad_attn = grad_top + grad_middle
    attention_reduced = grad_attn.astype(jnp.bfloat16)
    output_weight_gradient = jnp.einsum(
        "omi,omj->ij", mixed_state, attention_reduced, preferred_element_type=jnp.float32
    )
    grad_mixed = jnp.einsum(
        "bjw,gw->bjg", attention_reduced, output_weight_matrix, preferred_element_type=jnp.float32
    ).astype(jnp.bfloat16)
    projection_gradient = attend_grad(projected, kept, grad_mixed)
    query_key_value_gradient = jnp.einsum(
        "xgt,axgf->atf", attention_norm, projection_gradient, preferred_element_type=jnp.float32
    )
    input_part = jnp.einsum(
        "gurh,gih->uri",
        projection_gradient,
        query_key_value_weight,
        preferred_element_type=jnp.float32,
    )
    grad_norm_a = tensor_sum(input_part)
    grad_resid, grad_gain_a = jax.vjp(rms_scale, resid_in, gain_a)[1](grad_norm_a)
    return (
        grad_attn,
        grad_middle,
        grad_resid,
        (
            grad_gain_a,
            query_key_value_gradient,
            output_weight_gradient,
            grad_gain_m,
            up_weight_gradient,
            down_weight_gradient,
        ),
    )


def pack_grads(grad_list, dims, groups):
    flats = []
    shapes = []
    for grad_item, which_dim in zip(grad_list, dims):
        moved = jnp.moveaxis(grad_item, which_dim, 0)
        shapes.append(moved.shape)
        flats.append(moved.reshape(groups, -1))
    return (jnp.concatenate(flats, axis=1), shapes)


def unpack_grads(summed, shapes, dims, groups):
    results = []
    offset = 0
    for moved_shape, which_dim in zip(shapes, dims):
        share_shape = (moved_shape[0] // groups,) + tuple(moved_shape[1:])
        width = math_prod(share_shape)
        piece = summed[0, offset : offset + width].reshape(share_shape)
        results.append(jnp.moveaxis(piece, 0, which_dim))
        offset = offset + width
    return tuple(results)


def math_prod(shape):
    total = 1
    for extent in shape:
        total = total * extent
    return total


def spread_grads(grad_list, dims):
    groups = lax.axis_size("dp") * lax.axis_size("ctx")
    packed, shapes = pack_grads(grad_list, dims, groups)
    summed = lax.psum_scatter(packed, ("dp", "ctx"), scatter_dimension=0, tiled=True)
    return unpack_grads(summed, shapes, dims, groups)


def plain_local(
    hidden_in,
    teacher,
    seg_ids,
    valid,
    routed_idx,
    attn_gain,
    w_qkv,
    w_out,
    mlp_gain,
    w_up,
    w_down,
    w_router,
):
    seqs_local, local_len, model_width = hidden_in.shape
    seq_len = seg_ids.shape[1]
    routed = routed_idx.shape[1]
    ctx_count = lax.axis_size("ctx")
    ctx_place = lax.axis_index("ctx")
    routed_local = routed // ctx_count
    dense_qpos = jnp.broadcast_to(
        ctx_place * local_len + jnp.arange(local_len, dtype=jnp.int32), (seqs_local, local_len)
    )
    dense_kpos = jnp.broadcast_to(jnp.arange(seq_len, dtype=jnp.int32), (seqs_local, seq_len))
    dense_qseg = lax.dynamic_slice_in_dim(seg_ids, ctx_place * local_len, local_len, 1)
    routed_seg = take_rows(seg_ids, routed_idx)
    routed_qpos = lax.dynamic_slice_in_dim(routed_idx, ctx_place * routed_local, routed_local, 1)
    routed_qseg = lax.dynamic_slice_in_dim(routed_seg, ctx_place * routed_local, routed_local, 1)
    owner_mine = routed_idx // local_len == ctx_place
    owner_row = routed_idx % local_len
    dense_attend, dense_grad = make_attention(dense_qpos, dense_kpos, dense_qseg, seg_ids)
    routed_attend, routed_grad = make_attention(routed_qpos, routed_idx, routed_qseg, routed_seg)
    x_input = hidden_in.astype(jnp.float32)
    attn_d, mlp_d, saved_d = block_forward(
        x_input, attn_gain[0], w_qkv[0], w_out[0], mlp_gain[0], w_up[0], w_down[0], dense_attend
    )
    layer_mid = saved_d[5] + mlp_d
    picked = (
        jnp.where(owner_mine[..., None], take_rows(layer_mid, owner_row), 0.0)
        .astype(jnp.bfloat16)
        .astype(jnp.float32)
    )
    chosen = to_workers(picked).astype(jnp.bfloat16).astype(jnp.float32)
    gating = gating_fn(chosen, w_router)
    attn_r, mlp_r, saved_r = block_forward(
        chosen, attn_gain[1], w_qkv[1], w_out[1], mlp_gain[1], w_up[1], w_down[1], routed_attend
    )
    branch_sum = attn_r + mlp_r
    sent_rows = (gating[..., None] * branch_sum).astype(jnp.bfloat16)
    returned = to_owners(sent_rows).astype(jnp.float32)
    layer_out = add_rows(layer_mid, owner_row, jnp.where(owner_mine[..., None], returned, 0.0))
    valid_rows = valid.astype(jnp.float32)
    error_rows = layer_out - teacher.astype(jnp.float32)
    error_sum, valid_count = lax.psum(
        (jnp.sum(valid_rows[..., None] * error_rows * error_rows), jnp.sum(valid_rows)),
        ("dp", "ctx"),
    )
    loss_value = error_sum / (valid_count * model_width)
    token_total = float(seqs_local * seq_len * lax.axis_size("dp"))
    grad_final = token_total / valid_count * valid_rows[..., None] * error_rows
    picked_grad = (
        jnp.where(owner_mine[..., None], take_rows(grad_final, owner_row), 0.0)
        .astype(jnp.bfloat16)
        .astype(jnp.float32)
    )
    branch_grad = to_workers(picked_grad).astype(jnp.bfloat16).astype(jnp.float32)
    grad_top = gating[..., None] * branch_grad
    gating_share, gating_back = jax.vjp(gating_fn, chosen, w_router)
    grad_gating = jnp.sum(branch_grad * branch_sum, axis=-1)
    grad_chosen_gate, grad_router = gating_back(grad_gating)
    grad_attn_r, grad_middle_r, grad_resid_r, grads_r = block_backward(
        saved_r,
        grad_top,
        attn_gain[1],
        w_qkv[1],
        w_out[1],
        mlp_gain[1],
        w_up[1],
        w_down[1],
        routed_grad,
    )
    grad_chosen = (grad_middle_r + grad_resid_r + grad_chosen_gate).astype(jnp.bfloat16)
    grads_r = grads_r + (grad_router,)
    spread_r = spread_grads(grads_r, (0, 1, 1, 0, 0, 1, 0))
    grad_rows = to_owners(grad_chosen).astype(jnp.float32)
    grad_mid = add_rows(grad_final, owner_row, jnp.where(owner_mine[..., None], grad_rows, 0.0))
    grad_attn_d, grad_middle_d, grad_resid_d, grads_d = block_backward(
        saved_d,
        grad_mid,
        attn_gain[0],
        w_qkv[0],
        w_out[0],
        mlp_gain[0],
        w_up[0],
        w_down[0],
        dense_grad,
    )
    grad_input = grad_attn_d + grad_resid_d
    spread_d = spread_grads(grads_d, (0, 1, 1, 0, 0, 1))
    return (
        layer_out.astype(jnp.bfloat16),
        loss_value,
        grad_input,
        jnp.stack([spread_d[0], spread_r[0]]),
        jnp.stack([spread_d[1], spread_r[1]]),
        jnp.stack([spread_d[2], spread_r[2]]),
        jnp.stack([spread_d[3], spread_r[3]]),
        jnp.stack([spread_d[4], spread_r[4]]),
        jnp.stack([spread_d[5], spread_r[5]]),
        spread_r[6],
    )


def column(row, start, length):
    wanted = start + lax.broadcasted_iota(jnp.int32, (length, 1), 0)
    hit = lax.broadcasted_iota(jnp.int32, (length, row.shape[1]), 1) == wanted
    return jnp.sum(jnp.where(hit, row, jnp.zeros_like(row)), axis=-1, keepdims=True)


def head_pair(rows):
    lane = lax.broadcasted_iota(jnp.int32, rows.shape, 1)
    zero = jnp.zeros_like(rows)
    return jnp.concatenate([jnp.where(lane < HEAD, rows, zero), jnp.where(lane >= HEAD, rows, zero)], axis=0)


def pair_join(stacked):
    half = stacked.shape[0] // 2
    lane = lax.broadcasted_iota(jnp.int32, (half, stacked.shape[1]), 1)
    return jnp.where(lane < HEAD, stacked[:half], stacked[half:])


FWD_LAGS = (1, 2, 3, 4, 5, 6)
CHUNK = 128
SUB = 2


def dense_forward_kernel(
    sizes,
    x_ref, again_ref, mgain_ref, seg_ref, valid_ref, wqkv_h, wout_h, wup_h, wdn_h,
    x2_ref, q_h, k_h, v_h, mix_h, lse_h, mid_h, pre_h, cnt_out,
    q_ref, k_ref, v_ref, mix_ref, lse_ref, mid_ref, pre_ref,
    wqkv, wout, wup, wdn, part, part2,
    sE, rE, sI, rI, sO, sE2, rE2, sX, rX, cbuf,
    wsem, osem, kvs, kvr, cs, cr, ss, rs,
):
    NC, SUBS, R, D, L, S, NT, NDP, NCTX = sizes
    RS = R // SUBS
    NM = NC * SUBS
    ln = Line()
    ctx = lax.axis_index("ctx")
    half = RS // 2
    loads = [
        pltpu.make_async_copy(wqkv_h.at[0], wqkv, wsem.at[0]),
        pltpu.make_async_copy(wout_h.at[0], wout, wsem.at[1]),
        pltpu.make_async_copy(wup_h.at[0], wup, wsem.at[2]),
        pltpu.make_async_copy(wdn_h.at[0], wdn, wsem.at[3]),
    ]
    for ld in loads:
        ld.start()
    tpeers = tensor_peers(NT)
    rpeers = row_peers(NDP, NCTX)
    greet(tpeers + rpeers)

    cbuf[0] = jnp.full((8, 128), jnp.sum(valid_ref[...].astype(F32)))
    counts = [rcopy(cbuf.at[0], cbuf.at[j + 1], cs.at[j], cr.at[j], p) for j, p in enumerate(rpeers)]
    for cp in counts:
        cp.start()

    @pl.when(ln.is_end)
    def _():
        def zero(k, _):
            rE[k] = jnp.zeros((RS, D), BF)
            return 0

        lax.fori_loop(0, NM, zero, 0)

    loads[0].wait()
    RB = 128
    again = again_ref[0:1, :]

    def project(i, _):
        rows = pl.ds(pl.multiple_of(i * RB, RB), RB)
        xv = x_ref[rows, :].astype(F32)
        n1 = (rms_parts(xv)[1] * again).astype(BF)
        for c, ref in enumerate((q_ref, k_ref, v_ref)):
            y = dot_nn(n1, wqkv[c]).astype(BF)
            if c == 0:
                ref[rows, :] = y * jnp.asarray(0.125, BF)
            else:
                ref[pl.ds(pl.multiple_of(ctx * L + i * RB, RB), RB), :] = y
        return 0

    lax.fori_loop(0, L // RB, project, 0)

    own = pl.ds(pl.multiple_of(ctx * L, L), L)

    def kv_copy(ref, which, c_to):
        return rcopy(ref.at[own, :], ref.at[own, :], kvs.at[which, c_to], kvr.at[which, ctx], {"ctx": c_to})

    for c_to in range(1, NCTX):
        @pl.when(c_to > ctx)
        def _(c_to=c_to):
            kv_copy(k_ref, 0, c_to).start()
            kv_copy(v_ref, 1, c_to).start()

    for c_later in range(1, NCTX):
        @pl.when(c_later > ctx)
        def _(c_later=c_later):
            k_ref[pl.ds(c_later * L, L), :] = jnp.zeros((L, k_ref.shape[1]), BF)
            v_ref[pl.ds(c_later * L, L), :] = jnp.zeros((L, k_ref.shape[1]), BF)

    loads[1].wait()
    loads[2].wait()
    loads[3].wait()
    for c_from in range(NCTX - 1):
        @pl.when(c_from < ctx)
        def _(c_from=c_from):
            theirs = pl.ds(c_from * L, L)
            for which, ref in enumerate((k_ref, v_ref)):
                rcopy(ref.at[theirs, :], ref.at[theirs, :], kvs.at[which, c_from], kvr.at[which, c_from], {"ctx": c_from}).wait_recv()

    whole = [pltpu.make_async_copy(a, b, osem.at[n, 0]) for n, (a, b) in enumerate(((q_ref, q_h), (k_ref, k_h), (v_ref, v_h)))]
    for cp in whole:
        cp.start()
    mgain = mgain_ref[0:1, :]
    groups = q_ref.shape[1] // 128

    def keep_copy(n, src, dst, i):
        rows = pl.ds(pl.multiple_of(i * R, R), R)
        return pltpu.make_async_copy(src.at[rows, :], dst.at[rows, :], osem.at[n, i])

    def keep_early(i):
        return (keep_copy(3, mix_ref, mix_h, i), keep_copy(4, lse_ref, lse_h, i))

    def keep_late(i):
        return (keep_copy(5, mid_ref, mid_h, i), keep_copy(6, pre_ref, pre_h, i))

    def attend(i, keys):
        rows = pl.ds(pl.multiple_of(i * R, R), R)
        qpos = ctx * L + i * R + lax.broadcasted_iota(jnp.int32, (R, 1), 0)
        qseg = column(seg_ref[...], ctx * L + i * R, R)
        kpos = lax.broadcasted_iota(jnp.int32, (1, keys), 1)
        visible = (kpos <= qpos) & (seg_ref[:, :keys] == qseg)
        bias = jnp.where(visible, 0.0, masked_value)
        lane = lax.broadcasted_iota(jnp.int32, (R, 128), 1)
        lse_tile = jnp.zeros((R, 128), F32)
        for g in range(groups):
            cols = slice(128 * g, 128 * g + 128)
            q2 = head_pair(q_ref[rows, cols])
            s = dot_nt(q2, k_ref[:keys, cols]).reshape(2, R, keys) + bias[None]
            top = jnp.max(s, axis=-1, keepdims=True)
            p = jnp.exp(s - top)
            total = jnp.sum(p, axis=-1, keepdims=True)
            pr = (p * (1.0 / total)).astype(BF).reshape(2 * R, keys)
            lse = top + jnp.log(total)
            lse_tile = jnp.where(lane == 2 * g, lse[0], jnp.where(lane == 2 * g + 1, lse[1], lse_tile))
            o = dot_nn(pr, v_ref[:keys, cols])
            mix_ref[rows, cols] = pair_join(o).astype(BF)
        lse_ref[rows, :] = lse_tile

    a1, a2, a3, a4, a5, a6 = FWD_LAGS
    lag3 = jnp.where(ln.is_end, a3, a2)
    my_rows = pl.ds(pl.multiple_of(ln.side * half, half), half)
    ot_rows = pl.ds(pl.multiple_of((1 - ln.side) * half, half), half)

    def got(buf, flow, j):
        rcopy(buf.at[j], buf.at[j], ss.at[flow, j], rs.at[flow, j], ln.mid).wait_recv()

    def got_half(rows, flow, j):
        rcopy(x2_ref.at[j, rows, :], x2_ref.at[j, rows, :], ss.at[flow, j], rs.at[flow, j], ln.mid).wait_recv()

    def each(j, fn):
        for s in range(SUBS):
            fn(j * SUBS + s)

    def body(i, _):
        @pl.when(i < NC)
        def _():
            @pl.when(ctx == 0)
            def _():
                attend(i, L)

            @pl.when(ctx > 0)
            def _():
                attend(i, S)

            for s in range(SUBS):
                m = i * SUBS + s
                p = dot_nn(mix_ref[pl.ds(pl.multiple_of(i * R + s * RS, RS), RS), :], wout[...])
                part[m] = p

                @pl.when(ln.is_end)
                def _(m=m, p=p):
                    sE[m] = p.astype(BF)
                    rcopy(sE.at[m], rE.at[m], ss.at[0, m], rs.at[0, m], ln.mid).start()

            for cp in keep_early(i):
                cp.start()

        j1 = i - a1

        @pl.when(ln.is_mid & (j1 >= 0) & (j1 < NC))
        def _():
            def forward(m):
                got(rE, 0, m)
                sI[m] = (rE[m].astype(F32) + part[m]).astype(BF)
                rcopy(sI.at[m], rI.at[m], ss.at[1, m], rs.at[1, m], ln.other).start()

            each(j1, forward)

        j3 = i - lag3

        @pl.when((j3 >= 0) & (j3 < NC))
        def _():
            def arrive(m):
                got(rI, 1, m)

                @pl.when(ln.is_mid)
                def _():
                    sO[m] = (rI[m].astype(F32) + part[m]).astype(BF)
                    rcopy(sO.at[m], rI.at[m], ss.at[2, m], rs.at[1, m], ln.end).start()

            each(j3, arrive)
            ms = pl.ds(j3 * SUBS, SUBS)
            rows = pl.ds(pl.multiple_of(j3 * R, R), R)
            total = (rI[ms].astype(F32) + part[ms] + rE[ms].astype(F32)).reshape(R, D)
            mid = x_ref[rows, :].astype(F32) + total
            mid_ref[rows, :] = mid
            n2 = (rms_parts(mid)[1] * mgain).astype(BF)
            pre = dot_nn(n2, wup[...])
            pre_ref[rows, :] = pre
            for cp in keep_late(j3):
                cp.start()
            act = (0.5 * pre * (1.0 + gelu_pair(pre))).astype(BF)
            for s in range(SUBS):
                m = j3 * SUBS + s
                p2 = dot_nn(act[s * RS : (s + 1) * RS], wdn[...])

                @pl.when(ln.is_end)
                def _(m=m, p2=p2):
                    sE2[m] = p2.astype(BF)
                    rcopy(sE2.at[m], rE2.at[m], ss.at[3, m], rs.at[3, m], ln.mid).start()

                @pl.when(ln.is_mid)
                def _(m=m, p2=p2):
                    part2[m] = p2

        j4 = i - a4

        @pl.when(ln.is_mid & (j4 >= 0) & (j4 < NC))
        def _():
            def cross(m):
                got(rE2, 3, m)
                sX[m] = (rE2[m, ot_rows, :].astype(F32) + part2[m, ot_rows, :]).astype(BF)
                rcopy(sX.at[m], rX.at[m], ss.at[4, m], rs.at[4, m], ln.other).start()

            each(j4, cross)

        j5 = i - a5

        @pl.when(ln.is_mid & (j5 >= 0) & (j5 < NC))
        def _():
            def settle(m):
                got(rX, 4, m)
                rows = pl.ds(pl.multiple_of(m * RS + ln.side * half, half), half)
                mlp = part2[m, my_rows, :] + rE2[m, my_rows, :].astype(F32) + rX[m].astype(F32)
                x2_ref[m, my_rows, :] = (mid_ref[rows, :] + mlp).astype(BF)
                mine = x2_ref.at[m, my_rows, :]
                rcopy(mine, mine, ss.at[5, m], rs.at[5, m], ln.other).start()
                rcopy(mine, mine, ss.at[6, m], rs.at[6, m], ln.end).start()

            each(j5, settle)

        j6 = i - a6

        @pl.when(ln.is_mid & (j6 >= 0) & (j6 < NC))
        def _():
            def relay(m):
                got_half(ot_rows, 5, m)
                theirs = x2_ref.at[m, ot_rows, :]
                rcopy(theirs, theirs, ss.at[7, m], rs.at[7, m], ln.end).start()

            each(j6, relay)

        return 0

    lax.fori_loop(0, NC + a6, body, 0)

    for cp in counts:
        cp.wait()
    total = cbuf[0]
    for j in range(1, len(rpeers) + 1):
        total = total + cbuf[j]
    cnt_out[...] = total

    for c_to in range(1, NCTX):
        @pl.when(c_to > ctx)
        def _(c_to=c_to):
            kv_copy(k_ref, 0, c_to).wait_send()
            kv_copy(v_ref, 1, c_to).wait_send()

    for cp in whole:
        cp.wait()

    def kept(i, _):
        for cp in keep_early(i) + keep_late(i):
            cp.wait()
        return 0

    lax.fori_loop(0, NC, kept, 0)

    def drain(m, _):
        @pl.when(ln.is_end)
        def _():
            got_half(my_rows, 6, m)
            got_half(ot_rows, 7, m)
            rcopy(sE.at[m], rE.at[m], ss.at[0, m], rs.at[0, m], ln.mid).wait_send()
            rcopy(sE2.at[m], rE2.at[m], ss.at[3, m], rs.at[3, m], ln.mid).wait_send()

        @pl.when(ln.is_mid)
        def _():
            rcopy(sI.at[m], rI.at[m], ss.at[1, m], rs.at[1, m], ln.other).wait_send()
            rcopy(sO.at[m], rI.at[m], ss.at[2, m], rs.at[1, m], ln.end).wait_send()
            rcopy(sX.at[m], rX.at[m], ss.at[4, m], rs.at[4, m], ln.other).wait_send()
            mine = x2_ref.at[m, my_rows, :]
            theirs = x2_ref.at[m, ot_rows, :]
            rcopy(mine, mine, ss.at[5, m], rs.at[5, m], ln.other).wait_send()
            rcopy(mine, mine, ss.at[6, m], rs.at[6, m], ln.end).wait_send()
            rcopy(theirs, theirs, ss.at[7, m], rs.at[7, m], ln.end).wait_send()

        return 0

    lax.fori_loop(0, NM, drain, 0)


def dense_forward(x, again, mgain, seg, valid, w_qkv, w_out, w_up, w_down):
    L, D = x.shape
    S = seg.shape[1]
    NT, NDP, NCTX = lax.axis_size("tensor"), lax.axis_size("dp"), lax.axis_size("ctx")
    R = min(CHUNK, L)
    NC = L // R
    RS = R // SUB
    NM = NC * SUB
    Hd = w_out.shape[1]
    Fl = w_up.shape[2]
    sizes = (NC, SUB, R, D, L, S, NT, NDP, NCTX)
    flows = 8
    dma = pltpu.SemaphoreType.DMA
    rows = NDP * NCTX
    sd = jax.ShapeDtypeStruct
    v = pl.BlockSpec(memory_space=VM)
    a = pl.BlockSpec(memory_space=ANY)
    big = VM((NM, RS, D), BF)
    return pl.pallas_call(
        functools.partial(dense_forward_kernel, sizes),
        name="dense_forward",
        out_shape=(
            sd((NM, RS, D), BF), sd((L, Hd), BF), sd((S, Hd), BF), sd((S, Hd), BF), sd((L, Hd), BF),
            sd((L, 128), F32), sd((L, D), F32), sd((L, Fl), F32), sd((8, 128), F32),
        ),
        in_specs=[v] * 5 + [a] * 4,
        out_specs=(v,) + (a,) * 7 + (v,),
        scratch_shapes=[
            VM((L, Hd), BF), VM((S, Hd), BF), VM((S, Hd), BF), VM((L, Hd), BF), VM((L, 128), F32), VM((L, D), F32), VM((L, Fl), F32),
            VM((3, D, Hd), BF), VM((Hd, D), BF), VM((D, Fl), BF), VM((Fl, D), BF),
            VM((NM, RS, D), F32), VM((NM, RS, D), F32),
            big, big, big, big, big, big, big, VM((NM, RS // 2, D), BF), VM((NM, RS // 2, D), BF),
            VM((rows, 8, 128), F32),
            dma((4,)), dma((7, NC)), dma((2, NCTX)), dma((2, NCTX)), dma((rows,)), dma((rows,)), dma((flows, NM)), dma((flows, NM)),
        ],
        compiler_params=pltpu.CompilerParams(collective_id=1, has_side_effects=True, vmem_limit_bytes=58 << 20),
    )(x, again, mgain, seg, valid, w_qkv, w_out, w_up, w_down)


BWD_LAGS = (1, 2, 3)
TAIL_LAGS = (1, 2, 3)
BCHUNK = 128


def share_add(own, came):
    def add(j, _):
        own[j] = (own[j].astype(F32) + came[j].astype(F32)).astype(BF)
        return 0

    lax.fori_loop(0, own.shape[0], add, 0)


def dense_backward_kernel(
    sizes,
    x_ref, x2_ref, teach_ref, valid_ref, cnt_ref, sent_ref, gch_ref, ridx_ref, small_ref, again_ref, mgain_ref, seg_ref,
    q_h, k_h, v_h, mix_h, lse_h, mid_h, pre_h, wqkv_h, wout_h, wup_h, wdn_h, rdn_h, rup_h, rout_h, rqkv_h,
    hid_ref, loss_ref, gin_ref, dn_o, up_o, out_o, qkv_o, small_o,
    q_ref, k_ref, v_ref, mix_ref, lse_ref, mid_ref, pre_ref,
    wqkv, wout, wup, wdn, g_s, gm_s, act_s, gpre_s, n2_s, ga_s, n1_s, part, gqkv, dk_s, dv_s, rdk, rdv,
    sE, rE, sI, rI, sO, rE2, rX,
    tdn, odn, udn, wdn_r, tup, oup, uup, wup_r, tout, oout, uout, wout_r, tqkv, oqkv, uqkv, wqkv_r,
    ldn, lup, lout, lqkv, xdn, xup, xout, xqkv,
    acc_m, acc_a, lacc, lbuf, vec, vbuf, hbuf,
    isem, lsem, kvsem, s1, r1, s2, r2, s3, r3, cs, cr, ts, tr, ss, rs,
):
    NC, SUBS, R, D, L, S, NT, NDP, NCTX, scale_total = sizes
    RS = R // SUBS
    NM = NC * SUBS
    ln = Line()
    ctx = lax.axis_index("ctx")
    dp = lax.axis_index("dp")
    half = RS // 2
    G = NDP * NCTX
    W = D // G
    order = (
        (wdn_h.at[0], wdn), (pre_h, pre_ref), (wup_h.at[0], wup), (mid_h, mid_ref), (wout_h.at[0], wout), (q_h, q_ref),
        (k_h, k_ref), (v_h, v_ref), (lse_h, lse_ref), (mix_h, mix_ref), (wqkv_h.at[0], wqkv),
    )
    loads = [pltpu.make_async_copy(a, b, isem.at[n]) for n, (a, b) in enumerate(order)]
    for ld in loads:
        ld.start()
    tpeers = tensor_peers(NT)
    rpeers = row_peers(NDP, NCTX)
    greet(tpeers + rpeers)

    routed = ((rdn_h, ldn, xdn), (rup_h, lup, xup), (rout_h, lout, xout), (rqkv_h, lqkv, xqkv))

    def routed_copy(w, j):
        src, _, dst = routed[w]
        to = lax.rem(dp + j, NDP)
        return rcopy(src.at[to], dst.at[j - 1], s3.at[w, j - 1], r3.at[w, j - 1], {"dp": to})

    def routed_own(w):
        return pltpu.make_async_copy(routed[w][0].at[dp], routed[w][1], lsem.at[w])

    for w in range(4):
        routed_own(w).start()
        for j in range(1, NDP):
            routed_copy(w, j).start()

    @pl.when(ln.is_end)
    def _():
        def zero(m, _):
            rE[m] = jnp.zeros((RS, D), BF)
            return 0

        lax.fori_loop(0, NM, zero, 0)

    for ref in (dk_s, dv_s, acc_m, acc_a, lacc):
        ref[...] = jnp.zeros(ref.shape, F32)
    again = again_ref[0:1, :]
    mgain = mgain_ref[0:1, :]
    scale = scale_total / cnt_ref[0:1, 0:1]
    for ld in loads:
        ld.wait()

    Hd = q_ref.shape[1]
    groups = Hd // 128

    def attend_back(j, gmix, keys):
        rows = pl.ds(pl.multiple_of(j * R, R), R)
        qpos = ctx * L + j * R + lax.broadcasted_iota(jnp.int32, (R, 1), 0)
        qseg = column(seg_ref[...], ctx * L + j * R, R)
        kpos = lax.broadcasted_iota(jnp.int32, (1, keys), 1)
        visible = (kpos <= qpos) & (seg_ref[:, :keys] == qseg)
        bias = jnp.where(visible, 0.0, masked_value)
        lse = lse_ref[rows, :]
        for g in range(groups):
            cols = slice(128 * g, 128 * g + 128)
            q2 = head_pair(q_ref[rows, cols])
            g2 = head_pair(gmix[:, cols])
            kg = k_ref[:keys, cols]
            vg = v_ref[:keys, cols]
            l2 = jnp.concatenate([lse[:, 2 * g : 2 * g + 1], lse[:, 2 * g + 1 : 2 * g + 2]], axis=0)
            s = (dot_nt(q2, kg).reshape(2, R, keys) + bias[None]).reshape(2 * R, keys)
            p = jnp.exp(s - l2)
            dp_ = dot_nt(g2, vg)
            inner = jnp.sum(p * dp_, axis=-1, keepdims=True)
            ds = (p * (dp_ - inner)).astype(BF)
            gqkv[0, rows, cols] = (pair_join(dot_nn(ds, kg)) * 0.125).astype(BF)
            dk_s[:keys, cols] += dot_tn(ds, q2)
            dv_s[:keys, cols] += dot_tn(p.astype(BF), g2)

    a1, a2, a3 = BWD_LAGS
    lag3 = jnp.where(ln.is_end, a3, a2)
    my_rows = pl.ds(pl.multiple_of(ln.side * half, half), half)
    ot_rows = pl.ds(pl.multiple_of((1 - ln.side) * half, half), half)

    def got(buf, flow, j):
        rcopy(buf.at[j], buf.at[j], ss.at[flow, j], rs.at[flow, j], ln.mid).wait_recv()

    def got_half(rows, flow, j):
        rcopy(gin_ref.at[j, rows, :], gin_ref.at[j, rows, :], ss.at[flow, j], rs.at[flow, j], ln.mid).wait_recv()

    def each(j, fn):
        for s in range(SUBS):
            fn(j * SUBS + s)

    def both_of(d):
        return pl.ds(pl.multiple_of(d * NCTX * W, NCTX * W), NCTX * W)

    def by_share(piece, send, keep):
        def one(d, _):
            for lo, width, val in piece(both_of(d)):
                for c in range(NCTX):
                    rows = val[c * W : (c + 1) * W].astype(BF)

                    @pl.when(ctx == c)
                    def _(rows=rows, lo=lo, width=width):
                        keep[d, :, lo : lo + width] = rows

                    @pl.when(ctx != c)
                    def _(rows=rows, lo=lo, width=width):
                        send[d, :, lo : lo + width] = rows

            return 0

        lax.fori_loop(0, NDP, one, 0)

    def piece_dn(cols):
        return [(0, act_s.shape[1], dot_tn(gm_s[:, cols], act_s[...]))]

    def piece_up(cols):
        return [(0, gpre_s.shape[1], dot_tn(n2_s[:, cols], gpre_s[...]))]

    def piece_out(cols):
        return [(0, Hd, dot_tn(ga_s[:, cols], mix_ref[...]))]

    def piece_qkv(cols):
        lhs = n1_s[:, cols]
        return [(Hd * c, Hd, dot_tn(lhs, gqkv[c])) for c in range(3)]

    shares = (
        (piece_dn, tdn, odn, udn, wdn_r, dn_o),
        (piece_up, tup, oup, uup, wup_r, up_o),
        (piece_out, tout, oout, uout, wout_r, out_o),
        (piece_qkv, tqkv, oqkv, uqkv, wqkv_r, qkv_o),
    )
    across = {"ctx": 1 - ctx}

    def pair_copy(w):
        return rcopy(shares[w][1], shares[w][3], s1.at[w], r1.at[w], across)

    def share_first(w):
        by_share(shares[w][0], shares[w][1], shares[w][2])
        pair_copy(w).start()

    def dp_copy(w, j):
        to = lax.rem(dp + j, NDP)
        return rcopy(shares[w][2].at[to], shares[w][4].at[j - 1], s2.at[w, j - 1], r2.at[w, j - 1], {"dp": to})

    def share_second(w):
        pair_copy(w).wait_recv()
        share_add(shares[w][2], shares[w][3])
        for j in range(1, NDP):
            dp_copy(w, j).start()

    def put_total(w, layer, total):
        out = shares[w][5]
        if w == 3:
            for c in range(3):
                out[layer, c] = total[:, Hd * c : Hd * c + Hd]
        elif w == 1:
            out[layer] = total
        else:
            out[layer] = total.T

    def dense_total(w):
        for j in range(1, NDP):
            dp_copy(w, j).wait()
        total = shares[w][2][dp].astype(F32)
        for j in range(NDP - 1):
            total = total + shares[w][4][j].astype(F32)
        put_total(w, 0, total)

    def routed_total(w):
        routed_own(w).wait()
        for j in range(1, NDP):
            routed_copy(w, j).wait()
        total = routed[w][1][...].astype(F32)
        for j in range(NDP - 1):
            total = total + routed[w][2][j].astype(F32)
        put_total(w, 1, total)

    me = dp * NCTX + ctx

    def body(i, _):
        @pl.when(i < NC)
        def _():
            rows = pl.ds(pl.multiple_of(i * R, R), R)
            place = ctx * L + i * R + lax.broadcasted_iota(jnp.int32, (R, 1), 0)
            pick = (place == ridx_ref[...]).astype(F32).astype(BF)
            ms = pl.ds(i * SUBS, SUBS)
            x3 = x2_ref[ms].astype(F32).reshape(R, D) + dot_nn(pick, sent_ref[...])
            hid_ref[rows, :] = x3.astype(BF)
            err = x3 - teach_ref[rows, :].astype(F32)
            counted = column(valid_ref[...].astype(F32), i * R, R) * err
            lacc[...] += fold8(counted * err)
            g2 = scale * counted + dot_nn(pick, gch_ref[...])
            g_s[rows, :] = g2
            gm = g2.astype(BF)
            gm_s[rows, :] = gm
            gact = dot_nt(gm, wdn[...])
            u = pre_ref[rows, :]
            t = gelu_pair(u)
            act_s[rows, :] = (0.5 * u * (1.0 + t)).astype(BF)
            slope = 0.5 * (1.0 + t) + 0.5 * u * (1.0 - t * t) * (0.7978845608028654 * (1.0 + 3.0 * 0.044715 * u * u))
            gpre = (gact * slope).astype(BF)
            gpre_s[rows, :] = gpre
            for s in range(SUBS):
                m = i * SUBS + s
                p3 = dot_nt(gpre[s * RS : (s + 1) * RS], wup[...])
                part[m] = p3

                @pl.when(ln.is_end)
                def _(m=m, p3=p3):
                    sE[m] = p3.astype(BF)
                    rcopy(sE.at[m], rE.at[m], ss.at[0, m], rs.at[0, m], ln.mid).start()

            n1_s[rows, :] = (rms_parts(x_ref[rows, :].astype(F32))[1] * again).astype(BF)

        j1 = i - a1

        @pl.when(ln.is_mid & (j1 >= 0) & (j1 < NC))
        def _():
            def forward(m):
                got(rE, 0, m)
                sI[m] = (rE[m].astype(F32) + part[m]).astype(BF)
                rcopy(sI.at[m], rI.at[m], ss.at[1, m], rs.at[1, m], ln.other).start()

            each(j1, forward)

        j3 = i - lag3

        @pl.when((j3 >= 0) & (j3 < NC))
        def _():
            def arrive(m):
                got(rI, 1, m)

                @pl.when(ln.is_mid)
                def _():
                    sO[m] = (rI[m].astype(F32) + part[m]).astype(BF)
                    rcopy(sO.at[m], rI.at[m], ss.at[2, m], rs.at[1, m], ln.end).start()

            each(j3, arrive)
            ms = pl.ds(j3 * SUBS, SUBS)
            rows = pl.ds(pl.multiple_of(j3 * R, R), R)
            gn2 = (rI[ms].astype(F32) + part[ms] + rE[ms].astype(F32)).reshape(R, D)
            r, unit = rms_parts(mid_ref[rows, :])
            n2_s[rows, :] = (unit * mgain).astype(BF)
            scaled = gn2 * mgain
            gmid = r * (scaled - unit * jnp.mean(scaled * unit, axis=-1, keepdims=True))
            acc_m[...] += fold8(gn2 * unit)
            gattn = g_s[rows, :] + gmid
            g_s[rows, :] = gattn
            ga = gattn.astype(BF)
            ga_s[rows, :] = ga
            gmix = dot_nt(ga, wout[...]).astype(BF)

            @pl.when(ctx == 0)
            def _():
                attend_back(j3, gmix, L)

            @pl.when(ctx > 0)
            def _():
                attend_back(j3, gmix, S)

        @pl.when(i == NC)
        def _():
            lbuf[me] = jnp.full((8, 128), jnp.sum(lacc[...]))
            for j, p in enumerate(rpeers):
                rcopy(lbuf.at[me], lbuf.at[me], cs.at[j], cr.at[j], p).start()
            share_first(0)

        return 0

    lax.fori_loop(0, NC + a3, body, 0)

    def kv_copy(which):
        src, dst = ((dk_s, rdk), (dv_s, rdv))[which]
        return rcopy(src.at[pl.ds(0, L), :], dst, kvsem.at[which, 0], kvsem.at[which, 1], {"ctx": 0})

    @pl.when(ctx > 0)
    def _():
        kv_copy(0).start()
        kv_copy(1).start()
        for which, ref in enumerate((dk_s, dv_s)):
            gqkv[1 + which] = ref[pl.ds(L, L), :].astype(BF)

    def settle_sends(m, _):
        @pl.when(ln.is_end)
        def _():
            rcopy(sE.at[m], rE.at[m], ss.at[0, m], rs.at[0, m], ln.mid).wait_send()

        @pl.when(ln.is_mid)
        def _():
            rcopy(sI.at[m], rI.at[m], ss.at[1, m], rs.at[1, m], ln.other).wait_send()
            rcopy(sO.at[m], rI.at[m], ss.at[2, m], rs.at[1, m], ln.end).wait_send()

        return 0

    lax.fori_loop(0, NM, settle_sends, 0)

    @pl.when(ctx == 0)
    def _():
        for which, (ref, came) in enumerate(((dk_s, rdk), (dv_s, rdv))):
            kv_copy(which).wait_recv()
            gqkv[1 + which] = (ref[pl.ds(0, L), :] + came[...]).astype(BF)

    b4, b5, b6 = TAIL_LAGS
    sX = sI

    def tail(i, _):
        @pl.when(i < NC)
        def _():
            for s in range(SUBS):
                m = i * SUBS + s
                rows = pl.ds(pl.multiple_of(i * R + s * RS, RS), RS)
                p4 = dot_nt(gqkv[0, rows, :], wqkv[0])
                p4 = p4 + dot_nt(gqkv[1, rows, :], wqkv[1])
                p4 = p4 + dot_nt(gqkv[2, rows, :], wqkv[2])

                @pl.when(ln.is_end)
                def _(m=m, p4=p4):
                    sE[m] = p4.astype(BF)
                    rcopy(sE.at[m], rE2.at[m], ss.at[3, m], rs.at[3, m], ln.mid).start()

                @pl.when(ln.is_mid)
                def _(m=m, p4=p4):
                    part[m] = p4

        j4 = i - b4

        @pl.when(ln.is_mid & (j4 >= 0) & (j4 < NC))
        def _():
            def cross(m):
                got(rE2, 3, m)
                sX[m, pl.ds(0, half), :] = (rE2[m, ot_rows, :].astype(F32) + part[m, ot_rows, :]).astype(BF)
                rcopy(sX.at[m, pl.ds(0, half), :], rX.at[m], ss.at[4, m], rs.at[4, m], ln.other).start()

            each(j4, cross)

        j5 = i - b5

        @pl.when(ln.is_mid & (j5 >= 0) & (j5 < NC))
        def _():
            def settle(m):
                got(rX, 4, m)
                rows = pl.ds(pl.multiple_of(m * RS + ln.side * half, half), half)
                gn1 = part[m, my_rows, :] + rE2[m, my_rows, :].astype(F32) + rX[m].astype(F32)
                gin, gain_rows = rms_back(x_ref[rows, :].astype(F32), again, gn1)
                acc_a[...] += fold8(gain_rows)
                gin_ref[m, my_rows, :] = (g_s[rows, :] + gin).astype(BF)
                mine = gin_ref.at[m, my_rows, :]
                rcopy(mine, mine, ss.at[5, m], rs.at[5, m], ln.other).start()
                rcopy(mine, mine, ss.at[6, m], rs.at[6, m], ln.end).start()

            each(j5, settle)

        j6 = i - b6

        @pl.when(ln.is_mid & (j6 >= 0) & (j6 < NC))
        def _():
            def relay(m):
                got_half(ot_rows, 5, m)
                theirs = gin_ref.at[m, ot_rows, :]
                rcopy(theirs, theirs, ss.at[7, m], rs.at[7, m], ln.end).start()

            each(j6, relay)

        @pl.when(i == 0)
        def _():
            share_second(0)
            share_first(3)

        @pl.when(i == 1)
        def _():
            share_first(1)

        @pl.when(i == 2)
        def _():
            share_second(3)
            share_first(2)

        @pl.when(i == 3)
        def _():
            share_second(1)
            share_second(2)

        @pl.when(i == NC)
        def _():
            for w in range(4):
                routed_total(w)

        @pl.when(i == NC + 1)
        def _():
            dense_total(0)

        return 0

    lax.fori_loop(0, NC + b6, tail, 0)

    vec[...] = small_ref[...]
    vec[0:1, :] = vec[0:1, :] + jnp.sum(acc_a[...], axis=0, keepdims=True)
    vec[1:2, :] = vec[1:2, :] + jnp.sum(acc_m[...], axis=0, keepdims=True) * (1.0 / NT)
    places = []
    for j in range(NDP):
        for k in range(NCTX):
            if j or k:
                places.append((lax.rem(dp + j, NDP), lax.rem(ctx + k, NCTX)))

    def cols_of(g):
        return pl.ds(pl.multiple_of(g * W, W), W)

    def vec_copy(n):
        d2, c2 = places[n]
        return rcopy(vec.at[:, cols_of(d2 * NCTX + c2)], vbuf.at[me], ts.at[n], tr.at[n], {"dp": d2, "ctx": c2})

    for n in range(G - 1):
        vec_copy(n).start()
    vbuf[me] = vec[:, cols_of(me)]
    dense_total(3)
    for n in range(G - 1):
        vec_copy(n).wait()
    rows_sum = vbuf[0]
    for j in range(1, G):
        rows_sum = rows_sum + vbuf[j]
    hbuf[ln.t] = rows_sum

    def line_copy(n):
        return rcopy(hbuf.at[ln.t], hbuf.at[ln.t], ts.at[G - 1 + n], tr.at[G - 1 + n], tpeers[n])

    for n in range(NT - 1):
        line_copy(n).start()
    dense_total(1)
    dense_total(2)
    for j, p in enumerate(rpeers):
        rcopy(lbuf.at[me], lbuf.at[me], cs.at[j], cr.at[j], p).wait()
    loss = lbuf[0]
    for j in range(1, G):
        loss = loss + lbuf[j]
    loss_ref[...] = loss / (cnt_ref[...] * D)
    for n in range(NT - 1):
        line_copy(n).wait()
    line_sum = hbuf[0]
    for j in range(1, NT):
        line_sum = line_sum + hbuf[j]
    small_o[...] = line_sum

    for w in range(4):
        pair_copy(w).wait_send()

    @pl.when(ctx > 0)
    def _():
        kv_copy(0).wait_send()
        kv_copy(1).wait_send()

    def drain(m, _):
        @pl.when(ln.is_end)
        def _():
            got_half(my_rows, 6, m)
            got_half(ot_rows, 7, m)
            rcopy(sE.at[m], rE2.at[m], ss.at[3, m], rs.at[3, m], ln.mid).wait_send()

        @pl.when(ln.is_mid)
        def _():
            rcopy(sX.at[m, pl.ds(0, half), :], rX.at[m], ss.at[4, m], rs.at[4, m], ln.other).wait_send()
            mine = gin_ref.at[m, my_rows, :]
            theirs = gin_ref.at[m, ot_rows, :]
            rcopy(mine, mine, ss.at[5, m], rs.at[5, m], ln.other).wait_send()
            rcopy(mine, mine, ss.at[6, m], rs.at[6, m], ln.end).wait_send()
            rcopy(theirs, theirs, ss.at[7, m], rs.at[7, m], ln.end).wait_send()

        return 0

    lax.fori_loop(0, NM, drain, 0)


def dense_backward(x, x2, teacher, valid, cnt, sent, gchosen, ridx, small, again, mgain, seg, saved, w_qkv, w_out, w_up, w_down, routed):
    L, D = x.shape
    S = seg.shape[1]
    NT, NDP, NCTX = lax.axis_size("tensor"), lax.axis_size("dp"), lax.axis_size("ctx")
    R = min(BCHUNK, L)
    NC = L // R
    RS = R // SUB
    NM = NC * SUB
    Hd = w_out.shape[1]
    Fl = w_up.shape[2]
    G = NDP * NCTX
    W = D // G
    sizes = (NC, SUB, R, D, L, S, NT, NDP, NCTX, float(S * NDP))
    dma = pltpu.SemaphoreType.DMA
    sd = jax.ShapeDtypeStruct
    v_ = pl.BlockSpec(memory_space=VM)
    a_ = pl.BlockSpec(memory_space=ANY)

    def four(shape):
        return [VM((NDP,) + shape, BF)] * 3 + [VM((NDP - 1,) + shape, BF)]

    wshape = ((W, Fl), (W, Fl), (W, Hd), (W, 3 * Hd))
    dense_shares = sum((four(s) for s in wshape), [])
    routed_scratch = [VM(s, BF) for s in wshape] + [VM((NDP - 1,) + s, BF) for s in wshape]
    big = VM((NM, RS, D), BF)
    return pl.pallas_call(
        functools.partial(dense_backward_kernel, sizes),
        name="dense_backward",
        out_shape=(
            sd((L, D), BF), sd((8, 128), F32), sd((NM, RS, D), BF),
            sd((2, Fl, W), F32), sd((2, W, Fl), F32), sd((2, Hd, W), F32), sd((2, 3, W, Hd), F32), sd((8, W), F32),
        ),
        in_specs=[v_] * 12 + [a_] * 15,
        out_specs=(v_,) * 8,
        scratch_shapes=[
            VM((L, Hd), BF), VM((S, Hd), BF), VM((S, Hd), BF), VM((L, Hd), BF), VM((L, 128), F32), VM((L, D), F32), VM((L, Fl), F32),
            VM((3, D, Hd), BF), VM((Hd, D), BF), VM((D, Fl), BF), VM((Fl, D), BF),
            VM((L, D), F32), VM((L, D), BF), VM((L, Fl), BF), VM((L, Fl), BF), VM((L, D), BF), VM((L, D), BF), VM((L, D), BF),
            VM((NM, RS, D), F32), VM((3, L, Hd), BF), VM((S, Hd), F32), VM((S, Hd), F32), VM((L, Hd), F32), VM((L, Hd), F32),
            big, big, big, big, big, big, VM((NM, RS // 2, D), BF),
        ] + dense_shares + routed_scratch + [
            VM((8, D), F32), VM((8, D), F32), VM((8, D), F32), VM((G, 8, 128), F32),
            VM((8, D), F32), VM((G, 8, W), F32), VM((NT, 8, W), F32),
            dma((11,)), dma((4,)), dma((2, 2)), dma((4,)), dma((4,)), dma((4, NDP)), dma((4, NDP)), dma((4, NDP)), dma((4, NDP)),
            dma((G,)), dma((G,)), dma((G + NT,)), dma((G + NT,)), dma((8, NM)), dma((8, NM)),
        ],
        compiler_params=pltpu.CompilerParams(collective_id=3, has_side_effects=True, vmem_limit_bytes=62 << 20),
    )(
        x, x2, teacher, valid, cnt, sent, gchosen, ridx, small, again, mgain, seg, *saved, w_qkv, w_out, w_up, w_down, *routed,
    )


def routed_kernel(
    sizes,
    x2_ref, teach_ref, valid_ref, cnt_ref, idxr_ref, segr_ref, again_ref, mgain_ref, router_ref,
    wqkv_h, wout_h, wup_h, wdn_h,
    sent_ref, gch_ref, small_ref, dn_o, up_o, out_o, qkv_o,
    wqkv, wout, wup, wdn, xs, xc, tsel, tc, vsel, vc, n1_s, k_s, v_s, part, mix_s, n2_s, act_s, gpre_s, gm_s, ga_s, gqkv, dkv, dkvc,
    posc, segq, sbuf, rbuf, tdn, udn, tup, uup, tout, uout, tqkv, uqkv,
    wsem, xsem, xrem, dsem, drem, s1, r1, ps, pr_, gs, gr,
):
    L, D, S, RT, NT, NDP, NCTX, scale_total = sizes
    RL = RT // NCTX
    Q = RL // NT
    G = NDP * NCTX
    W = D // G
    t = lax.axis_index("tensor")
    ctx = lax.axis_index("ctx")
    across = {"ctx": 1 - ctx}
    loads = [
        pltpu.make_async_copy(wqkv_h.at[1], wqkv, wsem.at[0]),
        pltpu.make_async_copy(wout_h.at[1], wout, wsem.at[1]),
        pltpu.make_async_copy(wup_h.at[1], wup, wsem.at[2]),
        pltpu.make_async_copy(wdn_h.at[1], wdn, wsem.at[3]),
    ]
    for ld in loads:
        ld.start()
    greet(tensor_peers(NT) + [across])
    my = pl.ds(pl.multiple_of(ctx * RL, RL), RL)
    theirs = pl.ds(pl.multiple_of((1 - ctx) * RL, RL), RL)
    own = pl.ds(pl.multiple_of(t * Q, Q), Q)

    idxc = column(idxr_ref[...], 0, RT)
    held = idxc - ctx * L == lax.broadcasted_iota(jnp.int32, (RT, L), 1)
    pick = held.astype(F32).astype(BF)
    xs[...] = dot_nn(pick, x2_ref[...]).astype(BF)
    first = [rcopy(xs, xc, xsem.at[0], xrem.at[0], across)]
    first[0].start()
    tsel[...] = dot_nn(pick, teach_ref[...]).astype(BF)
    vsel[...] = jnp.broadcast_to(jnp.sum(jnp.where(held, valid_ref[...].astype(F32), 0.0), axis=-1, keepdims=True), (RT, 128))
    first.append(rcopy(tsel.at[theirs, :], tc, xsem.at[1], xrem.at[1], across))
    first.append(rcopy(vsel.at[theirs, :], vc, xsem.at[2], xrem.at[2], across))
    first[1].start()
    first[2].start()

    at = idxc == lax.broadcasted_iota(jnp.int32, (RT, S), 1)
    posc[...] = jnp.broadcast_to(idxc, (RT, 128))
    seg_col = jnp.sum(jnp.where(at, segr_ref[...], 0), axis=-1, keepdims=True)
    segq[...] = jnp.broadcast_to(seg_col, (RT, 128))
    same = lax.broadcasted_iota(jnp.int32, (RT, RT), 0) == lax.broadcasted_iota(jnp.int32, (RT, RT), 1)
    seg_row = jnp.sum(jnp.where(same, seg_col, 0), axis=0, keepdims=True)
    visible = (idxr_ref[...] <= posc[my, 0:1]) & (seg_row == segq[my, 0:1])
    bias = jnp.where(visible, 0.0, masked_value)
    again = again_ref[1:2, :]
    mgain = mgain_ref[1:2, :]
    router = router_ref[...]
    Hd = wout.shape[0]
    groups = Hd // 128

    for ld in loads:
        ld.wait()
    first[0].wait_recv()
    chosen = xs[...].astype(F32) + xc[...].astype(F32)
    xs_all = chosen.astype(BF)
    n1 = (rms_parts(chosen)[1] * again).astype(BF)
    n1_s[...] = n1
    first[0].wait_send()
    xs[...] = xs_all
    k_s[...] = dot_nn(n1, wqkv[1]).astype(BF)
    v_s[...] = dot_nn(n1, wqkv[2]).astype(BF)
    n1m = n1_s[my, :]
    q = (dot_nn(n1m, wqkv[0]).astype(BF) * jnp.asarray(0.125, BF))
    probs = []
    for g in range(groups):
        cols = slice(128 * g, 128 * g + 128)
        q2 = head_pair(q[:, cols])
        s = dot_nt(q2, k_s[:, cols]).reshape(2, RL, RT) + bias[None]
        p = jnp.exp(s - jnp.max(s, axis=-1, keepdims=True))
        p = (p * (1.0 / jnp.sum(p, axis=-1, keepdims=True))).reshape(2 * RL, RT)
        probs.append((q2, p))
        mix_s[:, cols] = pair_join(dot_nn(p.astype(BF), v_s[:, cols])).astype(BF)

    def piece_copy(step, j):
        to = lax.rem(t + j, NT)
        rows = pl.ds(pl.multiple_of(to * Q, Q), Q)
        return rcopy(sbuf.at[step, rows, :], rbuf.at[step, j - 1], ps.at[step, j - 1], pr_.at[step, j - 1], {"tensor": to})

    def spread(step, value):
        part[...] = value
        sbuf[step] = value.astype(BF)
        for j in range(1, NT):
            piece_copy(step, j).start()

    def collect(step):
        total = part[own, :]
        for j in range(1, NT):
            piece_copy(step, j).wait_recv()
            total = total + rbuf[step, j - 1].astype(F32)
        return total

    def gather_copy(step, ref, base_row, j):
        to = lax.rem(t + j, NT)
        rows = pl.ds(pl.multiple_of(base_row + t * Q, Q), Q)
        return rcopy(ref.at[rows, :], ref.at[rows, :], gs.at[step, j - 1], gr.at[step, j - 1], {"tensor": to})

    def gather(step, ref, base_row):
        for j in range(1, NT):
            gather_copy(step, ref, base_row, j).start()

    def gathered(step, ref, base_row):
        for j in range(1, NT):
            gather_copy(step, ref, base_row, j).wait()

    mine16 = pl.ds(pl.multiple_of(ctx * RL + t * Q, Q), Q)
    spread(0, dot_nn(mix_s[...], wout[...]))
    chosen_o = xs[mine16, :].astype(F32)
    gate_o = jax.nn.sigmoid(jnp.sum(chosen_o * router, axis=-1, keepdims=True))
    chosen_m = xs[my, :].astype(F32)
    gate_m = jax.nn.sigmoid(jnp.sum(chosen_m * router, axis=-1, keepdims=True))
    attn_o = collect(0)
    mid_o = chosen_o + attn_o
    n2_s[own, :] = (rms_parts(mid_o)[1] * mgain).astype(BF)
    gather(0, n2_s, 0)
    gathered(0, n2_s, 0)

    pre = dot_nn(n2_s[...], wup[...])
    th = gelu_pair(pre)
    act_s[...] = (0.5 * pre * (1.0 + th)).astype(BF)
    spread(1, dot_nn(act_s[...], wdn[...]))
    slope = 0.5 * (1.0 + th) + 0.5 * pre * (1.0 - th * th) * (0.7978845608028654 * (1.0 + 3.0 * 0.044715 * pre * pre))
    first[1].wait()
    first[2].wait()
    teach = tsel[my, :].astype(F32) + tc[...].astype(F32)
    counted = vsel[my, 0:1] + vc[:, 0:1]
    scale = scale_total / cnt_ref[0:1, 0:1]
    branch_o = attn_o + collect(1)
    sent_ref[mine16, :] = (gate_o * branch_o).astype(BF)
    gather(1, sent_ref, ctx * RL)
    gathered(1, sent_ref, ctx * RL)

    sent_pair = rcopy(sent_ref.at[my, :], sent_ref.at[my, :], dsem.at[0], drem.at[0], across)
    sent_pair.start()
    gsent = (scale * counted * (chosen_m + sent_ref[my, :].astype(F32) - teach)).astype(BF).astype(F32)
    top = gate_m * gsent
    part[...] = gsent
    gsent_o = part[own, :]
    gm = top.astype(BF)
    gm_s[...] = gm
    gpre = (dot_nt(gm, wdn[...]) * slope).astype(BF)
    gpre_s[...] = gpre
    spread(2, dot_nt(gpre, wup[...]))

    def both_of(d):
        return pl.ds(pl.multiple_of(d * NCTX * W, NCTX * W), NCTX * W)

    def by_share(piece, send, keep):
        def one(d, _):
            for lo, width, val in piece(both_of(d)):
                for c in range(NCTX):
                    rows = val[c * W : (c + 1) * W].astype(BF)

                    @pl.when(ctx == c)
                    def _(rows=rows, lo=lo, width=width):
                        keep[d, :, lo : lo + width] = rows

                    @pl.when(ctx != c)
                    def _(rows=rows, lo=lo, width=width):
                        send[d, :, lo : lo + width] = rows

            return 0

        lax.fori_loop(0, NDP, one, 0)

    def piece_dn(cols):
        return [(0, act_s.shape[1], dot_tn(gm_s[:, cols], act_s[...]))]

    def piece_up(cols):
        return [(0, gpre_s.shape[1], dot_tn(n2_s[:, cols], gpre_s[...]))]

    def piece_out(cols):
        return [(0, Hd, dot_tn(ga_s[:, cols], mix_s[...]))]

    def piece_qkv(cols):
        lhs = n1_s[my, cols]
        return [(Hd * c, Hd, dot_tn(lhs, gqkv[c])) for c in range(3)]

    shares = ((piece_dn, tdn, dn_o, udn), (piece_up, tup, up_o, uup), (piece_out, tout, out_o, uout), (piece_qkv, tqkv, qkv_o, uqkv))

    def pair_copy(w):
        return rcopy(shares[w][1], shares[w][3], s1.at[w], r1.at[w], across)

    def share_first(w):
        by_share(shares[w][0], shares[w][1], shares[w][2])
        pair_copy(w).start()

    ggate_o = jnp.sum(gsent_o * branch_o, axis=-1, keepdims=True) * gate_o * (1.0 - gate_o)
    small_ref[...] = jnp.zeros(small_ref.shape, F32)
    small_ref[4:5, :] = jnp.sum(ggate_o * chosen_o, axis=0, keepdims=True)
    top_o = gate_o * gsent_o
    share_first(0)
    gmid_o, gain_rows = rms_back(mid_o, mgain, collect(2))
    small_ref[3:4, :] = jnp.sum(gain_rows, axis=0, keepdims=True)
    ga_s[own, :] = (top_o + gmid_o).astype(BF)
    gather(2, ga_s, 0)
    share_first(1)
    gathered(2, ga_s, 0)

    gmix = dot_nt(ga_s[...], wout[...]).astype(BF)
    for g in range(groups):
        cols = slice(128 * g, 128 * g + 128)
        q2, p = probs[g]
        g2 = head_pair(gmix[:, cols])
        dp_ = dot_nt(g2, v_s[:, cols])
        ds = (p * (dp_ - jnp.sum(p * dp_, axis=-1, keepdims=True))).astype(BF)
        gqkv[0, :, cols] = (pair_join(dot_nn(ds, k_s[:, cols])) * 0.125).astype(BF)
        dkv[0, :, cols] = dot_tn(ds, q2)
        dkv[1, :, cols] = dot_tn(p.astype(BF), g2)
    kv_pair = [rcopy(dkv.at[c, theirs, :], dkvc.at[c], dsem.at[1 + c], drem.at[1 + c], across) for c in range(2)]
    for cp in kv_pair:
        cp.start()
    p4 = dot_nt(gqkv[0], wqkv[0])
    for c in range(2):
        kv_pair[c].wait()
        gqkv[1 + c] = (dkv[c, my, :] + dkvc[c]).astype(BF)
        p4 = p4 + dot_nt(gqkv[1 + c], wqkv[1 + c])
    spread(3, p4)
    share_first(2)
    gin_o, gain_rows = rms_back(chosen_o, again, collect(3))
    small_ref[2:3, :] = jnp.sum(gain_rows, axis=0, keepdims=True)
    gch_ref[mine16, :] = (gmid_o + gin_o + ggate_o * router).astype(BF)
    gather(3, gch_ref, ctx * RL)
    share_first(3)
    gathered(3, gch_ref, ctx * RL)
    gch_pair = rcopy(gch_ref.at[my, :], gch_ref.at[my, :], dsem.at[3], drem.at[3], across)
    gch_pair.start()

    for w, (_, _, keep, came) in enumerate(shares):
        pair_copy(w).wait()

        def add(j, _, keep=keep, came=came):
            keep[j] = (keep[j].astype(F32) + came[j].astype(F32)).astype(BF)
            return 0

        lax.fori_loop(0, NDP, add, 0)
    for step in range(4):
        for j in range(1, NT):
            piece_copy(step, j).wait_send()
    sent_pair.wait()
    gch_pair.wait()


def routed_block(x2, teacher, valid, cnt, ridx, seg, again, mgain, w_router, w_qkv, w_out, w_up, w_down):
    L, D = teacher.shape
    S = seg.shape[1]
    RT = ridx.shape[1]
    NT, NDP, NCTX = lax.axis_size("tensor"), lax.axis_size("dp"), lax.axis_size("ctx")
    Hd = w_out.shape[1]
    Fl = w_up.shape[2]
    RL = RT // NCTX
    Q = RL // NT
    G = NDP * NCTX
    W = D // G
    sizes = (L, D, S, RT, NT, NDP, NCTX, float(S * NDP))
    dma = pltpu.SemaphoreType.DMA
    sd = jax.ShapeDtypeStruct
    v_ = pl.BlockSpec(memory_space=VM)
    a_ = pl.BlockSpec(memory_space=ANY)
    wshape = ((W, Fl), (W, Fl), (W, Hd), (W, 3 * Hd))
    return pl.pallas_call(
        functools.partial(routed_kernel, sizes),
        name="routed_block",
        out_shape=(
            sd((RT, D), BF), sd((RT, D), BF), sd((8, D), F32),
            *[sd((NDP,) + s, BF) for s in wshape],
        ),
        in_specs=[v_] * 9 + [a_] * 4,
        out_specs=(v_,) * 7,
        scratch_shapes=[
            VM((3, D, Hd), BF), VM((Hd, D), BF), VM((D, Fl), BF), VM((Fl, D), BF),
            VM((RT, D), BF), VM((RT, D), BF), VM((RT, D), BF), VM((RL, D), BF), VM((RT, 128), F32), VM((RL, 128), F32),
            VM((RT, D), BF), VM((RT, Hd), BF), VM((RT, Hd), BF), VM((RL, D), F32), VM((RL, Hd), BF), VM((RL, D), BF),
            VM((RL, Fl), BF), VM((RL, Fl), BF), VM((RL, D), BF), VM((RL, D), BF), VM((3, RL, Hd), BF),
            VM((2, RT, Hd), F32), VM((2, RL, Hd), F32),
            VM((RT, 128), jnp.int32), VM((RT, 128), jnp.int32),
            VM((4, RL, D), BF), VM((4, NT - 1, Q, D), BF),
            *sum(([VM((NDP,) + s, BF)] * 2 for s in wshape), []),
            dma((4,)), dma((3,)), dma((3,)), dma((4,)), dma((4,)), dma((4,)), dma((4,)),
            dma((4, NT)), dma((4, NT)), dma((4, NT)), dma((4, NT)),
        ],
        compiler_params=pltpu.CompilerParams(collective_id=2, has_side_effects=True, vmem_limit_bytes=60 << 20),
    )(
        x2.reshape(L, D), teacher, valid, cnt, ridx, seg, again, mgain, w_router.reshape(1, D), w_qkv, w_out, w_up, w_down,
    )


def finish_kernel(
    hid_h, gin_h, dn_h, up_h, out_h, qkv_h, small_h, loss_h,
    hid_o, loss_o, gin_o, ag_o, qkv_o, out_o, mg_o, up_o, dn_o, router_o,
    hid, gin, dn, up, out, qkv, small, loss, wide, sem,
):
    pairs = ((gin_h, gin), (dn_h, dn), (up_h, up), (hid_h, hid), (qkv_h, qkv), (out_h, out), (small_h, small), (loss_h, loss))
    reads = [pltpu.make_async_copy(a, b, sem.at[n]) for n, (a, b) in enumerate(pairs)]
    for cp in reads:
        cp.start()
    backs = ((wide, gin_o), (dn, dn_o), (up, up_o), (hid, hid_o), (qkv, qkv_o), (out, out_o))
    writes = [pltpu.make_async_copy(a, b, sem.at[8 + n]) for n, (a, b) in enumerate(backs)]
    for n in range(6):
        reads[n].wait()
        if n == 0:
            wide[...] = gin[...].astype(F32)
        writes[n].start()
    reads[6].wait()
    reads[7].wait()
    loss_o[...] = loss[0:1, 0:1]
    for j in range(2):
        ag_o[j : j + 1, :] = small[2 * j : 2 * j + 1, :]
        mg_o[j : j + 1, :] = small[2 * j + 1 : 2 * j + 2, :]
    router_o[...] = small[4:5, :]
    for cp in writes:
        cp.wait()


def finish(hid, gin, dn, up, out, qkv, small, loss):
    sd = jax.ShapeDtypeStruct
    v_ = pl.BlockSpec(memory_space=VM)
    h_ = pl.BlockSpec(memory_space=pltpu.HBM)
    W = small.shape[1]

    def like(arr):
        return sd(arr.shape, arr.dtype)

    ins = (hid, gin, dn, up, out, qkv, small, loss)
    return pl.pallas_call(
        finish_kernel,
        name="finish",
        out_shape=(like(hid), sd((1, 1), F32), sd(gin.shape, F32), sd((2, W), F32), like(qkv), like(out), sd((2, W), F32), like(up), like(dn), sd((1, W), F32)),
        in_specs=[h_] * 8,
        out_specs=(h_, v_, h_, v_, h_, h_, v_, h_, h_, v_),
        scratch_shapes=[*[VM(a.shape, a.dtype) for a in ins], VM(gin.shape, F32), pltpu.SemaphoreType.DMA((14,))],
        compiler_params=pltpu.CompilerParams(vmem_limit_bytes=60 << 20),
    )(*ins)


def fast_local(hidden_in, teacher, seg_ids, valid, routed_idx, attn_gain, w_qkv, w_out, mlp_gain, w_up, w_down, w_router):
    L, D = hidden_in.shape[1:]
    x2, *saved, cnt = dense_forward(hidden_in[0], attn_gain, mlp_gain, seg_ids, valid, w_qkv, w_out, w_up, w_down)
    sent, gch, small, *routed = routed_block(
        x2, teacher[0], valid, cnt, routed_idx, seg_ids, attn_gain, mlp_gain, w_router, w_qkv, w_out, w_up, w_down
    )
    hid, loss, gin, dn, up, out, qkv, small = dense_backward(
        hidden_in[0], x2, teacher[0], valid, cnt, sent, gch, routed_idx, small, attn_gain, mlp_gain, seg_ids, saved,
        w_qkv, w_out, w_up, w_down, routed,
    )
    hid, loss, gin, ag, qkv, out, mg, up, dn, router = finish(hid, gin, dn, up, out, qkv, small, loss)
    return (hid[None], loss[0, 0], gin.reshape(1, L, D), ag, qkv, out, mg, up, dn, router[0])


def takes_kernels(mesh):
    shape = dict(mesh.shape)
    return shape["tensor"] == 4 and shape["ctx"] == 2


def solution(mesh):
    placed = (
        P("dp", "ctx", None),
        P("dp", "ctx", None),
        P("dp", None),
        P("dp", "ctx"),
        P("dp", None),
        P(),
        P(None, None, None, "tensor"),
        P(None, "tensor", None),
        P(),
        P(None, None, "tensor"),
        P(None, "tensor", None),
        P(),
    )
    return jax.shard_map(
        fast_local if takes_kernels(mesh) else plain_local,
        mesh=mesh,
        in_specs=placed,
        out_specs=(
            P("dp", "ctx", None),
            P(),
            P("dp", "ctx", None),
            P(None, ("dp", "ctx")),
            P(None, None, ("dp", "ctx"), "tensor"),
            P(None, "tensor", ("dp", "ctx")),
            P(None, ("dp", "ctx")),
            P(None, ("dp", "ctx"), "tensor"),
            P(None, "tensor", ("dp", "ctx")),
            P(("dp", "ctx")),
        ),
        check_vma=False,
    )
```

```python
import functools

import jax
import jax.numpy as jnp
from jax import lax
from jax.experimental import pallas as pl
from jax.experimental.pallas import tpu as pltpu
from jax.sharding import PartitionSpec as P

HEAD = 64
epsilon = 1e-06
masked_value = -1e30
MESH = pl.DeviceIdType.MESH
BF = jnp.bfloat16
F32 = jnp.float32
VM = pltpu.VMEM
ANY = pl.ANY


def rcopy(src, dst, send, recv, where):
    return pltpu.make_async_remote_copy(
        src_ref=src, dst_ref=dst, send_sem=send, recv_sem=recv, device_id=where, device_id_type=MESH
    )


def dot_nn(a, b):
    return lax.dot_general(a, b, (((1,), (0,)), ((), ())), preferred_element_type=F32)


def dot_nt(a, b):
    return lax.dot_general(a, b, (((1,), (1,)), ((), ())), preferred_element_type=F32)


def dot_tn(a, b):
    return lax.dot_general(a, b, (((0,), (0,)), ((), ())), preferred_element_type=F32)


def rms_parts(values):
    r = lax.rsqrt(jnp.mean(values * values, axis=-1, keepdims=True) + epsilon)
    return r, values * r


def rms_back(values, gain, grad):
    r, unit = rms_parts(values)
    scaled = grad * gain
    return r * (scaled - unit * jnp.mean(scaled * unit, axis=-1, keepdims=True)), grad * unit


def gelu_pair(u):
    c = 0.7978845608028654
    t = jnp.tanh(c * (u + 0.044715 * (u * u * u)))
    return t


def fold8(rows):
    return jnp.sum(rows.reshape(rows.shape[0] // 8, 8, rows.shape[1]), axis=0)


class Line:
    def __init__(self):
        t = lax.axis_index("tensor")
        self.t = t
        self.side = t // 2
        self.is_end = (t == 0) | (t == 3)
        self.is_mid = (t == 1) | (t == 2)
        self.end = {"tensor": self.side * 3}
        self.mid = {"tensor": 1 + self.side}
        self.other = {"tensor": 2 - self.side}


def greet(peers):
    bar = pltpu.get_barrier_semaphore()
    for p in peers:
        pl.semaphore_signal(bar, inc=1, device_id=p, device_id_type=MESH)
    pl.semaphore_wait(bar, len(peers))


def tensor_peers(n):
    t = lax.axis_index("tensor")
    return [{"tensor": lax.rem(t + j, n)} for j in range(1, n)]


def row_peers(n_dp, n_ctx):
    d, c = lax.axis_index("dp"), lax.axis_index("ctx")
    out = []
    for j in range(n_dp):
        for k in range(n_ctx):
            if j or k:
                out.append({"dp": lax.rem(d + j, n_dp), "ctx": lax.rem(c + k, n_ctx)})
    return out


def rms_scale(values, gain):
    return values * lax.rsqrt(jnp.mean(values * values, axis=-1, keepdims=True) + epsilon) * gain


def gelu_tanh(values):
    return jax.nn.gelu(values, approximate=True)


def gating_fn(chosen, router):
    return jax.nn.sigmoid(jnp.sum(chosen * router, axis=-1))


def tensor_sum(partial_sum):
    return lax.psum(partial_sum, "tensor")


def gather_keys(projected):
    return (
        lax.all_gather(projected[1], "ctx", axis=1, tiled=True),
        lax.all_gather(projected[2], "ctx", axis=1, tiled=True),
    )


def scatter_key_grads(grad_k, grad_v):
    stacked = jnp.stack([grad_k, grad_v])
    summed = lax.psum_scatter(stacked, "ctx", scatter_dimension=2, tiled=True)
    return (summed[0], summed[1])


def to_workers(picked):
    return lax.psum_scatter(
        picked.astype(jnp.bfloat16), "ctx", scatter_dimension=1, tiled=True
    ).astype(jnp.float32)


def to_owners(rows_low):
    return lax.all_gather(rows_low, "ctx", axis=1, tiled=True)


def take_rows(table, places):
    return jax.vmap(lambda t, i: t[i])(table, places)


def add_rows(table, places, addend):
    return jax.vmap(lambda t, i, a: t.at[i].add(a))(table, places, addend)


def tile_scores(q_tile, k_tile, qpos_tile, kpos_tile, qseg_tile, kseg_tile, score_scale):
    scores = (
        jnp.einsum("qhe,khe->hqk", q_tile, k_tile, preferred_element_type=jnp.float32) * score_scale
    )
    visible = (kpos_tile[None, :] <= qpos_tile[:, None]) & (
        kseg_tile[None, :] == qseg_tile[:, None]
    )
    return (scores, visible[None])


def tile_layout(queries, key_rows, value_rows, k_pos, k_seg):
    q_len, row_width = queries.shape
    k_len = key_rows.shape[0]
    head_count = row_width // HEAD
    q_step = min(512, q_len)
    k_step = min(2048, k_len)
    k_count = k_len // k_step
    key_tiles = key_rows.reshape(k_count, k_step, head_count, HEAD)
    value_tiles = value_rows.reshape(k_count, k_step, head_count, HEAD)
    kpos_tiles = k_pos.reshape(k_count, k_step)
    kseg_tiles = k_seg.reshape(k_count, k_step)
    return (
        q_len,
        row_width,
        k_len,
        head_count,
        q_step,
        (key_tiles, value_tiles, kpos_tiles, kseg_tiles),
    )


def attend_one(queries, key_rows, value_rows, q_pos, k_pos, q_seg, k_seg):
    q_len, row_width, k_len, head_count, q_step, tiles = tile_layout(
        queries, key_rows, value_rows, k_pos, k_seg
    )
    score_scale = 1.0 / HEAD**0.5

    def per_query(q_args):
        q_tile, qpos_tile, qseg_tile = q_args

        def total_step(carry, k_args):
            running, summed = carry
            k_tile, v_tile, kpos_tile, kseg_tile = k_args
            scores, visible = tile_scores(
                q_tile, k_tile, qpos_tile, kpos_tile, qseg_tile, kseg_tile, score_scale
            )
            raised = jnp.maximum(
                running, jnp.max(jnp.where(visible, scores, masked_value), axis=-1)
            )
            weights = jnp.where(visible, jnp.exp(scores - raised[..., None]), 0.0)
            return ((raised, summed * jnp.exp(running - raised) + jnp.sum(weights, axis=-1)), None)

        initial = (
            jnp.full((head_count, q_step), masked_value, jnp.float32),
            jnp.zeros((head_count, q_step), jnp.float32),
        )
        (running, summed), _ = lax.scan(total_step, initial, tiles)
        log_total = running + jnp.log(summed)

        def value_step(output, k_args):
            k_tile, v_tile, kpos_tile, kseg_tile = k_args
            scores, visible = tile_scores(
                q_tile, k_tile, qpos_tile, kpos_tile, qseg_tile, kseg_tile, score_scale
            )
            weights_low = jnp.where(visible, jnp.exp(scores - log_total[..., None]), 0.0).astype(
                jnp.bfloat16
            )
            return (
                output
                + jnp.einsum(
                    "hqk,khe->qhe", weights_low, v_tile, preferred_element_type=jnp.float32
                ),
                None,
            )

        output, _ = lax.scan(value_step, jnp.zeros((q_step, head_count, HEAD), jnp.float32), tiles)
        return (output, log_total)

    q_count = q_len // q_step
    output, log_total = lax.map(
        per_query,
        (
            queries.reshape(q_count, q_step, head_count, HEAD),
            q_pos.reshape(q_count, q_step),
            q_seg.reshape(q_count, q_step),
        ),
    )
    return (output.reshape(q_len, row_width), log_total)


def attend_back(queries, key_rows, value_rows, grad_mixed, log_total, q_pos, k_pos, q_seg, k_seg):
    q_len, row_width, k_len, head_count, q_step, tiles = tile_layout(
        queries, key_rows, value_rows, k_pos, k_seg
    )
    score_scale = 1.0 / HEAD**0.5

    def per_query(q_args):
        q_tile, g_tile, total_tile, qpos_tile, qseg_tile = q_args

        def tile_probs(k_tile, kpos_tile, kseg_tile):
            scores, visible = tile_scores(
                q_tile, k_tile, qpos_tile, kpos_tile, qseg_tile, kseg_tile, score_scale
            )
            return jnp.where(visible, jnp.exp(scores - total_tile[..., None]), 0.0)

        def inner_step(carry, k_args):
            k_tile, v_tile, kpos_tile, kseg_tile = k_args
            weights = tile_probs(k_tile, kpos_tile, kseg_tile)
            grad_weights = jnp.einsum(
                "qhe,khe->hqk", g_tile, v_tile, preferred_element_type=jnp.float32
            )
            return (carry + jnp.sum(weights * grad_weights, axis=-1), None)

        inner, _ = lax.scan(inner_step, jnp.zeros((head_count, q_step), jnp.float32), tiles)

        def grad_step(carry, k_args):
            k_tile, v_tile, kpos_tile, kseg_tile = k_args
            weights = tile_probs(k_tile, kpos_tile, kseg_tile)
            grad_weights = jnp.einsum(
                "qhe,khe->hqk", g_tile, v_tile, preferred_element_type=jnp.float32
            )
            grad_scores = (weights * (grad_weights - inner[..., None])).astype(jnp.bfloat16)
            carry = carry + jnp.einsum(
                "hqk,khe->qhe", grad_scores, k_tile, preferred_element_type=jnp.float32
            )
            grad_keys = jnp.einsum(
                "hqk,qhe->khe", grad_scores, q_tile, preferred_element_type=jnp.float32
            )
            grad_values = jnp.einsum(
                "hqk,qhe->khe",
                weights.astype(jnp.bfloat16),
                g_tile,
                preferred_element_type=jnp.float32,
            )
            return (carry, (grad_keys, grad_values))

        grad_q, (grad_keys, grad_values) = lax.scan(
            grad_step, jnp.zeros((q_step, head_count, HEAD), jnp.float32), tiles
        )
        return (
            grad_q * score_scale,
            grad_keys.reshape(k_len, row_width) * score_scale,
            grad_values.reshape(k_len, row_width),
        )

    q_count = q_len // q_step
    grad_q, grad_keys, grad_values = lax.map(
        per_query,
        (
            queries.reshape(q_count, q_step, head_count, HEAD),
            grad_mixed.reshape(q_count, q_step, head_count, HEAD),
            log_total,
            q_pos.reshape(q_count, q_step),
            q_seg.reshape(q_count, q_step),
        ),
    )
    return (
        grad_q.reshape(q_len, row_width),
        jnp.sum(grad_keys, axis=0),
        jnp.sum(grad_values, axis=0),
    )


def make_attention(q_pos, k_pos, q_seg, k_seg):

    def attend_fn(projected):
        key_all, value_all = gather_keys(projected)
        mixed_full, log_total = lax.map(
            lambda a: attend_one(*a), (projected[0], key_all, value_all, q_pos, k_pos, q_seg, k_seg)
        )
        return (mixed_full, (key_all, value_all, log_total))

    def attend_grad(projected, kept, grad_mixed):
        key_all, value_all, log_total = kept
        grad_q, grad_k, grad_v = lax.map(
            lambda a: attend_back(*a),
            (projected[0], key_all, value_all, grad_mixed, log_total, q_pos, k_pos, q_seg, k_seg),
        )
        grad_k, grad_v = scatter_key_grads(grad_k, grad_v)
        return jnp.stack(
            [grad_q.astype(jnp.bfloat16), grad_k.astype(jnp.bfloat16), grad_v.astype(jnp.bfloat16)]
        )

    return (attend_fn, attend_grad)


def block_forward(
    resid_in,
    gain_a,
    query_key_value_weight,
    output_weight_matrix,
    gain_m,
    up_weight_matrix,
    down_weight_matrix,
    attend_fn,
):
    attention_norm = rms_scale(resid_in, gain_a).astype(jnp.bfloat16)
    projected = jnp.einsum(
        "oym,qmh->qoyh", attention_norm, query_key_value_weight, preferred_element_type=jnp.float32
    ).astype(jnp.bfloat16)
    mixed_full, kept = attend_fn(projected)
    mixed_state = mixed_full.astype(jnp.bfloat16)
    attention_portion = jnp.einsum(
        "xtu,ua->xta", mixed_state, output_weight_matrix, preferred_element_type=jnp.float32
    )
    attn_out = tensor_sum(attention_portion)
    middle = resid_in + attn_out
    feedforward_norm = rms_scale(middle, gain_m).astype(jnp.bfloat16)
    hidden_preactivation = jnp.einsum(
        "iqp,po->iqo", feedforward_norm, up_weight_matrix, preferred_element_type=jnp.float32
    )
    hidden_activation = gelu_tanh(hidden_preactivation).astype(jnp.bfloat16)
    mlp_part = jnp.einsum(
        "euq,qt->eut", hidden_activation, down_weight_matrix, preferred_element_type=jnp.float32
    )
    mlp_out = tensor_sum(mlp_part)
    saved = (
        resid_in,
        attention_norm,
        projected,
        mixed_state,
        kept,
        middle,
        feedforward_norm,
        hidden_preactivation,
        hidden_activation,
    )
    return (attn_out, mlp_out, saved)


def block_backward(
    saved,
    grad_top,
    gain_a,
    query_key_value_weight,
    output_weight_matrix,
    gain_m,
    up_weight_matrix,
    down_weight_matrix,
    attend_grad,
):
    (
        resid_in,
        attention_norm,
        projected,
        mixed_state,
        kept,
        middle,
        feedforward_norm,
        hidden_preactivation,
        hidden_activation,
    ) = saved
    top_reduced = grad_top.astype(jnp.bfloat16)
    down_weight_gradient = jnp.einsum(
        "pgr,pgw->rw", hidden_activation, top_reduced, preferred_element_type=jnp.float32
    )
    activation_gradient = jnp.einsum(
        "ayx,cx->ayc", top_reduced, down_weight_matrix, preferred_element_type=jnp.float32
    )
    preactivation_gradient = jax.vjp(gelu_tanh, hidden_preactivation)[1](activation_gradient)[
        0
    ].astype(jnp.bfloat16)
    up_weight_gradient = jnp.einsum(
        "uzb,uzv->bv", feedforward_norm, preactivation_gradient, preferred_element_type=jnp.float32
    )
    norm_portion = jnp.einsum(
        "vok,hk->voh", preactivation_gradient, up_weight_matrix, preferred_element_type=jnp.float32
    )
    grad_norm_m = tensor_sum(norm_portion)
    grad_middle, grad_gain_m = jax.vjp(rms_scale, middle, gain_m)[1](grad_norm_m)
    grad_attn = grad_top + grad_middle
    attention_reduced = grad_attn.astype(jnp.bfloat16)
    output_weight_gradient = jnp.einsum(
        "omi,omj->ij", mixed_state, attention_reduced, preferred_element_type=jnp.float32
    )
    grad_mixed = jnp.einsum(
        "bjw,gw->bjg", attention_reduced, output_weight_matrix, preferred_element_type=jnp.float32
    ).astype(jnp.bfloat16)
    projection_gradient = attend_grad(projected, kept, grad_mixed)
    query_key_value_gradient = jnp.einsum(
        "xgt,axgf->atf", attention_norm, projection_gradient, preferred_element_type=jnp.float32
    )
    input_part = jnp.einsum(
        "gurh,gih->uri",
        projection_gradient,
        query_key_value_weight,
        preferred_element_type=jnp.float32,
    )
    grad_norm_a = tensor_sum(input_part)
    grad_resid, grad_gain_a = jax.vjp(rms_scale, resid_in, gain_a)[1](grad_norm_a)
    return (
        grad_attn,
        grad_middle,
        grad_resid,
        (
            grad_gain_a,
            query_key_value_gradient,
            output_weight_gradient,
            grad_gain_m,
            up_weight_gradient,
            down_weight_gradient,
        ),
    )


def pack_grads(grad_list, dims, groups):
    flats = []
    shapes = []
    for grad_item, which_dim in zip(grad_list, dims):
        moved = jnp.moveaxis(grad_item, which_dim, 0)
        shapes.append(moved.shape)
        flats.append(moved.reshape(groups, -1))
    return (jnp.concatenate(flats, axis=1), shapes)


def unpack_grads(summed, shapes, dims, groups):
    results = []
    offset = 0
    for moved_shape, which_dim in zip(shapes, dims):
        share_shape = (moved_shape[0] // groups,) + tuple(moved_shape[1:])
        width = math_prod(share_shape)
        piece = summed[0, offset : offset + width].reshape(share_shape)
        results.append(jnp.moveaxis(piece, 0, which_dim))
        offset = offset + width
    return tuple(results)


def math_prod(shape):
    total = 1
    for extent in shape:
        total = total * extent
    return total


def spread_grads(grad_list, dims):
    groups = lax.axis_size("dp") * lax.axis_size("ctx")
    packed, shapes = pack_grads(grad_list, dims, groups)
    summed = lax.psum_scatter(packed, ("dp", "ctx"), scatter_dimension=0, tiled=True)
    return unpack_grads(summed, shapes, dims, groups)


def plain_local(
    hidden_in,
    teacher,
    seg_ids,
    valid,
    routed_idx,
    attn_gain,
    w_qkv,
    w_out,
    mlp_gain,
    w_up,
    w_down,
    w_router,
):
    seqs_local, local_len, model_width = hidden_in.shape
    seq_len = seg_ids.shape[1]
    routed = routed_idx.shape[1]
    ctx_count = lax.axis_size("ctx")
    ctx_place = lax.axis_index("ctx")
    routed_local = routed // ctx_count
    dense_qpos = jnp.broadcast_to(
        ctx_place * local_len + jnp.arange(local_len, dtype=jnp.int32), (seqs_local, local_len)
    )
    dense_kpos = jnp.broadcast_to(jnp.arange(seq_len, dtype=jnp.int32), (seqs_local, seq_len))
    dense_qseg = lax.dynamic_slice_in_dim(seg_ids, ctx_place * local_len, local_len, 1)
    routed_seg = take_rows(seg_ids, routed_idx)
    routed_qpos = lax.dynamic_slice_in_dim(routed_idx, ctx_place * routed_local, routed_local, 1)
    routed_qseg = lax.dynamic_slice_in_dim(routed_seg, ctx_place * routed_local, routed_local, 1)
    owner_mine = routed_idx // local_len == ctx_place
    owner_row = routed_idx % local_len
    dense_attend, dense_grad = make_attention(dense_qpos, dense_kpos, dense_qseg, seg_ids)
    routed_attend, routed_grad = make_attention(routed_qpos, routed_idx, routed_qseg, routed_seg)
    x_input = hidden_in.astype(jnp.float32)
    attn_d, mlp_d, saved_d = block_forward(
        x_input, attn_gain[0], w_qkv[0], w_out[0], mlp_gain[0], w_up[0], w_down[0], dense_attend
    )
    layer_mid = saved_d[5] + mlp_d
    picked = (
        jnp.where(owner_mine[..., None], take_rows(layer_mid, owner_row), 0.0)
        .astype(jnp.bfloat16)
        .astype(jnp.float32)
    )
    chosen = to_workers(picked).astype(jnp.bfloat16).astype(jnp.float32)
    gating = gating_fn(chosen, w_router)
    attn_r, mlp_r, saved_r = block_forward(
        chosen, attn_gain[1], w_qkv[1], w_out[1], mlp_gain[1], w_up[1], w_down[1], routed_attend
    )
    branch_sum = attn_r + mlp_r
    sent_rows = (gating[..., None] * branch_sum).astype(jnp.bfloat16)
    returned = to_owners(sent_rows).astype(jnp.float32)
    layer_out = add_rows(layer_mid, owner_row, jnp.where(owner_mine[..., None], returned, 0.0))
    valid_rows = valid.astype(jnp.float32)
    error_rows = layer_out - teacher.astype(jnp.float32)
    error_sum, valid_count = lax.psum(
        (jnp.sum(valid_rows[..., None] * error_rows * error_rows), jnp.sum(valid_rows)),
        ("dp", "ctx"),
    )
    loss_value = error_sum / (valid_count * model_width)
    token_total = float(seqs_local * seq_len * lax.axis_size("dp"))
    grad_final = token_total / valid_count * valid_rows[..., None] * error_rows
    picked_grad = (
        jnp.where(owner_mine[..., None], take_rows(grad_final, owner_row), 0.0)
        .astype(jnp.bfloat16)
        .astype(jnp.float32)
    )
    branch_grad = to_workers(picked_grad).astype(jnp.bfloat16).astype(jnp.float32)
    grad_top = gating[..., None] * branch_grad
    gating_share, gating_back = jax.vjp(gating_fn, chosen, w_router)
    grad_gating = jnp.sum(branch_grad * branch_sum, axis=-1)
    grad_chosen_gate, grad_router = gating_back(grad_gating)
    grad_attn_r, grad_middle_r, grad_resid_r, grads_r = block_backward(
        saved_r,
        grad_top,
        attn_gain[1],
        w_qkv[1],
        w_out[1],
        mlp_gain[1],
        w_up[1],
        w_down[1],
        routed_grad,
    )
    grad_chosen = (grad_middle_r + grad_resid_r + grad_chosen_gate).astype(jnp.bfloat16)
    grads_r = grads_r + (grad_router,)
    spread_r = spread_grads(grads_r, (0, 1, 1, 0, 0, 1, 0))
    grad_rows = to_owners(grad_chosen).astype(jnp.float32)
    grad_mid = add_rows(grad_final, owner_row, jnp.where(owner_mine[..., None], grad_rows, 0.0))
    grad_attn_d, grad_middle_d, grad_resid_d, grads_d = block_backward(
        saved_d,
        grad_mid,
        attn_gain[0],
        w_qkv[0],
        w_out[0],
        mlp_gain[0],
        w_up[0],
        w_down[0],
        dense_grad,
    )
    grad_input = grad_attn_d + grad_resid_d
    spread_d = spread_grads(grads_d, (0, 1, 1, 0, 0, 1))
    return (
        layer_out.astype(jnp.bfloat16),
        loss_value,
        grad_input,
        jnp.stack([spread_d[0], spread_r[0]]),
        jnp.stack([spread_d[1], spread_r[1]]),
        jnp.stack([spread_d[2], spread_r[2]]),
        jnp.stack([spread_d[3], spread_r[3]]),
        jnp.stack([spread_d[4], spread_r[4]]),
        jnp.stack([spread_d[5], spread_r[5]]),
        spread_r[6],
    )


def column(row, start, length):
    wanted = start + lax.broadcasted_iota(jnp.int32, (length, 1), 0)
    hit = lax.broadcasted_iota(jnp.int32, (length, row.shape[1]), 1) == wanted
    return jnp.sum(jnp.where(hit, row, jnp.zeros_like(row)), axis=-1, keepdims=True)


def head_pair(rows):
    lane = lax.broadcasted_iota(jnp.int32, rows.shape, 1)
    zero = jnp.zeros_like(rows)
    return jnp.concatenate([jnp.where(lane < HEAD, rows, zero), jnp.where(lane >= HEAD, rows, zero)], axis=0)


def pair_join(stacked):
    half = stacked.shape[0] // 2
    lane = lax.broadcasted_iota(jnp.int32, (half, stacked.shape[1]), 1)
    return jnp.where(lane < HEAD, stacked[:half], stacked[half:])


FWD_LAGS = (1, 2, 3, 4, 5, 6)
CHUNK = 128
SUB = 2


def dense_forward_kernel(
    sizes,
    x_ref, again_ref, mgain_ref, seg_ref, valid_ref, wqkv_h, wout_h, wup_h, wdn_h,
    x2_ref, q_h, k_h, v_h, mix_h, lse_h, mid_h, pre_h, cnt_out,
    q_ref, k_ref, v_ref, mix_ref, lse_ref, mid_ref, pre_ref,
    wqkv, wout, wup, wdn, part, part2,
    sE, rE, sI, rI, sO, sE2, rE2, sX, rX, cbuf,
    wsem, osem, kvs, kvr, cs, cr, ss, rs,
):
    NC, SUBS, R, D, L, S, NT, NDP, NCTX = sizes
    RS = R // SUBS
    NM = NC * SUBS
    ln = Line()
    ctx = lax.axis_index("ctx")
    half = RS // 2
    loads = [
        pltpu.make_async_copy(wqkv_h.at[0], wqkv, wsem.at[0]),
        pltpu.make_async_copy(wout_h.at[0], wout, wsem.at[1]),
        pltpu.make_async_copy(wup_h.at[0], wup, wsem.at[2]),
        pltpu.make_async_copy(wdn_h.at[0], wdn, wsem.at[3]),
    ]
    for ld in loads:
        ld.start()
    tpeers = tensor_peers(NT)
    rpeers = row_peers(NDP, NCTX)
    greet(tpeers + rpeers)

    cbuf[0] = jnp.full((8, 128), jnp.sum(valid_ref[...].astype(F32)))
    counts = [rcopy(cbuf.at[0], cbuf.at[j + 1], cs.at[j], cr.at[j], p) for j, p in enumerate(rpeers)]
    for cp in counts:
        cp.start()

    @pl.when(ln.is_end)
    def _():
        def zero(k, _):
            rE[k] = jnp.zeros((RS, D), BF)
            return 0

        lax.fori_loop(0, NM, zero, 0)

    loads[0].wait()
    RB = 128
    again = again_ref[0:1, :]

    def project(i, _):
        rows = pl.ds(pl.multiple_of(i * RB, RB), RB)
        xv = x_ref[rows, :].astype(F32)
        n1 = (rms_parts(xv)[1] * again).astype(BF)
        for c, ref in enumerate((q_ref, k_ref, v_ref)):
            y = dot_nn(n1, wqkv[c]).astype(BF)
            if c == 0:
                ref[rows, :] = y * jnp.asarray(0.125, BF)
            else:
                ref[pl.ds(pl.multiple_of(ctx * L + i * RB, RB), RB), :] = y
        return 0

    lax.fori_loop(0, L // RB, project, 0)

    own = pl.ds(pl.multiple_of(ctx * L, L), L)

    def kv_copy(ref, which, c_to):
        return rcopy(ref.at[own, :], ref.at[own, :], kvs.at[which, c_to], kvr.at[which, ctx], {"ctx": c_to})

    def kv_arrive(c_from):
        theirs = pl.ds(c_from * L, L)
        for which, ref in enumerate((k_ref, v_ref)):
            rcopy(ref.at[theirs, :], ref.at[theirs, :], kvs.at[which, c_from], kvr.at[which, c_from], {"ctx": c_from}).wait_recv()

    for c_to in range(NCTX):
        @pl.when(c_to != ctx)
        def _(c_to=c_to):
            kv_copy(k_ref, 0, c_to).start()
            kv_copy(v_ref, 1, c_to).start()

    loads[1].wait()
    loads[2].wait()
    loads[3].wait()
    for c_from in range(NCTX - 1):
        pl.when(c_from < ctx)(functools.partial(kv_arrive, c_from))

    whole = [pltpu.make_async_copy(a, b, osem.at[n, 0]) for n, (a, b) in enumerate(((q_ref, q_h), (k_ref, k_h), (v_ref, v_h)))]
    whole[0].start()
    mgain = mgain_ref[0:1, :]
    groups = q_ref.shape[1] // 128

    def keep_copy(n, src, dst, i):
        rows = pl.ds(pl.multiple_of(i * R, R), R)
        return pltpu.make_async_copy(src.at[rows, :], dst.at[rows, :], osem.at[n, i])

    def keep_early(i):
        return (keep_copy(3, mix_ref, mix_h, i), keep_copy(4, lse_ref, lse_h, i))

    def keep_late(i):
        return (keep_copy(5, mid_ref, mid_h, i), keep_copy(6, pre_ref, pre_h, i))

    def attend(i, keys):
        rows = pl.ds(pl.multiple_of(i * R, R), R)
        qpos = ctx * L + i * R + lax.broadcasted_iota(jnp.int32, (R, 1), 0)
        qseg = column(seg_ref[...], ctx * L + i * R, R)
        kpos = lax.broadcasted_iota(jnp.int32, (1, keys), 1)
        visible = (kpos <= qpos) & (seg_ref[:, :keys] == qseg)
        bias = jnp.where(visible, 0.0, masked_value)
        lane = lax.broadcasted_iota(jnp.int32, (R, 128), 1)
        lse_tile = jnp.zeros((R, 128), F32)
        for g in range(groups):
            cols = slice(128 * g, 128 * g + 128)
            q2 = head_pair(q_ref[rows, cols])
            s = dot_nt(q2, k_ref[:keys, cols]).reshape(2, R, keys) + bias[None]
            top = jnp.max(s, axis=-1, keepdims=True)
            p = jnp.exp(s - top)
            total = jnp.sum(p, axis=-1, keepdims=True)
            pr = (p * (1.0 / total)).astype(BF).reshape(2 * R, keys)
            lse = top + jnp.log(total)
            lse_tile = jnp.where(lane == 2 * g, lse[0], jnp.where(lane == 2 * g + 1, lse[1], lse_tile))
            o = dot_nn(pr, v_ref[:keys, cols])
            mix_ref[rows, cols] = pair_join(o).astype(BF)
        lse_ref[rows, :] = lse_tile

    a1, a2, a3, a4, a5, a6 = FWD_LAGS
    lag3 = jnp.where(ln.is_end, a3, a2)
    my_rows = pl.ds(pl.multiple_of(ln.side * half, half), half)
    ot_rows = pl.ds(pl.multiple_of((1 - ln.side) * half, half), half)

    def got(buf, flow, j):
        rcopy(buf.at[j], buf.at[j], ss.at[flow, j], rs.at[flow, j], ln.mid).wait_recv()

    def got_half(rows, flow, j):
        rcopy(x2_ref.at[j, rows, :], x2_ref.at[j, rows, :], ss.at[flow, j], rs.at[flow, j], ln.mid).wait_recv()

    def each(j, fn):
        for s in range(SUBS):
            fn(j * SUBS + s)

    def body(i, _):
        @pl.when(i < NC)
        def _():
            @pl.when(ctx == 0)
            def _():
                attend(i, L)

            @pl.when(ctx > 0)
            def _():
                attend(i, S)

            for s in range(SUBS):
                m = i * SUBS + s
                p = dot_nn(mix_ref[pl.ds(pl.multiple_of(i * R + s * RS, RS), RS), :], wout[...])
                part[m] = p

                @pl.when(ln.is_end)
                def _(m=m, p=p):
                    sE[m] = p.astype(BF)
                    rcopy(sE.at[m], rE.at[m], ss.at[0, m], rs.at[0, m], ln.mid).start()

            for cp in keep_early(i):
                cp.start()

        j1 = i - a1

        @pl.when(ln.is_mid & (j1 >= 0) & (j1 < NC))
        def _():
            def forward(m):
                got(rE, 0, m)
                sI[m] = (rE[m].astype(F32) + part[m]).astype(BF)
                rcopy(sI.at[m], rI.at[m], ss.at[1, m], rs.at[1, m], ln.other).start()

            each(j1, forward)

        j3 = i - lag3

        @pl.when((j3 >= 0) & (j3 < NC))
        def _():
            def arrive(m):
                got(rI, 1, m)

                @pl.when(ln.is_mid)
                def _():
                    sO[m] = (rI[m].astype(F32) + part[m]).astype(BF)
                    rcopy(sO.at[m], rI.at[m], ss.at[2, m], rs.at[1, m], ln.end).start()

            each(j3, arrive)
            ms = pl.ds(j3 * SUBS, SUBS)
            rows = pl.ds(pl.multiple_of(j3 * R, R), R)
            total = (rI[ms].astype(F32) + part[ms] + rE[ms].astype(F32)).reshape(R, D)
            mid = x_ref[rows, :].astype(F32) + total
            mid_ref[rows, :] = mid
            n2 = (rms_parts(mid)[1] * mgain).astype(BF)
            pre = dot_nn(n2, wup[...])
            pre_ref[rows, :] = pre
            for cp in keep_late(j3):
                cp.start()
            act = (0.5 * pre * (1.0 + gelu_pair(pre))).astype(BF)
            for s in range(SUBS):
                m = j3 * SUBS + s
                p2 = dot_nn(act[s * RS : (s + 1) * RS], wdn[...])

                @pl.when(ln.is_end)
                def _(m=m, p2=p2):
                    sE2[m] = p2.astype(BF)
                    rcopy(sE2.at[m], rE2.at[m], ss.at[3, m], rs.at[3, m], ln.mid).start()

                @pl.when(ln.is_mid)
                def _(m=m, p2=p2):
                    part2[m] = p2

        j4 = i - a4

        @pl.when(ln.is_mid & (j4 >= 0) & (j4 < NC))
        def _():
            def cross(m):
                got(rE2, 3, m)
                sX[m] = (rE2[m, ot_rows, :].astype(F32) + part2[m, ot_rows, :]).astype(BF)
                rcopy(sX.at[m], rX.at[m], ss.at[4, m], rs.at[4, m], ln.other).start()

            each(j4, cross)

        j5 = i - a5

        @pl.when(ln.is_mid & (j5 >= 0) & (j5 < NC))
        def _():
            def settle(m):
                got(rX, 4, m)
                rows = pl.ds(pl.multiple_of(m * RS + ln.side * half, half), half)
                mlp = part2[m, my_rows, :] + rE2[m, my_rows, :].astype(F32) + rX[m].astype(F32)
                x2_ref[m, my_rows, :] = (mid_ref[rows, :] + mlp).astype(BF)
                mine = x2_ref.at[m, my_rows, :]
                rcopy(mine, mine, ss.at[5, m], rs.at[5, m], ln.other).start()
                rcopy(mine, mine, ss.at[6, m], rs.at[6, m], ln.end).start()

            each(j5, settle)

        j6 = i - a6

        @pl.when(ln.is_mid & (j6 >= 0) & (j6 < NC))
        def _():
            def relay(m):
                got_half(ot_rows, 5, m)
                theirs = x2_ref.at[m, ot_rows, :]
                rcopy(theirs, theirs, ss.at[7, m], rs.at[7, m], ln.end).start()

            each(j6, relay)

        return 0

    lax.fori_loop(0, NC + a6, body, 0)

    for cp in counts:
        cp.wait()
    total = cbuf[0]
    for j in range(1, len(rpeers) + 1):
        total = total + cbuf[j]
    cnt_out[...] = total

    for c in range(NCTX):
        pl.when(c > ctx)(functools.partial(kv_arrive, c))

        @pl.when(c != ctx)
        def _(c=c):
            kv_copy(k_ref, 0, c).wait_send()
            kv_copy(v_ref, 1, c).wait_send()

    whole[1].start()
    whole[2].start()
    for cp in whole:
        cp.wait()

    def kept(i, _):
        for cp in keep_early(i) + keep_late(i):
            cp.wait()
        return 0

    lax.fori_loop(0, NC, kept, 0)

    def drain(m, _):
        @pl.when(ln.is_end)
        def _():
            got_half(my_rows, 6, m)
            got_half(ot_rows, 7, m)
            rcopy(sE.at[m], rE.at[m], ss.at[0, m], rs.at[0, m], ln.mid).wait_send()
            rcopy(sE2.at[m], rE2.at[m], ss.at[3, m], rs.at[3, m], ln.mid).wait_send()

        @pl.when(ln.is_mid)
        def _():
            rcopy(sI.at[m], rI.at[m], ss.at[1, m], rs.at[1, m], ln.other).wait_send()
            rcopy(sO.at[m], rI.at[m], ss.at[2, m], rs.at[1, m], ln.end).wait_send()
            rcopy(sX.at[m], rX.at[m], ss.at[4, m], rs.at[4, m], ln.other).wait_send()
            mine = x2_ref.at[m, my_rows, :]
            theirs = x2_ref.at[m, ot_rows, :]
            rcopy(mine, mine, ss.at[5, m], rs.at[5, m], ln.other).wait_send()
            rcopy(mine, mine, ss.at[6, m], rs.at[6, m], ln.end).wait_send()
            rcopy(theirs, theirs, ss.at[7, m], rs.at[7, m], ln.end).wait_send()

        return 0

    lax.fori_loop(0, NM, drain, 0)


def dense_forward(x, again, mgain, seg, valid, w_qkv, w_out, w_up, w_down):
    L, D = x.shape
    S = seg.shape[1]
    NT, NDP, NCTX = lax.axis_size("tensor"), lax.axis_size("dp"), lax.axis_size("ctx")
    R = min(CHUNK, L)
    NC = L // R
    RS = R // SUB
    NM = NC * SUB
    Hd = w_out.shape[1]
    Fl = w_up.shape[2]
    sizes = (NC, SUB, R, D, L, S, NT, NDP, NCTX)
    flows = 8
    dma = pltpu.SemaphoreType.DMA
    rows = NDP * NCTX
    sd = jax.ShapeDtypeStruct
    v = pl.BlockSpec(memory_space=VM)
    a = pl.BlockSpec(memory_space=ANY)
    big = VM((NM, RS, D), BF)
    return pl.pallas_call(
        functools.partial(dense_forward_kernel, sizes),
        name="dense_forward",
        out_shape=(
            sd((NM, RS, D), BF), sd((L, Hd), BF), sd((S, Hd), BF), sd((S, Hd), BF), sd((L, Hd), BF),
            sd((L, 128), F32), sd((L, D), F32), sd((L, Fl), F32), sd((8, 128), F32),
        ),
        in_specs=[v] * 5 + [a] * 4,
        out_specs=(v,) + (a,) * 7 + (v,),
        scratch_shapes=[
            VM((L, Hd), BF), VM((S, Hd), BF), VM((S, Hd), BF), VM((L, Hd), BF), VM((L, 128), F32), VM((L, D), F32), VM((L, Fl), F32),
            VM((3, D, Hd), BF), VM((Hd, D), BF), VM((D, Fl), BF), VM((Fl, D), BF),
            VM((NM, RS, D), F32), VM((NM, RS, D), F32),
            big, big, big, big, big, big, big, VM((NM, RS // 2, D), BF), VM((NM, RS // 2, D), BF),
            VM((rows, 8, 128), F32),
            dma((4,)), dma((7, NC)), dma((2, NCTX)), dma((2, NCTX)), dma((rows,)), dma((rows,)), dma((flows, NM)), dma((flows, NM)),
        ],
        compiler_params=pltpu.CompilerParams(collective_id=1, has_side_effects=True, vmem_limit_bytes=58 << 20),
    )(x, again, mgain, seg, valid, w_qkv, w_out, w_up, w_down)


TAIL_LAGS = (1, 2, 3)
BCHUNK = 128


def split_pick(pick, values, terms):
    total = None
    rest = values
    for _ in range(terms):
        low = rest.astype(BF)
        got = dot_nn(pick, low)
        total = got if total is None else total + got
        rest = rest - low.astype(F32)
    return total


def gelu_slope(u, t):
    return 0.5 * (1.0 + t) + 0.5 * u * (1.0 - t * t) * (0.7978845608028654 * (1.0 + 3.0 * 0.044715 * u * u))


def backward_kernel(
    sizes,
    x_ref, valid_ref, cnt_ref, ridx_ref, seg_ref, again_ref, mgain_ref, router_ref,
    x2_h, teach_h, q_h, k_h, v_h, mix_h, lse_h, mid_h, pre_h, wqkv_h, wout_h, wup_h, wdn_h,
    hid_ref, loss_ref, gin_ref, dn_o, up_o, out_o, qkv_o, small_o,
    q_ref, k_ref, v_ref, mix_ref, lse_ref, mid_ref, g_s,
    wqkv, wout_r, wup_r, wdn_r, wout, wup, wdn,
    gm_s, act_s, gpre_s, n2_s, ga_s, part, gqkv, dk_s, dv_s,
    sE, rE, sI, rI, sO, rX,
    out_buf, odn, udn, xdn, oup, uup, xup, oout, uout, xout, oqkv, uqkv, xqkv,
    pick_s, xs, xc, tsel, tc, vsel, vc, posc, segq, n1_r, k_r, v_r, q2_r, p_r, mix_r, n2_r, act_r, slope_r, gpre_r, gm_r, ga_r, gqkv_r, dkv_r, dkvc,
    part_r, attn_o, mid_o, gate_o, branch_o, gmid_o, ggate_o, top_o, g3c, gch_s, sent_s, h_all, gq_all, sbuf, rbuf,
    psel, pc, msel, mc, qsel, qc, lsel, lc,
    acc_m, acc_a, lacc, lbuf, vec, vbuf, hbuf,
    isem, xsem, xrem, free, ps, pr_, gs, gr, kvs, kvr, s1, r1, s1d, r1d, s2, r2, s3, r3, cs, cr, ts, tr, ss, rs,
):
    NC, SUBS, R, D, L, S, RT, NT, NDP, NCTX, scale_total = sizes
    RS = R // SUBS
    NM = NC * SUBS
    RL = RT // NCTX
    Q = RL // NT
    G = NDP * NCTX
    W = D // G
    ln = Line()
    t = ln.t
    ctx = lax.axis_index("ctx")
    dp = lax.axis_index("dp")
    me = dp * NCTX + ctx
    across = {"ctx": 1 - ctx}
    half = RS // 2
    order = (
        (x2_h, hid_ref), (teach_h, gin_ref), (wqkv_h.at[1], wqkv), (wout_h.at[1], wout_r), (wup_h.at[1], wup_r), (wdn_h.at[1], wdn_r),
        (pre_h, g_s), (mid_h, mid_ref), (q_h, q_ref), (lse_h, lse_ref), (wdn_h.at[0], wdn), (wup_h.at[0], wup), (wout_h.at[0], wout),
        (k_h, k_ref), (v_h, v_ref), (mix_h, mix_ref), (wqkv_h.at[0], wqkv),
    )
    loads = [pltpu.make_async_copy(a, b, isem.at[n]) for n, (a, b) in enumerate(order)]
    for ld in loads[:16]:
        ld.start()
    tpeers = tensor_peers(NT)
    rpeers = row_peers(NDP, NCTX)
    greet(tpeers + rpeers)
    my = pl.ds(pl.multiple_of(ctx * RL, RL), RL)
    theirs = pl.ds(pl.multiple_of((1 - ctx) * RL, RL), RL)
    own = pl.ds(pl.multiple_of(t * Q, Q), Q)
    mine16 = pl.ds(pl.multiple_of(ctx * RL + t * Q, Q), Q)
    late = pl.ds(L, RL)
    again = again_ref[0:1, :]
    mgain = mgain_ref[0:1, :]
    again_r = again_ref[1:2, :]
    mgain_r = mgain_ref[1:2, :]
    router = router_ref[...]
    ga_all = xc
    scale = scale_total / cnt_ref[0:1, 0:1]
    Hd = q_ref.shape[1]
    groups = Hd // 128

    def pair(n, src, dst):
        return rcopy(src, dst, xsem.at[n], xrem.at[n], across)

    def pair_rows(n, ref):
        return pair(n, ref.at[my, :], ref.at[my, :])

    def pair_rows_in(n, ref):
        return pair(n, ref.at[theirs, :], ref.at[theirs, :])

    idxc = column(ridx_ref[...], 0, RT)
    held = idxc - ctx * L == lax.broadcasted_iota(jnp.int32, (RT, L), 1)
    pick_s[...] = held.astype(F32).astype(BF)
    loads[0].wait()
    xs[...] = dot_nn(pick_s[...], hid_ref[...].reshape(L, D)).astype(BF)
    pair(0, xs, xc).start()
    loads[1].wait()
    tsel[...] = dot_nn(pick_s[...], gin_ref[...].reshape(L, D)).astype(BF)
    vsel[...] = jnp.broadcast_to(jnp.sum(jnp.where(held, valid_ref[...].astype(F32), 0.0), axis=-1, keepdims=True), (RT, 128))
    pair(1, tsel.at[theirs, :], tc).start()
    pair(2, vsel.at[theirs, :], vc).start()
    at = idxc == lax.broadcasted_iota(jnp.int32, (RT, S), 1)
    posc[...] = jnp.broadcast_to(idxc, (RT, 128))
    seg_col = jnp.sum(jnp.where(at, seg_ref[...], 0), axis=-1, keepdims=True)
    segq[...] = jnp.broadcast_to(seg_col, (RT, 128))
    same = lax.broadcasted_iota(jnp.int32, (RT, RT), 0) == lax.broadcasted_iota(jnp.int32, (RT, RT), 1)
    seg_row = jnp.sum(jnp.where(same, seg_col, 0), axis=0, keepdims=True)
    bias_r = jnp.where((ridx_ref[...] <= posc[my, 0:1]) & (seg_row == segq[my, 0:1]), 0.0, masked_value)

    for n in range(2, 6):
        loads[n].wait()
    pair(0, xs, xc).wait()
    chosen = xs[...].astype(F32) + xc[...].astype(F32)
    xs[...] = chosen.astype(BF)
    n1 = (rms_parts(chosen)[1] * again_r).astype(BF)
    n1_r[...] = n1
    k_r[...] = dot_nn(n1, wqkv[1]).astype(BF)
    v_r[...] = dot_nn(n1, wqkv[2]).astype(BF)
    q = dot_nn(n1_r[my, :], wqkv[0]).astype(BF) * jnp.asarray(0.125, BF)
    for g in range(groups):
        cols = slice(128 * g, 128 * g + 128)
        q2 = head_pair(q[:, cols])
        s = dot_nt(q2, k_r[:, cols]).reshape(2, RL, RT) + bias_r[None]
        p = jnp.exp(s - jnp.max(s, axis=-1, keepdims=True))
        p = (p * (1.0 / jnp.sum(p, axis=-1, keepdims=True))).reshape(2 * RL, RT)
        q2_r[g] = q2
        p_r[g] = p
        mix_r[:, cols] = pair_join(dot_nn(p.astype(BF), v_r[:, cols])).astype(BF)

    def piece_copy(step, j):
        to = lax.rem(t + j, NT)
        rows = pl.ds(pl.multiple_of(to * Q, Q), Q)
        return rcopy(sbuf.at[step % 2, rows, :], rbuf.at[step, j - 1], ps.at[step, j - 1], pr_.at[step, j - 1], {"tensor": to})

    def spread(step, value):
        part_r[...] = value
        if step >= 2:
            for j in range(1, NT):
                piece_copy(step - 2, j).wait_send()
        sbuf[step % 2] = value.astype(BF)
        for j in range(1, NT):
            piece_copy(step, j).start()

    def collect(step):
        total = part_r[own, :]
        for j in range(1, NT):
            piece_copy(step, j).wait_recv()
            total = total + rbuf[step, j - 1].astype(F32)
        return total

    def gather_copy(step, ref, base_row, j):
        to = lax.rem(t + j, NT)
        rows = pl.ds(pl.multiple_of(base_row + t * Q, Q), Q)
        return rcopy(ref.at[rows, :], ref.at[rows, :], gs.at[step, j - 1], gr.at[step, j - 1], {"tensor": to})

    def gather(step, ref, base_row):
        for j in range(1, NT):
            gather_copy(step, ref, base_row, j).start()

    def gathered(step, ref, base_row):
        for j in range(1, NT):
            gather_copy(step, ref, base_row, j).wait()

    def both_of(d):
        return pl.ds(pl.multiple_of(d * NCTX * W, NCTX * W), NCTX * W)

    def by_share(piece, send, keep):
        def one(d, _):
            for lo, width, val in piece(both_of(d)):
                for c in range(NCTX):
                    rows = val[c * W : (c + 1) * W].astype(BF)

                    @pl.when(ctx == c)
                    def _(rows=rows, lo=lo, width=width):
                        keep[d, :, lo : lo + width] = rows

                    @pl.when(ctx != c)
                    def _(rows=rows, lo=lo, width=width):
                        send[d, :, lo : lo + width] = rows

            return 0

        lax.fori_loop(0, NDP, one, 0)

    bufs = (
        (out_buf, odn, udn, wdn_r, xdn, dn_o),
        (out_buf, oup, uup, wup_r, xup, up_o),
        (out_buf.at[:, :, pl.ds(0, Hd)], oout, uout, wup, xout, out_o),
        (out_buf.at[:, :, pl.ds(0, 3 * Hd)], oqkv, uqkv, wdn, xqkv, qkv_o),
    )
    widths = (act_s.shape[1], gpre_s.shape[1], Hd, 3 * Hd)
    routed_piece = (
        lambda cols: [(0, act_r.shape[1], dot_tn(gm_r[:, cols], act_r[...]))],
        lambda cols: [(0, gpre_r.shape[1], dot_tn(n2_r[:, cols], gpre_r[...]))],
        lambda cols: [(0, Hd, dot_tn(ga_r[:, cols], mix_r[...]))],
        lambda cols: [(Hd * c, Hd, dot_tn(n1_r[my, cols], gqkv_r[c])) for c in range(3)],
    )
    dense_piece = (
        lambda cols: [(0, act_s.shape[1], dot_tn(gm_s[:, cols], act_s[...]))],
        lambda cols: [(0, gpre_s.shape[1], dot_tn(n2_s[:, cols], gpre_s[...]))],
        lambda cols: [(0, Hd, dot_tn(ga_s[:, cols], mix_ref[...]))],
        lambda cols: [(Hd * c, Hd, dot_tn(sO[:, :, cols].reshape(L, NCTX * W), gqkv[c])) for c in range(3)],
    )

    def routed_pair(w):
        return rcopy(bufs[w][0], bufs[w][2], s1.at[w], r1.at[w], across)

    def dense_pair(w):
        return rcopy(bufs[w][0], bufs[w][2], s1d.at[w], r1d.at[w], across)

    def routed_dp(w, j):
        to = lax.rem(dp + j, NDP)
        return rcopy(bufs[w][1].at[to], bufs[w][4].at[j - 1], s3.at[w, j - 1], r3.at[w, j - 1], {"dp": to})

    def dense_dp(w, j):
        to = lax.rem(dp + j, NDP)
        land = bufs[w][3].at[pl.ds((j - 1) * W, W), pl.ds(0, widths[w])]
        return rcopy(bufs[w][1].at[to], land, s2.at[w, j - 1], r2.at[w, j - 1], {"dp": to})

    def add_pairs(w):
        keep, came = bufs[w][1], bufs[w][2]

        def add(j, _):
            keep[j] = (keep[j].astype(F32) + came[j].astype(F32)).astype(BF)
            return 0

        lax.fori_loop(0, NDP, add, 0)

    def routed_first(w):
        if w:
            routed_pair(w - 1).wait_send()
        by_share(routed_piece[w], bufs[w][0], bufs[w][1])
        routed_pair(w).start()

    def routed_second(w):
        routed_pair(w).wait_recv()
        add_pairs(w)
        put_total(w, 1, bufs[w][1][dp].astype(F32))
        for j in range(1, NDP):
            routed_dp(w, j).start()
        pl.semaphore_signal(free.at[w], inc=1, device_id=across, device_id_type=MESH)

    def dense_first(w):
        before = {0: routed_pair(3), 3: dense_pair(0), 1: dense_pair(3), 2: dense_pair(1)}
        before[w].wait_send()
        for j in range(1, NDP):
            routed_dp(w, j).wait_send()
        by_share(dense_piece[w], bufs[w][0], bufs[w][1])
        pl.semaphore_wait(free.at[w], 1)
        dense_pair(w).start()

    def dense_second(w):
        dense_pair(w).wait_recv()
        add_pairs(w)
        for j in range(1, NDP):
            dense_dp(w, j).start()

    def put_total(w, layer, total, more=False):
        out = bufs[w][5]
        if w == 3:
            for c in range(3):
                piece = total[:, Hd * c : Hd * c + Hd]
                out[layer, c] = out[layer, c] + piece if more else piece
        else:
            piece = total if w == 1 else total.T
            out[layer] = out[layer] + piece if more else piece

    def dense_total(w):
        for j in range(1, NDP):
            dense_dp(w, j).wait()
        total = bufs[w][1][dp].astype(F32)
        for j in range(NDP - 1):
            total = total + bufs[w][3][pl.ds(j * W, W), : widths[w]].astype(F32)
        put_total(w, 0, total)

    def routed_total(w):
        for j in range(1, NDP):
            routed_dp(w, j).wait_recv()
        total = bufs[w][4][0].astype(F32)
        for j in range(1, NDP - 1):
            total = total + bufs[w][4][j].astype(F32)
        put_total(w, 1, total, more=True)

    def got(buf, flow, m):
        rcopy(buf.at[m], buf.at[m], ss.at[flow, m], rs.at[flow, m], ln.mid).wait_recv()

    def each(j, fn):
        for s in range(SUBS):
            fn(j * SUBS + s)

    def place_of(i):
        place = ctx * L + i * R + lax.broadcasted_iota(jnp.int32, (R, 1), 0)
        return (place == ridx_ref[...]).astype(F32)

    def pick_rows():
        psel[...] = split_pick(pick_s[...], g_s[...], 2)
        pair(3, psel.at[theirs, :], pc).start()
        msel[...] = split_pick(pick_s[...], mid_ref[...], 2)
        pair(4, msel.at[theirs, :], mc).start()
        qsel[...] = dot_nn(pick_s[...], q_ref[...]).astype(BF)
        pair(5, qsel.at[theirs, :], qc).start()
        lsel[...] = split_pick(pick_s[...], lse_ref[...], 3)
        pair(6, lsel.at[theirs, :], lc).start()

    def mlp_back(i):
        rows = pl.ds(pl.multiple_of(i * R, R), R)
        ms = pl.ds(i * SUBS, SUBS)
        others = 1.0 - jnp.sum(place_of(i), axis=-1, keepdims=True)
        err = hid_ref[ms].astype(F32).reshape(R, D) - gin_ref[ms].astype(F32).reshape(R, D)
        counted = (column(valid_ref[...].astype(F32), i * R, R) * others) * err
        lacc[...] += fold8(counted * err)
        g2 = scale * counted
        gm = g2.astype(BF)
        gm_s[rows, :] = gm
        gact = dot_nt(gm, wdn[...])
        u = g_s[rows, :]
        th = gelu_pair(u)
        act_s[rows, :] = (0.5 * u * (1.0 + th)).astype(BF)
        gpre = (gact * gelu_slope(u, th)).astype(BF)
        gpre_s[rows, :] = gpre
        g_s[rows, :] = g2
        for s in range(SUBS):
            m = i * SUBS + s
            p3 = dot_nt(gpre[s * RS : (s + 1) * RS], wup[...])
            part[m] = p3

            @pl.when(ln.is_end)
            def _(m=m, p3=p3):
                sE[m] = p3.astype(BF)
                rcopy(sE.at[m], rE.at[m], ss.at[0, m], rs.at[0, m], ln.mid).start()

    def forward_in(j):
        def one(m):
            got(rE, 0, m)
            sI[m] = (rE[m].astype(F32) + part[m]).astype(BF)
            rcopy(sI.at[m], rI.at[m], ss.at[1, m], rs.at[1, m], ln.other).start()

        each(j, one)

    def forward_out(j):
        def one(m):
            got(rI, 1, m)
            sO[m] = (rI[m].astype(F32) + part[m]).astype(BF)
            rcopy(sO.at[m], rI.at[m], ss.at[2, m], rs.at[1, m], ln.end).start()

        each(j, one)

    def attend_back(q_rows, gmix, lse, bias, keys, put):
        n = bias.shape[0]
        for g in range(groups):
            cols = slice(128 * g, 128 * g + 128)
            q2 = head_pair(q_rows[:, cols])
            g2 = head_pair(gmix[:, cols])
            kg = k_ref[:keys, cols]
            vg = v_ref[:keys, cols]
            l2 = jnp.concatenate([lse[:, 2 * g : 2 * g + 1], lse[:, 2 * g + 1 : 2 * g + 2]], axis=0)
            s = (dot_nt(q2, kg).reshape(2, n, keys) + bias[None]).reshape(2 * n, keys)
            p = jnp.exp(s - l2)
            dp_ = dot_nt(g2, vg)
            inner = jnp.sum(p * dp_, axis=-1, keepdims=True)
            ds = (p * (dp_ - inner)).astype(BF)
            put(cols, (pair_join(dot_nn(ds, kg)) * 0.125).astype(BF))
            dk_s[:keys, cols] += dot_tn(ds, q2)
            dv_s[:keys, cols] += dot_tn(p.astype(BF), g2)

    def attention_back(j):
        @pl.when(ln.is_end)
        def _():
            each(j, lambda m: got(rI, 1, m))

        ms = pl.ds(j * SUBS, SUBS)
        rows = pl.ds(pl.multiple_of(j * R, R), R)
        gn2 = (rI[ms].astype(F32) + part[ms] + rE[ms].astype(F32)).reshape(R, D)
        r, unit = rms_parts(mid_ref[rows, :])
        n2_s[rows, :] = (unit * mgain).astype(BF)
        scaled = gn2 * mgain
        gmid = r * (scaled - unit * jnp.mean(scaled * unit, axis=-1, keepdims=True))
        acc_m[...] += fold8(gn2 * unit)
        gattn = g_s[rows, :] + gmid
        g_s[rows, :] = gattn
        ga = gattn.astype(BF)
        ga_s[rows, :] = ga
        gmix = dot_nt(ga, wout[...]).astype(BF)
        qpos = ctx * L + j * R + lax.broadcasted_iota(jnp.int32, (R, 1), 0)
        qseg = column(seg_ref[...], ctx * L + j * R, R)

        def put(cols, gq):
            gqkv[0, rows, cols] = gq

        def run(keys):
            kpos = lax.broadcasted_iota(jnp.int32, (1, keys), 1)
            bias = jnp.where((kpos <= qpos) & (seg_ref[:, :keys] == qseg), 0.0, masked_value)
            attend_back(q_ref[rows, :], gmix, lse_ref[rows, :], bias, keys, put)

        @pl.when(ctx == 0)
        def _():
            run(L)

        @pl.when(ctx > 0)
        def _():
            run(S)

    def send_loss():
        lbuf[me] = jnp.full((8, 128), jnp.sum(lacc[...]))
        for j, p in enumerate(rpeers):
            rcopy(lbuf.at[me], lbuf.at[me], cs.at[j], cr.at[j], p).start()

    def seg0():
        spread(0, dot_nn(mix_r[...], wout_r[...]))
        chosen_o = xs[mine16, :].astype(F32)
        gate_o[...] = jnp.broadcast_to(jax.nn.sigmoid(jnp.sum(chosen_o * router, axis=-1, keepdims=True)), (Q, 128))
        for n in range(6, 10):
            loads[n].wait()
        pick_rows()
        for n in range(10, 16):
            loads[n].wait()

    def seg1():
        attn = collect(0)
        attn_o[...] = attn
        mid = xs[mine16, :].astype(F32) + attn
        mid_o[...] = mid
        n2_r[own, :] = (rms_parts(mid)[1] * mgain_r).astype(BF)
        gather(0, n2_r, 0)

    def seg2():
        gathered(0, n2_r, 0)
        pre = dot_nn(n2_r[...], wup_r[...])
        th = gelu_pair(pre)
        act = (0.5 * pre * (1.0 + th)).astype(BF)
        act_r[...] = act
        spread(1, dot_nn(act, wdn_r[...]))
        slope_r[...] = gelu_slope(pre, th)

    def seg3():
        branch = attn_o[...] + collect(1)
        branch_o[...] = branch
        sent_s[own, :] = (gate_o[:, 0:1] * branch).astype(BF)
        gather(1, sent_s, 0)

    def seg4():
        pair(1, tsel.at[theirs, :], tc).wait()
        pair(2, vsel.at[theirs, :], vc).wait()
        chosen_m = xs[my, :].astype(F32)
        gate_m = jax.nn.sigmoid(jnp.sum(chosen_m * router, axis=-1, keepdims=True))
        target = tsel[my, :].astype(F32) + tc[...].astype(F32)
        counted = vsel[my, 0:1] + vc[:, 0:1]
        gathered(1, sent_s, 0)
        x3 = chosen_m + sent_s[...].astype(F32)
        err = x3 - target
        g3 = scale * counted * err
        gsent = g3.astype(BF).astype(F32)
        part_r[...] = gsent
        ggate_o[...] = part_r[own, :]
        top = gate_m * gsent
        part_r[...] = top
        top_o[...] = part_r[own, :]
        gm = top.astype(BF)
        gm_r[...] = gm
        gpre = (dot_nt(gm, wdn_r[...]) * slope_r[...]).astype(BF)
        gpre_r[...] = gpre
        spread(2, dot_nt(gpre, wup_r[...]))
        h_all[my, :] = x3.astype(BF)
        pair_rows(7, h_all).start()
        g3c[...] = g3
        lacc[...] += fold8(counted * err * err)
        gate = gate_o[:, 0:1]
        share = jnp.sum(ggate_o[...] * branch_o[...], axis=-1, keepdims=True) * gate * (1.0 - gate)
        ggate_o[:, 0:128] = jnp.broadcast_to(share, (Q, 128))
        vec[...] = jnp.zeros(vec.shape, F32)
        vec[4:5, :] = jnp.sum(share * xs[mine16, :].astype(F32), axis=0, keepdims=True)

    def seg5():
        gmid, gain_rows = rms_back(mid_o[...], mgain_r, collect(2))
        gmid_o[...] = gmid
        vec[3:4, :] = jnp.sum(gain_rows, axis=0, keepdims=True)
        ga_r[own, :] = (top_o[...] + gmid).astype(BF)
        gather(2, ga_r, 0)

    def seg6():
        gathered(2, ga_r, 0)
        gmix = dot_nt(ga_r[...], wout_r[...]).astype(BF)
        for g in range(groups):
            cols = slice(128 * g, 128 * g + 128)
            p = p_r[g]
            g2 = head_pair(gmix[:, cols])
            dp_ = dot_nt(g2, v_r[:, cols])
            ds = (p * (dp_ - jnp.sum(p * dp_, axis=-1, keepdims=True))).astype(BF)
            gqkv_r[0, :, cols] = (pair_join(dot_nn(ds, k_r[:, cols])) * 0.125).astype(BF)
            dkv_r[0, :, cols] = dot_tn(ds, q2_r[g])
            dkv_r[1, :, cols] = dot_tn(p.astype(BF), g2)
        swaps = [pair(8 + c, dkv_r.at[c, theirs, :], dkvc.at[c]) for c in range(2)]
        for cp in swaps:
            cp.start()
        p4 = dot_nt(gqkv_r[0], wqkv[0])
        for c in range(2):
            swaps[c].wait()
            gqkv_r[1 + c] = (dkv_r[c, my, :] + dkvc[c]).astype(BF)
            p4 = p4 + dot_nt(gqkv_r[1 + c], wqkv[1 + c])
        spread(3, p4)
        loads[16].start()

    def seg7():
        chosen_o = xs[mine16, :].astype(F32)
        gin, gain_rows = rms_back(chosen_o, again_r, collect(3))
        vec[2:3, :] = jnp.sum(gain_rows, axis=0, keepdims=True)
        gch_s[own, :] = (gmid_o[...] + gin + ggate_o[:, 0:1] * router).astype(BF)
        gather(3, gch_s, 0)

    def seg8():
        for n, (src, dst) in enumerate(((psel, pc), (msel, mc), (qsel, qc), (lsel, lc))):
            pair(3 + n, src.at[theirs, :], dst).wait()
        u = psel[my, :] + pc[...]
        th = gelu_pair(u)
        slope = gelu_slope(u, th)
        act_s[late, :] = (0.5 * u * (1.0 + th)).astype(BF)
        mid = msel[my, :] + mc[...]
        mc[...] = mid
        n2_s[late, :] = (rms_parts(mid)[1] * mgain).astype(BF)
        gathered(3, gch_s, 0)
        g2 = g3c[...] + gch_s[...].astype(F32)
        g3c[...] = g2
        gm = g2.astype(BF)
        gm_s[late, :] = gm
        gpre = (dot_nt(gm, wdn[...]) * slope).astype(BF)
        gpre_s[late, :] = gpre
        spread(4, dot_nt(gpre, wup[...]))

    def seg9():
        gmid, gain_rows = rms_back(mc[own, :], mgain, collect(4))
        vec[1:2, :] = jnp.sum(gain_rows, axis=0, keepdims=True)
        ga_all[mine16, :] = (g3c[own, :] + gmid).astype(BF)
        gather(4, ga_all, ctx * RL)

    def kv_copy(which):
        src = (dk_s, dv_s)[which]
        rows = pl.ds(pl.multiple_of((1 - ctx) * L, L), L)
        return rcopy(src.at[rows, :], mid_ref.at[:, pl.ds(which * Hd, Hd)], kvs.at[which], kvr.at[which], across)

    def seg10():
        gathered(4, ga_all, ctx * RL)
        pair_rows(10, ga_all).start()
        gmix = dot_nt(ga_all[my, :], wout[...]).astype(BF)
        kpos = lax.broadcasted_iota(jnp.int32, (1, S), 1)
        bias = jnp.where((kpos <= posc[my, 0:1]) & (seg_ref[...] == segq[my, 0:1]), 0.0, masked_value)

        def put(cols, gq):
            gq_all[my, cols] = gq

        attend_back((qsel[my, :].astype(F32) + qc[...].astype(F32)).astype(BF), gmix, lsel[my, :] + lc[...], bias, S, put)
        pl.semaphore_wait(free.at[4], 1)
        kv_copy(0).start()
        kv_copy(1).start()
        pair_rows(11, gq_all).start()

    @pl.when(ln.is_end)
    def _():
        def zero(m, _):
            rE[m] = jnp.zeros((RS, D), BF)
            return 0

        lax.fori_loop(0, NM, zero, 0)

    for ref in (dk_s, dv_s, acc_m, acc_a, lacc):
        ref[...] = jnp.zeros(ref.shape, F32)

    def mid_is_free():
        pl.semaphore_signal(free.at[4], inc=1, device_id=across, device_id_type=MESH)

    segments = (seg0, seg1, seg2, seg3, seg4, seg5, seg6, seg7, seg8, seg9)
    extras = {
        4: (lambda: routed_first(0),),
        5: (lambda: routed_first(1),),
        6: (lambda: routed_first(2), lambda: routed_second(0)),
        7: (lambda: routed_first(3), lambda: routed_second(1)),
        8: (lambda: routed_second(2),),
        9: (mid_is_free, lambda: routed_second(3), send_loss, lambda: dense_first(0)),
    }
    LF, LO, LC = CHAIN_LAGS

    def step(w, _):
        for n, fn in enumerate(segments):
            pl.when(w == n)(fn)

        for n, fns in extras.items():
            @pl.when(w == n)
            def _(fns=fns):
                for fn in fns:
                    fn()

        @pl.when(w < NC)
        def _():
            mlp_back(w)

        jf = w - LF

        @pl.when(ln.is_mid & (jf >= 0) & (jf < NC))
        def _():
            forward_in(jf)

        jo = w - LO

        @pl.when(ln.is_mid & (jo >= 0) & (jo < NC))
        def _():
            forward_out(jo)

        jc = w - LC

        @pl.when((jc >= 0) & (jc < NC))
        def _():
            attention_back(jc)

        return 0

    lax.fori_loop(0, len(segments), step, 0)
    seg10()

    def settle_sends(m, _):
        @pl.when(ln.is_end)
        def _():
            rcopy(sE.at[m], rE.at[m], ss.at[0, m], rs.at[0, m], ln.mid).wait_send()

        @pl.when(ln.is_mid)
        def _():
            rcopy(sI.at[m], rI.at[m], ss.at[1, m], rs.at[1, m], ln.other).wait_send()
            rcopy(sO.at[m], rI.at[m], ss.at[2, m], rs.at[1, m], ln.end).wait_send()

        n1_rows = x_ref[pl.ds(pl.multiple_of(m * RS, RS), RS), :].astype(F32)
        sO[m] = (rms_parts(n1_rows)[1] * again).astype(BF)
        return 0

    lax.fori_loop(0, NM, settle_sends, 0)
    pair_rows(10, ga_all).wait_send()
    pair_rows(11, gq_all).wait_send()
    pair_rows_in(10, ga_all).wait_recv()
    pair_rows_in(11, gq_all).wait_recv()
    own_keys = pl.ds(pl.multiple_of(ctx * L, L), L)
    for i in range(NC):
        rows = pl.ds(i * R, R)
        gqkv[0, rows, :] = (gqkv[0, rows, :].astype(F32) + dot_nn(place_of(i).astype(BF), gq_all[...])).astype(BF)
    loads[16].wait()
    for which, ref in enumerate((dk_s, dv_s)):
        kv_copy(which).wait()
        gqkv[1 + which] = (ref[own_keys, :] + mid_ref[:, which * Hd : which * Hd + Hd]).astype(BF)
    pair_rows(7, h_all).wait_send()
    pair_rows_in(7, h_all).wait_recv()

    b4, b5, b6 = TAIL_LAGS
    sX = sI
    rE2 = rE
    my_rows = pl.ds(pl.multiple_of(ln.side * half, half), half)
    ot_rows = pl.ds(pl.multiple_of((1 - ln.side) * half, half), half)

    def got_half(rows, flow, m):
        rcopy(gin_ref.at[m, rows, :], gin_ref.at[m, rows, :], ss.at[flow, m], rs.at[flow, m], ln.mid).wait_recv()

    def tail(i, _):
        @pl.when(i < NC)
        def _():
            for s in range(SUBS):
                m = i * SUBS + s
                rows = pl.ds(pl.multiple_of(i * R + s * RS, RS), RS)
                p4 = dot_nt(gqkv[0, rows, :], wqkv[0])
                p4 = p4 + dot_nt(gqkv[1, rows, :], wqkv[1])
                p4 = p4 + dot_nt(gqkv[2, rows, :], wqkv[2])

                @pl.when(ln.is_end)
                def _(m=m, p4=p4):
                    sE[m] = p4.astype(BF)
                    rcopy(sE.at[m], rE2.at[m], ss.at[3, m], rs.at[3, m], ln.mid).start()

                @pl.when(ln.is_mid)
                def _(m=m, p4=p4):
                    part[m] = p4

            rows = pl.ds(pl.multiple_of(i * R, R), R)
            ms = pl.ds(i * SUBS, SUBS)
            place = place_of(i)
            chosen_here = jnp.sum(place, axis=-1, keepdims=True) > 0.5
            place = place.astype(BF)
            late_ga = dot_nn(place, ga_all[...])
            g_s[rows, :] += late_ga
            ga_s[rows, :] = (ga_s[rows, :].astype(F32) + late_ga).astype(BF)
            new_hid = dot_nn(place, h_all[...])
            old_hid = hid_ref[ms].astype(F32).reshape(R, D)
            hid_ref[ms] = jnp.where(chosen_here, new_hid, old_hid).astype(BF).reshape(SUBS, RS, D)

        j4 = i - b4

        @pl.when(ln.is_mid & (j4 >= 0) & (j4 < NC))
        def _():
            def cross(m):
                got(rE2, 3, m)
                sX[m, pl.ds(0, half), :] = (rE2[m, ot_rows, :].astype(F32) + part[m, ot_rows, :]).astype(BF)
                rcopy(sX.at[m, pl.ds(0, half), :], rX.at[m], ss.at[4, m], rs.at[4, m], ln.other).start()

            each(j4, cross)

        j5 = i - b5

        @pl.when(ln.is_mid & (j5 >= 0) & (j5 < NC))
        def _():
            def settle(m):
                got(rX, 4, m)
                rows = pl.ds(pl.multiple_of(m * RS + ln.side * half, half), half)
                gn1 = part[m, my_rows, :] + rE2[m, my_rows, :].astype(F32) + rX[m].astype(F32)
                gin, gain_rows = rms_back(x_ref[rows, :].astype(F32), again, gn1)
                acc_a[...] += fold8(gain_rows)
                gin_ref[m, my_rows, :] = (g_s[rows, :] + gin).astype(BF)
                mine = gin_ref.at[m, my_rows, :]
                rcopy(mine, mine, ss.at[5, m], rs.at[5, m], ln.other).start()
                rcopy(mine, mine, ss.at[6, m], rs.at[6, m], ln.end).start()

            each(j5, settle)

        j6 = i - b6

        @pl.when(ln.is_mid & (j6 >= 0) & (j6 < NC))
        def _():
            def relay(m):
                got_half(ot_rows, 5, m)
                theirs_m = gin_ref.at[m, ot_rows, :]
                rcopy(theirs_m, theirs_m, ss.at[7, m], rs.at[7, m], ln.end).start()

            each(j6, relay)

        for n, fns in tail_extras.items():
            @pl.when(i == n)
            def _(fns=fns):
                for fn in fns:
                    fn()

        return 0

    tail_extras = {
        0: (lambda: routed_total(0), lambda: dense_second(0), lambda: dense_first(3)),
        1: (lambda: dense_first(1),),
        2: (lambda: routed_total(3), lambda: dense_second(3), lambda: dense_second(1)),
        3: (lambda: routed_total(1), lambda: routed_total(2)),
        4: (lambda: dense_first(2),),
        5: (lambda: dense_total(0),),
        6: (lambda: dense_second(2),),
    }
    lax.fori_loop(0, NC + b6, tail, 0)

    vec[0:1, :] = jnp.sum(acc_a[...], axis=0, keepdims=True)
    vec[1:2, :] = vec[1:2, :] + jnp.sum(acc_m[...], axis=0, keepdims=True) * (1.0 / NT)
    places = []
    for j in range(NDP):
        for k in range(NCTX):
            if j or k:
                places.append((lax.rem(dp + j, NDP), lax.rem(ctx + k, NCTX)))

    def cols_of(g):
        return pl.ds(pl.multiple_of(g * W, W), W)

    def vec_copy(n):
        d2, c2 = places[n]
        return rcopy(vec.at[:, cols_of(d2 * NCTX + c2)], vbuf.at[me], ts.at[n], tr.at[n], {"dp": d2, "ctx": c2})

    for n in range(G - 1):
        vec_copy(n).start()
    vbuf[me] = vec[:, cols_of(me)]
    dense_total(3)
    for n in range(G - 1):
        vec_copy(n).wait()
    rows_sum = vbuf[0]
    for j in range(1, G):
        rows_sum = rows_sum + vbuf[j]
    hbuf[t] = rows_sum

    def line_copy(n):
        return rcopy(hbuf.at[t], hbuf.at[t], ts.at[G - 1 + n], tr.at[G - 1 + n], tpeers[n])

    for n in range(NT - 1):
        line_copy(n).start()
    dense_total(1)
    dense_total(2)
    for j, p in enumerate(rpeers):
        rcopy(lbuf.at[me], lbuf.at[me], cs.at[j], cr.at[j], p).wait()
    loss = lbuf[0]
    for j in range(1, G):
        loss = loss + lbuf[j]
    loss_ref[...] = loss / (cnt_ref[...] * D)
    for n in range(NT - 1):
        line_copy(n).wait()
    line_sum = hbuf[0]
    for j in range(1, NT):
        line_sum = line_sum + hbuf[j]
    small_o[...] = line_sum

    dense_pair(2).wait_send()
    for n in (3, 4):
        for j in range(1, NT):
            piece_copy(n, j).wait_send()

    def drain(m, _):
        @pl.when(ln.is_end)
        def _():
            got_half(my_rows, 6, m)
            got_half(ot_rows, 7, m)
            rcopy(sE.at[m], rE2.at[m], ss.at[3, m], rs.at[3, m], ln.mid).wait_send()

        @pl.when(ln.is_mid)
        def _():
            rcopy(sX.at[m, pl.ds(0, half), :], rX.at[m], ss.at[4, m], rs.at[4, m], ln.other).wait_send()
            mine = gin_ref.at[m, my_rows, :]
            theirs_m = gin_ref.at[m, ot_rows, :]
            rcopy(mine, mine, ss.at[5, m], rs.at[5, m], ln.other).wait_send()
            rcopy(mine, mine, ss.at[6, m], rs.at[6, m], ln.end).wait_send()
            rcopy(theirs_m, theirs_m, ss.at[7, m], rs.at[7, m], ln.end).wait_send()

        return 0

    lax.fori_loop(0, NM, drain, 0)


CHAIN_LAGS = (2, 3, 5)


def routed_and_backward(x, x2, teacher, valid, cnt, ridx, seg, again, mgain, w_router, saved, w_qkv, w_out, w_up, w_down):
    L, D = x.shape
    S = seg.shape[1]
    RT = ridx.shape[1]
    NT, NDP, NCTX = lax.axis_size("tensor"), lax.axis_size("dp"), lax.axis_size("ctx")
    R = min(BCHUNK, L)
    NC = L // R
    RS = R // SUB
    NM = NC * SUB
    Hd = w_out.shape[1]
    Fl = w_up.shape[2]
    RL = RT // NCTX
    Q = RL // NT
    G = NDP * NCTX
    W = D // G
    HG = Hd // 128
    sizes = (NC, SUB, R, D, L, S, RT, NT, NDP, NCTX, float(S * NDP))
    dma = pltpu.SemaphoreType.DMA
    sd = jax.ShapeDtypeStruct
    v_ = pl.BlockSpec(memory_space=VM)
    a_ = pl.BlockSpec(memory_space=pltpu.HBM)
    shares = [VM((NDP, W, max(Fl, 3 * Hd)), BF)]
    for s in ((W, Fl), (W, Fl), (W, Hd), (W, 3 * Hd)):
        shares += [VM((NDP,) + s, BF)] * 2 + [VM((NDP - 1,) + s, BF)]
    big = VM((NM, RS, D), BF)
    i32 = jnp.int32
    return pl.pallas_call(
        functools.partial(backward_kernel, sizes),
        name="routed_and_backward",
        out_shape=(
            sd((NM, RS, D), BF), sd((8, 128), F32), sd((NM, RS, D), BF),
            sd((2, Fl, W), F32), sd((2, W, Fl), F32), sd((2, Hd, W), F32), sd((2, 3, W, Hd), F32), sd((8, W), F32),
        ),
        in_specs=[v_] * 8 + [a_] * 13,
        out_specs=(v_,) * 8,
        scratch_shapes=[
            VM((L, Hd), BF), VM((S, Hd), BF), VM((S, Hd), BF), VM((L, Hd), BF), VM((L, 128), F32), VM((L, D), F32), VM((L, Fl), F32),
            VM((3, D, Hd), BF), VM((Hd, D), BF), VM((D, Fl), BF), VM((Fl, D), BF), VM((Hd, D), BF), VM((D, Fl), BF), VM((Fl, D), BF),
            VM((L + RL, D), BF), VM((L + RL, Fl), BF), VM((L + RL, Fl), BF), VM((L + RL, D), BF), VM((L, D), BF),
            VM((NM, RS, D), F32), VM((3, L, Hd), BF), VM((S, Hd), F32), VM((S, Hd), F32),
            big, big, big, big, big, VM((NM, RS // 2, D), BF),
            *shares,
            VM((RT, L), BF), VM((RT, D), BF), VM((RT, D), BF), VM((RT, D), BF), VM((RL, D), BF), VM((RT, 128), F32), VM((RL, 128), F32),
            VM((RT, 128), i32), VM((RT, 128), i32), VM((RT, D), BF), VM((RT, Hd), BF), VM((RT, Hd), BF),
            VM((HG, 2 * RL, 128), BF), VM((HG, 2 * RL, RT), F32), VM((RL, Hd), BF), VM((RL, D), BF), VM((RL, Fl), BF), VM((RL, Fl), F32),
            VM((RL, Fl), BF), VM((RL, D), BF), VM((RL, D), BF), VM((3, RL, Hd), BF), VM((2, RT, Hd), F32), VM((2, RL, Hd), F32),
            VM((RL, D), F32), VM((Q, D), F32), VM((Q, D), F32), VM((Q, 128), F32), VM((Q, D), F32), VM((Q, D), F32), VM((Q, D), F32),
            VM((Q, D), F32), VM((RL, D), F32), VM((RL, D), BF), VM((RL, D), BF), VM((RT, D), BF), VM((RT, Hd), BF),
            VM((2, RL, D), BF), VM((5, NT - 1, Q, D), BF),
            VM((RT, Fl), F32), VM((RL, Fl), F32), VM((RT, D), F32), VM((RL, D), F32), VM((RT, Hd), BF), VM((RL, Hd), BF), VM((RT, 128), F32), VM((RL, 128), F32),
            VM((8, D), F32), VM((8, D), F32), VM((8, D), F32), VM((G, 8, 128), F32), VM((8, D), F32), VM((G, 8, W), F32), VM((NT, 8, W), F32),
            dma((17,)), dma((12,)), dma((12,)), pltpu.SemaphoreType.REGULAR((5,)),
            dma((5, NT)), dma((5, NT)), dma((5, NT)), dma((5, NT)), dma((2,)), dma((2,)),
            dma((4,)), dma((4,)), dma((4,)), dma((4,)), dma((4, NDP)), dma((4, NDP)), dma((4, NDP)), dma((4, NDP)),
            dma((G,)), dma((G,)), dma((G + NT,)), dma((G + NT,)), dma((8, NM)), dma((8, NM)),
        ],
        compiler_params=pltpu.CompilerParams(collective_id=2, has_side_effects=True, vmem_limit_bytes=62 << 20),
    )(
        x, valid, cnt, ridx, seg, again, mgain, w_router.reshape(1, D),
        x2, teacher.reshape(NM, RS, D), *saved, w_qkv, w_out, w_up, w_down,
    )


def finish_kernel(
    hid_h, gin_h, dn_h, up_h, out_h, qkv_h, small_h, loss_h,
    hid_o, loss_o, gin_o, ag_o, qkv_o, out_o, mg_o, up_o, dn_o, router_o,
    hid, gin, dn, up, out, qkv, small, loss, wide, sem,
):
    pairs = ((gin_h, gin), (dn_h, dn), (up_h, up), (hid_h, hid), (qkv_h, qkv), (out_h, out), (small_h, small), (loss_h, loss))
    reads = [pltpu.make_async_copy(a, b, sem.at[n]) for n, (a, b) in enumerate(pairs)]
    for cp in reads:
        cp.start()
    backs = ((wide, gin_o), (dn, dn_o), (up, up_o), (hid, hid_o), (qkv, qkv_o), (out, out_o))
    writes = [pltpu.make_async_copy(a, b, sem.at[8 + n]) for n, (a, b) in enumerate(backs)]
    for n in range(6):
        reads[n].wait()
        if n == 0:
            wide[...] = gin[...].astype(F32)
        writes[n].start()
    reads[6].wait()
    reads[7].wait()
    loss_o[...] = loss[0:1, 0:1]
    for j in range(2):
        ag_o[j : j + 1, :] = small[2 * j : 2 * j + 1, :]
        mg_o[j : j + 1, :] = small[2 * j + 1 : 2 * j + 2, :]
    router_o[...] = small[4:5, :]
    for cp in writes:
        cp.wait()


def finish(hid, gin, dn, up, out, qkv, small, loss):
    sd = jax.ShapeDtypeStruct
    v_ = pl.BlockSpec(memory_space=VM)
    h_ = pl.BlockSpec(memory_space=pltpu.HBM)
    W = small.shape[1]

    def like(arr):
        return sd(arr.shape, arr.dtype)

    ins = (hid, gin, dn, up, out, qkv, small, loss)
    return pl.pallas_call(
        finish_kernel,
        name="finish",
        out_shape=(like(hid), sd((1, 1), F32), sd(gin.shape, F32), sd((2, W), F32), like(qkv), like(out), sd((2, W), F32), like(up), like(dn), sd((1, W), F32)),
        in_specs=[h_] * 8,
        out_specs=(h_, v_, h_, v_, h_, h_, v_, h_, h_, v_),
        scratch_shapes=[*[VM(a.shape, a.dtype) for a in ins], VM(gin.shape, F32), pltpu.SemaphoreType.DMA((14,))],
        compiler_params=pltpu.CompilerParams(vmem_limit_bytes=60 << 20),
    )(*ins)


def fast_local(hidden_in, teacher, seg_ids, valid, routed_idx, attn_gain, w_qkv, w_out, mlp_gain, w_up, w_down, w_router):
    L, D = hidden_in.shape[1:]
    x2, *saved, cnt = dense_forward(hidden_in[0], attn_gain, mlp_gain, seg_ids, valid, w_qkv, w_out, w_up, w_down)
    hid, loss, gin, dn, up, out, qkv, small = routed_and_backward(
        hidden_in[0], x2, teacher[0], valid, cnt, routed_idx, seg_ids, attn_gain, mlp_gain, w_router, saved, w_qkv, w_out, w_up, w_down
    )
    hid, loss, gin, ag, qkv, out, mg, up, dn, router = finish(hid, gin, dn, up, out, qkv, small, loss)
    return (hid.reshape(1, L, D), loss[0, 0], gin.reshape(1, L, D), ag, qkv, out, mg, up, dn, router[0])


def takes_kernels(mesh):
    shape = dict(mesh.shape)
    return shape["tensor"] == 4 and shape["ctx"] == 2


def solution(mesh):
    placed = (
        P("dp", "ctx", None),
        P("dp", "ctx", None),
        P("dp", None),
        P("dp", "ctx"),
        P("dp", None),
        P(),
        P(None, None, None, "tensor"),
        P(None, "tensor", None),
        P(),
        P(None, None, "tensor"),
        P(None, "tensor", None),
        P(),
    )
    return jax.shard_map(
        fast_local if takes_kernels(mesh) else plain_local,
        mesh=mesh,
        in_specs=placed,
        out_specs=(
            P("dp", "ctx", None),
            P(),
            P("dp", "ctx", None),
            P(None, ("dp", "ctx")),
            P(None, None, ("dp", "ctx"), "tensor"),
            P(None, "tensor", ("dp", "ctx")),
            P(None, ("dp", "ctx")),
            P(None, ("dp", "ctx"), "tensor"),
            P(None, "tensor", ("dp", "ctx")),
            P(("dp", "ctx")),
        ),
        check_vma=False,
    )
```

```python
import functools

import jax
import jax.numpy as jnp
from jax import lax
from jax.experimental import pallas as pl
from jax.experimental.pallas import tpu as pltpu
from jax.sharding import PartitionSpec as P

HEAD = 64
epsilon = 1e-06
masked_value = -1e30
MESH = pl.DeviceIdType.MESH
BF = jnp.bfloat16
F32 = jnp.float32
VM = pltpu.VMEM
ANY = pl.ANY


def rcopy(src, dst, send, recv, where):
    return pltpu.make_async_remote_copy(
        src_ref=src, dst_ref=dst, send_sem=send, recv_sem=recv, device_id=where, device_id_type=MESH
    )


def dot_nn(a, b):
    return lax.dot_general(a, b, (((1,), (0,)), ((), ())), preferred_element_type=F32)


def dot_nt(a, b):
    return lax.dot_general(a, b, (((1,), (1,)), ((), ())), preferred_element_type=F32)


def dot_tn(a, b):
    return lax.dot_general(a, b, (((0,), (0,)), ((), ())), preferred_element_type=F32)


def rms_parts(values):
    r = lax.rsqrt(jnp.mean(values * values, axis=-1, keepdims=True) + epsilon)
    return r, values * r


def rms_back(values, gain, grad):
    r, unit = rms_parts(values)
    scaled = grad * gain
    return r * (scaled - unit * jnp.mean(scaled * unit, axis=-1, keepdims=True)), grad * unit


def gelu_pair(u):
    c = 0.7978845608028654
    t = jnp.tanh(c * (u + 0.044715 * (u * u * u)))
    return t


def fold8(rows):
    return jnp.sum(rows.reshape(rows.shape[0] // 8, 8, rows.shape[1]), axis=0)


class Line:
    def __init__(self):
        t = lax.axis_index("tensor")
        self.t = t
        self.side = t // 2
        self.is_end = (t == 0) | (t == 3)
        self.is_mid = (t == 1) | (t == 2)
        self.end = {"tensor": self.side * 3}
        self.mid = {"tensor": 1 + self.side}
        self.other = {"tensor": 2 - self.side}
        self.far = {"tensor": 3 - 3 * self.side}


def greet(peers):
    bar = pltpu.get_barrier_semaphore()
    for p in peers:
        pl.semaphore_signal(bar, inc=1, device_id=p, device_id_type=MESH)
    pl.semaphore_wait(bar, len(peers))


def tensor_peers(n):
    t = lax.axis_index("tensor")
    return [{"tensor": lax.rem(t + j, n)} for j in range(1, n)]


def row_peers(n_dp, n_ctx):
    d, c = lax.axis_index("dp"), lax.axis_index("ctx")
    out = []
    for j in range(n_dp):
        for k in range(n_ctx):
            if j or k:
                out.append({"dp": lax.rem(d + j, n_dp), "ctx": lax.rem(c + k, n_ctx)})
    return out


def rms_scale(values, gain):
    return values * lax.rsqrt(jnp.mean(values * values, axis=-1, keepdims=True) + epsilon) * gain


def gelu_tanh(values):
    return jax.nn.gelu(values, approximate=True)


def gating_fn(chosen, router):
    return jax.nn.sigmoid(jnp.sum(chosen * router, axis=-1))


def tensor_sum(partial_sum):
    return lax.psum(partial_sum, "tensor")


def gather_keys(projected):
    return (
        lax.all_gather(projected[1], "ctx", axis=1, tiled=True),
        lax.all_gather(projected[2], "ctx", axis=1, tiled=True),
    )


def scatter_key_grads(grad_k, grad_v):
    stacked = jnp.stack([grad_k, grad_v])
    summed = lax.psum_scatter(stacked, "ctx", scatter_dimension=2, tiled=True)
    return (summed[0], summed[1])


def to_workers(picked):
    return lax.psum_scatter(
        picked.astype(jnp.bfloat16), "ctx", scatter_dimension=1, tiled=True
    ).astype(jnp.float32)


def to_owners(rows_low):
    return lax.all_gather(rows_low, "ctx", axis=1, tiled=True)


def take_rows(table, places):
    return jax.vmap(lambda t, i: t[i])(table, places)


def add_rows(table, places, addend):
    return jax.vmap(lambda t, i, a: t.at[i].add(a))(table, places, addend)


def tile_scores(q_tile, k_tile, qpos_tile, kpos_tile, qseg_tile, kseg_tile, score_scale):
    scores = (
        jnp.einsum("qhe,khe->hqk", q_tile, k_tile, preferred_element_type=jnp.float32) * score_scale
    )
    visible = (kpos_tile[None, :] <= qpos_tile[:, None]) & (
        kseg_tile[None, :] == qseg_tile[:, None]
    )
    return (scores, visible[None])


def tile_layout(queries, key_rows, value_rows, k_pos, k_seg):
    q_len, row_width = queries.shape
    k_len = key_rows.shape[0]
    head_count = row_width // HEAD
    q_step = min(512, q_len)
    k_step = min(2048, k_len)
    k_count = k_len // k_step
    key_tiles = key_rows.reshape(k_count, k_step, head_count, HEAD)
    value_tiles = value_rows.reshape(k_count, k_step, head_count, HEAD)
    kpos_tiles = k_pos.reshape(k_count, k_step)
    kseg_tiles = k_seg.reshape(k_count, k_step)
    return (
        q_len,
        row_width,
        k_len,
        head_count,
        q_step,
        (key_tiles, value_tiles, kpos_tiles, kseg_tiles),
    )


def attend_one(queries, key_rows, value_rows, q_pos, k_pos, q_seg, k_seg):
    q_len, row_width, k_len, head_count, q_step, tiles = tile_layout(
        queries, key_rows, value_rows, k_pos, k_seg
    )
    score_scale = 1.0 / HEAD**0.5

    def per_query(q_args):
        q_tile, qpos_tile, qseg_tile = q_args

        def total_step(carry, k_args):
            running, summed = carry
            k_tile, v_tile, kpos_tile, kseg_tile = k_args
            scores, visible = tile_scores(
                q_tile, k_tile, qpos_tile, kpos_tile, qseg_tile, kseg_tile, score_scale
            )
            raised = jnp.maximum(
                running, jnp.max(jnp.where(visible, scores, masked_value), axis=-1)
            )
            weights = jnp.where(visible, jnp.exp(scores - raised[..., None]), 0.0)
            return ((raised, summed * jnp.exp(running - raised) + jnp.sum(weights, axis=-1)), None)

        initial = (
            jnp.full((head_count, q_step), masked_value, jnp.float32),
            jnp.zeros((head_count, q_step), jnp.float32),
        )
        (running, summed), _ = lax.scan(total_step, initial, tiles)
        log_total = running + jnp.log(summed)

        def value_step(output, k_args):
            k_tile, v_tile, kpos_tile, kseg_tile = k_args
            scores, visible = tile_scores(
                q_tile, k_tile, qpos_tile, kpos_tile, qseg_tile, kseg_tile, score_scale
            )
            weights_low = jnp.where(visible, jnp.exp(scores - log_total[..., None]), 0.0).astype(
                jnp.bfloat16
            )
            return (
                output
                + jnp.einsum(
                    "hqk,khe->qhe", weights_low, v_tile, preferred_element_type=jnp.float32
                ),
                None,
            )

        output, _ = lax.scan(value_step, jnp.zeros((q_step, head_count, HEAD), jnp.float32), tiles)
        return (output, log_total)

    q_count = q_len // q_step
    output, log_total = lax.map(
        per_query,
        (
            queries.reshape(q_count, q_step, head_count, HEAD),
            q_pos.reshape(q_count, q_step),
            q_seg.reshape(q_count, q_step),
        ),
    )
    return (output.reshape(q_len, row_width), log_total)


def attend_back(queries, key_rows, value_rows, grad_mixed, log_total, q_pos, k_pos, q_seg, k_seg):
    q_len, row_width, k_len, head_count, q_step, tiles = tile_layout(
        queries, key_rows, value_rows, k_pos, k_seg
    )
    score_scale = 1.0 / HEAD**0.5

    def per_query(q_args):
        q_tile, g_tile, total_tile, qpos_tile, qseg_tile = q_args

        def tile_probs(k_tile, kpos_tile, kseg_tile):
            scores, visible = tile_scores(
                q_tile, k_tile, qpos_tile, kpos_tile, qseg_tile, kseg_tile, score_scale
            )
            return jnp.where(visible, jnp.exp(scores - total_tile[..., None]), 0.0)

        def inner_step(carry, k_args):
            k_tile, v_tile, kpos_tile, kseg_tile = k_args
            weights = tile_probs(k_tile, kpos_tile, kseg_tile)
            grad_weights = jnp.einsum(
                "qhe,khe->hqk", g_tile, v_tile, preferred_element_type=jnp.float32
            )
            return (carry + jnp.sum(weights * grad_weights, axis=-1), None)

        inner, _ = lax.scan(inner_step, jnp.zeros((head_count, q_step), jnp.float32), tiles)

        def grad_step(carry, k_args):
            k_tile, v_tile, kpos_tile, kseg_tile = k_args
            weights = tile_probs(k_tile, kpos_tile, kseg_tile)
            grad_weights = jnp.einsum(
                "qhe,khe->hqk", g_tile, v_tile, preferred_element_type=jnp.float32
            )
            grad_scores = (weights * (grad_weights - inner[..., None])).astype(jnp.bfloat16)
            carry = carry + jnp.einsum(
                "hqk,khe->qhe", grad_scores, k_tile, preferred_element_type=jnp.float32
            )
            grad_keys = jnp.einsum(
                "hqk,qhe->khe", grad_scores, q_tile, preferred_element_type=jnp.float32
            )
            grad_values = jnp.einsum(
                "hqk,qhe->khe",
                weights.astype(jnp.bfloat16),
                g_tile,
                preferred_element_type=jnp.float32,
            )
            return (carry, (grad_keys, grad_values))

        grad_q, (grad_keys, grad_values) = lax.scan(
            grad_step, jnp.zeros((q_step, head_count, HEAD), jnp.float32), tiles
        )
        return (
            grad_q * score_scale,
            grad_keys.reshape(k_len, row_width) * score_scale,
            grad_values.reshape(k_len, row_width),
        )

    q_count = q_len // q_step
    grad_q, grad_keys, grad_values = lax.map(
        per_query,
        (
            queries.reshape(q_count, q_step, head_count, HEAD),
            grad_mixed.reshape(q_count, q_step, head_count, HEAD),
            log_total,
            q_pos.reshape(q_count, q_step),
            q_seg.reshape(q_count, q_step),
        ),
    )
    return (
        grad_q.reshape(q_len, row_width),
        jnp.sum(grad_keys, axis=0),
        jnp.sum(grad_values, axis=0),
    )


def make_attention(q_pos, k_pos, q_seg, k_seg):

    def attend_fn(projected):
        key_all, value_all = gather_keys(projected)
        mixed_full, log_total = lax.map(
            lambda a: attend_one(*a), (projected[0], key_all, value_all, q_pos, k_pos, q_seg, k_seg)
        )
        return (mixed_full, (key_all, value_all, log_total))

    def attend_grad(projected, kept, grad_mixed):
        key_all, value_all, log_total = kept
        grad_q, grad_k, grad_v = lax.map(
            lambda a: attend_back(*a),
            (projected[0], key_all, value_all, grad_mixed, log_total, q_pos, k_pos, q_seg, k_seg),
        )
        grad_k, grad_v = scatter_key_grads(grad_k, grad_v)
        return jnp.stack(
            [grad_q.astype(jnp.bfloat16), grad_k.astype(jnp.bfloat16), grad_v.astype(jnp.bfloat16)]
        )

    return (attend_fn, attend_grad)


def block_forward(
    resid_in,
    gain_a,
    query_key_value_weight,
    output_weight_matrix,
    gain_m,
    up_weight_matrix,
    down_weight_matrix,
    attend_fn,
):
    attention_norm = rms_scale(resid_in, gain_a).astype(jnp.bfloat16)
    projected = jnp.einsum(
        "oym,qmh->qoyh", attention_norm, query_key_value_weight, preferred_element_type=jnp.float32
    ).astype(jnp.bfloat16)
    mixed_full, kept = attend_fn(projected)
    mixed_state = mixed_full.astype(jnp.bfloat16)
    attention_portion = jnp.einsum(
        "xtu,ua->xta", mixed_state, output_weight_matrix, preferred_element_type=jnp.float32
    )
    attn_out = tensor_sum(attention_portion)
    middle = resid_in + attn_out
    feedforward_norm = rms_scale(middle, gain_m).astype(jnp.bfloat16)
    hidden_preactivation = jnp.einsum(
        "iqp,po->iqo", feedforward_norm, up_weight_matrix, preferred_element_type=jnp.float32
    )
    hidden_activation = gelu_tanh(hidden_preactivation).astype(jnp.bfloat16)
    mlp_part = jnp.einsum(
        "euq,qt->eut", hidden_activation, down_weight_matrix, preferred_element_type=jnp.float32
    )
    mlp_out = tensor_sum(mlp_part)
    saved = (
        resid_in,
        attention_norm,
        projected,
        mixed_state,
        kept,
        middle,
        feedforward_norm,
        hidden_preactivation,
        hidden_activation,
    )
    return (attn_out, mlp_out, saved)


def block_backward(
    saved,
    grad_top,
    gain_a,
    query_key_value_weight,
    output_weight_matrix,
    gain_m,
    up_weight_matrix,
    down_weight_matrix,
    attend_grad,
):
    (
        resid_in,
        attention_norm,
        projected,
        mixed_state,
        kept,
        middle,
        feedforward_norm,
        hidden_preactivation,
        hidden_activation,
    ) = saved
    top_reduced = grad_top.astype(jnp.bfloat16)
    down_weight_gradient = jnp.einsum(
        "pgr,pgw->rw", hidden_activation, top_reduced, preferred_element_type=jnp.float32
    )
    activation_gradient = jnp.einsum(
        "ayx,cx->ayc", top_reduced, down_weight_matrix, preferred_element_type=jnp.float32
    )
    preactivation_gradient = jax.vjp(gelu_tanh, hidden_preactivation)[1](activation_gradient)[
        0
    ].astype(jnp.bfloat16)
    up_weight_gradient = jnp.einsum(
        "uzb,uzv->bv", feedforward_norm, preactivation_gradient, preferred_element_type=jnp.float32
    )
    norm_portion = jnp.einsum(
        "vok,hk->voh", preactivation_gradient, up_weight_matrix, preferred_element_type=jnp.float32
    )
    grad_norm_m = tensor_sum(norm_portion)
    grad_middle, grad_gain_m = jax.vjp(rms_scale, middle, gain_m)[1](grad_norm_m)
    grad_attn = grad_top + grad_middle
    attention_reduced = grad_attn.astype(jnp.bfloat16)
    output_weight_gradient = jnp.einsum(
        "omi,omj->ij", mixed_state, attention_reduced, preferred_element_type=jnp.float32
    )
    grad_mixed = jnp.einsum(
        "bjw,gw->bjg", attention_reduced, output_weight_matrix, preferred_element_type=jnp.float32
    ).astype(jnp.bfloat16)
    projection_gradient = attend_grad(projected, kept, grad_mixed)
    query_key_value_gradient = jnp.einsum(
        "xgt,axgf->atf", attention_norm, projection_gradient, preferred_element_type=jnp.float32
    )
    input_part = jnp.einsum(
        "gurh,gih->uri",
        projection_gradient,
        query_key_value_weight,
        preferred_element_type=jnp.float32,
    )
    grad_norm_a = tensor_sum(input_part)
    grad_resid, grad_gain_a = jax.vjp(rms_scale, resid_in, gain_a)[1](grad_norm_a)
    return (
        grad_attn,
        grad_middle,
        grad_resid,
        (
            grad_gain_a,
            query_key_value_gradient,
            output_weight_gradient,
            grad_gain_m,
            up_weight_gradient,
            down_weight_gradient,
        ),
    )


def pack_grads(grad_list, dims, groups):
    flats = []
    shapes = []
    for grad_item, which_dim in zip(grad_list, dims):
        moved = jnp.moveaxis(grad_item, which_dim, 0)
        shapes.append(moved.shape)
        flats.append(moved.reshape(groups, -1))
    return (jnp.concatenate(flats, axis=1), shapes)


def unpack_grads(summed, shapes, dims, groups):
    results = []
    offset = 0
    for moved_shape, which_dim in zip(shapes, dims):
        share_shape = (moved_shape[0] // groups,) + tuple(moved_shape[1:])
        width = math_prod(share_shape)
        piece = summed[0, offset : offset + width].reshape(share_shape)
        results.append(jnp.moveaxis(piece, 0, which_dim))
        offset = offset + width
    return tuple(results)


def math_prod(shape):
    total = 1
    for extent in shape:
        total = total * extent
    return total


def spread_grads(grad_list, dims):
    groups = lax.axis_size("dp") * lax.axis_size("ctx")
    packed, shapes = pack_grads(grad_list, dims, groups)
    summed = lax.psum_scatter(packed, ("dp", "ctx"), scatter_dimension=0, tiled=True)
    return unpack_grads(summed, shapes, dims, groups)


def plain_local(
    hidden_in,
    teacher,
    seg_ids,
    valid,
    routed_idx,
    attn_gain,
    w_qkv,
    w_out,
    mlp_gain,
    w_up,
    w_down,
    w_router,
):
    seqs_local, local_len, model_width = hidden_in.shape
    seq_len = seg_ids.shape[1]
    routed = routed_idx.shape[1]
    ctx_count = lax.axis_size("ctx")
    ctx_place = lax.axis_index("ctx")
    routed_local = routed // ctx_count
    dense_qpos = jnp.broadcast_to(
        ctx_place * local_len + jnp.arange(local_len, dtype=jnp.int32), (seqs_local, local_len)
    )
    dense_kpos = jnp.broadcast_to(jnp.arange(seq_len, dtype=jnp.int32), (seqs_local, seq_len))
    dense_qseg = lax.dynamic_slice_in_dim(seg_ids, ctx_place * local_len, local_len, 1)
    routed_seg = take_rows(seg_ids, routed_idx)
    routed_qpos = lax.dynamic_slice_in_dim(routed_idx, ctx_place * routed_local, routed_local, 1)
    routed_qseg = lax.dynamic_slice_in_dim(routed_seg, ctx_place * routed_local, routed_local, 1)
    owner_mine = routed_idx // local_len == ctx_place
    owner_row = routed_idx % local_len
    dense_attend, dense_grad = make_attention(dense_qpos, dense_kpos, dense_qseg, seg_ids)
    routed_attend, routed_grad = make_attention(routed_qpos, routed_idx, routed_qseg, routed_seg)
    x_input = hidden_in.astype(jnp.float32)
    attn_d, mlp_d, saved_d = block_forward(
        x_input, attn_gain[0], w_qkv[0], w_out[0], mlp_gain[0], w_up[0], w_down[0], dense_attend
    )
    layer_mid = saved_d[5] + mlp_d
    picked = (
        jnp.where(owner_mine[..., None], take_rows(layer_mid, owner_row), 0.0)
        .astype(jnp.bfloat16)
        .astype(jnp.float32)
    )
    chosen = to_workers(picked).astype(jnp.bfloat16).astype(jnp.float32)
    gating = gating_fn(chosen, w_router)
    attn_r, mlp_r, saved_r = block_forward(
        chosen, attn_gain[1], w_qkv[1], w_out[1], mlp_gain[1], w_up[1], w_down[1], routed_attend
    )
    branch_sum = attn_r + mlp_r
    sent_rows = (gating[..., None] * branch_sum).astype(jnp.bfloat16)
    returned = to_owners(sent_rows).astype(jnp.float32)
    layer_out = add_rows(layer_mid, owner_row, jnp.where(owner_mine[..., None], returned, 0.0))
    valid_rows = valid.astype(jnp.float32)
    error_rows = layer_out - teacher.astype(jnp.float32)
    error_sum, valid_count = lax.psum(
        (jnp.sum(valid_rows[..., None] * error_rows * error_rows), jnp.sum(valid_rows)),
        ("dp", "ctx"),
    )
    loss_value = error_sum / (valid_count * model_width)
    token_total = float(seqs_local * seq_len * lax.axis_size("dp"))
    grad_final = token_total / valid_count * valid_rows[..., None] * error_rows
    picked_grad = (
        jnp.where(owner_mine[..., None], take_rows(grad_final, owner_row), 0.0)
        .astype(jnp.bfloat16)
        .astype(jnp.float32)
    )
    branch_grad = to_workers(picked_grad).astype(jnp.bfloat16).astype(jnp.float32)
    grad_top = gating[..., None] * branch_grad
    gating_share, gating_back = jax.vjp(gating_fn, chosen, w_router)
    grad_gating = jnp.sum(branch_grad * branch_sum, axis=-1)
    grad_chosen_gate, grad_router = gating_back(grad_gating)
    grad_attn_r, grad_middle_r, grad_resid_r, grads_r = block_backward(
        saved_r,
        grad_top,
        attn_gain[1],
        w_qkv[1],
        w_out[1],
        mlp_gain[1],
        w_up[1],
        w_down[1],
        routed_grad,
    )
    grad_chosen = (grad_middle_r + grad_resid_r + grad_chosen_gate).astype(jnp.bfloat16)
    grads_r = grads_r + (grad_router,)
    spread_r = spread_grads(grads_r, (0, 1, 1, 0, 0, 1, 0))
    grad_rows = to_owners(grad_chosen).astype(jnp.float32)
    grad_mid = add_rows(grad_final, owner_row, jnp.where(owner_mine[..., None], grad_rows, 0.0))
    grad_attn_d, grad_middle_d, grad_resid_d, grads_d = block_backward(
        saved_d,
        grad_mid,
        attn_gain[0],
        w_qkv[0],
        w_out[0],
        mlp_gain[0],
        w_up[0],
        w_down[0],
        dense_grad,
    )
    grad_input = grad_attn_d + grad_resid_d
    spread_d = spread_grads(grads_d, (0, 1, 1, 0, 0, 1))
    return (
        layer_out.astype(jnp.bfloat16),
        loss_value,
        grad_input,
        jnp.stack([spread_d[0], spread_r[0]]),
        jnp.stack([spread_d[1], spread_r[1]]),
        jnp.stack([spread_d[2], spread_r[2]]),
        jnp.stack([spread_d[3], spread_r[3]]),
        jnp.stack([spread_d[4], spread_r[4]]),
        jnp.stack([spread_d[5], spread_r[5]]),
        spread_r[6],
    )


def column(row, start, length):
    wanted = start + lax.broadcasted_iota(jnp.int32, (length, 1), 0)
    hit = lax.broadcasted_iota(jnp.int32, (length, row.shape[1]), 1) == wanted
    return jnp.sum(jnp.where(hit, row, jnp.zeros_like(row)), axis=-1, keepdims=True)


def head_pair(rows):
    lane = lax.broadcasted_iota(jnp.int32, rows.shape, 1)
    zero = jnp.zeros_like(rows)
    return jnp.concatenate([jnp.where(lane < HEAD, rows, zero), jnp.where(lane >= HEAD, rows, zero)], axis=0)


def pair_join(stacked):
    half = stacked.shape[0] // 2
    lane = lax.broadcasted_iota(jnp.int32, (half, stacked.shape[1]), 1)
    return jnp.where(lane < HEAD, stacked[:half], stacked[half:])


FWD_LAGS = (1, 2, 3, 4, 5, 6)
CHUNK = 128
SUB = 2
FSUB = 2


def dense_forward_kernel(
    sizes,
    x_ref, again_ref, mgain_ref, seg_ref, valid_ref, wqkv_h, wout_h, wup_h, wdn_h,
    x2_ref, q_h, k_h, v_h, mix_h, lse_h, mid_h, pre_h, cnt_out,
    q_ref, k_ref, v_ref, mix_ref, lse_ref, mid_ref, pre_ref,
    wqkv, wout, wup, wdn, part, part2,
    sE, rE, sI, rI, sO, sE2, rE2, sX, rX, cbuf,
    wsem, osem, kvs, kvr, cs, cr, ss, rs,
):
    NC, SUBS, R, D, L, S, NT, NDP, NCTX = sizes
    RS = R // SUBS
    NM = NC * SUBS
    ln = Line()
    ctx = lax.axis_index("ctx")
    half = RS // 2
    loads = [
        pltpu.make_async_copy(wqkv_h.at[0], wqkv, wsem.at[0]),
        pltpu.make_async_copy(wout_h.at[0], wout, wsem.at[1]),
        pltpu.make_async_copy(wup_h.at[0], wup, wsem.at[2]),
        pltpu.make_async_copy(wdn_h.at[0], wdn, wsem.at[3]),
    ]
    for ld in loads:
        ld.start()
    tpeers = tensor_peers(NT)
    rpeers = row_peers(NDP, NCTX)
    greet(tpeers + rpeers)

    cbuf[0] = jnp.full((8, 128), jnp.sum(valid_ref[...].astype(F32)))
    counts = [rcopy(cbuf.at[0], cbuf.at[j + 1], cs.at[j], cr.at[j], p) for j, p in enumerate(rpeers)]
    for cp in counts:
        cp.start()

    @pl.when(ln.is_end)
    def _():
        def zero(k, _):
            rE[k] = jnp.zeros((RS, D), BF)
            return 0

        lax.fori_loop(0, NM, zero, 0)

    loads[0].wait()
    RB = 128
    again = again_ref[0:1, :]

    def project(i, _):
        rows = pl.ds(pl.multiple_of(i * RB, RB), RB)
        xv = x_ref[rows, :].astype(F32)
        n1 = (rms_parts(xv)[1] * again).astype(BF)
        for c, ref in enumerate((q_ref, k_ref, v_ref)):
            y = dot_nn(n1, wqkv[c]).astype(BF)
            if c == 0:
                ref[rows, :] = y * jnp.asarray(0.125, BF)
            else:
                ref[pl.ds(pl.multiple_of(ctx * L + i * RB, RB), RB), :] = y
        return 0

    lax.fori_loop(0, L // RB, project, 0)

    own = pl.ds(pl.multiple_of(ctx * L, L), L)

    def kv_copy(ref, which, c_to):
        return rcopy(ref.at[own, :], ref.at[own, :], kvs.at[which, c_to], kvr.at[which, ctx], {"ctx": c_to})

    def kv_arrive(c_from):
        theirs = pl.ds(c_from * L, L)
        for which, ref in enumerate((k_ref, v_ref)):
            rcopy(ref.at[theirs, :], ref.at[theirs, :], kvs.at[which, c_from], kvr.at[which, c_from], {"ctx": c_from}).wait_recv()

    for c_to in range(NCTX):
        @pl.when(c_to != ctx)
        def _(c_to=c_to):
            kv_copy(k_ref, 0, c_to).start()
            kv_copy(v_ref, 1, c_to).start()

    loads[1].wait()
    loads[2].wait()
    loads[3].wait()
    for c_from in range(NCTX - 1):
        pl.when(c_from < ctx)(functools.partial(kv_arrive, c_from))

    whole = [pltpu.make_async_copy(a, b, osem.at[n, 0]) for n, (a, b) in enumerate(((q_ref, q_h), (k_ref, k_h), (v_ref, v_h)))]
    whole[0].start()
    mgain = mgain_ref[0:1, :]
    groups = q_ref.shape[1] // 128

    def keep_copy(n, src, dst, i):
        rows = pl.ds(pl.multiple_of(i * R, R), R)
        return pltpu.make_async_copy(src.at[rows, :], dst.at[rows, :], osem.at[n, i])

    def keep_early(i):
        return (keep_copy(3, mix_ref, mix_h, i), keep_copy(4, lse_ref, lse_h, i))

    def keep_late(i):
        return (keep_copy(5, mid_ref, mid_h, i), keep_copy(6, pre_ref, pre_h, i))

    def attend(i, keys):
        rows = pl.ds(pl.multiple_of(i * R, R), R)
        qpos = ctx * L + i * R + lax.broadcasted_iota(jnp.int32, (R, 1), 0)
        qseg = column(seg_ref[...], ctx * L + i * R, R)
        kpos = lax.broadcasted_iota(jnp.int32, (1, keys), 1)
        visible = (kpos <= qpos) & (seg_ref[:, :keys] == qseg)
        bias = jnp.where(visible, 0.0, masked_value)
        lane = lax.broadcasted_iota(jnp.int32, (R, 128), 1)
        lse_tile = jnp.zeros((R, 128), F32)
        for g in range(groups):
            cols = slice(128 * g, 128 * g + 128)
            q2 = head_pair(q_ref[rows, cols])
            s = dot_nt(q2, k_ref[:keys, cols]).reshape(2, R, keys) + bias[None]
            top = jnp.max(s, axis=-1, keepdims=True)
            p = jnp.exp(s - top)
            total = jnp.sum(p, axis=-1, keepdims=True)
            pr = (p * (1.0 / total)).astype(BF).reshape(2 * R, keys)
            lse = top + jnp.log(total)
            lse_tile = jnp.where(lane == 2 * g, lse[0], jnp.where(lane == 2 * g + 1, lse[1], lse_tile))
            o = dot_nn(pr, v_ref[:keys, cols])
            mix_ref[rows, cols] = pair_join(o).astype(BF)
        lse_ref[rows, :] = lse_tile

    a1, a2, a3, a4, a5, a6 = FWD_LAGS
    lag3 = jnp.where(ln.is_end, a3, a2)
    my_rows = pl.ds(pl.multiple_of(ln.side * half, half), half)
    ot_rows = pl.ds(pl.multiple_of((1 - ln.side) * half, half), half)

    def got(buf, flow, j):
        rcopy(buf.at[j], buf.at[j], ss.at[flow, j], rs.at[flow, j], ln.mid).wait_recv()

    def got_half(rows, flow, j):
        rcopy(x2_ref.at[j, rows, :], x2_ref.at[j, rows, :], ss.at[flow, j], rs.at[flow, j], ln.mid).wait_recv()

    def each(j, fn):
        for s in range(SUBS):
            fn(j * SUBS + s)

    def body(i, _):
        @pl.when(i < NC)
        def _():
            @pl.when(ctx == 0)
            def _():
                attend(i, L)

            @pl.when(ctx > 0)
            def _():
                attend(i, S)

            for s in range(SUBS):
                m = i * SUBS + s
                p = dot_nn(mix_ref[pl.ds(pl.multiple_of(i * R + s * RS, RS), RS), :], wout[...])
                part[m] = p

                @pl.when(ln.is_end)
                def _(m=m, p=p):
                    sE[m] = p.astype(BF)
                    rcopy(sE.at[m], rE.at[m], ss.at[0, m], rs.at[0, m], ln.mid).start()

            for cp in keep_early(i):
                cp.start()

        j1 = i - a1

        @pl.when(ln.is_mid & (j1 >= 0) & (j1 < NC))
        def _():
            def forward(m):
                got(rE, 0, m)
                sI[m] = (rE[m].astype(F32) + part[m]).astype(BF)
                rcopy(sI.at[m], rI.at[m], ss.at[1, m], rs.at[1, m], ln.other).start()

            each(j1, forward)

        j3 = i - lag3

        @pl.when((j3 >= 0) & (j3 < NC))
        def _():
            def arrive(m):
                got(rI, 1, m)

                @pl.when(ln.is_mid)
                def _():
                    sO[m] = (rI[m].astype(F32) + part[m]).astype(BF)
                    rcopy(sO.at[m], rI.at[m], ss.at[2, m], rs.at[1, m], ln.end).start()

            each(j3, arrive)
            ms = pl.ds(j3 * SUBS, SUBS)
            rows = pl.ds(pl.multiple_of(j3 * R, R), R)
            total = (rI[ms].astype(F32) + part[ms] + rE[ms].astype(F32)).reshape(R, D)
            mid = x_ref[rows, :].astype(F32) + total
            mid_ref[rows, :] = mid
            n2 = (rms_parts(mid)[1] * mgain).astype(BF)
            pre = dot_nn(n2, wup[...])
            pre_ref[rows, :] = pre
            for cp in keep_late(j3):
                cp.start()
            act = (0.5 * pre * (1.0 + gelu_pair(pre))).astype(BF)
            for s in range(SUBS):
                m = j3 * SUBS + s
                p2 = dot_nn(act[s * RS : (s + 1) * RS], wdn[...])

                @pl.when(ln.is_end)
                def _(m=m, p2=p2):
                    sE2[m] = p2.astype(BF)
                    rcopy(sE2.at[m], rE2.at[m], ss.at[3, m], rs.at[3, m], ln.mid).start()

                @pl.when(ln.is_mid)
                def _(m=m, p2=p2):
                    part2[m] = p2

        j6 = i - a6

        @pl.when(ln.is_mid & (j6 >= 0) & (j6 < NC))
        def _():
            def relay(m):
                got_half(ot_rows, 5, m)
                theirs = x2_ref.at[m, ot_rows, :]
                rcopy(theirs, theirs, ss.at[7, m], rs.at[7, m], ln.end).start()

            each(j6, relay)

        j5 = i - a5

        @pl.when(ln.is_mid & (j5 >= 0) & (j5 < NC))
        def _():
            def settle(m):
                got(rX, 4, m)
                rows = pl.ds(pl.multiple_of(m * RS + ln.side * half, half), half)
                mlp = part2[m, my_rows, :] + rE2[m, my_rows, :].astype(F32) + rX[m].astype(F32)
                x2_ref[m, my_rows, :] = (mid_ref[rows, :] + mlp).astype(BF)
                mine = x2_ref.at[m, my_rows, :]
                rcopy(mine, mine, ss.at[5, m], rs.at[5, m], ln.other).start()
                rcopy(mine, mine, ss.at[6, m], rs.at[6, m], ln.end).start()

            each(j5, settle)

        j4 = i - a4

        @pl.when(ln.is_mid & (j4 >= 0) & (j4 < NC))
        def _():
            def cross(m):
                got(rE2, 3, m)
                sX[m] = (rE2[m, ot_rows, :].astype(F32) + part2[m, ot_rows, :]).astype(BF)
                rcopy(sX.at[m], rX.at[m], ss.at[4, m], rs.at[4, m], ln.other).start()

            each(j4, cross)

        return 0

    lax.fori_loop(0, NC + a6, body, 0)

    for cp in counts:
        cp.wait()
    total = cbuf[0]
    for j in range(1, len(rpeers) + 1):
        total = total + cbuf[j]
    cnt_out[...] = total

    for c in range(NCTX):
        pl.when(c > ctx)(functools.partial(kv_arrive, c))

        @pl.when(c != ctx)
        def _(c=c):
            kv_copy(k_ref, 0, c).wait_send()
            kv_copy(v_ref, 1, c).wait_send()

    whole[1].start()
    whole[2].start()
    for cp in whole:
        cp.wait()

    def kept(i, _):
        for cp in keep_early(i) + keep_late(i):
            cp.wait()
        return 0

    lax.fori_loop(0, NC, kept, 0)

    def drain(m, _):
        @pl.when(ln.is_end)
        def _():
            got_half(my_rows, 6, m)
            got_half(ot_rows, 7, m)
            rcopy(sE.at[m], rE.at[m], ss.at[0, m], rs.at[0, m], ln.mid).wait_send()
            rcopy(sE2.at[m], rE2.at[m], ss.at[3, m], rs.at[3, m], ln.mid).wait_send()

        @pl.when(ln.is_mid)
        def _():
            rcopy(sI.at[m], rI.at[m], ss.at[1, m], rs.at[1, m], ln.other).wait_send()
            rcopy(sO.at[m], rI.at[m], ss.at[2, m], rs.at[1, m], ln.end).wait_send()
            rcopy(sX.at[m], rX.at[m], ss.at[4, m], rs.at[4, m], ln.other).wait_send()
            mine = x2_ref.at[m, my_rows, :]
            theirs = x2_ref.at[m, ot_rows, :]
            rcopy(mine, mine, ss.at[5, m], rs.at[5, m], ln.other).wait_send()
            rcopy(mine, mine, ss.at[6, m], rs.at[6, m], ln.end).wait_send()
            rcopy(theirs, theirs, ss.at[7, m], rs.at[7, m], ln.end).wait_send()

        return 0

    lax.fori_loop(0, NM, drain, 0)


def dense_forward(x, again, mgain, seg, valid, w_qkv, w_out, w_up, w_down):
    L, D = x.shape
    S = seg.shape[1]
    NT, NDP, NCTX = lax.axis_size("tensor"), lax.axis_size("dp"), lax.axis_size("ctx")
    R = min(CHUNK, L)
    NC = L // R
    RS = R // FSUB
    NM = NC * FSUB
    Hd = w_out.shape[1]
    Fl = w_up.shape[2]
    sizes = (NC, FSUB, R, D, L, S, NT, NDP, NCTX)
    flows = 8
    dma = pltpu.SemaphoreType.DMA
    rows = NDP * NCTX
    sd = jax.ShapeDtypeStruct
    v = pl.BlockSpec(memory_space=VM)
    a = pl.BlockSpec(memory_space=ANY)
    big = VM((NM, RS, D), BF)
    return pl.pallas_call(
        functools.partial(dense_forward_kernel, sizes),
        name="dense_forward",
        out_shape=(
            sd((NM, RS, D), BF), sd((L, Hd), BF), sd((S, Hd), BF), sd((S, Hd), BF), sd((L, Hd), BF),
            sd((L, 128), F32), sd((L, D), F32), sd((L, Fl), F32), sd((8, 128), F32),
        ),
        in_specs=[v] * 5 + [a] * 4,
        out_specs=(v,) + (a,) * 7 + (v,),
        scratch_shapes=[
            VM((L, Hd), BF), VM((S, Hd), BF), VM((S, Hd), BF), VM((L, Hd), BF), VM((L, 128), F32), VM((L, D), F32), VM((L, Fl), F32),
            VM((3, D, Hd), BF), VM((Hd, D), BF), VM((D, Fl), BF), VM((Fl, D), BF),
            VM((NM, RS, D), F32), VM((NM, RS, D), F32),
            big, big, big, big, big, big, big, VM((NM, RS // 2, D), BF), VM((NM, RS // 2, D), BF),
            VM((rows, 8, 128), F32),
            dma((4,)), dma((7, NC)), dma((2, NCTX)), dma((2, NCTX)), dma((rows,)), dma((rows,)), dma((flows, NM)), dma((flows, NM)),
        ],
        compiler_params=pltpu.CompilerParams(collective_id=1, has_side_effects=True, vmem_limit_bytes=58 << 20),
    )(x, again, mgain, seg, valid, w_qkv, w_out, w_up, w_down)


TAIL_LAGS = (1, 2, 3)
BCHUNK = 128


def split_pick(pick, values, terms):
    total = None
    rest = values
    for _ in range(terms):
        low = rest.astype(BF)
        got = dot_nn(pick, low)
        total = got if total is None else total + got
        rest = rest - low.astype(F32)
    return total


def gelu_slope(u, t):
    return 0.5 * (1.0 + t) + 0.5 * u * (1.0 - t * t) * (0.7978845608028654 * (1.0 + 3.0 * 0.044715 * u * u))


def backward_kernel(
    sizes,
    x_ref, valid_ref, cnt_ref, ridx_ref, seg_ref, again_ref, mgain_ref, router_ref,
    x2_h, teach_h, q_h, k_h, v_h, mix_h, lse_h, mid_h, pre_h, wqkv_h, wout_h, wup_h, wdn_h,
    hid_ref, loss_ref, gin_ref, dn_o, up_o, out_o, qkv_o, small_o,
    q_ref, k_ref, v_ref, mix_ref, lse_ref, mid_ref, g_s,
    wqkv, wout_r, wup_r, wdn_r, wout, wup, wdn,
    gm_s, act_s, gpre_s, n2_s, ga_s, part, gqkv, dk_s, dv_s,
    sE, rE, sI, rI, sO, rX,
    out_buf, odn, udn, xdn, oup, uup, xup, oout, uout, xout, oqkv, uqkv, xqkv,
    pick_s, xs, xc, tsel, tc, vsel, vc, posc, segq, n1_r, k_r, v_r, q2_r, p_r, mix_r, n2_r, act_r, slope_r, gpre_r, gm_r, ga_r, gqkv_r, dkv_r, dkvc,
    part_r, attn_o, mid_o, gate_o, branch_o, gmid_o, ggate_o, top_o, g3c, gch_s, sent_s, h_all, gq_all, sbuf, rbuf,
    psel, pc, msel, mc, qsel, qc, lsel, lc,
    acc_m, acc_a, lacc, lbuf, vec, vbuf, hbuf,
    isem, xsem, xrem, free, ps, pr_, gs, gr, kvs, kvr, s1, r1, s1d, r1d, s2, r2, s3, r3, cs, cr, ts, tr, ss, rs,
):
    NC, SUBS, R, D, L, S, RT, NT, NDP, NCTX, scale_total = sizes
    RS = R // SUBS
    NM = NC * SUBS
    RL = RT // NCTX
    Q = RL // NT
    G = NDP * NCTX
    W = D // G
    ln = Line()
    t = ln.t
    ctx = lax.axis_index("ctx")
    dp = lax.axis_index("dp")
    me = dp * NCTX + ctx
    across = {"ctx": 1 - ctx}
    half = RS // 2
    order = (
        (x2_h, hid_ref), (teach_h, gin_ref), (wqkv_h.at[1], wqkv), (wout_h.at[1], wout_r), (wup_h.at[1], wup_r), (wdn_h.at[1], wdn_r),
        (pre_h, g_s), (mid_h, mid_ref), (q_h, q_ref), (lse_h, lse_ref), (wdn_h.at[0], wdn), (wup_h.at[0], wup), (wout_h.at[0], wout),
        (k_h, k_ref), (v_h, v_ref), (mix_h, mix_ref), (wqkv_h.at[0], wqkv),
    )
    loads = [pltpu.make_async_copy(a, b, isem.at[n]) for n, (a, b) in enumerate(order)]
    for ld in loads[:16]:
        ld.start()
    tpeers = tensor_peers(NT)
    rpeers = row_peers(NDP, NCTX)
    greet(tpeers + rpeers)
    my = pl.ds(pl.multiple_of(ctx * RL, RL), RL)
    theirs = pl.ds(pl.multiple_of((1 - ctx) * RL, RL), RL)
    own = pl.ds(pl.multiple_of(t * Q, Q), Q)
    mine16 = pl.ds(pl.multiple_of(ctx * RL + t * Q, Q), Q)
    late = pl.ds(L, RL)
    again = again_ref[0:1, :]
    mgain = mgain_ref[0:1, :]
    again_r = again_ref[1:2, :]
    mgain_r = mgain_ref[1:2, :]
    router = router_ref[...]
    ga_all = xc
    scale = scale_total / cnt_ref[0:1, 0:1]
    Hd = q_ref.shape[1]
    groups = Hd // 128

    def pair(n, src, dst):
        return rcopy(src, dst, xsem.at[n], xrem.at[n], across)

    def pair_rows(n, ref):
        return pair(n, ref.at[my, :], ref.at[my, :])

    def pair_rows_in(n, ref):
        return pair(n, ref.at[theirs, :], ref.at[theirs, :])

    idxc = column(ridx_ref[...], 0, RT)
    held = idxc - ctx * L == lax.broadcasted_iota(jnp.int32, (RT, L), 1)
    pick_s[...] = held.astype(F32).astype(BF)
    loads[0].wait()
    xs[...] = dot_nn(pick_s[...], hid_ref[...].reshape(L, D)).astype(BF)
    pair(0, xs, xc).start()
    loads[1].wait()
    tsel[...] = dot_nn(pick_s[...], gin_ref[...].reshape(L, D)).astype(BF)
    vsel[...] = jnp.broadcast_to(jnp.sum(jnp.where(held, valid_ref[...].astype(F32), 0.0), axis=-1, keepdims=True), (RT, 128))
    pair(1, tsel.at[theirs, :], tc).start()
    pair(2, vsel.at[theirs, :], vc).start()
    at = idxc == lax.broadcasted_iota(jnp.int32, (RT, S), 1)
    posc[...] = jnp.broadcast_to(idxc, (RT, 128))
    seg_col = jnp.sum(jnp.where(at, seg_ref[...], 0), axis=-1, keepdims=True)
    segq[...] = jnp.broadcast_to(seg_col, (RT, 128))
    same = lax.broadcasted_iota(jnp.int32, (RT, RT), 0) == lax.broadcasted_iota(jnp.int32, (RT, RT), 1)
    seg_row = jnp.sum(jnp.where(same, seg_col, 0), axis=0, keepdims=True)
    bias_r = jnp.where((ridx_ref[...] <= posc[my, 0:1]) & (seg_row == segq[my, 0:1]), 0.0, masked_value)

    for n in range(2, 6):
        loads[n].wait()
    pair(0, xs, xc).wait()
    chosen = xs[...].astype(F32) + xc[...].astype(F32)
    xs[...] = chosen.astype(BF)
    n1 = (rms_parts(chosen)[1] * again_r).astype(BF)
    n1_r[...] = n1
    k_r[...] = dot_nn(n1, wqkv[1]).astype(BF)
    v_r[...] = dot_nn(n1, wqkv[2]).astype(BF)
    q = dot_nn(n1_r[my, :], wqkv[0]).astype(BF) * jnp.asarray(0.125, BF)
    for g in range(groups):
        cols = slice(128 * g, 128 * g + 128)
        q2 = head_pair(q[:, cols])
        s = dot_nt(q2, k_r[:, cols]).reshape(2, RL, RT) + bias_r[None]
        p = jnp.exp(s - jnp.max(s, axis=-1, keepdims=True))
        p = (p * (1.0 / jnp.sum(p, axis=-1, keepdims=True))).reshape(2 * RL, RT)
        q2_r[g] = q2
        p_r[g] = p
        mix_r[:, cols] = pair_join(dot_nn(p.astype(BF), v_r[:, cols])).astype(BF)

    def piece_copy(step, j):
        to = lax.rem(t + j, NT)
        rows = pl.ds(pl.multiple_of(to * Q, Q), Q)
        return rcopy(sbuf.at[step % 2, rows, :], rbuf.at[step, j - 1], ps.at[step, j - 1], pr_.at[step, j - 1], {"tensor": to})

    def spread(step, value):
        part_r[...] = value
        if step >= 2:
            for j in range(1, NT):
                piece_copy(step - 2, j).wait_send()
        sbuf[step % 2] = value.astype(BF)
        for j in range(1, NT):
            piece_copy(step, j).start()

    def collect(step):
        total = part_r[own, :]
        for j in range(1, NT):
            piece_copy(step, j).wait_recv()
            total = total + rbuf[step, j - 1].astype(F32)
        return total

    def gather_copy(step, ref, base_row, j):
        to = lax.rem(t + j, NT)
        rows = pl.ds(pl.multiple_of(base_row + t * Q, Q), Q)
        return rcopy(ref.at[rows, :], ref.at[rows, :], gs.at[step, j - 1], gr.at[step, j - 1], {"tensor": to})

    def gather(step, ref, base_row):
        for j in range(1, NT):
            gather_copy(step, ref, base_row, j).start()

    def gathered(step, ref, base_row):
        for j in range(1, NT):
            gather_copy(step, ref, base_row, j).wait()

    def both_of(d):
        return pl.ds(pl.multiple_of(d * NCTX * W, NCTX * W), NCTX * W)

    def by_share(piece, send, keep):
        def one(d, _):
            for lo, width, val in piece(both_of(d)):
                for c in range(NCTX):
                    rows = val[c * W : (c + 1) * W].astype(BF)

                    @pl.when(ctx == c)
                    def _(rows=rows, lo=lo, width=width):
                        keep[d, :, lo : lo + width] = rows

                    @pl.when(ctx != c)
                    def _(rows=rows, lo=lo, width=width):
                        send[d, :, lo : lo + width] = rows

            return 0

        lax.fori_loop(0, NDP, one, 0)

    bufs = (
        (out_buf, odn, udn, wdn_r, xdn, dn_o),
        (out_buf, oup, uup, wup_r, xup, up_o),
        (out_buf.at[:, :, pl.ds(0, Hd)], oout, uout, wup, xout, out_o),
        (out_buf.at[:, :, pl.ds(0, 3 * Hd)], oqkv, uqkv, wdn, xqkv, qkv_o),
    )
    widths = (act_s.shape[1], gpre_s.shape[1], Hd, 3 * Hd)
    routed_piece = (
        lambda cols: [(0, act_r.shape[1], dot_tn(gm_r[:, cols], act_r[...]))],
        lambda cols: [(0, gpre_r.shape[1], dot_tn(n2_r[:, cols], gpre_r[...]))],
        lambda cols: [(0, Hd, dot_tn(ga_r[:, cols], mix_r[...]))],
        lambda cols: [(Hd * c, Hd, dot_tn(n1_r[my, cols], gqkv_r[c])) for c in range(3)],
    )
    dense_piece = (
        lambda cols: [(0, act_s.shape[1], dot_tn(gm_s[:, cols], act_s[...]))],
        lambda cols: [(0, gpre_s.shape[1], dot_tn(n2_s[:, cols], gpre_s[...]))],
        lambda cols: [(0, Hd, dot_tn(ga_s[:, cols], mix_ref[...]))],
        lambda cols: [(Hd * c, Hd, dot_tn(sO[:, :, cols].reshape(L, NCTX * W), gqkv[c])) for c in range(3)],
    )

    def routed_pair(w):
        return rcopy(bufs[w][0], bufs[w][2], s1.at[w], r1.at[w], across)

    def dense_pair(w):
        return rcopy(bufs[w][0], bufs[w][2], s1d.at[w], r1d.at[w], across)

    def routed_dp(w, j):
        to = lax.rem(dp + j, NDP)
        return rcopy(bufs[w][1].at[to], bufs[w][4].at[j - 1], s3.at[w, j - 1], r3.at[w, j - 1], {"dp": to})

    def dense_dp(w, j):
        to = lax.rem(dp + j, NDP)
        land = bufs[w][3].at[pl.ds((j - 1) * W, W), pl.ds(0, widths[w])]
        return rcopy(bufs[w][1].at[to], land, s2.at[w, j - 1], r2.at[w, j - 1], {"dp": to})

    def add_pairs(w):
        keep, came = bufs[w][1], bufs[w][2]

        def add(j, _):
            keep[j] = (keep[j].astype(F32) + came[j].astype(F32)).astype(BF)
            return 0

        lax.fori_loop(0, NDP, add, 0)

    def routed_first(w):
        if w:
            routed_pair(w - 1).wait_send()
        by_share(routed_piece[w], bufs[w][0], bufs[w][1])
        routed_pair(w).start()

    def routed_second(w):
        routed_pair(w).wait_recv()
        add_pairs(w)
        put_total(w, 1, bufs[w][1][dp].astype(F32))
        for j in range(1, NDP):
            routed_dp(w, j).start()
        pl.semaphore_signal(free.at[w], inc=1, device_id=across, device_id_type=MESH)

    def dense_first(w):
        before = {0: routed_pair(3), 3: dense_pair(0), 2: dense_pair(3), 1: dense_pair(2)}
        before[w].wait_send()
        for j in range(1, NDP):
            routed_dp(w, j).wait_send()
        by_share(dense_piece[w], bufs[w][0], bufs[w][1])
        pl.semaphore_wait(free.at[w], 1)
        dense_pair(w).start()

    def dense_second(w):
        dense_pair(w).wait_recv()
        add_pairs(w)
        for j in range(1, NDP):
            dense_dp(w, j).start()

    def put_total(w, layer, total, more=False):
        out = bufs[w][5]
        if w == 3:
            for c in range(3):
                piece = total[:, Hd * c : Hd * c + Hd]
                out[layer, c] = out[layer, c] + piece if more else piece
        else:
            piece = total if w == 1 else total.T
            out[layer] = out[layer] + piece if more else piece

    def dense_total(w):
        for j in range(1, NDP):
            dense_dp(w, j).wait()
        total = bufs[w][1][dp].astype(F32)
        for j in range(NDP - 1):
            total = total + bufs[w][3][pl.ds(j * W, W), : widths[w]].astype(F32)
        put_total(w, 0, total)

    def routed_total(w):
        for j in range(1, NDP):
            routed_dp(w, j).wait_recv()
        total = bufs[w][4][0].astype(F32)
        for j in range(1, NDP - 1):
            total = total + bufs[w][4][j].astype(F32)
        put_total(w, 1, total, more=True)

    def got(buf, flow, m):
        rcopy(buf.at[m], buf.at[m], ss.at[flow, m], rs.at[flow, m], ln.mid).wait_recv()

    def each(j, fn):
        for s in range(SUBS):
            fn(j * SUBS + s)

    def place_of(i):
        place = ctx * L + i * R + lax.broadcasted_iota(jnp.int32, (R, 1), 0)
        return (place == ridx_ref[...]).astype(F32)

    def pick_rows():
        psel[...] = split_pick(pick_s[...], g_s[...], 2)
        pair(3, psel.at[theirs, :], pc).start()
        msel[...] = split_pick(pick_s[...], mid_ref[...], 2)
        pair(4, msel.at[theirs, :], mc).start()
        qsel[...] = dot_nn(pick_s[...], q_ref[...]).astype(BF)
        pair(5, qsel.at[theirs, :], qc).start()
        lsel[...] = split_pick(pick_s[...], lse_ref[...], 3)
        pair(6, lsel.at[theirs, :], lc).start()

    def mlp_back(i):
        rows = pl.ds(pl.multiple_of(i * R, R), R)
        ms = pl.ds(i * SUBS, SUBS)
        others = 1.0 - jnp.sum(place_of(i), axis=-1, keepdims=True)
        err = hid_ref[ms].astype(F32).reshape(R, D) - gin_ref[ms].astype(F32).reshape(R, D)
        counted = (column(valid_ref[...].astype(F32), i * R, R) * others) * err
        lacc[...] += fold8(counted * err)
        g2 = scale * counted
        gm = g2.astype(BF)
        gm_s[rows, :] = gm
        gact = dot_nt(gm, wdn[...])
        u = g_s[rows, :]
        th = gelu_pair(u)
        act_s[rows, :] = (0.5 * u * (1.0 + th)).astype(BF)
        gpre = (gact * gelu_slope(u, th)).astype(BF)
        gpre_s[rows, :] = gpre
        g_s[rows, :] = g2
        for s in range(SUBS):
            m = i * SUBS + s
            p3 = dot_nt(gpre[s * RS : (s + 1) * RS], wup[...])
            part[m] = p3

            @pl.when(ln.is_end)
            def _(m=m, p3=p3):
                sE[m] = p3.astype(BF)
                rcopy(sE.at[m], rE.at[m], ss.at[0, m], rs.at[0, m], ln.mid).start()

    def forward_in(j):
        def one(m):
            got(rE, 0, m)
            sI[m] = (rE[m].astype(F32) + part[m]).astype(BF)
            rcopy(sI.at[m], rI.at[m], ss.at[1, m], rs.at[1, m], ln.other).start()

        each(j, one)

    def forward_out(j):
        def one(m):
            got(rI, 1, m)
            sO[m] = (rI[m].astype(F32) + part[m]).astype(BF)
            rcopy(sO.at[m], rI.at[m], ss.at[2, m], rs.at[1, m], ln.end).start()

        each(j, one)

    def attend_back(q_rows, gmix, lse, bias, keys, put):
        n = bias.shape[0]
        for g in range(groups):
            cols = slice(128 * g, 128 * g + 128)
            q2 = head_pair(q_rows[:, cols])
            g2 = head_pair(gmix[:, cols])
            kg = k_ref[:keys, cols]
            vg = v_ref[:keys, cols]
            l2 = jnp.concatenate([lse[:, 2 * g : 2 * g + 1], lse[:, 2 * g + 1 : 2 * g + 2]], axis=0)
            s = (dot_nt(q2, kg).reshape(2, n, keys) + bias[None]).reshape(2 * n, keys)
            p = jnp.exp(s - l2)
            dp_ = dot_nt(g2, vg)
            inner = jnp.sum(p * dp_, axis=-1, keepdims=True)
            ds = (p * (dp_ - inner)).astype(BF)
            put(cols, (pair_join(dot_nn(ds, kg)) * 0.125).astype(BF))
            dk_s[:keys, cols] += dot_tn(ds, q2)
            dv_s[:keys, cols] += dot_tn(p.astype(BF), g2)

    def attention_back(j):
        @pl.when(ln.is_end)
        def _():
            each(j, lambda m: got(rI, 1, m))

        ms = pl.ds(j * SUBS, SUBS)
        rows = pl.ds(pl.multiple_of(j * R, R), R)
        gn2 = (rI[ms].astype(F32) + part[ms] + rE[ms].astype(F32)).reshape(R, D)
        r, unit = rms_parts(mid_ref[rows, :])
        n2_s[rows, :] = (unit * mgain).astype(BF)
        scaled = gn2 * mgain
        gmid = r * (scaled - unit * jnp.mean(scaled * unit, axis=-1, keepdims=True))
        acc_m[...] += fold8(gn2 * unit)
        gattn = g_s[rows, :] + gmid
        g_s[rows, :] = gattn
        ga = gattn.astype(BF)
        ga_s[rows, :] = ga
        gmix = dot_nt(ga, wout[...]).astype(BF)
        qpos = ctx * L + j * R + lax.broadcasted_iota(jnp.int32, (R, 1), 0)
        qseg = column(seg_ref[...], ctx * L + j * R, R)

        def put(cols, gq):
            gqkv[0, rows, cols] = gq

        def run(keys):
            kpos = lax.broadcasted_iota(jnp.int32, (1, keys), 1)
            bias = jnp.where((kpos <= qpos) & (seg_ref[:, :keys] == qseg), 0.0, masked_value)
            attend_back(q_ref[rows, :], gmix, lse_ref[rows, :], bias, keys, put)

        @pl.when(ctx == 0)
        def _():
            run(L)

        @pl.when(ctx > 0)
        def _():
            run(S)

    def send_loss():
        lbuf[me] = jnp.full((8, 128), jnp.sum(lacc[...]))
        for j, p in enumerate(rpeers):
            rcopy(lbuf.at[me], lbuf.at[me], cs.at[j], cr.at[j], p).start()

    def seg0():
        spread(0, dot_nn(mix_r[...], wout_r[...]))
        chosen_o = xs[mine16, :].astype(F32)
        gate_o[...] = jnp.broadcast_to(jax.nn.sigmoid(jnp.sum(chosen_o * router, axis=-1, keepdims=True)), (Q, 128))
        for n in range(6, 10):
            loads[n].wait()
        pick_rows()
        for n in range(10, 16):
            loads[n].wait()

    def seg1():
        attn = collect(0)
        attn_o[...] = attn
        mid = xs[mine16, :].astype(F32) + attn
        mid_o[...] = mid
        n2_r[own, :] = (rms_parts(mid)[1] * mgain_r).astype(BF)
        gather(0, n2_r, 0)

    def seg2():
        gathered(0, n2_r, 0)
        pre = dot_nn(n2_r[...], wup_r[...])
        th = gelu_pair(pre)
        act = (0.5 * pre * (1.0 + th)).astype(BF)
        act_r[...] = act
        spread(1, dot_nn(act, wdn_r[...]))
        slope_r[...] = gelu_slope(pre, th)

    def seg3():
        branch = attn_o[...] + collect(1)
        branch_o[...] = branch
        sent_s[own, :] = (gate_o[:, 0:1] * branch).astype(BF)
        gather(1, sent_s, 0)

    def seg4():
        pair(1, tsel.at[theirs, :], tc).wait()
        pair(2, vsel.at[theirs, :], vc).wait()
        chosen_m = xs[my, :].astype(F32)
        gate_m = jax.nn.sigmoid(jnp.sum(chosen_m * router, axis=-1, keepdims=True))
        target = tsel[my, :].astype(F32) + tc[...].astype(F32)
        counted = vsel[my, 0:1] + vc[:, 0:1]
        gathered(1, sent_s, 0)
        x3 = chosen_m + sent_s[...].astype(F32)
        err = x3 - target
        g3 = scale * counted * err
        gsent = g3.astype(BF).astype(F32)
        part_r[...] = gsent
        ggate_o[...] = part_r[own, :]
        top = gate_m * gsent
        part_r[...] = top
        top_o[...] = part_r[own, :]
        gm = top.astype(BF)
        gm_r[...] = gm
        gpre = (dot_nt(gm, wdn_r[...]) * slope_r[...]).astype(BF)
        gpre_r[...] = gpre
        spread(2, dot_nt(gpre, wup_r[...]))
        h_all[my, :] = x3.astype(BF)
        pair_rows(7, h_all).start()
        g3c[...] = g3
        lacc[...] += fold8(counted * err * err)
        gate = gate_o[:, 0:1]
        share = jnp.sum(ggate_o[...] * branch_o[...], axis=-1, keepdims=True) * gate * (1.0 - gate)
        ggate_o[:, 0:128] = jnp.broadcast_to(share, (Q, 128))
        vec[...] = jnp.zeros(vec.shape, F32)
        vec[4:5, :] = jnp.sum(share * xs[mine16, :].astype(F32), axis=0, keepdims=True)

    def seg5():
        gmid, gain_rows = rms_back(mid_o[...], mgain_r, collect(2))
        gmid_o[...] = gmid
        vec[3:4, :] = jnp.sum(gain_rows, axis=0, keepdims=True)
        ga_r[own, :] = (top_o[...] + gmid).astype(BF)
        gather(2, ga_r, 0)

    def seg6():
        gathered(2, ga_r, 0)
        gmix = dot_nt(ga_r[...], wout_r[...]).astype(BF)
        for g in range(groups):
            cols = slice(128 * g, 128 * g + 128)
            p = p_r[g]
            g2 = head_pair(gmix[:, cols])
            dp_ = dot_nt(g2, v_r[:, cols])
            ds = (p * (dp_ - jnp.sum(p * dp_, axis=-1, keepdims=True))).astype(BF)
            gqkv_r[0, :, cols] = (pair_join(dot_nn(ds, k_r[:, cols])) * 0.125).astype(BF)
            dkv_r[0, :, cols] = dot_tn(ds, q2_r[g])
            dkv_r[1, :, cols] = dot_tn(p.astype(BF), g2)
        swaps = [pair(8 + c, dkv_r.at[c, theirs, :], dkvc.at[c]) for c in range(2)]
        for cp in swaps:
            cp.start()
        p4 = dot_nt(gqkv_r[0], wqkv[0])
        for c in range(2):
            swaps[c].wait()
            gqkv_r[1 + c] = (dkv_r[c, my, :] + dkvc[c]).astype(BF)
            p4 = p4 + dot_nt(gqkv_r[1 + c], wqkv[1 + c])
        spread(3, p4)
        loads[16].start()

    def seg7():
        chosen_o = xs[mine16, :].astype(F32)
        gin, gain_rows = rms_back(chosen_o, again_r, collect(3))
        vec[2:3, :] = jnp.sum(gain_rows, axis=0, keepdims=True)
        gch_s[own, :] = (gmid_o[...] + gin + ggate_o[:, 0:1] * router).astype(BF)
        gather(3, gch_s, 0)

    def seg8():
        for n, (src, dst) in enumerate(((psel, pc), (msel, mc), (qsel, qc), (lsel, lc))):
            pair(3 + n, src.at[theirs, :], dst).wait()
        u = psel[my, :] + pc[...]
        th = gelu_pair(u)
        slope = gelu_slope(u, th)
        act_s[late, :] = (0.5 * u * (1.0 + th)).astype(BF)
        mid = msel[my, :] + mc[...]
        mc[...] = mid
        n2_s[late, :] = (rms_parts(mid)[1] * mgain).astype(BF)
        gathered(3, gch_s, 0)
        g2 = g3c[...] + gch_s[...].astype(F32)
        g3c[...] = g2
        gm = g2.astype(BF)
        gm_s[late, :] = gm
        gpre = (dot_nt(gm, wdn[...]) * slope).astype(BF)
        gpre_s[late, :] = gpre
        spread(4, dot_nt(gpre, wup[...]))

    def seg9():
        gmid, gain_rows = rms_back(mc[own, :], mgain, collect(4))
        vec[1:2, :] = jnp.sum(gain_rows, axis=0, keepdims=True)
        ga_all[mine16, :] = (g3c[own, :] + gmid).astype(BF)
        gather(4, ga_all, ctx * RL)

    def kv_copy(which):
        src = (dk_s, dv_s)[which]
        rows = pl.ds(pl.multiple_of((1 - ctx) * L, L), L)
        return rcopy(src.at[rows, :], mid_ref.at[:, pl.ds(which * Hd, Hd)], kvs.at[which], kvr.at[which], across)

    def seg10():
        gathered(4, ga_all, ctx * RL)
        pair_rows(10, ga_all).start()
        gmix = dot_nt(ga_all[my, :], wout[...]).astype(BF)
        kpos = lax.broadcasted_iota(jnp.int32, (1, S), 1)
        bias = jnp.where((kpos <= posc[my, 0:1]) & (seg_ref[...] == segq[my, 0:1]), 0.0, masked_value)

        def put(cols, gq):
            gq_all[my, cols] = gq

        attend_back((qsel[my, :].astype(F32) + qc[...].astype(F32)).astype(BF), gmix, lsel[my, :] + lc[...], bias, S, put)
        pl.semaphore_wait(free.at[4], 1)
        kv_copy(0).start()
        kv_copy(1).start()
        pair_rows(11, gq_all).start()

    @pl.when(ln.is_end)
    def _():
        def zero(m, _):
            rE[m] = jnp.zeros((RS, D), BF)
            return 0

        lax.fori_loop(0, NM, zero, 0)

    for ref in (dk_s, dv_s, acc_m, acc_a, lacc):
        ref[...] = jnp.zeros(ref.shape, F32)

    def mid_is_free():
        pl.semaphore_signal(free.at[4], inc=1, device_id=across, device_id_type=MESH)

    segments = (seg0, seg1, seg2, seg3, seg4, seg5, seg6, seg7, seg8, seg9)
    extras = {
        4: (lambda: routed_first(0),),
        5: (lambda: routed_first(1),),
        6: (lambda: routed_first(2), lambda: routed_second(0)),
        7: (lambda: routed_first(3), lambda: routed_second(1)),
        8: (lambda: routed_second(2),),
        9: (mid_is_free, lambda: routed_second(3), send_loss, lambda: dense_first(0)),
    }
    LF, LO, LC = CHAIN_LAGS

    def step(w, _):
        for n, fn in enumerate(segments):
            pl.when(w == n)(fn)

        for n, fns in extras.items():
            @pl.when(w == n)
            def _(fns=fns):
                for fn in fns:
                    fn()

        @pl.when(w < NC)
        def _():
            mlp_back(w)

        jf = w - LF

        @pl.when(ln.is_mid & (jf >= 0) & (jf < NC))
        def _():
            forward_in(jf)

        jo = w - LO

        @pl.when(ln.is_mid & (jo >= 0) & (jo < NC))
        def _():
            forward_out(jo)

        jc = w - LC

        @pl.when((jc >= 0) & (jc < NC))
        def _():
            attention_back(jc)

        return 0

    lax.fori_loop(0, len(segments), step, 0)
    seg10()

    def settle_sends(m, _):
        @pl.when(ln.is_end)
        def _():
            rcopy(sE.at[m], rE.at[m], ss.at[0, m], rs.at[0, m], ln.mid).wait_send()

        @pl.when(ln.is_mid)
        def _():
            rcopy(sI.at[m], rI.at[m], ss.at[1, m], rs.at[1, m], ln.other).wait_send()
            rcopy(sO.at[m], rI.at[m], ss.at[2, m], rs.at[1, m], ln.end).wait_send()

        n1_rows = x_ref[pl.ds(pl.multiple_of(m * RS, RS), RS), :].astype(F32)
        sO[m] = (rms_parts(n1_rows)[1] * again).astype(BF)
        return 0

    lax.fori_loop(0, NM, settle_sends, 0)
    pair_rows(10, ga_all).wait_send()
    pair_rows(11, gq_all).wait_send()
    pair_rows_in(10, ga_all).wait_recv()
    pair_rows_in(11, gq_all).wait_recv()
    own_keys = pl.ds(pl.multiple_of(ctx * L, L), L)

    def put_late(i, _):
        rows = pl.ds(pl.multiple_of(i * R, R), R)
        place = place_of(i).astype(BF)
        gqkv[0, rows, :] = (gqkv[0, rows, :].astype(F32) + dot_nn(place, gq_all[...])).astype(BF)
        late_ga = dot_nn(place, ga_all[...])
        g_s[rows, :] += late_ga
        ga_s[rows, :] = (ga_s[rows, :].astype(F32) + late_ga).astype(BF)
        return 0

    lax.fori_loop(0, NC, put_late, 0)
    loads[16].wait()
    for which, ref in enumerate((dk_s, dv_s)):
        kv_copy(which).wait()
        gqkv[1 + which] = (ref[own_keys, :] + mid_ref[:, which * Hd : which * Hd + Hd]).astype(BF)
    pair_rows(7, h_all).wait_send()
    pair_rows_in(7, h_all).wait_recv()

    b4, b5, b6 = TAIL_LAGS
    sX = sI
    rE2 = rE
    my_rows = pl.ds(pl.multiple_of(ln.side * half, half), half)
    ot_rows = pl.ds(pl.multiple_of((1 - ln.side) * half, half), half)

    def got_half(rows, flow, m):
        rcopy(gin_ref.at[m, rows, :], gin_ref.at[m, rows, :], ss.at[flow, m], rs.at[flow, m], ln.mid).wait_recv()

    def tail(i, _):
        @pl.when(i < NC)
        def _():
            for s in range(SUBS):
                m = i * SUBS + s
                rows = pl.ds(pl.multiple_of(i * R + s * RS, RS), RS)
                p4 = dot_nt(gqkv[0, rows, :], wqkv[0])
                p4 = p4 + dot_nt(gqkv[1, rows, :], wqkv[1])
                p4 = p4 + dot_nt(gqkv[2, rows, :], wqkv[2])

                @pl.when(ln.is_end)
                def _(m=m, p4=p4):
                    sE[m] = p4.astype(BF)
                    rcopy(sE.at[m], rE2.at[m], ss.at[3, m], rs.at[3, m], ln.mid).start()

                @pl.when(ln.is_mid)
                def _(m=m, p4=p4):
                    part[m] = p4

            rows = pl.ds(pl.multiple_of(i * R, R), R)
            ms = pl.ds(i * SUBS, SUBS)
            place = place_of(i)
            chosen_here = jnp.sum(place, axis=-1, keepdims=True) > 0.5
            place = place.astype(BF)
            new_hid = dot_nn(place, h_all[...])
            old_hid = hid_ref[ms].astype(F32).reshape(R, D)
            hid_ref[ms] = jnp.where(chosen_here, new_hid, old_hid).astype(BF).reshape(SUBS, RS, D)

        j4 = i - b4

        @pl.when(ln.is_mid & (j4 >= 0) & (j4 < NC))
        def _():
            def cross(m):
                got(rE2, 3, m)
                sX[m, pl.ds(0, half), :] = (rE2[m, ot_rows, :].astype(F32) + part[m, ot_rows, :]).astype(BF)
                rcopy(sX.at[m, pl.ds(0, half), :], rX.at[m], ss.at[4, m], rs.at[4, m], ln.other).start()

            each(j4, cross)

        j5 = i - b5

        @pl.when(ln.is_mid & (j5 >= 0) & (j5 < NC))
        def _():
            def settle(m):
                got(rX, 4, m)
                rows = pl.ds(pl.multiple_of(m * RS + ln.side * half, half), half)
                gn1 = part[m, my_rows, :] + rE2[m, my_rows, :].astype(F32) + rX[m].astype(F32)
                gin, gain_rows = rms_back(x_ref[rows, :].astype(F32), again, gn1)
                acc_a[...] += fold8(gain_rows)
                gin_ref[m, my_rows, :] = (g_s[rows, :] + gin).astype(BF)
                mine = gin_ref.at[m, my_rows, :]
                rcopy(mine, mine, ss.at[5, m], rs.at[5, m], ln.other).start()
                rcopy(mine, mine, ss.at[6, m], rs.at[6, m], ln.end).start()

            each(j5, settle)

        j6 = i - b6

        @pl.when(ln.is_mid & (j6 >= 0) & (j6 < NC))
        def _():
            def relay(m):
                got_half(ot_rows, 5, m)
                theirs_m = gin_ref.at[m, ot_rows, :]
                rcopy(theirs_m, theirs_m, ss.at[7, m], rs.at[7, m], ln.end).start()

            each(j6, relay)

        for n, fns in tail_extras.items():
            @pl.when(i == n)
            def _(fns=fns):
                for fn in fns:
                    fn()

        return 0

    tail_extras = {
        0: (lambda: routed_total(0), lambda: dense_second(0), lambda: dense_first(3)),
        1: (lambda: dense_first(2), lambda: dense_first(1)),
        2: (lambda: routed_total(3), lambda: dense_second(3), lambda: dense_second(2)),
        3: (lambda: dense_second(1), lambda: routed_total(1)),
        4: (lambda: routed_total(2), lambda: dense_total(0)),
        5: (lambda: dense_total(3),),
        6: (lambda: dense_total(2),),
    }
    lax.fori_loop(0, NC + b6, tail, 0)

    vec[0:1, :] = jnp.sum(acc_a[...], axis=0, keepdims=True)
    vec[1:2, :] = vec[1:2, :] + jnp.sum(acc_m[...], axis=0, keepdims=True) * (1.0 / NT)
    places = []
    for j in range(NDP):
        for k in range(NCTX):
            if j or k:
                places.append((lax.rem(dp + j, NDP), lax.rem(ctx + k, NCTX)))

    def cols_of(g):
        return pl.ds(pl.multiple_of(g * W, W), W)

    def vec_copy(n):
        d2, c2 = places[n]
        return rcopy(vec.at[:, cols_of(d2 * NCTX + c2)], vbuf.at[me], ts.at[n], tr.at[n], {"dp": d2, "ctx": c2})

    for n in range(G - 1):
        vec_copy(n).start()
    vbuf[me] = vec[:, cols_of(me)]
    for n in range(G - 1):
        vec_copy(n).wait()
    rows_sum = vbuf[0]
    for j in range(1, G):
        rows_sum = rows_sum + vbuf[j]
    hbuf[t] = rows_sum

    def line_copy(n):
        return rcopy(hbuf.at[t], hbuf.at[t], ts.at[G - 1 + n], tr.at[G - 1 + n], tpeers[n])

    for n in range(NT - 1):
        line_copy(n).start()
    dense_total(1)
    for j, p in enumerate(rpeers):
        rcopy(lbuf.at[me], lbuf.at[me], cs.at[j], cr.at[j], p).wait()
    loss = lbuf[0]
    for j in range(1, G):
        loss = loss + lbuf[j]
    loss_ref[...] = loss / (cnt_ref[...] * D)
    for n in range(NT - 1):
        line_copy(n).wait()
    line_sum = hbuf[0]
    for j in range(1, NT):
        line_sum = line_sum + hbuf[j]
    small_o[...] = line_sum

    dense_pair(1).wait_send()
    for n in (3, 4):
        for j in range(1, NT):
            piece_copy(n, j).wait_send()

    def drain(m, _):
        @pl.when(ln.is_end)
        def _():
            got_half(my_rows, 6, m)
            got_half(ot_rows, 7, m)
            rcopy(sE.at[m], rE2.at[m], ss.at[3, m], rs.at[3, m], ln.mid).wait_send()

        @pl.when(ln.is_mid)
        def _():
            rcopy(sX.at[m, pl.ds(0, half), :], rX.at[m], ss.at[4, m], rs.at[4, m], ln.other).wait_send()
            mine = gin_ref.at[m, my_rows, :]
            theirs_m = gin_ref.at[m, ot_rows, :]
            rcopy(mine, mine, ss.at[5, m], rs.at[5, m], ln.other).wait_send()
            rcopy(mine, mine, ss.at[6, m], rs.at[6, m], ln.end).wait_send()
            rcopy(theirs_m, theirs_m, ss.at[7, m], rs.at[7, m], ln.end).wait_send()

        return 0

    lax.fori_loop(0, NM, drain, 0)


CHAIN_LAGS = (2, 3, 5)


def routed_and_backward(x, x2, teacher, valid, cnt, ridx, seg, again, mgain, w_router, saved, w_qkv, w_out, w_up, w_down):
    L, D = x.shape
    S = seg.shape[1]
    RT = ridx.shape[1]
    NT, NDP, NCTX = lax.axis_size("tensor"), lax.axis_size("dp"), lax.axis_size("ctx")
    R = min(BCHUNK, L)
    NC = L // R
    RS = R // SUB
    NM = NC * SUB
    Hd = w_out.shape[1]
    Fl = w_up.shape[2]
    RL = RT // NCTX
    Q = RL // NT
    G = NDP * NCTX
    W = D // G
    HG = Hd // 128
    sizes = (NC, SUB, R, D, L, S, RT, NT, NDP, NCTX, float(S * NDP))
    dma = pltpu.SemaphoreType.DMA
    sd = jax.ShapeDtypeStruct
    v_ = pl.BlockSpec(memory_space=VM)
    a_ = pl.BlockSpec(memory_space=pltpu.HBM)
    shares = [VM((NDP, W, max(Fl, 3 * Hd)), BF)]
    for s in ((W, Fl), (W, Fl), (W, Hd), (W, 3 * Hd)):
        shares += [VM((NDP,) + s, BF)] * 2 + [VM((NDP - 1,) + s, BF)]
    big = VM((NM, RS, D), BF)
    i32 = jnp.int32
    return pl.pallas_call(
        functools.partial(backward_kernel, sizes),
        name="routed_and_backward",
        out_shape=(
            sd((NM, RS, D), BF), sd((8, 128), F32), sd((NM, RS, D), BF),
            sd((2, Fl, W), F32), sd((2, W, Fl), F32), sd((2, Hd, W), F32), sd((2, 3, W, Hd), F32), sd((8, W), F32),
        ),
        in_specs=[v_] * 8 + [a_] * 13,
        out_specs=(v_,) * 8,
        scratch_shapes=[
            VM((L, Hd), BF), VM((S, Hd), BF), VM((S, Hd), BF), VM((L, Hd), BF), VM((L, 128), F32), VM((L, D), F32), VM((L, Fl), F32),
            VM((3, D, Hd), BF), VM((Hd, D), BF), VM((D, Fl), BF), VM((Fl, D), BF), VM((Hd, D), BF), VM((D, Fl), BF), VM((Fl, D), BF),
            VM((L + RL, D), BF), VM((L + RL, Fl), BF), VM((L + RL, Fl), BF), VM((L + RL, D), BF), VM((L, D), BF),
            VM((NM, RS, D), F32), VM((3, L, Hd), BF), VM((S, Hd), F32), VM((S, Hd), F32),
            big, big, big, big, big, VM((NM, RS // 2, D), BF),
            *shares,
            VM((RT, L), BF), VM((RT, D), BF), VM((RT, D), BF), VM((RT, D), BF), VM((RL, D), BF), VM((RT, 128), F32), VM((RL, 128), F32),
            VM((RT, 128), i32), VM((RT, 128), i32), VM((RT, D), BF), VM((RT, Hd), BF), VM((RT, Hd), BF),
            VM((HG, 2 * RL, 128), BF), VM((HG, 2 * RL, RT), F32), VM((RL, Hd), BF), VM((RL, D), BF), VM((RL, Fl), BF), VM((RL, Fl), F32),
            VM((RL, Fl), BF), VM((RL, D), BF), VM((RL, D), BF), VM((3, RL, Hd), BF), VM((2, RT, Hd), F32), VM((2, RL, Hd), F32),
            VM((RL, D), F32), VM((Q, D), F32), VM((Q, D), F32), VM((Q, 128), F32), VM((Q, D), F32), VM((Q, D), F32), VM((Q, D), F32),
            VM((Q, D), F32), VM((RL, D), F32), VM((RL, D), BF), VM((RL, D), BF), VM((RT, D), BF), VM((RT, Hd), BF),
            VM((2, RL, D), BF), VM((5, NT - 1, Q, D), BF),
            VM((RT, Fl), F32), VM((RL, Fl), F32), VM((RT, D), F32), VM((RL, D), F32), VM((RT, Hd), BF), VM((RL, Hd), BF), VM((RT, 128), F32), VM((RL, 128), F32),
            VM((8, D), F32), VM((8, D), F32), VM((8, D), F32), VM((G, 8, 128), F32), VM((8, D), F32), VM((G, 8, W), F32), VM((NT, 8, W), F32),
            dma((17,)), dma((12,)), dma((12,)), pltpu.SemaphoreType.REGULAR((5,)),
            dma((5, NT)), dma((5, NT)), dma((5, NT)), dma((5, NT)), dma((2,)), dma((2,)),
            dma((4,)), dma((4,)), dma((4,)), dma((4,)), dma((4, NDP)), dma((4, NDP)), dma((4, NDP)), dma((4, NDP)),
            dma((G,)), dma((G,)), dma((G + NT,)), dma((G + NT,)), dma((8, NM)), dma((8, NM)),
        ],
        compiler_params=pltpu.CompilerParams(collective_id=2, has_side_effects=True, vmem_limit_bytes=62 << 20),
    )(
        x, valid, cnt, ridx, seg, again, mgain, w_router.reshape(1, D),
        x2, teacher.reshape(NM, RS, D), *saved, w_qkv, w_out, w_up, w_down,
    )


def finish_kernel(
    hid_h, gin_h, dn_h, up_h, out_h, qkv_h, small_h, loss_h,
    hid_o, loss_o, gin_o, ag_o, qkv_o, out_o, mg_o, up_o, dn_o, router_o,
    hid, gin, dn, up, out, qkv, small, loss, wide, sem,
):
    pairs = ((gin_h, gin), (dn_h, dn), (up_h, up), (hid_h, hid), (qkv_h, qkv), (out_h, out), (small_h, small), (loss_h, loss))
    reads = [pltpu.make_async_copy(a, b, sem.at[n]) for n, (a, b) in enumerate(pairs)]
    for cp in reads:
        cp.start()
    backs = ((wide, gin_o), (dn, dn_o), (up, up_o), (hid, hid_o), (qkv, qkv_o), (out, out_o))
    writes = [pltpu.make_async_copy(a, b, sem.at[8 + n]) for n, (a, b) in enumerate(backs)]
    for n in range(6):
        reads[n].wait()
        if n == 0:
            wide[...] = gin[...].astype(F32)
        writes[n].start()
    reads[6].wait()
    reads[7].wait()
    loss_o[...] = loss[0:1, 0:1]
    for j in range(2):
        ag_o[j : j + 1, :] = small[2 * j : 2 * j + 1, :]
        mg_o[j : j + 1, :] = small[2 * j + 1 : 2 * j + 2, :]
    router_o[...] = small[4:5, :]
    for cp in writes:
        cp.wait()


def finish(hid, gin, dn, up, out, qkv, small, loss):
    sd = jax.ShapeDtypeStruct
    v_ = pl.BlockSpec(memory_space=VM)
    h_ = pl.BlockSpec(memory_space=pltpu.HBM)
    W = small.shape[1]

    def like(arr):
        return sd(arr.shape, arr.dtype)

    ins = (hid, gin, dn, up, out, qkv, small, loss)
    return pl.pallas_call(
        finish_kernel,
        name="finish",
        out_shape=(like(hid), sd((1, 1), F32), sd(gin.shape, F32), sd((2, W), F32), like(qkv), like(out), sd((2, W), F32), like(up), like(dn), sd((1, W), F32)),
        in_specs=[h_] * 8,
        out_specs=(h_, v_, h_, v_, h_, h_, v_, h_, h_, v_),
        scratch_shapes=[*[VM(a.shape, a.dtype) for a in ins], VM(gin.shape, F32), pltpu.SemaphoreType.DMA((14,))],
        compiler_params=pltpu.CompilerParams(vmem_limit_bytes=60 << 20),
    )(*ins)


def fast_local(hidden_in, teacher, seg_ids, valid, routed_idx, attn_gain, w_qkv, w_out, mlp_gain, w_up, w_down, w_router):
    L, D = hidden_in.shape[1:]
    x2, *saved, cnt = dense_forward(hidden_in[0], attn_gain, mlp_gain, seg_ids, valid, w_qkv, w_out, w_up, w_down)
    hid, loss, gin, dn, up, out, qkv, small = routed_and_backward(
        hidden_in[0], x2, teacher[0], valid, cnt, routed_idx, seg_ids, attn_gain, mlp_gain, w_router, saved, w_qkv, w_out, w_up, w_down
    )
    hid, loss, gin, ag, qkv, out, mg, up, dn, router = finish(hid, gin, dn, up, out, qkv, small, loss)
    return (hid.reshape(1, L, D), loss[0, 0], gin.reshape(1, L, D), ag, qkv, out, mg, up, dn, router[0])


def takes_kernels(mesh):
    shape = dict(mesh.shape)
    return shape["tensor"] == 4 and shape["ctx"] == 2


def solution(mesh):
    placed = (
        P("dp", "ctx", None),
        P("dp", "ctx", None),
        P("dp", None),
        P("dp", "ctx"),
        P("dp", None),
        P(),
        P(None, None, None, "tensor"),
        P(None, "tensor", None),
        P(),
        P(None, None, "tensor"),
        P(None, "tensor", None),
        P(),
    )
    return jax.shard_map(
        fast_local if takes_kernels(mesh) else plain_local,
        mesh=mesh,
        in_specs=placed,
        out_specs=(
            P("dp", "ctx", None),
            P(),
            P("dp", "ctx", None),
            P(None, ("dp", "ctx")),
            P(None, None, ("dp", "ctx"), "tensor"),
            P(None, "tensor", ("dp", "ctx")),
            P(None, ("dp", "ctx")),
            P(None, ("dp", "ctx"), "tensor"),
            P(None, "tensor", ("dp", "ctx")),
            P(("dp", "ctx")),
        ),
        check_vma=False,
    )
```

```python
import functools

import jax
import jax.numpy as jnp
from jax import lax
from jax.experimental import pallas as pl
from jax.experimental.pallas import tpu as pltpu
from jax.sharding import PartitionSpec as P

HEAD = 64
epsilon = 1e-06
masked_value = -1e30
MESH = pl.DeviceIdType.MESH
BF = jnp.bfloat16
F32 = jnp.float32
VM = pltpu.VMEM
ANY = pl.ANY


def rcopy(src, dst, send, recv, where):
    return pltpu.make_async_remote_copy(
        src_ref=src, dst_ref=dst, send_sem=send, recv_sem=recv, device_id=where, device_id_type=MESH
    )


def dot_nn(a, b):
    return lax.dot_general(a, b, (((1,), (0,)), ((), ())), preferred_element_type=F32)


def dot_nt(a, b):
    return lax.dot_general(a, b, (((1,), (1,)), ((), ())), preferred_element_type=F32)


def dot_tn(a, b):
    return lax.dot_general(a, b, (((0,), (0,)), ((), ())), preferred_element_type=F32)


def rms_parts(values):
    r = lax.rsqrt(jnp.mean(values * values, axis=-1, keepdims=True) + epsilon)
    return r, values * r


def rms_back(values, gain, grad):
    r, unit = rms_parts(values)
    scaled = grad * gain
    return r * (scaled - unit * jnp.mean(scaled * unit, axis=-1, keepdims=True)), grad * unit


def gelu_pair(u):
    c = 0.7978845608028654
    t = jnp.tanh(c * (u + 0.044715 * (u * u * u)))
    return t


def fold8(rows):
    return jnp.sum(rows.reshape(rows.shape[0] // 8, 8, rows.shape[1]), axis=0)


class Line:
    def __init__(self):
        t = lax.axis_index("tensor")
        self.t = t
        self.side = t // 2
        self.is_end = (t == 0) | (t == 3)
        self.is_mid = (t == 1) | (t == 2)
        self.end = {"tensor": self.side * 3}
        self.mid = {"tensor": 1 + self.side}
        self.other = {"tensor": 2 - self.side}
        self.far = {"tensor": 3 - 3 * self.side}


def greet(peers):
    bar = pltpu.get_barrier_semaphore()
    for p in peers:
        pl.semaphore_signal(bar, inc=1, device_id=p, device_id_type=MESH)
    pl.semaphore_wait(bar, len(peers))


def tensor_peers(n):
    t = lax.axis_index("tensor")
    return [{"tensor": lax.rem(t + j, n)} for j in range(1, n)]


def row_peers(n_dp, n_ctx):
    d, c = lax.axis_index("dp"), lax.axis_index("ctx")
    out = []
    for j in range(n_dp):
        for k in range(n_ctx):
            if j or k:
                out.append({"dp": lax.rem(d + j, n_dp), "ctx": lax.rem(c + k, n_ctx)})
    return out


def rms_scale(values, gain):
    return values * lax.rsqrt(jnp.mean(values * values, axis=-1, keepdims=True) + epsilon) * gain


def gelu_tanh(values):
    return jax.nn.gelu(values, approximate=True)


def gating_fn(chosen, router):
    return jax.nn.sigmoid(jnp.sum(chosen * router, axis=-1))


def tensor_sum(partial_sum):
    return lax.psum(partial_sum, "tensor")


def gather_keys(projected):
    return (
        lax.all_gather(projected[1], "ctx", axis=1, tiled=True),
        lax.all_gather(projected[2], "ctx", axis=1, tiled=True),
    )


def scatter_key_grads(grad_k, grad_v):
    stacked = jnp.stack([grad_k, grad_v])
    summed = lax.psum_scatter(stacked, "ctx", scatter_dimension=2, tiled=True)
    return (summed[0], summed[1])


def to_workers(picked):
    return lax.psum_scatter(
        picked.astype(jnp.bfloat16), "ctx", scatter_dimension=1, tiled=True
    ).astype(jnp.float32)


def to_owners(rows_low):
    return lax.all_gather(rows_low, "ctx", axis=1, tiled=True)


def take_rows(table, places):
    return jax.vmap(lambda t, i: t[i])(table, places)


def add_rows(table, places, addend):
    return jax.vmap(lambda t, i, a: t.at[i].add(a))(table, places, addend)


def tile_scores(q_tile, k_tile, qpos_tile, kpos_tile, qseg_tile, kseg_tile, score_scale):
    scores = (
        jnp.einsum("qhe,khe->hqk", q_tile, k_tile, preferred_element_type=jnp.float32) * score_scale
    )
    visible = (kpos_tile[None, :] <= qpos_tile[:, None]) & (
        kseg_tile[None, :] == qseg_tile[:, None]
    )
    return (scores, visible[None])


def tile_layout(queries, key_rows, value_rows, k_pos, k_seg):
    q_len, row_width = queries.shape
    k_len = key_rows.shape[0]
    head_count = row_width // HEAD
    q_step = min(512, q_len)
    k_step = min(2048, k_len)
    k_count = k_len // k_step
    key_tiles = key_rows.reshape(k_count, k_step, head_count, HEAD)
    value_tiles = value_rows.reshape(k_count, k_step, head_count, HEAD)
    kpos_tiles = k_pos.reshape(k_count, k_step)
    kseg_tiles = k_seg.reshape(k_count, k_step)
    return (
        q_len,
        row_width,
        k_len,
        head_count,
        q_step,
        (key_tiles, value_tiles, kpos_tiles, kseg_tiles),
    )


def attend_one(queries, key_rows, value_rows, q_pos, k_pos, q_seg, k_seg):
    q_len, row_width, k_len, head_count, q_step, tiles = tile_layout(
        queries, key_rows, value_rows, k_pos, k_seg
    )
    score_scale = 1.0 / HEAD**0.5

    def per_query(q_args):
        q_tile, qpos_tile, qseg_tile = q_args

        def total_step(carry, k_args):
            running, summed = carry
            k_tile, v_tile, kpos_tile, kseg_tile = k_args
            scores, visible = tile_scores(
                q_tile, k_tile, qpos_tile, kpos_tile, qseg_tile, kseg_tile, score_scale
            )
            raised = jnp.maximum(
                running, jnp.max(jnp.where(visible, scores, masked_value), axis=-1)
            )
            weights = jnp.where(visible, jnp.exp(scores - raised[..., None]), 0.0)
            return ((raised, summed * jnp.exp(running - raised) + jnp.sum(weights, axis=-1)), None)

        initial = (
            jnp.full((head_count, q_step), masked_value, jnp.float32),
            jnp.zeros((head_count, q_step), jnp.float32),
        )
        (running, summed), _ = lax.scan(total_step, initial, tiles)
        log_total = running + jnp.log(summed)

        def value_step(output, k_args):
            k_tile, v_tile, kpos_tile, kseg_tile = k_args
            scores, visible = tile_scores(
                q_tile, k_tile, qpos_tile, kpos_tile, qseg_tile, kseg_tile, score_scale
            )
            weights_low = jnp.where(visible, jnp.exp(scores - log_total[..., None]), 0.0).astype(
                jnp.bfloat16
            )
            return (
                output
                + jnp.einsum(
                    "hqk,khe->qhe", weights_low, v_tile, preferred_element_type=jnp.float32
                ),
                None,
            )

        output, _ = lax.scan(value_step, jnp.zeros((q_step, head_count, HEAD), jnp.float32), tiles)
        return (output, log_total)

    q_count = q_len // q_step
    output, log_total = lax.map(
        per_query,
        (
            queries.reshape(q_count, q_step, head_count, HEAD),
            q_pos.reshape(q_count, q_step),
            q_seg.reshape(q_count, q_step),
        ),
    )
    return (output.reshape(q_len, row_width), log_total)


def attend_back(queries, key_rows, value_rows, grad_mixed, log_total, q_pos, k_pos, q_seg, k_seg):
    q_len, row_width, k_len, head_count, q_step, tiles = tile_layout(
        queries, key_rows, value_rows, k_pos, k_seg
    )
    score_scale = 1.0 / HEAD**0.5

    def per_query(q_args):
        q_tile, g_tile, total_tile, qpos_tile, qseg_tile = q_args

        def tile_probs(k_tile, kpos_tile, kseg_tile):
            scores, visible = tile_scores(
                q_tile, k_tile, qpos_tile, kpos_tile, qseg_tile, kseg_tile, score_scale
            )
            return jnp.where(visible, jnp.exp(scores - total_tile[..., None]), 0.0)

        def inner_step(carry, k_args):
            k_tile, v_tile, kpos_tile, kseg_tile = k_args
            weights = tile_probs(k_tile, kpos_tile, kseg_tile)
            grad_weights = jnp.einsum(
                "qhe,khe->hqk", g_tile, v_tile, preferred_element_type=jnp.float32
            )
            return (carry + jnp.sum(weights * grad_weights, axis=-1), None)

        inner, _ = lax.scan(inner_step, jnp.zeros((head_count, q_step), jnp.float32), tiles)

        def grad_step(carry, k_args):
            k_tile, v_tile, kpos_tile, kseg_tile = k_args
            weights = tile_probs(k_tile, kpos_tile, kseg_tile)
            grad_weights = jnp.einsum(
                "qhe,khe->hqk", g_tile, v_tile, preferred_element_type=jnp.float32
            )
            grad_scores = (weights * (grad_weights - inner[..., None])).astype(jnp.bfloat16)
            carry = carry + jnp.einsum(
                "hqk,khe->qhe", grad_scores, k_tile, preferred_element_type=jnp.float32
            )
            grad_keys = jnp.einsum(
                "hqk,qhe->khe", grad_scores, q_tile, preferred_element_type=jnp.float32
            )
            grad_values = jnp.einsum(
                "hqk,qhe->khe",
                weights.astype(jnp.bfloat16),
                g_tile,
                preferred_element_type=jnp.float32,
            )
            return (carry, (grad_keys, grad_values))

        grad_q, (grad_keys, grad_values) = lax.scan(
            grad_step, jnp.zeros((q_step, head_count, HEAD), jnp.float32), tiles
        )
        return (
            grad_q * score_scale,
            grad_keys.reshape(k_len, row_width) * score_scale,
            grad_values.reshape(k_len, row_width),
        )

    q_count = q_len // q_step
    grad_q, grad_keys, grad_values = lax.map(
        per_query,
        (
            queries.reshape(q_count, q_step, head_count, HEAD),
            grad_mixed.reshape(q_count, q_step, head_count, HEAD),
            log_total,
            q_pos.reshape(q_count, q_step),
            q_seg.reshape(q_count, q_step),
        ),
    )
    return (
        grad_q.reshape(q_len, row_width),
        jnp.sum(grad_keys, axis=0),
        jnp.sum(grad_values, axis=0),
    )


def make_attention(q_pos, k_pos, q_seg, k_seg):

    def attend_fn(projected):
        key_all, value_all = gather_keys(projected)
        mixed_full, log_total = lax.map(
            lambda a: attend_one(*a), (projected[0], key_all, value_all, q_pos, k_pos, q_seg, k_seg)
        )
        return (mixed_full, (key_all, value_all, log_total))

    def attend_grad(projected, kept, grad_mixed):
        key_all, value_all, log_total = kept
        grad_q, grad_k, grad_v = lax.map(
            lambda a: attend_back(*a),
            (projected[0], key_all, value_all, grad_mixed, log_total, q_pos, k_pos, q_seg, k_seg),
        )
        grad_k, grad_v = scatter_key_grads(grad_k, grad_v)
        return jnp.stack(
            [grad_q.astype(jnp.bfloat16), grad_k.astype(jnp.bfloat16), grad_v.astype(jnp.bfloat16)]
        )

    return (attend_fn, attend_grad)


def block_forward(
    resid_in,
    gain_a,
    query_key_value_weight,
    output_weight_matrix,
    gain_m,
    up_weight_matrix,
    down_weight_matrix,
    attend_fn,
):
    attention_norm = rms_scale(resid_in, gain_a).astype(jnp.bfloat16)
    projected = jnp.einsum(
        "oym,qmh->qoyh", attention_norm, query_key_value_weight, preferred_element_type=jnp.float32
    ).astype(jnp.bfloat16)
    mixed_full, kept = attend_fn(projected)
    mixed_state = mixed_full.astype(jnp.bfloat16)
    attention_portion = jnp.einsum(
        "xtu,ua->xta", mixed_state, output_weight_matrix, preferred_element_type=jnp.float32
    )
    attn_out = tensor_sum(attention_portion)
    middle = resid_in + attn_out
    feedforward_norm = rms_scale(middle, gain_m).astype(jnp.bfloat16)
    hidden_preactivation = jnp.einsum(
        "iqp,po->iqo", feedforward_norm, up_weight_matrix, preferred_element_type=jnp.float32
    )
    hidden_activation = gelu_tanh(hidden_preactivation).astype(jnp.bfloat16)
    mlp_part = jnp.einsum(
        "euq,qt->eut", hidden_activation, down_weight_matrix, preferred_element_type=jnp.float32
    )
    mlp_out = tensor_sum(mlp_part)
    saved = (
        resid_in,
        attention_norm,
        projected,
        mixed_state,
        kept,
        middle,
        feedforward_norm,
        hidden_preactivation,
        hidden_activation,
    )
    return (attn_out, mlp_out, saved)


def block_backward(
    saved,
    grad_top,
    gain_a,
    query_key_value_weight,
    output_weight_matrix,
    gain_m,
    up_weight_matrix,
    down_weight_matrix,
    attend_grad,
):
    (
        resid_in,
        attention_norm,
        projected,
        mixed_state,
        kept,
        middle,
        feedforward_norm,
        hidden_preactivation,
        hidden_activation,
    ) = saved
    top_reduced = grad_top.astype(jnp.bfloat16)
    down_weight_gradient = jnp.einsum(
        "pgr,pgw->rw", hidden_activation, top_reduced, preferred_element_type=jnp.float32
    )
    activation_gradient = jnp.einsum(
        "ayx,cx->ayc", top_reduced, down_weight_matrix, preferred_element_type=jnp.float32
    )
    preactivation_gradient = jax.vjp(gelu_tanh, hidden_preactivation)[1](activation_gradient)[
        0
    ].astype(jnp.bfloat16)
    up_weight_gradient = jnp.einsum(
        "uzb,uzv->bv", feedforward_norm, preactivation_gradient, preferred_element_type=jnp.float32
    )
    norm_portion = jnp.einsum(
        "vok,hk->voh", preactivation_gradient, up_weight_matrix, preferred_element_type=jnp.float32
    )
    grad_norm_m = tensor_sum(norm_portion)
    grad_middle, grad_gain_m = jax.vjp(rms_scale, middle, gain_m)[1](grad_norm_m)
    grad_attn = grad_top + grad_middle
    attention_reduced = grad_attn.astype(jnp.bfloat16)
    output_weight_gradient = jnp.einsum(
        "omi,omj->ij", mixed_state, attention_reduced, preferred_element_type=jnp.float32
    )
    grad_mixed = jnp.einsum(
        "bjw,gw->bjg", attention_reduced, output_weight_matrix, preferred_element_type=jnp.float32
    ).astype(jnp.bfloat16)
    projection_gradient = attend_grad(projected, kept, grad_mixed)
    query_key_value_gradient = jnp.einsum(
        "xgt,axgf->atf", attention_norm, projection_gradient, preferred_element_type=jnp.float32
    )
    input_part = jnp.einsum(
        "gurh,gih->uri",
        projection_gradient,
        query_key_value_weight,
        preferred_element_type=jnp.float32,
    )
    grad_norm_a = tensor_sum(input_part)
    grad_resid, grad_gain_a = jax.vjp(rms_scale, resid_in, gain_a)[1](grad_norm_a)
    return (
        grad_attn,
        grad_middle,
        grad_resid,
        (
            grad_gain_a,
            query_key_value_gradient,
            output_weight_gradient,
            grad_gain_m,
            up_weight_gradient,
            down_weight_gradient,
        ),
    )


def pack_grads(grad_list, dims, groups):
    flats = []
    shapes = []
    for grad_item, which_dim in zip(grad_list, dims):
        moved = jnp.moveaxis(grad_item, which_dim, 0)
        shapes.append(moved.shape)
        flats.append(moved.reshape(groups, -1))
    return (jnp.concatenate(flats, axis=1), shapes)


def unpack_grads(summed, shapes, dims, groups):
    results = []
    offset = 0
    for moved_shape, which_dim in zip(shapes, dims):
        share_shape = (moved_shape[0] // groups,) + tuple(moved_shape[1:])
        width = math_prod(share_shape)
        piece = summed[0, offset : offset + width].reshape(share_shape)
        results.append(jnp.moveaxis(piece, 0, which_dim))
        offset = offset + width
    return tuple(results)


def math_prod(shape):
    total = 1
    for extent in shape:
        total = total * extent
    return total


def spread_grads(grad_list, dims):
    groups = lax.axis_size("dp") * lax.axis_size("ctx")
    packed, shapes = pack_grads(grad_list, dims, groups)
    summed = lax.psum_scatter(packed, ("dp", "ctx"), scatter_dimension=0, tiled=True)
    return unpack_grads(summed, shapes, dims, groups)


def plain_local(
    hidden_in,
    teacher,
    seg_ids,
    valid,
    routed_idx,
    attn_gain,
    w_qkv,
    w_out,
    mlp_gain,
    w_up,
    w_down,
    w_router,
):
    seqs_local, local_len, model_width = hidden_in.shape
    seq_len = seg_ids.shape[1]
    routed = routed_idx.shape[1]
    ctx_count = lax.axis_size("ctx")
    ctx_place = lax.axis_index("ctx")
    routed_local = routed // ctx_count
    dense_qpos = jnp.broadcast_to(
        ctx_place * local_len + jnp.arange(local_len, dtype=jnp.int32), (seqs_local, local_len)
    )
    dense_kpos = jnp.broadcast_to(jnp.arange(seq_len, dtype=jnp.int32), (seqs_local, seq_len))
    dense_qseg = lax.dynamic_slice_in_dim(seg_ids, ctx_place * local_len, local_len, 1)
    routed_seg = take_rows(seg_ids, routed_idx)
    routed_qpos = lax.dynamic_slice_in_dim(routed_idx, ctx_place * routed_local, routed_local, 1)
    routed_qseg = lax.dynamic_slice_in_dim(routed_seg, ctx_place * routed_local, routed_local, 1)
    owner_mine = routed_idx // local_len == ctx_place
    owner_row = routed_idx % local_len
    dense_attend, dense_grad = make_attention(dense_qpos, dense_kpos, dense_qseg, seg_ids)
    routed_attend, routed_grad = make_attention(routed_qpos, routed_idx, routed_qseg, routed_seg)
    x_input = hidden_in.astype(jnp.float32)
    attn_d, mlp_d, saved_d = block_forward(
        x_input, attn_gain[0], w_qkv[0], w_out[0], mlp_gain[0], w_up[0], w_down[0], dense_attend
    )
    layer_mid = saved_d[5] + mlp_d
    picked = (
        jnp.where(owner_mine[..., None], take_rows(layer_mid, owner_row), 0.0)
        .astype(jnp.bfloat16)
        .astype(jnp.float32)
    )
    chosen = to_workers(picked).astype(jnp.bfloat16).astype(jnp.float32)
    gating = gating_fn(chosen, w_router)
    attn_r, mlp_r, saved_r = block_forward(
        chosen, attn_gain[1], w_qkv[1], w_out[1], mlp_gain[1], w_up[1], w_down[1], routed_attend
    )
    branch_sum = attn_r + mlp_r
    sent_rows = (gating[..., None] * branch_sum).astype(jnp.bfloat16)
    returned = to_owners(sent_rows).astype(jnp.float32)
    layer_out = add_rows(layer_mid, owner_row, jnp.where(owner_mine[..., None], returned, 0.0))
    valid_rows = valid.astype(jnp.float32)
    error_rows = layer_out - teacher.astype(jnp.float32)
    error_sum, valid_count = lax.psum(
        (jnp.sum(valid_rows[..., None] * error_rows * error_rows), jnp.sum(valid_rows)),
        ("dp", "ctx"),
    )
    loss_value = error_sum / (valid_count * model_width)
    token_total = float(seqs_local * seq_len * lax.axis_size("dp"))
    grad_final = token_total / valid_count * valid_rows[..., None] * error_rows
    picked_grad = (
        jnp.where(owner_mine[..., None], take_rows(grad_final, owner_row), 0.0)
        .astype(jnp.bfloat16)
        .astype(jnp.float32)
    )
    branch_grad = to_workers(picked_grad).astype(jnp.bfloat16).astype(jnp.float32)
    grad_top = gating[..., None] * branch_grad
    gating_share, gating_back = jax.vjp(gating_fn, chosen, w_router)
    grad_gating = jnp.sum(branch_grad * branch_sum, axis=-1)
    grad_chosen_gate, grad_router = gating_back(grad_gating)
    grad_attn_r, grad_middle_r, grad_resid_r, grads_r = block_backward(
        saved_r,
        grad_top,
        attn_gain[1],
        w_qkv[1],
        w_out[1],
        mlp_gain[1],
        w_up[1],
        w_down[1],
        routed_grad,
    )
    grad_chosen = (grad_middle_r + grad_resid_r + grad_chosen_gate).astype(jnp.bfloat16)
    grads_r = grads_r + (grad_router,)
    spread_r = spread_grads(grads_r, (0, 1, 1, 0, 0, 1, 0))
    grad_rows = to_owners(grad_chosen).astype(jnp.float32)
    grad_mid = add_rows(grad_final, owner_row, jnp.where(owner_mine[..., None], grad_rows, 0.0))
    grad_attn_d, grad_middle_d, grad_resid_d, grads_d = block_backward(
        saved_d,
        grad_mid,
        attn_gain[0],
        w_qkv[0],
        w_out[0],
        mlp_gain[0],
        w_up[0],
        w_down[0],
        dense_grad,
    )
    grad_input = grad_attn_d + grad_resid_d
    spread_d = spread_grads(grads_d, (0, 1, 1, 0, 0, 1))
    return (
        layer_out.astype(jnp.bfloat16),
        loss_value,
        grad_input,
        jnp.stack([spread_d[0], spread_r[0]]),
        jnp.stack([spread_d[1], spread_r[1]]),
        jnp.stack([spread_d[2], spread_r[2]]),
        jnp.stack([spread_d[3], spread_r[3]]),
        jnp.stack([spread_d[4], spread_r[4]]),
        jnp.stack([spread_d[5], spread_r[5]]),
        spread_r[6],
    )


def column(row, start, length):
    wanted = start + lax.broadcasted_iota(jnp.int32, (length, 1), 0)
    hit = lax.broadcasted_iota(jnp.int32, (length, row.shape[1]), 1) == wanted
    return jnp.sum(jnp.where(hit, row, jnp.zeros_like(row)), axis=-1, keepdims=True)


def head_pair(rows):
    lane = lax.broadcasted_iota(jnp.int32, rows.shape, 1)
    zero = jnp.zeros_like(rows)
    return jnp.concatenate([jnp.where(lane < HEAD, rows, zero), jnp.where(lane >= HEAD, rows, zero)], axis=0)


def pair_join(stacked):
    half = stacked.shape[0] // 2
    lane = lax.broadcasted_iota(jnp.int32, (half, stacked.shape[1]), 1)
    return jnp.where(lane < HEAD, stacked[:half], stacked[half:])


FWD_LAGS = (1, 2, 3, 4, 5, 6)
CHUNK = 128
SUB = 2
FSUB = 2


def dense_forward_kernel(
    sizes,
    x_ref, again_ref, mgain_ref, seg_ref, valid_ref, wqkv_h, wout_h, wup_h, wdn_h,
    x2_ref, q_h, k_h, v_h, mix_h, lse_h, mid_h, pre_h, cnt_out,
    q_ref, k_ref, v_ref, mix_ref, lse_ref, mid_ref, pre_ref,
    wqkv, wout, wup, wdn, part, part2,
    sE, rE, sI, rI, sO, sE2, rE2, sX, rX, cbuf,
    wsem, osem, kvs, kvr, cs, cr, ss, rs,
):
    NC, SUBS, R, D, L, S, NT, NDP, NCTX = sizes
    RS = R // SUBS
    NM = NC * SUBS
    ln = Line()
    ctx = lax.axis_index("ctx")
    half = RS // 2
    loads = [
        pltpu.make_async_copy(wqkv_h.at[0], wqkv, wsem.at[0]),
        pltpu.make_async_copy(wout_h.at[0], wout, wsem.at[1]),
        pltpu.make_async_copy(wup_h.at[0], wup, wsem.at[2]),
        pltpu.make_async_copy(wdn_h.at[0], wdn, wsem.at[3]),
    ]
    for ld in loads:
        ld.start()
    tpeers = tensor_peers(NT)
    rpeers = row_peers(NDP, NCTX)
    greet(tpeers + rpeers)

    cbuf[0] = jnp.full((8, 128), jnp.sum(valid_ref[...].astype(F32)))
    counts = [rcopy(cbuf.at[0], cbuf.at[j + 1], cs.at[j], cr.at[j], p) for j, p in enumerate(rpeers)]
    for cp in counts:
        cp.start()

    @pl.when(ln.is_end)
    def _():
        def zero(k, _):
            rE[k] = jnp.zeros((RS, D), BF)
            return 0

        lax.fori_loop(0, NM, zero, 0)

    loads[0].wait()
    RB = 128
    again = again_ref[0:1, :]

    def project(i, _):
        rows = pl.ds(pl.multiple_of(i * RB, RB), RB)
        xv = x_ref[rows, :].astype(F32)
        n1 = (rms_parts(xv)[1] * again).astype(BF)
        for c, ref in enumerate((q_ref, k_ref, v_ref)):
            y = dot_nn(n1, wqkv[c]).astype(BF)
            if c == 0:
                ref[rows, :] = y * jnp.asarray(0.125, BF)
            else:
                ref[pl.ds(pl.multiple_of(ctx * L + i * RB, RB), RB), :] = y
        return 0

    lax.fori_loop(0, L // RB, project, 0)

    own = pl.ds(pl.multiple_of(ctx * L, L), L)

    def kv_copy(ref, which, c_to):
        return rcopy(ref.at[own, :], ref.at[own, :], kvs.at[which, c_to], kvr.at[which, ctx], {"ctx": c_to})

    def kv_arrive(c_from):
        theirs = pl.ds(c_from * L, L)
        for which, ref in enumerate((k_ref, v_ref)):
            rcopy(ref.at[theirs, :], ref.at[theirs, :], kvs.at[which, c_from], kvr.at[which, c_from], {"ctx": c_from}).wait_recv()

    for c_to in range(NCTX):
        @pl.when(c_to != ctx)
        def _(c_to=c_to):
            kv_copy(k_ref, 0, c_to).start()
            kv_copy(v_ref, 1, c_to).start()

    loads[1].wait()
    loads[2].wait()
    loads[3].wait()
    for c_from in range(NCTX - 1):
        pl.when(c_from < ctx)(functools.partial(kv_arrive, c_from))

    whole = [pltpu.make_async_copy(a, b, osem.at[n, 0]) for n, (a, b) in enumerate(((q_ref, q_h), (k_ref, k_h), (v_ref, v_h)))]
    whole[0].start()
    mgain = mgain_ref[0:1, :]
    groups = q_ref.shape[1] // 128

    def keep_copy(n, src, dst, i):
        rows = pl.ds(pl.multiple_of(i * R, R), R)
        return pltpu.make_async_copy(src.at[rows, :], dst.at[rows, :], osem.at[n, i])

    def keep_early(i):
        return (keep_copy(3, mix_ref, mix_h, i), keep_copy(4, lse_ref, lse_h, i))

    def keep_late(i):
        return (keep_copy(5, mid_ref, mid_h, i), keep_copy(6, pre_ref, pre_h, i))

    def attend(i, keys):
        rows = pl.ds(pl.multiple_of(i * R, R), R)
        qpos = ctx * L + i * R + lax.broadcasted_iota(jnp.int32, (R, 1), 0)
        qseg = column(seg_ref[...], ctx * L + i * R, R)
        kpos = lax.broadcasted_iota(jnp.int32, (1, keys), 1)
        visible = (kpos <= qpos) & (seg_ref[:, :keys] == qseg)
        bias = jnp.where(visible, 0.0, masked_value)
        lane = lax.broadcasted_iota(jnp.int32, (R, 128), 1)
        lse_tile = jnp.zeros((R, 128), F32)
        for g in range(groups):
            cols = slice(128 * g, 128 * g + 128)
            q2 = head_pair(q_ref[rows, cols])
            s = dot_nt(q2, k_ref[:keys, cols]).reshape(2, R, keys) + bias[None]
            top = jnp.max(s, axis=-1, keepdims=True)
            p = jnp.exp(s - top)
            total = jnp.sum(p, axis=-1, keepdims=True)
            pr = (p * (1.0 / total)).astype(BF).reshape(2 * R, keys)
            lse = top + jnp.log(total)
            lse_tile = jnp.where(lane == 2 * g, lse[0], jnp.where(lane == 2 * g + 1, lse[1], lse_tile))
            o = dot_nn(pr, v_ref[:keys, cols])
            mix_ref[rows, cols] = pair_join(o).astype(BF)
        lse_ref[rows, :] = lse_tile

    a1, a2, a3, a4, a5, a6 = FWD_LAGS
    lag3 = jnp.where(ln.is_end, a3, a2)
    my_rows = pl.ds(pl.multiple_of(ln.side * half, half), half)
    ot_rows = pl.ds(pl.multiple_of((1 - ln.side) * half, half), half)

    def got(buf, flow, j):
        rcopy(buf.at[j], buf.at[j], ss.at[flow, j], rs.at[flow, j], ln.mid).wait_recv()

    def got_half(rows, flow, j):
        rcopy(x2_ref.at[j, rows, :], x2_ref.at[j, rows, :], ss.at[flow, j], rs.at[flow, j], ln.mid).wait_recv()

    def each(j, fn):
        for s in range(SUBS):
            fn(j * SUBS + s)

    def body(i, _):
        @pl.when(i < NC)
        def _():
            @pl.when(ctx == 0)
            def _():
                attend(i, L)

            @pl.when(ctx > 0)
            def _():
                attend(i, S)

            for s in range(SUBS):
                m = i * SUBS + s
                p = dot_nn(mix_ref[pl.ds(pl.multiple_of(i * R + s * RS, RS), RS), :], wout[...])
                part[m] = p

                @pl.when(ln.is_end)
                def _(m=m, p=p):
                    sE[m] = p.astype(BF)
                    rcopy(sE.at[m], rE.at[m], ss.at[0, m], rs.at[0, m], ln.mid).start()

            for cp in keep_early(i):
                cp.start()

        j1 = i - a1

        @pl.when(ln.is_mid & (j1 >= 0) & (j1 < NC))
        def _():
            def forward(m):
                got(rE, 0, m)
                sI[m] = (rE[m].astype(F32) + part[m]).astype(BF)
                rcopy(sI.at[m], rI.at[m], ss.at[1, m], rs.at[1, m], ln.other).start()

            each(j1, forward)

        j3 = i - lag3

        @pl.when((j3 >= 0) & (j3 < NC))
        def _():
            def arrive(m):
                got(rI, 1, m)

                @pl.when(ln.is_mid)
                def _():
                    sO[m] = (rI[m].astype(F32) + part[m]).astype(BF)
                    rcopy(sO.at[m], rI.at[m], ss.at[2, m], rs.at[1, m], ln.end).start()

            each(j3, arrive)
            ms = pl.ds(j3 * SUBS, SUBS)
            rows = pl.ds(pl.multiple_of(j3 * R, R), R)
            total = (rI[ms].astype(F32) + part[ms] + rE[ms].astype(F32)).reshape(R, D)
            mid = x_ref[rows, :].astype(F32) + total
            mid_ref[rows, :] = mid
            n2 = (rms_parts(mid)[1] * mgain).astype(BF)
            pre = dot_nn(n2, wup[...])
            pre_ref[rows, :] = pre
            for cp in keep_late(j3):
                cp.start()
            act = (0.5 * pre * (1.0 + gelu_pair(pre))).astype(BF)
            for s in range(SUBS):
                m = j3 * SUBS + s
                p2 = dot_nn(act[s * RS : (s + 1) * RS], wdn[...])

                @pl.when(ln.is_end)
                def _(m=m, p2=p2):
                    sE2[m] = p2.astype(BF)
                    rcopy(sE2.at[m], rE2.at[m], ss.at[3, m], rs.at[3, m], ln.mid).start()

                @pl.when(ln.is_mid)
                def _(m=m, p2=p2):
                    part2[m] = p2

        j6 = i - a6

        @pl.when(ln.is_mid & (j6 >= 0) & (j6 < NC))
        def _():
            def relay(m):
                got_half(ot_rows, 5, m)
                theirs = x2_ref.at[m, ot_rows, :]
                rcopy(theirs, theirs, ss.at[7, m], rs.at[7, m], ln.end).start()

            each(j6, relay)

        j5 = i - a5

        @pl.when(ln.is_mid & (j5 >= 0) & (j5 < NC))
        def _():
            def settle(m):
                got(rX, 4, m)
                rows = pl.ds(pl.multiple_of(m * RS + ln.side * half, half), half)
                mlp = part2[m, my_rows, :] + rE2[m, my_rows, :].astype(F32) + rX[m].astype(F32)
                x2_ref[m, my_rows, :] = (mid_ref[rows, :] + mlp).astype(BF)
                mine = x2_ref.at[m, my_rows, :]
                rcopy(mine, mine, ss.at[5, m], rs.at[5, m], ln.other).start()
                rcopy(mine, mine, ss.at[6, m], rs.at[6, m], ln.end).start()

            each(j5, settle)

        j4 = i - a4

        @pl.when(ln.is_mid & (j4 >= 0) & (j4 < NC))
        def _():
            def cross(m):
                got(rE2, 3, m)
                sX[m] = (rE2[m, ot_rows, :].astype(F32) + part2[m, ot_rows, :]).astype(BF)
                rcopy(sX.at[m], rX.at[m], ss.at[4, m], rs.at[4, m], ln.other).start()

            each(j4, cross)

        return 0

    lax.fori_loop(0, NC + a6, body, 0)

    for cp in counts:
        cp.wait()
    total = cbuf[0]
    for j in range(1, len(rpeers) + 1):
        total = total + cbuf[j]
    cnt_out[...] = total

    for c in range(NCTX):
        pl.when(c > ctx)(functools.partial(kv_arrive, c))

        @pl.when(c != ctx)
        def _(c=c):
            kv_copy(k_ref, 0, c).wait_send()
            kv_copy(v_ref, 1, c).wait_send()

    whole[1].start()
    whole[2].start()
    for cp in whole:
        cp.wait()

    def kept(i, _):
        for cp in keep_early(i) + keep_late(i):
            cp.wait()
        return 0

    lax.fori_loop(0, NC, kept, 0)

    def drain(m, _):
        @pl.when(ln.is_end)
        def _():
            got_half(my_rows, 6, m)
            got_half(ot_rows, 7, m)
            rcopy(sE.at[m], rE.at[m], ss.at[0, m], rs.at[0, m], ln.mid).wait_send()
            rcopy(sE2.at[m], rE2.at[m], ss.at[3, m], rs.at[3, m], ln.mid).wait_send()

        @pl.when(ln.is_mid)
        def _():
            rcopy(sI.at[m], rI.at[m], ss.at[1, m], rs.at[1, m], ln.other).wait_send()
            rcopy(sO.at[m], rI.at[m], ss.at[2, m], rs.at[1, m], ln.end).wait_send()
            rcopy(sX.at[m], rX.at[m], ss.at[4, m], rs.at[4, m], ln.other).wait_send()
            mine = x2_ref.at[m, my_rows, :]
            theirs = x2_ref.at[m, ot_rows, :]
            rcopy(mine, mine, ss.at[5, m], rs.at[5, m], ln.other).wait_send()
            rcopy(mine, mine, ss.at[6, m], rs.at[6, m], ln.end).wait_send()
            rcopy(theirs, theirs, ss.at[7, m], rs.at[7, m], ln.end).wait_send()

        return 0

    lax.fori_loop(0, NM, drain, 0)


def dense_forward(x, again, mgain, seg, valid, w_qkv, w_out, w_up, w_down):
    L, D = x.shape
    S = seg.shape[1]
    NT, NDP, NCTX = lax.axis_size("tensor"), lax.axis_size("dp"), lax.axis_size("ctx")
    R = min(CHUNK, L)
    NC = L // R
    RS = R // FSUB
    NM = NC * FSUB
    Hd = w_out.shape[1]
    Fl = w_up.shape[2]
    sizes = (NC, FSUB, R, D, L, S, NT, NDP, NCTX)
    flows = 8
    dma = pltpu.SemaphoreType.DMA
    rows = NDP * NCTX
    sd = jax.ShapeDtypeStruct
    v = pl.BlockSpec(memory_space=VM)
    a = pl.BlockSpec(memory_space=ANY)
    big = VM((NM, RS, D), BF)
    return pl.pallas_call(
        functools.partial(dense_forward_kernel, sizes),
        name="dense_forward",
        out_shape=(
            sd((NM, RS, D), BF), sd((L, Hd), BF), sd((S, Hd), BF), sd((S, Hd), BF), sd((L, Hd), BF),
            sd((L, 128), F32), sd((L, D), F32), sd((L, Fl), F32), sd((8, 128), F32),
        ),
        in_specs=[v] * 5 + [a] * 4,
        out_specs=(v,) + (a,) * 7 + (v,),
        scratch_shapes=[
            VM((L, Hd), BF), VM((S, Hd), BF), VM((S, Hd), BF), VM((L, Hd), BF), VM((L, 128), F32), VM((L, D), F32), VM((L, Fl), F32),
            VM((3, D, Hd), BF), VM((Hd, D), BF), VM((D, Fl), BF), VM((Fl, D), BF),
            VM((NM, RS, D), F32), VM((NM, RS, D), F32),
            big, big, big, big, big, big, big, VM((NM, RS // 2, D), BF), VM((NM, RS // 2, D), BF),
            VM((rows, 8, 128), F32),
            dma((4,)), dma((7, NC)), dma((2, NCTX)), dma((2, NCTX)), dma((rows,)), dma((rows,)), dma((flows, NM)), dma((flows, NM)),
        ],
        compiler_params=pltpu.CompilerParams(collective_id=1, has_side_effects=True, vmem_limit_bytes=58 << 20),
    )(x, again, mgain, seg, valid, w_qkv, w_out, w_up, w_down)


TAIL_LAGS = (1, 2, 3)
BCHUNK = 128


def split_pick(pick, values, terms):
    total = None
    rest = values
    for _ in range(terms):
        low = rest.astype(BF)
        got = dot_nn(pick, low)
        total = got if total is None else total + got
        rest = rest - low.astype(F32)
    return total


def gelu_slope(u, t):
    return 0.5 * (1.0 + t) + 0.5 * u * (1.0 - t * t) * (0.7978845608028654 * (1.0 + 3.0 * 0.044715 * u * u))


def backward_kernel(
    sizes,
    x_ref, valid_ref, cnt_ref, ridx_ref, seg_ref, again_ref, mgain_ref, router_ref,
    x2_h, teach_h, q_h, k_h, v_h, mix_h, lse_h, mid_h, pre_h, wqkv_h, wout_h, wup_h, wdn_h,
    hid_ref, loss_ref, gin_ref, dn_o, up_o, out_o, qkv_o, small_o,
    q_ref, k_ref, v_ref, mix_ref, lse_ref, mid_ref, g_s,
    wqkv, wout_r, wup_r, wdn_r, wout, wup, wdn,
    gm_s, act_s, gpre_s, n2_s, ga_s, part, gqkv, dk_s, dv_s,
    sE, rE, sI, rI, sO, rX,
    out_buf, odn, udn, xdn, oup, uup, xup, oout, uout, xout, oqkv, uqkv, xqkv,
    pick_s, xs, xc, tsel, tc, vsel, vc, posc, segq, n1_r, k_r, v_r, q2_r, p_r, mix_r, n2_r, act_r, slope_r, gpre_r, gm_r, ga_r, gqkv_r, dkv_r, dkvc,
    part_r, attn_o, mid_o, gate_o, branch_o, gmid_o, ggate_o, top_o, g3c, gch_s, sent_s, h_all, gq_all, sbuf, rbuf,
    psel, pc, msel, mc, qsel, qc, lsel, lc,
    acc_m, acc_a, lacc, lbuf, vec, vbuf, hbuf,
    isem, xsem, xrem, free, ps, pr_, gs, gr, kvs, kvr, s1, r1, s1d, r1d, s2, r2, s3, r3, cs, cr, ts, tr, ss, rs,
):
    NC, SUBS, R, D, L, S, RT, NT, NDP, NCTX, scale_total = sizes
    RS = R // SUBS
    NM = NC * SUBS
    RL = RT // NCTX
    Q = RL // NT
    G = NDP * NCTX
    W = D // G
    ln = Line()
    t = ln.t
    ctx = lax.axis_index("ctx")
    dp = lax.axis_index("dp")
    me = dp * NCTX + ctx
    across = {"ctx": 1 - ctx}
    half = RS // 2
    order = (
        (x2_h, hid_ref), (teach_h, gin_ref), (wqkv_h.at[1], wqkv), (wout_h.at[1], wout_r), (wup_h.at[1], wup_r), (wdn_h.at[1], wdn_r),
        (pre_h, g_s), (mid_h, mid_ref), (q_h, q_ref), (lse_h, lse_ref), (wdn_h.at[0], wdn), (wup_h.at[0], wup), (wout_h.at[0], wout),
        (k_h, k_ref), (v_h, v_ref), (mix_h, mix_ref), (wqkv_h.at[0], wqkv),
    )
    loads = [pltpu.make_async_copy(a, b, isem.at[n]) for n, (a, b) in enumerate(order)]
    for ld in loads[:16]:
        ld.start()
    tpeers = tensor_peers(NT)
    rpeers = row_peers(NDP, NCTX)
    greet(tpeers + rpeers)
    my = pl.ds(pl.multiple_of(ctx * RL, RL), RL)
    theirs = pl.ds(pl.multiple_of((1 - ctx) * RL, RL), RL)
    own = pl.ds(pl.multiple_of(t * Q, Q), Q)
    mine16 = pl.ds(pl.multiple_of(ctx * RL + t * Q, Q), Q)
    late = pl.ds(L, RL)
    again = again_ref[0:1, :]
    mgain = mgain_ref[0:1, :]
    again_r = again_ref[1:2, :]
    mgain_r = mgain_ref[1:2, :]
    router = router_ref[...]
    ga_all = xc
    scale = scale_total / cnt_ref[0:1, 0:1]
    Hd = q_ref.shape[1]
    groups = Hd // 128

    def pair(n, src, dst):
        return rcopy(src, dst, xsem.at[n], xrem.at[n], across)

    def pair_rows(n, ref):
        return pair(n, ref.at[my, :], ref.at[my, :])

    def pair_rows_in(n, ref):
        return pair(n, ref.at[theirs, :], ref.at[theirs, :])

    idxc = column(ridx_ref[...], 0, RT)
    held = idxc - ctx * L == lax.broadcasted_iota(jnp.int32, (RT, L), 1)
    pick_s[...] = held.astype(F32).astype(BF)
    loads[0].wait()
    xs[...] = dot_nn(pick_s[...], hid_ref[...].reshape(L, D)).astype(BF)
    pair(0, xs, xc).start()
    loads[1].wait()
    tsel[...] = dot_nn(pick_s[...], gin_ref[...].reshape(L, D)).astype(BF)
    vsel[...] = jnp.broadcast_to(jnp.sum(jnp.where(held, valid_ref[...].astype(F32), 0.0), axis=-1, keepdims=True), (RT, 128))
    pair(1, tsel.at[theirs, :], tc).start()
    pair(2, vsel.at[theirs, :], vc).start()
    at = idxc == lax.broadcasted_iota(jnp.int32, (RT, S), 1)
    posc[...] = jnp.broadcast_to(idxc, (RT, 128))
    seg_col = jnp.sum(jnp.where(at, seg_ref[...], 0), axis=-1, keepdims=True)
    segq[...] = jnp.broadcast_to(seg_col, (RT, 128))
    same = lax.broadcasted_iota(jnp.int32, (RT, RT), 0) == lax.broadcasted_iota(jnp.int32, (RT, RT), 1)
    seg_row = jnp.sum(jnp.where(same, seg_col, 0), axis=0, keepdims=True)
    bias_r = jnp.where((ridx_ref[...] <= posc[my, 0:1]) & (seg_row == segq[my, 0:1]), 0.0, masked_value)

    for n in range(2, 6):
        loads[n].wait()
    pair(0, xs, xc).wait()
    chosen = xs[...].astype(F32) + xc[...].astype(F32)
    xs[...] = chosen.astype(BF)
    n1 = (rms_parts(chosen)[1] * again_r).astype(BF)
    n1_r[...] = n1
    k_r[...] = dot_nn(n1, wqkv[1]).astype(BF)
    v_r[...] = dot_nn(n1, wqkv[2]).astype(BF)
    q = dot_nn(n1_r[my, :], wqkv[0]).astype(BF) * jnp.asarray(0.125, BF)
    for g in range(groups):
        cols = slice(128 * g, 128 * g + 128)
        q2 = head_pair(q[:, cols])
        s = dot_nt(q2, k_r[:, cols]).reshape(2, RL, RT) + bias_r[None]
        p = jnp.exp(s - jnp.max(s, axis=-1, keepdims=True))
        p = (p * (1.0 / jnp.sum(p, axis=-1, keepdims=True))).reshape(2 * RL, RT)
        q2_r[g] = q2
        p_r[g] = p
        mix_r[:, cols] = pair_join(dot_nn(p.astype(BF), v_r[:, cols])).astype(BF)

    def piece_copy(step, j):
        to = lax.rem(t + j, NT)
        rows = pl.ds(pl.multiple_of(to * Q, Q), Q)
        return rcopy(sbuf.at[step % 2, rows, :], rbuf.at[step, j - 1], ps.at[step, j - 1], pr_.at[step, j - 1], {"tensor": to})

    def spread(step, value):
        part_r[...] = value
        if step >= 2:
            for j in range(1, NT):
                piece_copy(step - 2, j).wait_send()
        sbuf[step % 2] = value.astype(BF)
        for j in range(1, NT):
            piece_copy(step, j).start()

    def collect(step):
        total = part_r[own, :]
        for j in range(1, NT):
            piece_copy(step, j).wait_recv()
            total = total + rbuf[step, j - 1].astype(F32)
        return total

    def gather_copy(step, ref, base_row, j):
        to = lax.rem(t + j, NT)
        rows = pl.ds(pl.multiple_of(base_row + t * Q, Q), Q)
        return rcopy(ref.at[rows, :], ref.at[rows, :], gs.at[step, j - 1], gr.at[step, j - 1], {"tensor": to})

    def gather(step, ref, base_row):
        for j in range(1, NT):
            gather_copy(step, ref, base_row, j).start()

    def gathered(step, ref, base_row):
        for j in range(1, NT):
            gather_copy(step, ref, base_row, j).wait()

    def both_of(d):
        return pl.ds(pl.multiple_of(d * NCTX * W, NCTX * W), NCTX * W)

    def by_share(piece, send, keep):
        def one(d, _):
            for lo, width, val in piece(both_of(d)):
                for c in range(NCTX):
                    rows = val[c * W : (c + 1) * W].astype(BF)

                    @pl.when(ctx == c)
                    def _(rows=rows, lo=lo, width=width):
                        keep[d, :, lo : lo + width] = rows

                    @pl.when(ctx != c)
                    def _(rows=rows, lo=lo, width=width):
                        send[d, :, lo : lo + width] = rows

            return 0

        lax.fori_loop(0, NDP, one, 0)

    bufs = (
        (out_buf, odn, udn, wdn_r, xdn, dn_o),
        (out_buf, oup, uup, wup_r, xup, up_o),
        (out_buf.at[:, :, pl.ds(0, Hd)], oout, uout, wup, xout, out_o),
        (out_buf.at[:, :, pl.ds(0, 3 * Hd)], oqkv, uqkv, wdn, xqkv, qkv_o),
    )
    widths = (act_s.shape[1], gpre_s.shape[1], Hd, 3 * Hd)
    routed_piece = (
        lambda cols: [(0, act_r.shape[1], dot_tn(gm_r[:, cols], act_r[...]))],
        lambda cols: [(0, gpre_r.shape[1], dot_tn(n2_r[:, cols], gpre_r[...]))],
        lambda cols: [(0, Hd, dot_tn(ga_r[:, cols], mix_r[...]))],
        lambda cols: [(Hd * c, Hd, dot_tn(n1_r[my, cols], gqkv_r[c])) for c in range(3)],
    )
    dense_piece = (
        lambda cols: [(0, act_s.shape[1], dot_tn(gm_s[:, cols], act_s[...]))],
        lambda cols: [(0, gpre_s.shape[1], dot_tn(n2_s[:, cols], gpre_s[...]))],
        lambda cols: [(0, Hd, dot_tn(ga_s[:, cols], mix_ref[...]))],
        lambda cols: [(Hd * c, Hd, dot_tn(sO[:, :, cols].reshape(L, NCTX * W), gqkv[c])) for c in range(3)],
    )

    def routed_pair(w):
        return rcopy(bufs[w][0], bufs[w][2], s1.at[w], r1.at[w], across)

    def dense_pair(w):
        return rcopy(bufs[w][0], bufs[w][2], s1d.at[w], r1d.at[w], across)

    def routed_dp(w, j):
        to = lax.rem(dp + j, NDP)
        return rcopy(bufs[w][1].at[to], bufs[w][4].at[j - 1], s3.at[w, j - 1], r3.at[w, j - 1], {"dp": to})

    def dense_dp(w, j):
        to = lax.rem(dp + j, NDP)
        land = bufs[w][3].at[pl.ds((j - 1) * W, W), pl.ds(0, widths[w])]
        return rcopy(bufs[w][1].at[to], land, s2.at[w, j - 1], r2.at[w, j - 1], {"dp": to})

    def add_pairs(w):
        keep, came = bufs[w][1], bufs[w][2]

        def add(j, _):
            keep[j] = (keep[j].astype(F32) + came[j].astype(F32)).astype(BF)
            return 0

        lax.fori_loop(0, NDP, add, 0)

    def routed_first(w):
        if w:
            routed_pair(w - 1).wait_send()
        by_share(routed_piece[w], bufs[w][0], bufs[w][1])
        routed_pair(w).start()

    def routed_second(w):
        routed_pair(w).wait_recv()
        add_pairs(w)
        put_total(w, 1, bufs[w][1][dp].astype(F32))
        for j in range(1, NDP):
            routed_dp(w, j).start()
        pl.semaphore_signal(free.at[w], inc=1, device_id=across, device_id_type=MESH)

    def dense_first(w):
        before = {0: routed_pair(3), 3: dense_pair(0), 2: dense_pair(3), 1: dense_pair(2)}
        before[w].wait_send()
        for j in range(1, NDP):
            routed_dp(w, j).wait_send()
        by_share(dense_piece[w], bufs[w][0], bufs[w][1])
        pl.semaphore_wait(free.at[w], 1)
        dense_pair(w).start()

    def dense_second(w):
        dense_pair(w).wait_recv()
        add_pairs(w)
        for j in range(1, NDP):
            dense_dp(w, j).start()

    def put_total(w, layer, total, more=False):
        out = bufs[w][5]
        if w == 3:
            for c in range(3):
                piece = total[:, Hd * c : Hd * c + Hd]
                out[layer, c] = out[layer, c] + piece if more else piece
        else:
            piece = total if w == 1 else total.T
            out[layer] = out[layer] + piece if more else piece

    def dense_total(w):
        for j in range(1, NDP):
            dense_dp(w, j).wait()
        total = bufs[w][1][dp].astype(F32)
        for j in range(NDP - 1):
            total = total + bufs[w][3][pl.ds(j * W, W), : widths[w]].astype(F32)
        put_total(w, 0, total)

    def routed_total(w):
        for j in range(1, NDP):
            routed_dp(w, j).wait_recv()
        total = bufs[w][4][0].astype(F32)
        for j in range(1, NDP - 1):
            total = total + bufs[w][4][j].astype(F32)
        put_total(w, 1, total, more=True)

    def got(buf, flow, m):
        rcopy(buf.at[m], buf.at[m], ss.at[flow, m], rs.at[flow, m], ln.mid).wait_recv()

    def each(j, fn):
        for s in range(SUBS):
            fn(j * SUBS + s)

    def place_of(i):
        place = ctx * L + i * R + lax.broadcasted_iota(jnp.int32, (R, 1), 0)
        return (place == ridx_ref[...]).astype(F32)

    def pick_rows():
        psel[...] = split_pick(pick_s[...], g_s[...], 2)
        pair(3, psel.at[theirs, :], pc).start()

    def pick_middle():
        msel[...] = split_pick(pick_s[...], mid_ref[...], 2)
        pair(4, msel.at[theirs, :], mc).start()

    def pick_queries():
        qsel[...] = dot_nn(pick_s[...], q_ref[...]).astype(BF)
        pair(5, qsel.at[theirs, :], qc).start()
        lsel[...] = split_pick(pick_s[...], lse_ref[...], 3)
        pair(6, lsel.at[theirs, :], lc).start()

    def mlp_back(i):
        rows = pl.ds(pl.multiple_of(i * R, R), R)
        ms = pl.ds(i * SUBS, SUBS)
        others = 1.0 - jnp.sum(place_of(i), axis=-1, keepdims=True)
        err = hid_ref[ms].astype(F32).reshape(R, D) - gin_ref[ms].astype(F32).reshape(R, D)
        counted = (column(valid_ref[...].astype(F32), i * R, R) * others) * err
        lacc[...] += fold8(counted * err)
        g2 = scale * counted
        gm = g2.astype(BF)
        gm_s[rows, :] = gm
        gact = dot_nt(gm, wdn[...])
        u = g_s[rows, :]
        th = gelu_pair(u)
        act_s[rows, :] = (0.5 * u * (1.0 + th)).astype(BF)
        gpre = (gact * gelu_slope(u, th)).astype(BF)
        gpre_s[rows, :] = gpre
        g_s[rows, :] = g2
        for s in range(SUBS):
            m = i * SUBS + s
            p3 = dot_nt(gpre[s * RS : (s + 1) * RS], wup[...])
            part[m] = p3

            @pl.when(ln.is_end)
            def _(m=m, p3=p3):
                sE[m] = p3.astype(BF)
                rcopy(sE.at[m], rE.at[m], ss.at[0, m], rs.at[0, m], ln.mid).start()

    def forward_in(j):
        def one(m):
            got(rE, 0, m)
            sI[m] = (rE[m].astype(F32) + part[m]).astype(BF)
            rcopy(sI.at[m], rI.at[m], ss.at[1, m], rs.at[1, m], ln.other).start()

        each(j, one)

    def forward_out(j):
        def one(m):
            got(rI, 1, m)
            sO[m] = (rI[m].astype(F32) + part[m]).astype(BF)
            rcopy(sO.at[m], rI.at[m], ss.at[2, m], rs.at[1, m], ln.end).start()

        each(j, one)

    def attend_back(q_rows, gmix, lse, bias, keys, put):
        n = bias.shape[0]
        for g in range(groups):
            cols = slice(128 * g, 128 * g + 128)
            q2 = head_pair(q_rows[:, cols])
            g2 = head_pair(gmix[:, cols])
            kg = k_ref[:keys, cols]
            vg = v_ref[:keys, cols]
            l2 = jnp.concatenate([lse[:, 2 * g : 2 * g + 1], lse[:, 2 * g + 1 : 2 * g + 2]], axis=0)
            s = (dot_nt(q2, kg).reshape(2, n, keys) + bias[None]).reshape(2 * n, keys)
            p = jnp.exp(s - l2)
            dp_ = dot_nt(g2, vg)
            inner = jnp.sum(p * dp_, axis=-1, keepdims=True)
            ds = (p * (dp_ - inner)).astype(BF)
            put(cols, (pair_join(dot_nn(ds, kg)) * 0.125).astype(BF))
            dk_s[:keys, cols] += dot_tn(ds, q2)
            dv_s[:keys, cols] += dot_tn(p.astype(BF), g2)

    def attention_back(j):
        @pl.when(ln.is_end)
        def _():
            each(j, lambda m: got(rI, 1, m))

        ms = pl.ds(j * SUBS, SUBS)
        rows = pl.ds(pl.multiple_of(j * R, R), R)
        gn2 = (rI[ms].astype(F32) + part[ms] + rE[ms].astype(F32)).reshape(R, D)
        r, unit = rms_parts(mid_ref[rows, :])
        n2_s[rows, :] = (unit * mgain).astype(BF)
        scaled = gn2 * mgain
        gmid = r * (scaled - unit * jnp.mean(scaled * unit, axis=-1, keepdims=True))
        acc_m[...] += fold8(gn2 * unit)
        gattn = g_s[rows, :] + gmid
        g_s[rows, :] = gattn
        ga = gattn.astype(BF)
        ga_s[rows, :] = ga
        gmix = dot_nt(ga, wout[...]).astype(BF)
        qpos = ctx * L + j * R + lax.broadcasted_iota(jnp.int32, (R, 1), 0)
        qseg = column(seg_ref[...], ctx * L + j * R, R)

        def put(cols, gq):
            gqkv[0, rows, cols] = gq

        def run(keys):
            kpos = lax.broadcasted_iota(jnp.int32, (1, keys), 1)
            bias = jnp.where((kpos <= qpos) & (seg_ref[:, :keys] == qseg), 0.0, masked_value)
            attend_back(q_ref[rows, :], gmix, lse_ref[rows, :], bias, keys, put)

        @pl.when(ctx == 0)
        def _():
            run(L)

        @pl.when(ctx > 0)
        def _():
            run(S)

    def send_loss():
        lbuf[me] = jnp.full((8, 128), jnp.sum(lacc[...]))
        for j, p in enumerate(rpeers):
            rcopy(lbuf.at[me], lbuf.at[me], cs.at[j], cr.at[j], p).start()

    def seg0():
        spread(0, dot_nn(mix_r[...], wout_r[...]))

        @pl.when(ln.is_end)
        def _():
            def zero(m, _):
                rE[m] = jnp.zeros((RS, D), BF)
                return 0

            lax.fori_loop(0, NM, zero, 0)

        for ref in (dk_s, dv_s, acc_m, acc_a, lacc):
            ref[...] = jnp.zeros(ref.shape, F32)

        chosen_o = xs[mine16, :].astype(F32)
        gate_o[...] = jnp.broadcast_to(jax.nn.sigmoid(jnp.sum(chosen_o * router, axis=-1, keepdims=True)), (Q, 128))
        for n in range(6, 10):
            loads[n].wait()
        pick_rows()
        for n in range(10, 16):
            loads[n].wait()

    def seg1():
        attn = collect(0)
        attn_o[...] = attn
        mid = xs[mine16, :].astype(F32) + attn
        mid_o[...] = mid
        n2_r[own, :] = (rms_parts(mid)[1] * mgain_r).astype(BF)
        gather(0, n2_r, 0)

    def seg2():
        gathered(0, n2_r, 0)
        pre = dot_nn(n2_r[...], wup_r[...])
        th = gelu_pair(pre)
        act = (0.5 * pre * (1.0 + th)).astype(BF)
        act_r[...] = act
        spread(1, dot_nn(act, wdn_r[...]))
        slope_r[...] = gelu_slope(pre, th)

    def seg3():
        branch = attn_o[...] + collect(1)
        branch_o[...] = branch
        sent_s[own, :] = (gate_o[:, 0:1] * branch).astype(BF)
        gather(1, sent_s, 0)

    def seg4():
        pair(1, tsel.at[theirs, :], tc).wait()
        pair(2, vsel.at[theirs, :], vc).wait()
        chosen_m = xs[my, :].astype(F32)
        gate_m = jax.nn.sigmoid(jnp.sum(chosen_m * router, axis=-1, keepdims=True))
        target = tsel[my, :].astype(F32) + tc[...].astype(F32)
        counted = vsel[my, 0:1] + vc[:, 0:1]
        gathered(1, sent_s, 0)
        x3 = chosen_m + sent_s[...].astype(F32)
        err = x3 - target
        g3 = scale * counted * err
        gsent = g3.astype(BF).astype(F32)
        part_r[...] = gsent
        ggate_o[...] = part_r[own, :]
        top = gate_m * gsent
        part_r[...] = top
        top_o[...] = part_r[own, :]
        gm = top.astype(BF)
        gm_r[...] = gm
        gpre = (dot_nt(gm, wdn_r[...]) * slope_r[...]).astype(BF)
        gpre_r[...] = gpre
        spread(2, dot_nt(gpre, wup_r[...]))
        h_all[my, :] = x3.astype(BF)
        pair_rows(7, h_all).start()
        g3c[...] = g3
        lacc[...] += fold8(counted * err * err)
        gate = gate_o[:, 0:1]
        share = jnp.sum(ggate_o[...] * branch_o[...], axis=-1, keepdims=True) * gate * (1.0 - gate)
        ggate_o[:, 0:128] = jnp.broadcast_to(share, (Q, 128))
        vec[...] = jnp.zeros(vec.shape, F32)
        vec[4:5, :] = jnp.sum(share * xs[mine16, :].astype(F32), axis=0, keepdims=True)

    def seg5():
        gmid, gain_rows = rms_back(mid_o[...], mgain_r, collect(2))
        gmid_o[...] = gmid
        vec[3:4, :] = jnp.sum(gain_rows, axis=0, keepdims=True)
        ga_r[own, :] = (top_o[...] + gmid).astype(BF)
        gather(2, ga_r, 0)

    def seg6():
        gathered(2, ga_r, 0)
        gmix = dot_nt(ga_r[...], wout_r[...]).astype(BF)
        for g in range(groups):
            cols = slice(128 * g, 128 * g + 128)
            p = p_r[g]
            g2 = head_pair(gmix[:, cols])
            dp_ = dot_nt(g2, v_r[:, cols])
            ds = (p * (dp_ - jnp.sum(p * dp_, axis=-1, keepdims=True))).astype(BF)
            gqkv_r[0, :, cols] = (pair_join(dot_nn(ds, k_r[:, cols])) * 0.125).astype(BF)
            dkv_r[0, :, cols] = dot_tn(ds, q2_r[g])
            dkv_r[1, :, cols] = dot_tn(p.astype(BF), g2)
        swaps = [pair(8 + c, dkv_r.at[c, theirs, :], dkvc.at[c]) for c in range(2)]
        for cp in swaps:
            cp.start()
        p4 = dot_nt(gqkv_r[0], wqkv[0])
        for c in range(2):
            swaps[c].wait()
            gqkv_r[1 + c] = (dkv_r[c, my, :] + dkvc[c]).astype(BF)
            p4 = p4 + dot_nt(gqkv_r[1 + c], wqkv[1 + c])
        spread(3, p4)
        loads[16].start()

    def seg7():
        chosen_o = xs[mine16, :].astype(F32)
        gin, gain_rows = rms_back(chosen_o, again_r, collect(3))
        vec[2:3, :] = jnp.sum(gain_rows, axis=0, keepdims=True)
        gch_s[own, :] = (gmid_o[...] + gin + ggate_o[:, 0:1] * router).astype(BF)
        gather(3, gch_s, 0)

    def seg8():
        for n, (src, dst) in enumerate(((psel, pc), (msel, mc), (qsel, qc), (lsel, lc))):
            pair(3 + n, src.at[theirs, :], dst).wait()
        u = psel[my, :] + pc[...]
        th = gelu_pair(u)
        slope = gelu_slope(u, th)
        act_s[late, :] = (0.5 * u * (1.0 + th)).astype(BF)
        mid = msel[my, :] + mc[...]
        mc[...] = mid
        n2_s[late, :] = (rms_parts(mid)[1] * mgain).astype(BF)
        gathered(3, gch_s, 0)
        g2 = g3c[...] + gch_s[...].astype(F32)
        g3c[...] = g2
        gm = g2.astype(BF)
        gm_s[late, :] = gm
        gpre = (dot_nt(gm, wdn[...]) * slope).astype(BF)
        gpre_s[late, :] = gpre
        spread(4, dot_nt(gpre, wup[...]))

    def seg9():
        gmid, gain_rows = rms_back(mc[own, :], mgain, collect(4))
        vec[1:2, :] = jnp.sum(gain_rows, axis=0, keepdims=True)
        ga_all[mine16, :] = (g3c[own, :] + gmid).astype(BF)
        gather(4, ga_all, ctx * RL)

    def kv_copy(which):
        src = (dk_s, dv_s)[which]
        rows = pl.ds(pl.multiple_of((1 - ctx) * L, L), L)
        return rcopy(src.at[rows, :], mid_ref.at[:, pl.ds(which * Hd, Hd)], kvs.at[which], kvr.at[which], across)

    def seg10():
        gathered(4, ga_all, ctx * RL)
        pair_rows(10, ga_all).start()
        gmix = dot_nt(ga_all[my, :], wout[...]).astype(BF)
        kpos = lax.broadcasted_iota(jnp.int32, (1, S), 1)
        bias = jnp.where((kpos <= posc[my, 0:1]) & (seg_ref[...] == segq[my, 0:1]), 0.0, masked_value)

        def put(cols, gq):
            gq_all[my, cols] = gq

        attend_back((qsel[my, :].astype(F32) + qc[...].astype(F32)).astype(BF), gmix, lsel[my, :] + lc[...], bias, S, put)
        pl.semaphore_wait(free.at[4], 1)
        kv_copy(0).start()
        kv_copy(1).start()
        pair_rows(11, gq_all).start()

    def mid_is_free():
        pl.semaphore_signal(free.at[4], inc=1, device_id=across, device_id_type=MESH)

    segments = (seg0, seg1, seg2, seg3, seg4, seg5, seg6, seg7, seg8, seg9)
    extras = {
        1: (pick_middle,),
        2: (pick_queries,),
        4: (lambda: routed_first(0),),
        5: (lambda: routed_first(1),),
        6: (lambda: routed_first(2), lambda: routed_second(0)),
        7: (lambda: routed_first(3), lambda: routed_second(1)),
        8: (lambda: routed_second(2),),
        9: (mid_is_free, lambda: routed_second(3), send_loss, lambda: dense_first(0)),
    }
    LF, LO, LC = CHAIN_LAGS

    def step(w, _):
        for n, fn in enumerate(segments):
            pl.when(w == n)(fn)

        for n, fns in extras.items():
            @pl.when(w == n)
            def _(fns=fns):
                for fn in fns:
                    fn()

        @pl.when(w < NC)
        def _():
            mlp_back(w)

        jf = w - LF

        @pl.when(ln.is_mid & (jf >= 0) & (jf < NC))
        def _():
            forward_in(jf)

        jo = w - LO

        @pl.when(ln.is_mid & (jo >= 0) & (jo < NC))
        def _():
            forward_out(jo)

        jc = w - LC

        @pl.when((jc >= 0) & (jc < NC))
        def _():
            attention_back(jc)

        return 0

    lax.fori_loop(0, len(segments), step, 0)
    seg10()

    def settle_sends(m, _):
        @pl.when(ln.is_end)
        def _():
            rcopy(sE.at[m], rE.at[m], ss.at[0, m], rs.at[0, m], ln.mid).wait_send()

        @pl.when(ln.is_mid)
        def _():
            rcopy(sI.at[m], rI.at[m], ss.at[1, m], rs.at[1, m], ln.other).wait_send()
            rcopy(sO.at[m], rI.at[m], ss.at[2, m], rs.at[1, m], ln.end).wait_send()

        n1_rows = x_ref[pl.ds(pl.multiple_of(m * RS, RS), RS), :].astype(F32)
        sO[m] = (rms_parts(n1_rows)[1] * again).astype(BF)
        return 0

    lax.fori_loop(0, NM, settle_sends, 0)
    pair_rows(10, ga_all).wait_send()
    pair_rows(11, gq_all).wait_send()
    pair_rows_in(10, ga_all).wait_recv()
    pair_rows_in(11, gq_all).wait_recv()
    own_keys = pl.ds(pl.multiple_of(ctx * L, L), L)

    def put_late(i, _):
        rows = pl.ds(pl.multiple_of(i * R, R), R)
        place = place_of(i).astype(BF)
        gqkv[0, rows, :] = (gqkv[0, rows, :].astype(F32) + dot_nn(place, gq_all[...])).astype(BF)
        late_ga = dot_nn(place, ga_all[...])
        g_s[rows, :] += late_ga
        ga_s[rows, :] = (ga_s[rows, :].astype(F32) + late_ga).astype(BF)
        return 0

    lax.fori_loop(0, NC, put_late, 0)
    loads[16].wait()
    for which, ref in enumerate((dk_s, dv_s)):
        kv_copy(which).wait()
        gqkv[1 + which] = (ref[own_keys, :] + mid_ref[:, which * Hd : which * Hd + Hd]).astype(BF)
    pair_rows(7, h_all).wait_send()
    pair_rows_in(7, h_all).wait_recv()

    b4, b5, b6 = TAIL_LAGS
    sX = sI
    rE2 = rE
    my_rows = pl.ds(pl.multiple_of(ln.side * half, half), half)
    ot_rows = pl.ds(pl.multiple_of((1 - ln.side) * half, half), half)

    def got_half(rows, flow, m):
        rcopy(gin_ref.at[m, rows, :], gin_ref.at[m, rows, :], ss.at[flow, m], rs.at[flow, m], ln.mid).wait_recv()

    def tail(i, _):
        @pl.when(i < NC)
        def _():
            for s in range(SUBS):
                m = i * SUBS + s
                rows = pl.ds(pl.multiple_of(i * R + s * RS, RS), RS)
                p4 = dot_nt(gqkv[0, rows, :], wqkv[0])
                p4 = p4 + dot_nt(gqkv[1, rows, :], wqkv[1])
                p4 = p4 + dot_nt(gqkv[2, rows, :], wqkv[2])

                @pl.when(ln.is_end)
                def _(m=m, p4=p4):
                    sE[m] = p4.astype(BF)
                    rcopy(sE.at[m], rE2.at[m], ss.at[3, m], rs.at[3, m], ln.mid).start()

                @pl.when(ln.is_mid)
                def _(m=m, p4=p4):
                    part[m] = p4

            rows = pl.ds(pl.multiple_of(i * R, R), R)
            ms = pl.ds(i * SUBS, SUBS)
            place = place_of(i)
            chosen_here = jnp.sum(place, axis=-1, keepdims=True) > 0.5
            place = place.astype(BF)
            new_hid = dot_nn(place, h_all[...])
            old_hid = hid_ref[ms].astype(F32).reshape(R, D)
            hid_ref[ms] = jnp.where(chosen_here, new_hid, old_hid).astype(BF).reshape(SUBS, RS, D)

        j4 = i - b4

        @pl.when(ln.is_mid & (j4 >= 0) & (j4 < NC))
        def _():
            def cross(m):
                got(rE2, 3, m)
                sX[m, pl.ds(0, half), :] = (rE2[m, ot_rows, :].astype(F32) + part[m, ot_rows, :]).astype(BF)
                rcopy(sX.at[m, pl.ds(0, half), :], rX.at[m], ss.at[4, m], rs.at[4, m], ln.other).start()

            each(j4, cross)

        j5 = i - b5

        @pl.when(ln.is_mid & (j5 >= 0) & (j5 < NC))
        def _():
            def settle(m):
                got(rX, 4, m)
                rows = pl.ds(pl.multiple_of(m * RS + ln.side * half, half), half)
                gn1 = part[m, my_rows, :] + rE2[m, my_rows, :].astype(F32) + rX[m].astype(F32)
                gin, gain_rows = rms_back(x_ref[rows, :].astype(F32), again, gn1)
                acc_a[...] += fold8(gain_rows)
                gin_ref[m, my_rows, :] = (g_s[rows, :] + gin).astype(BF)
                mine = gin_ref.at[m, my_rows, :]
                rcopy(mine, mine, ss.at[5, m], rs.at[5, m], ln.other).start()
                rcopy(mine, mine, ss.at[6, m], rs.at[6, m], ln.end).start()

            each(j5, settle)

        j6 = i - b6

        @pl.when(ln.is_mid & (j6 >= 0) & (j6 < NC))
        def _():
            def relay(m):
                got_half(ot_rows, 5, m)
                theirs_m = gin_ref.at[m, ot_rows, :]
                rcopy(theirs_m, theirs_m, ss.at[7, m], rs.at[7, m], ln.end).start()

            each(j6, relay)

        for n, fns in tail_extras.items():
            @pl.when(i == n)
            def _(fns=fns):
                for fn in fns:
                    fn()

        return 0

    tail_extras = {
        0: (lambda: routed_total(0), lambda: dense_second(0), lambda: dense_first(3)),
        1: (lambda: dense_first(2), lambda: dense_first(1)),
        2: (lambda: routed_total(3), lambda: dense_second(3), lambda: dense_second(2)),
        3: (lambda: dense_second(1), lambda: routed_total(1)),
        4: (lambda: routed_total(2), lambda: dense_total(0)),
        5: (lambda: dense_total(3),),
        6: (lambda: dense_total(2),),
    }
    lax.fori_loop(0, NC + b6, tail, 0)

    vec[0:1, :] = jnp.sum(acc_a[...], axis=0, keepdims=True)
    vec[1:2, :] = vec[1:2, :] + jnp.sum(acc_m[...], axis=0, keepdims=True) * (1.0 / NT)
    places = []
    for j in range(NDP):
        for k in range(NCTX):
            if j or k:
                places.append((lax.rem(dp + j, NDP), lax.rem(ctx + k, NCTX)))

    def cols_of(g):
        return pl.ds(pl.multiple_of(g * W, W), W)

    def vec_copy(n):
        d2, c2 = places[n]
        return rcopy(vec.at[:, cols_of(d2 * NCTX + c2)], vbuf.at[me], ts.at[n], tr.at[n], {"dp": d2, "ctx": c2})

    for n in range(G - 1):
        vec_copy(n).start()
    vbuf[me] = vec[:, cols_of(me)]
    for n in range(G - 1):
        vec_copy(n).wait()
    rows_sum = vbuf[0]
    for j in range(1, G):
        rows_sum = rows_sum + vbuf[j]
    hbuf[t] = rows_sum

    def line_copy(n):
        return rcopy(hbuf.at[t], hbuf.at[t], ts.at[G - 1 + n], tr.at[G - 1 + n], tpeers[n])

    for n in range(NT - 1):
        line_copy(n).start()
    dense_total(1)
    for j, p in enumerate(rpeers):
        rcopy(lbuf.at[me], lbuf.at[me], cs.at[j], cr.at[j], p).wait()
    loss = lbuf[0]
    for j in range(1, G):
        loss = loss + lbuf[j]
    loss_ref[...] = loss / (cnt_ref[...] * D)
    for n in range(NT - 1):
        line_copy(n).wait()
    line_sum = hbuf[0]
    for j in range(1, NT):
        line_sum = line_sum + hbuf[j]
    small_o[...] = line_sum

    dense_pair(1).wait_send()
    for n in (3, 4):
        for j in range(1, NT):
            piece_copy(n, j).wait_send()

    def drain(m, _):
        @pl.when(ln.is_end)
        def _():
            got_half(my_rows, 6, m)
            got_half(ot_rows, 7, m)
            rcopy(sE.at[m], rE2.at[m], ss.at[3, m], rs.at[3, m], ln.mid).wait_send()

        @pl.when(ln.is_mid)
        def _():
            rcopy(sX.at[m, pl.ds(0, half), :], rX.at[m], ss.at[4, m], rs.at[4, m], ln.other).wait_send()
            mine = gin_ref.at[m, my_rows, :]
            theirs_m = gin_ref.at[m, ot_rows, :]
            rcopy(mine, mine, ss.at[5, m], rs.at[5, m], ln.other).wait_send()
            rcopy(mine, mine, ss.at[6, m], rs.at[6, m], ln.end).wait_send()
            rcopy(theirs_m, theirs_m, ss.at[7, m], rs.at[7, m], ln.end).wait_send()

        return 0

    lax.fori_loop(0, NM, drain, 0)


CHAIN_LAGS = (1, 2, 4)


def routed_and_backward(x, x2, teacher, valid, cnt, ridx, seg, again, mgain, w_router, saved, w_qkv, w_out, w_up, w_down):
    L, D = x.shape
    S = seg.shape[1]
    RT = ridx.shape[1]
    NT, NDP, NCTX = lax.axis_size("tensor"), lax.axis_size("dp"), lax.axis_size("ctx")
    R = min(BCHUNK, L)
    NC = L // R
    RS = R // SUB
    NM = NC * SUB
    Hd = w_out.shape[1]
    Fl = w_up.shape[2]
    RL = RT // NCTX
    Q = RL // NT
    G = NDP * NCTX
    W = D // G
    HG = Hd // 128
    sizes = (NC, SUB, R, D, L, S, RT, NT, NDP, NCTX, float(S * NDP))
    dma = pltpu.SemaphoreType.DMA
    sd = jax.ShapeDtypeStruct
    v_ = pl.BlockSpec(memory_space=VM)
    a_ = pl.BlockSpec(memory_space=pltpu.HBM)
    shares = [VM((NDP, W, max(Fl, 3 * Hd)), BF)]
    for s in ((W, Fl), (W, Fl), (W, Hd), (W, 3 * Hd)):
        shares += [VM((NDP,) + s, BF)] * 2 + [VM((NDP - 1,) + s, BF)]
    big = VM((NM, RS, D), BF)
    i32 = jnp.int32
    return pl.pallas_call(
        functools.partial(backward_kernel, sizes),
        name="routed_and_backward",
        out_shape=(
            sd((NM, RS, D), BF), sd((8, 128), F32), sd((NM, RS, D), BF),
            sd((2, Fl, W), F32), sd((2, W, Fl), F32), sd((2, Hd, W), F32), sd((2, 3, W, Hd), F32), sd((8, W), F32),
        ),
        in_specs=[v_] * 8 + [a_] * 13,
        out_specs=(v_,) * 8,
        scratch_shapes=[
            VM((L, Hd), BF), VM((S, Hd), BF), VM((S, Hd), BF), VM((L, Hd), BF), VM((L, 128), F32), VM((L, D), F32), VM((L, Fl), F32),
            VM((3, D, Hd), BF), VM((Hd, D), BF), VM((D, Fl), BF), VM((Fl, D), BF), VM((Hd, D), BF), VM((D, Fl), BF), VM((Fl, D), BF),
            VM((L + RL, D), BF), VM((L + RL, Fl), BF), VM((L + RL, Fl), BF), VM((L + RL, D), BF), VM((L, D), BF),
            VM((NM, RS, D), F32), VM((3, L, Hd), BF), VM((S, Hd), F32), VM((S, Hd), F32),
            big, big, big, big, big, VM((NM, RS // 2, D), BF),
            *shares,
            VM((RT, L), BF), VM((RT, D), BF), VM((RT, D), BF), VM((RT, D), BF), VM((RL, D), BF), VM((RT, 128), F32), VM((RL, 128), F32),
            VM((RT, 128), i32), VM((RT, 128), i32), VM((RT, D), BF), VM((RT, Hd), BF), VM((RT, Hd), BF),
            VM((HG, 2 * RL, 128), BF), VM((HG, 2 * RL, RT), F32), VM((RL, Hd), BF), VM((RL, D), BF), VM((RL, Fl), BF), VM((RL, Fl), F32),
            VM((RL, Fl), BF), VM((RL, D), BF), VM((RL, D), BF), VM((3, RL, Hd), BF), VM((2, RT, Hd), F32), VM((2, RL, Hd), F32),
            VM((RL, D), F32), VM((Q, D), F32), VM((Q, D), F32), VM((Q, 128), F32), VM((Q, D), F32), VM((Q, D), F32), VM((Q, D), F32),
            VM((Q, D), F32), VM((RL, D), F32), VM((RL, D), BF), VM((RL, D), BF), VM((RT, D), BF), VM((RT, Hd), BF),
            VM((2, RL, D), BF), VM((5, NT - 1, Q, D), BF),
            VM((RT, Fl), F32), VM((RL, Fl), F32), VM((RT, D), F32), VM((RL, D), F32), VM((RT, Hd), BF), VM((RL, Hd), BF), VM((RT, 128), F32), VM((RL, 128), F32),
            VM((8, D), F32), VM((8, D), F32), VM((8, D), F32), VM((G, 8, 128), F32), VM((8, D), F32), VM((G, 8, W), F32), VM((NT, 8, W), F32),
            dma((17,)), dma((12,)), dma((12,)), pltpu.SemaphoreType.REGULAR((5,)),
            dma((5, NT)), dma((5, NT)), dma((5, NT)), dma((5, NT)), dma((2,)), dma((2,)),
            dma((4,)), dma((4,)), dma((4,)), dma((4,)), dma((4, NDP)), dma((4, NDP)), dma((4, NDP)), dma((4, NDP)),
            dma((G,)), dma((G,)), dma((G + NT,)), dma((G + NT,)), dma((8, NM)), dma((8, NM)),
        ],
        compiler_params=pltpu.CompilerParams(collective_id=2, has_side_effects=True, vmem_limit_bytes=62 << 20),
    )(
        x, valid, cnt, ridx, seg, again, mgain, w_router.reshape(1, D),
        x2, teacher.reshape(NM, RS, D), *saved, w_qkv, w_out, w_up, w_down,
    )


def finish_kernel(
    hid_h, gin_h, dn_h, up_h, out_h, qkv_h, small_h, loss_h,
    hid_o, loss_o, gin_o, ag_o, qkv_o, out_o, mg_o, up_o, dn_o, router_o,
    hid, gin, dn, up, out, qkv, small, loss, wide, sem,
):
    pairs = ((gin_h, gin), (dn_h, dn), (up_h, up), (hid_h, hid), (qkv_h, qkv), (out_h, out), (small_h, small), (loss_h, loss))
    reads = [pltpu.make_async_copy(a, b, sem.at[n]) for n, (a, b) in enumerate(pairs)]
    for cp in reads:
        cp.start()
    backs = ((wide, gin_o), (dn, dn_o), (up, up_o), (hid, hid_o), (qkv, qkv_o), (out, out_o))
    writes = [pltpu.make_async_copy(a, b, sem.at[8 + n]) for n, (a, b) in enumerate(backs)]
    for n in range(6):
        reads[n].wait()
        if n == 0:
            wide[...] = gin[...].astype(F32)
        writes[n].start()
    reads[6].wait()
    reads[7].wait()
    loss_o[...] = loss[0:1, 0:1]
    for j in range(2):
        ag_o[j : j + 1, :] = small[2 * j : 2 * j + 1, :]
        mg_o[j : j + 1, :] = small[2 * j + 1 : 2 * j + 2, :]
    router_o[...] = small[4:5, :]
    for cp in writes:
        cp.wait()


def finish(hid, gin, dn, up, out, qkv, small, loss):
    sd = jax.ShapeDtypeStruct
    v_ = pl.BlockSpec(memory_space=VM)
    h_ = pl.BlockSpec(memory_space=pltpu.HBM)
    W = small.shape[1]

    def like(arr):
        return sd(arr.shape, arr.dtype)

    ins = (hid, gin, dn, up, out, qkv, small, loss)
    return pl.pallas_call(
        finish_kernel,
        name="finish",
        out_shape=(like(hid), sd((1, 1), F32), sd(gin.shape, F32), sd((2, W), F32), like(qkv), like(out), sd((2, W), F32), like(up), like(dn), sd((1, W), F32)),
        in_specs=[h_] * 8,
        out_specs=(h_, v_, h_, v_, h_, h_, v_, h_, h_, v_),
        scratch_shapes=[*[VM(a.shape, a.dtype) for a in ins], VM(gin.shape, F32), pltpu.SemaphoreType.DMA((14,))],
        compiler_params=pltpu.CompilerParams(vmem_limit_bytes=60 << 20),
    )(*ins)


def fast_local(hidden_in, teacher, seg_ids, valid, routed_idx, attn_gain, w_qkv, w_out, mlp_gain, w_up, w_down, w_router):
    L, D = hidden_in.shape[1:]
    x2, *saved, cnt = dense_forward(hidden_in[0], attn_gain, mlp_gain, seg_ids, valid, w_qkv, w_out, w_up, w_down)
    hid, loss, gin, dn, up, out, qkv, small = routed_and_backward(
        hidden_in[0], x2, teacher[0], valid, cnt, routed_idx, seg_ids, attn_gain, mlp_gain, w_router, saved, w_qkv, w_out, w_up, w_down
    )
    hid, loss, gin, ag, qkv, out, mg, up, dn, router = finish(hid, gin, dn, up, out, qkv, small, loss)
    return (hid.reshape(1, L, D), loss[0, 0], gin.reshape(1, L, D), ag, qkv, out, mg, up, dn, router[0])


def takes_kernels(mesh):
    shape = dict(mesh.shape)
    return shape["tensor"] == 4 and shape["ctx"] == 2


def solution(mesh):
    placed = (
        P("dp", "ctx", None),
        P("dp", "ctx", None),
        P("dp", None),
        P("dp", "ctx"),
        P("dp", None),
        P(),
        P(None, None, None, "tensor"),
        P(None, "tensor", None),
        P(),
        P(None, None, "tensor"),
        P(None, "tensor", None),
        P(),
    )
    return jax.shard_map(
        fast_local if takes_kernels(mesh) else plain_local,
        mesh=mesh,
        in_specs=placed,
        out_specs=(
            P("dp", "ctx", None),
            P(),
            P("dp", "ctx", None),
            P(None, ("dp", "ctx")),
            P(None, None, ("dp", "ctx"), "tensor"),
            P(None, "tensor", ("dp", "ctx")),
            P(None, ("dp", "ctx")),
            P(None, ("dp", "ctx"), "tensor"),
            P(None, "tensor", ("dp", "ctx")),
            P(("dp", "ctx")),
        ),
        check_vma=False,
    )
```
